32 devices in a mesh: seq: 2 (over y), group: 8 (over z, x), replica: 2 (over core).
Axes of the slice: x: 2, y: 2, z: 4, core: 2. Of those that a mesh axis runs over, the one named last changes fastest.
Arguments:
- tokens: bfloat16 [16, 1024, 1024], P(('group', 'replica'), 'seq'), may hold values from -6 to 6
- ffn_in: bfloat16 [2, 1024, 4096], P(None, 'group'), may hold values from -0.1875 to 0.1875
- ffn_out: bfloat16 [2, 4096, 1024], P(None, 'group'), may hold values from -0.09375 to 0.09375
- qkv: bfloat16 [3, 1024, 1024], P(None, 'group'), may hold values from -0.1875 to 0.1875
- attn_out: bfloat16 [1024, 1024], P('group'), may hold values from -1.5 to 1.5
- conv_in: bfloat16 [1024, 2048], P('group'), may hold values from -0.1875 to 0.1875
- conv_out: bfloat16 [1024, 1024], P('group'), may hold values from -0.1875 to 0.1875
- depthwise: bfloat16 [31, 1024], P(None, 'group'), may hold values from -1 to 1
- gains: bfloat16 [6, 1024], P(None, 'group'), may hold values from 0.5 to 1.5
- rel_table: bfloat16 [73, 64], replicated, may hold values from -6 to 6
- cotangent: bfloat16 [16, 1024, 1024], P(('group', 'replica'), 'seq'), may hold values from -6 to 6
Outputs:
- output: bfloat16 [16, 1024, 1024], P(('group', 'replica'), 'seq')
- input_grad: bfloat16 [16, 1024, 1024], P(('group', 'replica'), 'seq')
- grad_ffn_in: float32 [2, 1024, 4096], P(None, 'group')
- grad_ffn_out: float32 [2, 4096, 1024], P(None, 'group')
- grad_qkv: float32 [3, 1024, 1024], P(None, 'group')
- grad_attn_out: float32 [1024, 1024], P('group')
- grad_conv_in: float32 [1024, 2048], P('group')
- grad_conv_out: float32 [1024, 1024], P('group')
- grad_depthwise: float32 [31, 1024], P(None, 'group')
- grad_gains: float32 [6, 1024], P(None, 'group')
- grad_rel_table: float32 [73, 64], replicated
- stats: float32 [5], replicated
The draws below stay inside these ranges and needn't reach their ends.
All inputs are finite; a program needn't handle non-finite values.
Results may differ from the reference program's by a relative error of at most 0.023.
Values may be sent and summed in bfloat16 or wider, within the bound.
A program may use at most 320 MiB of HBM per device.

```python
import jax
import jax.numpy as jnp
from jax import lax

D = 1024
HEADS = 16
HEAD_DIM = 64
FF = 4096
KERNEL = 31
LEFT = 64
RIGHT = 8
WIN = 73
CLIP_LEN = 1024
CLIPS = 16


def shard_levels(rng, dims, pieces, low, high):
    factor_of, own = 1.0, jax.random.fold_in(rng, 6)
    for axis_at, blocks in pieces:
        draws = jnp.exp(jax.random.uniform(jax.random.fold_in(own, axis_at), (blocks,), jnp.float32, low / len(pieces), high / len(pieces)))
        factor_of = factor_of * jnp.repeat(draws, dims[axis_at] // blocks).reshape([-1 if axis == axis_at else 1 for axis in range(len(dims))])
    return factor_of


def scatter_about(stream_key, shape, width, limit, cuts=(), kind=jnp.bfloat16):
    drawn = width * jax.random.normal(stream_key, shape, jnp.float32)
    if cuts:
        drawn = drawn * shard_levels(stream_key, shape, cuts, -0.22, 0.18)
    return jnp.clip(drawn, -limit, limit).astype(kind)


def setup_inputs(seed: int = 0) -> dict:
    seeds = jax.random.split(jax.random.key(seed), 12)
    return {
        "tokens": scatter_about(seeds[0], (CLIPS, CLIP_LEN, D), 1.0, 6.0, ((0, 16), (1, 2))),
        "ffn_in": scatter_about(seeds[1], (2, D, FF), D ** -0.5, 0.1875, ((1, 8),)),
        "ffn_out": scatter_about(seeds[2], (2, FF, D), FF ** -0.5, 0.09375, ((1, 8),)),
        "qkv": scatter_about(seeds[3], (3, D, D), D ** -0.5, 0.1875, ((1, 8),)),
        "attn_out": scatter_about(seeds[4], (D, D), (D // 64) ** -0.5, 1.5, ((0, 8),)),
        "conv_in": scatter_about(seeds[5], (D, 2 * D), D ** -0.5, 0.1875, ((0, 8),)),
        "conv_out": scatter_about(seeds[6], (D, D), D ** -0.5, 0.1875, ((0, 8),)),
        "depthwise": scatter_about(seeds[7], (KERNEL, D), KERNEL ** -0.5, 1.0, ((1, 8),)),
        "gains": jnp.clip(1.0 + 0.1 * jax.random.normal(seeds[8], (6, D), jnp.float32), 0.5, 1.5).astype(jnp.bfloat16),
        "rel_table": scatter_about(seeds[9], (WIN, HEAD_DIM), 1.0, 6.0),
        "cotangent": scatter_about(seeds[10], (CLIPS, CLIP_LEN, D), 1.0, 6.0, ((0, 16), (1, 2))),
    }


EPSILON = 1e-05
HIGHEST = lax.Precision.HIGHEST
NEGATIVE = -1e+30

@jax.custom_vjp
def low(v):
    return lax.optimization_barrier(v.astype(jnp.bfloat16)).astype(jnp.float32)

@jax.custom_vjp
def low_back(v):
    return v

def low_keep(v):
    return (low(v), None)

def low_pass(kept, grad):
    return (grad,)

def back_keep(v):
    return (v, None)

def back_low(kept, grad):
    return (low(grad),)
low.defvjp(low_keep, low_pass)
low_back.defvjp(back_keep, back_low)

def both_low(values):
    return low(low_back(values))

def layer_norm(values, gain):
    centered = values - lax.optimization_barrier(jnp.mean(values, -1, keepdims=True))
    inverse = lax.rsqrt(lax.optimization_barrier(jnp.mean(centered * centered, -1, keepdims=True)) + EPSILON)
    return centered * inverse * gain

def matmul(left, right):
    return jnp.dot(left, right, precision=HIGHEST)

def swish(values):
    return values * jax.nn.sigmoid(values)

def skew(relative, span):
    rows = relative.shape[-2]
    lead = relative.shape[:-2]
    padded = jnp.pad(relative, [(0, 0)] * len(lead) + [(0, 0), (0, span + 1 - relative.shape[-1])])
    flat = padded.reshape(lead + (rows * (span + 1),))[..., :rows * span]
    return flat.reshape(lead + (rows, span))

def feed_forward(resid, gain, w_in, w_out):
    entry = low(layer_norm(resid, gain))
    hidden_pre = low_back(matmul(entry, w_in))
    hidden = low(swish(hidden_pre))
    return low_back(matmul(hidden, w_out))

def attention(resid, gain, qkv, attn_out, table):
    entry = low(layer_norm(resid, gain))
    query = both_low(matmul(entry, qkv[0])).reshape(CLIP_LEN, HEADS, HEAD_DIM)
    keys = both_low(matmul(entry, qkv[1])).reshape(CLIP_LEN, HEADS, HEAD_DIM)
    values = both_low(matmul(entry, qkv[2])).reshape(CLIP_LEN, HEADS, HEAD_DIM)
    rows = min(512, CLIP_LEN)
    span = LEFT + rows + RIGHT
    key_pad = jnp.pad(keys, ((LEFT, RIGHT), (0, 0), (0, 0)))
    value_pad = jnp.pad(values, ((LEFT, RIGHT), (0, 0), (0, 0)))
    scale = HEAD_DIM ** (-0.5)
    row_ids = jnp.arange(rows).astype(jnp.int32)[:, None]
    col_ids = jnp.arange(span).astype(jnp.int32)[None, :]
    band = (col_ids - row_ids >= 0) & (col_ids - row_ids < WIN)

    def block(start):
        query_block = lax.dynamic_slice_in_dim(query, start, rows, 0)
        key_block = lax.dynamic_slice_in_dim(key_pad, start, span, 0)
        value_block = lax.dynamic_slice_in_dim(value_pad, start, span, 0)
        place = start + col_ids - LEFT
        mask = band & (place >= 0) & (place < CLIP_LEN)
        direct = jnp.einsum('shd,uhd->hsu', query_block, key_block, precision=HIGHEST)
        relative = jnp.einsum('shd,wd->hsw', query_block, table, precision=HIGHEST)
        raw = low_back((direct + skew(relative, span)) * scale)
        raw = jnp.where(mask[None], raw, NEGATIVE)
        probs = jax.nn.softmax(raw, axis=-1)
        return jnp.einsum('hsu,uhd->shd', low(probs), value_block, precision=HIGHEST)
    starts = (jnp.arange(CLIP_LEN // rows) * rows).astype(jnp.int32)
    mixed = lax.map(jax.checkpoint(block), starts)
    mixed = both_low(mixed.reshape(CLIP_LEN, D))
    return low_back(matmul(mixed, attn_out))

def convolution(resid, gain_in, gain_mid, conv_in, depthwise, conv_out):
    entry = low(layer_norm(resid, gain_in))
    joined = low_back(matmul(entry, conv_in))
    glu = low(joined[:, :D] * jax.nn.sigmoid(joined[:, D:]))
    padded = jnp.pad(glu, ((KERNEL - 1, 0), (0, 0)))
    summed = jnp.zeros(glu.shape, jnp.float32)
    for tap in range(KERNEL):
        summed = summed + depthwise[tap] * padded[tap:tap + CLIP_LEN]
    swished = low(swish(layer_norm(summed, gain_mid)))
    return low_back(matmul(swished, conv_out))

def layer(clip, ffn_in, ffn_out, qkv, attn_out, conv_in, conv_out, depthwise, gains, table):
    first = feed_forward(clip, gains[0], ffn_in[0], ffn_out[0])
    after_first = clip + 0.5 * first
    attn = attention(after_first, gains[1], qkv, attn_out, table)
    after_attn = after_first + attn
    conv = convolution(after_attn, gains[2], gains[3], conv_in, depthwise, conv_out)
    after_conv = after_attn + conv
    second = feed_forward(after_conv, gains[4], ffn_in[1], ffn_out[1])
    final = after_conv + 0.5 * second
    result = layer_norm(final, gains[5])
    squares = jnp.stack([jnp.sum(member * member) for member in (final, first, attn, conv, second)])
    return (result, squares)

def reference(tokens, ffn_in, ffn_out, qkv, attn_out, conv_in, conv_out, depthwise, gains, rel_table, cotangent):
    weights = tuple((w.astype(jnp.float32) for w in (ffn_in, ffn_out, qkv, attn_out, conv_in, conv_out, depthwise, gains, rel_table)))

    def step(carry, item):
        sums, square_sum = carry
        clip, grad_out = item
        result, pullback, squares = jax.vjp(layer, clip.astype(jnp.float32), *weights, has_aux=True)
        grads = pullback(grad_out.astype(jnp.float32))
        sums = tuple((total + grad for total, grad in zip(sums, grads[1:])))
        return ((sums, square_sum + squares), (result.astype(jnp.bfloat16), grads[0].astype(jnp.bfloat16)))
    init = (tuple((jnp.zeros(w.shape, jnp.float32) for w in weights)), jnp.zeros((5,), jnp.float32))
    (sums, square_sum), (output, input_grad) = lax.scan(step, init, (tokens, cotangent))
    stats = jnp.sqrt(square_sum / (CLIPS * CLIP_LEN * D))
    return (output, input_grad, sums[0], sums[1], sums[2], sums[3], sums[4], sums[5], sums[6], sums[7], sums[8], stats)
```

```python
import functools

import jax
import jax.numpy as jnp
from jax import lax
from jax.experimental import pallas as pl
from jax.experimental.pallas import tpu as pltpu
from jax.sharding import PartitionSpec as P

HEAD_DIM = 64
KERNEL = 31
LEFT = 64
RIGHT = 8
WIN = 73
LANES = 128
BLOCK = 128
SPAN = 256
BACK_PAD = 64


EPSILON = 1e-05
NEGATIVE = -1e30


MESH = pl.DeviceIdType.MESH


def from_behind(value, axis, steps):
    count = lax.axis_size(axis)
    initial, last = (max(0, -steps), min(count, count - steps))
    return lax.ppermute(value, axis, [(source, source + steps) for source in range(initial, last)])


def norm_forward(values, gain):
    centered = values - jnp.mean(values, -1, keepdims=True)
    inverse = lax.rsqrt(jnp.mean(centered * centered, -1, keepdims=True) + EPSILON)
    normal = centered * inverse
    return (normal * gain, normal, inverse)


def norm_backward(grad_out, normal, inverse, gain):
    grad_normal = grad_out * gain
    grad_in = inverse * (
        grad_normal
        - jnp.mean(grad_normal, -1, keepdims=True)
        - normal * jnp.mean(grad_normal * normal, -1, keepdims=True)
    )
    grad_gain = jnp.sum(grad_out * normal, 0)
    return (grad_in, grad_gain)


def matmul(left, right):
    return jnp.dot(left, right, preferred_element_type=jnp.float32)


def matmul_left_t(left, right):
    return lax.dot_general(
        left, right, (((0,), (0,)), ((), ())), preferred_element_type=jnp.float32
    )


def matmul_right_t(left, right):
    return lax.dot_general(
        left, right, (((1,), (1,)), ((), ())), preferred_element_type=jnp.float32
    )


def swish_grad(values):
    logistic = jax.nn.sigmoid(values)
    return logistic + values * logistic * (1.0 - logistic)


def nt(left,right):
    return lax.dot_general(left,right,(((1,),(1,)),((),())),preferred_element_type=jnp.float32)
def tn(left,right):
    return lax.dot_general(left,right,(((0,),(0,)),((),())),preferred_element_type=jnp.float32)
def nn(left,right):
    return jnp.dot(left,right,preferred_element_type=jnp.float32)

def block_mask(first, block, limit):
    rows=lax.broadcasted_iota(jnp.int32,(BLOCK,SPAN),0)
    cols=lax.broadcasted_iota(jnp.int32,(BLOCK,SPAN),1)
    offset=cols-rows
    place=first+block*BLOCK+cols-LEFT
    return (offset>=0)&(offset<WIN)&(place>=0)&(place<limit)

def head_lanes(head):
    lanes=lax.broadcasted_iota(jnp.int32,(BLOCK,LANES),1)
    return (lanes>=head*HEAD_DIM)&(lanes<(head+1)*HEAD_DIM)

def block_probs(query, keys, table, mask):
    relative=pltpu.roll(nt(query,table),0,1,stride=1,stride_axis=0)
    raw=jnp.where(mask,(nt(query,keys)+relative)*(HEAD_DIM**-0.5),NEGATIVE)
    expo=jnp.exp(raw-jnp.max(raw,-1,keepdims=True))
    return expo*(1.0/jnp.sum(expo,-1,keepdims=True))

def attend_kernel(limit, first_ref, q_ref, k_ref, v_ref, t_ref, c_ref):
    table=t_ref[...]
    zero=jnp.zeros((BLOCK,LANES),jnp.bfloat16)
    for block in range(q_ref.shape[1]//BLOCK):
        rows=pl.ds(block*BLOCK,BLOCK); span=pl.ds(block*BLOCK,SPAN)
        query=q_ref[0,rows,:]; keys=k_ref[0,span,:]; values=v_ref[0,span,:]
        mask=block_mask(first_ref[0],block,limit)
        mixed=[]
        for head in range(2):
            probs=block_probs(jnp.where(head_lanes(head),query,zero),keys,table,mask)
            mixed.append(nn(probs.astype(jnp.bfloat16),values))
        c_ref[0,rows,:]=jnp.where(head_lanes(0),mixed[0],mixed[1]).astype(jnp.bfloat16)

def attend_back_kernel(limit, first_ref, q_ref, k_ref, v_ref, t_ref, g_ref, dq_ref, dk_ref, dv_ref, dt_ref, dk_sum, dv_sum):
    table=t_ref[...]
    zero=jnp.zeros((BLOCK,LANES),jnp.bfloat16)
    flip=(lax.broadcasted_iota(jnp.int32,(BLOCK,BLOCK),0)+lax.broadcasted_iota(jnp.int32,(BLOCK,BLOCK),1)==BLOCK-1).astype(jnp.float32).astype(jnp.bfloat16)
    dk_sum[...]=jnp.zeros_like(dk_sum); dv_sum[...]=jnp.zeros_like(dv_sum)
    @pl.when((pl.program_id(0)==0)&(pl.program_id(1)==0))
    def _(): dt_ref[...]=jnp.zeros_like(dt_ref)
    for block in range(q_ref.shape[1]//BLOCK):
        rows=pl.ds(block*BLOCK,BLOCK); span=pl.ds(block*BLOCK,SPAN)
        keys=k_ref[0,span,:]; values=v_ref[0,span,:]
        mask=block_mask(first_ref[0],block,limit)
        grad_query=[]
        for head in range(2):
            query=jnp.where(head_lanes(head),q_ref[0,rows,:],zero)
            grad=jnp.where(head_lanes(head),g_ref[0,rows,:],zero)
            probs=block_probs(query,keys,table,mask)
            grad_probs=nt(grad,values)
            grad_raw=probs*(grad_probs-jnp.sum(probs*grad_probs,-1,keepdims=True))
            grad_raw=grad_raw.astype(jnp.bfloat16)
            turned=pltpu.roll(nn(flip,grad_raw),SPAN-BLOCK+1,1,stride=1,stride_axis=0)
            unskewed=nn(flip,turned.astype(jnp.bfloat16)).astype(jnp.bfloat16)
            dv_sum[span,:]+=tn(probs.astype(jnp.bfloat16),grad)
            dk_sum[span,:]+=tn(grad_raw,query)
            dt_ref[...]+=tn(unskewed,query)
            grad_query.append(nn(grad_raw,keys)+nn(unskewed,table))
        dq_ref[0,rows,:]=(jnp.where(head_lanes(0),grad_query[0],grad_query[1])*(HEAD_DIM**-0.5)).astype(jnp.bfloat16)
    dk_ref[0]=(dk_sum[...]*(HEAD_DIM**-0.5)).astype(jnp.bfloat16)
    dv_ref[0]=dv_sum[...].astype(jnp.bfloat16)

def wide_table(table):
    return jnp.tile(jnp.pad(table,((0,SPAN-table.shape[0]),(0,0))),(1,LANES//HEAD_DIM))

def specs(clips,rows,width):
    own=pl.BlockSpec((1,rows,LANES),lambda c,h:(c,0,h))
    ext=pl.BlockSpec((1,rows+LEFT+BACK_PAD,LANES),lambda c,h:(c,0,h))
    tab=pl.BlockSpec((SPAN,LANES),lambda c,h:(0,0))
    return (pl.BlockSpec(memory_space=pltpu.SMEM),own,ext,tab),(clips,width//LANES)

def attend(query,keys,values,table,rows):
    clips,_,width=query.shape
    first=lax.axis_index('seq').astype(jnp.int32)[None]*rows
    limit=rows*lax.axis_size('seq')
    (sc,own,ext,tab),grid=specs(clips,rows,width)
    return pl.pallas_call(functools.partial(attend_kernel,limit),grid=grid,
        in_specs=[sc,own,ext,ext,tab],out_specs=own,
        out_shape=jax.ShapeDtypeStruct(query.shape,jnp.bfloat16),name="attend",
    )(first,query,keys,values,wide_table(table))

def attend_back(query,keys,values,table,grad,rows):
    clips,_,width=query.shape
    first=lax.axis_index('seq').astype(jnp.int32)[None]*rows
    limit=rows*lax.axis_size('seq')
    (sc,own,ext,tab),grid=specs(clips,rows,width)
    dq,dk,dv,dt=pl.pallas_call(functools.partial(attend_back_kernel,limit),grid=grid,
        in_specs=[sc,own,ext,ext,tab,own],out_specs=[own,ext,ext,tab],
        out_shape=[jax.ShapeDtypeStruct(query.shape,jnp.bfloat16),jax.ShapeDtypeStruct(keys.shape,jnp.bfloat16),jax.ShapeDtypeStruct(keys.shape,jnp.bfloat16),jax.ShapeDtypeStruct((SPAN,LANES),jnp.float32)],
        scratch_shapes=[pltpu.VMEM((rows+LEFT+BACK_PAD,LANES),jnp.float32)]*2,name="attend_back",
    )(first,query,keys,values,wide_table(table),grad)
    return dq,dk,dv,(dt[:WIN,:HEAD_DIM]+dt[:WIN,HEAD_DIM:])*(HEAD_DIM**-0.5)
def depth_of():
    return lax.axis_size("group") // 2


def place():
    group = lax.axis_index("group")
    return (group // 2, group % 2, lax.axis_index("seq"), lax.axis_index("replica"))


def greet(peers):
    barrier = pltpu.get_barrier_semaphore()
    for peer in peers:
        pl.semaphore_signal(barrier, inc=1, device_id=peer, device_id_type=MESH)
    pl.semaphore_wait(barrier, len(peers))


def neighbours():
    z, x, seq, replica = place()
    depth = depth_of()
    deep = [{"group": (z + steps) % depth * 2 + x} for steps in range(1, depth)]
    across = {"group": z * 2 + 1 - x}
    beside = {"seq": 1 - seq}
    twin = {"replica": 1 - replica}
    return (deep, across, beside, twin)


class Gather:
    def __init__(self, source, target, cut, low, high, rows, sends, recvs, at):
        depth = depth_of()
        self.source, self.target, self.cut, self.low, self.rows = (source, target, cut, low, rows)
        self.piece = (high - low) // (1, 2, 4)[cut]
        self.sends, self.recvs, self.at = (sends, recvs, at)
        self.z, self.x, self.seq, self.replica = place()
        self.deep, self.across, self.beside, self.twin = neighbours()
        self.depth = depth
        self.firsts = (0, depth - 1, 2 * depth - 1, 4 * depth - 2)
        self.started = []

    def spot(self, ref, owner, dy, dc):
        part = 0
        if self.cut:
            part = (self.replica + dc) % 2
        if self.cut == 2:
            part = part + 2 * ((self.seq + dy) % 2)
        first = pl.multiple_of(owner * self.rows + self.low + part * self.piece, self.piece)
        return ref.at[:, pl.ds(first, self.piece)]

    def owner(self, steps, dx):
        return (self.z + self.depth - steps) % self.depth * 2 + (self.x + dx) % 2

    def copy(self, steps, dx, dy, dc, kind, index, peer):
        mine = steps == 0 and dx == 0
        slot = self.at + self.firsts[kind] + index
        spot = self.spot(self.target, self.owner(steps, dx), dy, dc)
        return pltpu.make_async_remote_copy(
            src_ref=self.spot(self.source, 0, dy, dc) if mine else spot,
            dst_ref=spot,
            send_sem=self.sends.at[slot],
            recv_sem=self.recvs.at[slot],
            device_id=peer,
            device_id_type=MESH,
        )

    def send(self, copy):
        copy.start()
        self.started.append(copy)

    def to_beside(self, steps, dx):
        if self.cut == 2:
            index = dx * self.depth + steps - 1
            self.send(self.copy(steps, dx, 0, 0, 2, index, self.beside))

    def to_twin(self, steps, dx, dy):
        if self.cut:
            index = dy * (2 * self.depth - 1) + dx * self.depth + steps - 1
            self.send(self.copy(steps, dx, dy, 0, 3, index, self.twin))

    def open(self):
        for steps, peer in enumerate(self.deep, 1):
            self.send(self.copy(0, 0, 0, 0, 0, steps - 1, peer))
        self.send(self.copy(0, 0, 0, 0, 1, 0, self.across))

    def got(self, steps, dx, dy, dc, kind, index):
        self.copy(steps or self.depth, dx, dy, dc, kind, index, self.twin).wait_recv()

    def forward_deep(self):
        for steps in range(1, self.depth):
            self.got(steps, 0, 0, 0, 0, steps - 1)
            self.send(self.copy(steps, 0, 0, 0, 1, steps, self.across))
            self.to_beside(steps, 0)
            self.to_twin(steps, 0, 0)

    def forward_across(self):
        for steps in range(self.depth):
            self.got(steps, 1, 0, 0, 1, steps)
            self.to_beside(steps, 1)
            self.to_twin(steps, 1, 0)

    def others(self):
        return [(steps, dx) for dx in range(2) for steps in range(self.depth) if steps or dx]

    def forward_beside(self):
        if self.cut == 2:
            for steps, dx in self.others():
                self.got(steps, dx, 1, 0, 2, dx * self.depth + steps - 1)
                self.to_twin(steps, dx, 1)

    def close(self):
        if self.cut:
            for dy in range(self.cut):
                for steps, dx in self.others():
                    index = dy * (2 * self.depth - 1) + dx * self.depth + steps - 1
                    self.got(steps, dx, dy, 1, 3, index)
        for copy in self.started:
            copy.wait_send()


def gather_kernel(plan, count, *refs):
    ins, outs = (refs[:count], refs[count : count + len(plan)])
    helds, (sends, recvs, local) = (refs[count + len(plan) : -3], refs[-3:])
    deep, across, beside, twin = neighbours()
    peers = deep + [across, twin]
    if any(cut == 2 for _, _, cut, _ in plan):
        peers.append(beside)
    greet(peers)
    loads = [
        pltpu.make_async_copy(ins[at], held, local.at[0, at]) for at, held in enumerate(helds)
    ]
    for load in loads:
        load.start()
    jobs, stores, at = ([], [], 0)
    for number, (source, layers, cut, chunks) in enumerate(plan):
        ref = ins[source].at[pl.ds(layers[0], layers[1])]
        rows = ins[source].shape[1]
        for chunk in range(chunks):
            low, high = (rows * chunk // chunks, rows * (chunk + 1) // chunks)
            jobs.append(Gather(ref, outs[number], cut, low, high, rows, sends, recvs, at))
            at += (2, 6, 8)[cut] * depth_of()
    z, x, _, _ = place()
    ready = set()
    for tick in range(len(jobs) + 4):
        if tick < len(jobs):
            jobs[tick].open()
        if 1 <= tick < len(jobs) + 1:
            jobs[tick - 1].forward_deep()
        if 2 <= tick < len(jobs) + 2:
            jobs[tick - 2].forward_across()
        if 3 <= tick < len(jobs) + 3:
            jobs[tick - 3].forward_beside()
        if 4 <= tick:
            jobs[tick - 4].close()
        if tick < len(plan):
            source, layers, _, _ = plan[tick]
            if source not in ready:
                loads[source].wait()
                ready.add(source)
            rows = ins[source].shape[1]
            first = pl.multiple_of((z * 2 + x) * rows, rows)
            store = pltpu.make_async_copy(
                helds[source].at[pl.ds(layers[0], layers[1])],
                outs[tick].at[:, pl.ds(first, rows)],
                local.at[1, tick],
            )
            store.start()
            stores.append(store)
    for store in stores:
        store.wait()


def gather_weights(shards, plan):
    groups = lax.axis_size("group")
    total = sum((2, 6, 8)[cut] * depth_of() * chunks for _, _, cut, chunks in plan)
    return pl.pallas_call(
        functools.partial(gather_kernel, plan, len(shards)),
        in_specs=[pl.BlockSpec(memory_space=pl.ANY)] * len(shards),
        out_specs=[pl.BlockSpec(memory_space=pl.ANY)] * len(plan),
        out_shape=[
            jax.ShapeDtypeStruct(
                (layers[1], groups * shards[source].shape[1], shards[source].shape[2]), jnp.bfloat16
            )
            for source, layers, _, _ in plan
        ],
        scratch_shapes=[pltpu.VMEM(shard.shape, jnp.bfloat16) for shard in shards]
        + [
            pltpu.SemaphoreType.DMA((total,)),
            pltpu.SemaphoreType.DMA((total,)),
            pltpu.SemaphoreType.DMA((2, len(plan))),
        ],
        compiler_params=pltpu.CompilerParams(
            collective_id=1, has_side_effects=True, vmem_limit_bytes=24 << 20
        ),
        name="gather_weights",
    )(*shards)


def swap(value, axis, bit=1):
    return lax.ppermute(value, axis, [(i, i ^ bit) for i in range(lax.axis_size(axis))])


def along_depth(value, steps):
    depth = depth_of()
    pairs = [(i, (i // 2 + steps) % depth * 2 + i % 2) for i in range(2 * depth)]
    return lax.ppermute(value, "group", pairs)


def butterfly(value):
    for axis in ("replica", "seq", "group"):
        bit = 1
        while bit < lax.axis_size(axis):
            value = value + swap(value, axis, bit)
            bit *= 2
    return value


def reduce_gradient(left, right, halve):
    own_z, own_x, own_seq, own_replica = place()
    depth = depth_of()
    rows = left.shape[1] // (2 * depth)
    half = right.shape[1] // 2
    size = half // 2 if halve else half

    def product(part, replica, seq):
        first = replica * half + (seq * size if halve else 0)
        return matmul_left_t(part, lax.dynamic_slice_in_dim(right, first, size, 1))

    def side(value, x, axis):
        lead = value.shape[:axis]
        split = value.reshape(lead + (depth, 2, rows) + value.shape[axis + 1 :])
        picked = lax.dynamic_index_in_dim(split, x, axis + 1, False)
        return picked.reshape(lead + (depth * rows,) + value.shape[axis + 1 :])

    arrived = []
    if halve:
        far = swap(product(left, 1 - own_replica, 1 - own_seq).astype(jnp.bfloat16), "replica")
        arrived.append(swap(product(left, 1 - own_replica, own_seq).astype(jnp.bfloat16), "replica"))
        far = product(left, own_replica, 1 - own_seq) + far.astype(jnp.float32)
        arrived.append(swap(far.astype(jnp.bfloat16), "seq"))
    else:
        arrived.append(swap(product(left, 1 - own_replica, 0).astype(jnp.bfloat16), "replica"))

    def near(x):
        total = product(side(left, x, 1), own_replica, own_seq)
        for member in arrived:
            total = total + side(member, x, 0).astype(jnp.float32)
        return total

    away = swap(near((own_x + 1) % 2).astype(jnp.bfloat16), "group")
    mine = (near(own_x) + away.astype(jnp.float32)).astype(jnp.bfloat16).reshape(depth, rows, size)
    total = lax.dynamic_index_in_dim(mine, own_z, 0, False).astype(jnp.float32)
    for steps in range(1, depth):
        sent = lax.dynamic_index_in_dim(mine, (own_z + steps) % depth, 0, False)
        total = total + along_depth(sent, steps).astype(jnp.float32)
    owned = total.astype(jnp.bfloat16)
    if halve:
        other = swap(owned, "seq")
        owned = jnp.where(
            own_seq == 0, jnp.concatenate([owned, other], 1), jnp.concatenate([other, owned], 1)
        )
    else:
        bit = 1
        while bit < lax.axis_size("seq"):
            owned = owned.astype(jnp.float32) + swap(owned, "seq", bit).astype(jnp.float32)
            owned = owned.astype(jnp.bfloat16)
            bit *= 2
    other = swap(owned, "replica")
    owned = jnp.where(
        own_replica == 0, jnp.concatenate([owned, other], 1), jnp.concatenate([other, owned], 1)
    )
    return owned.astype(jnp.float32)


def feed_forward(resid, gain, w_in, w_out):
    normed, normal, inverse = norm_forward(resid, gain)
    entry = normed.astype(jnp.bfloat16)
    hidden_pre = matmul(entry, w_in)
    hidden = (hidden_pre * jax.nn.sigmoid(hidden_pre)).astype(jnp.bfloat16)
    return (matmul(hidden, w_out), (normal, inverse, entry, hidden_pre, hidden))


def feed_back(grad_branch, kept, gain, w_in, w_out, halve):
    normal, inverse, entry, hidden_pre, hidden = kept
    grad_low = grad_branch.astype(jnp.bfloat16)
    grad_w_out = reduce_gradient(hidden, grad_low, halve)
    grad_hidden = (matmul_right_t(grad_low, w_out) * swish_grad(hidden_pre)).astype(jnp.bfloat16)
    grad_w_in = reduce_gradient(entry, grad_hidden, halve)
    grad_in, grad_gain = norm_backward(matmul_right_t(grad_hidden, w_in), normal, inverse, gain)
    return (grad_in, grad_gain, grad_w_in, grad_w_out)


def attention_forward(resid, gain, qkv, attn_out, table, shape):
    clips, rows, width = shape
    normed, normal, inverse = norm_forward(resid, gain)
    entry = normed.astype(jnp.bfloat16)
    query, keys, values = [
        matmul(entry, qkv[part]).astype(jnp.bfloat16).reshape(shape) for part in range(3)
    ]
    tail = jnp.zeros((clips, BACK_PAD - RIGHT, width), jnp.bfloat16)

    def extend(value):
        before = from_behind(value[:, rows - LEFT :], "seq", 1)
        after = from_behind(value[:, :RIGHT], "seq", -1)
        return jnp.concatenate([before, value, after, tail], 1)

    keys, values = (extend(keys), extend(values))
    mixed = attend(query, keys, values, table, rows).reshape(clips * rows, width)
    return (matmul(mixed, attn_out), (normal, inverse, entry, query, keys, values, mixed))


def attention_back(grad_branch, kept, gain, qkv, attn_out, table, shape):
    clips, rows, width = shape
    normal, inverse, entry, query, keys, values, mixed = kept
    grad_low = grad_branch.astype(jnp.bfloat16)
    grad_attn_out = reduce_gradient(mixed, grad_low, False)
    grad_mixed = matmul_right_t(grad_low, attn_out).astype(jnp.bfloat16).reshape(shape)
    grad_query, grad_keys, grad_values, grad_table = attend_back(
        query, keys, values, table, grad_mixed, rows
    )

    def fold(grad):
        from_later = from_behind(grad[:, :LEFT], "seq", -1).astype(jnp.float32)
        from_earlier = from_behind(grad[:, LEFT + rows : LEFT + rows + RIGHT], "seq", 1)
        own = grad[:, LEFT : LEFT + rows].astype(jnp.float32)
        own = own + jnp.pad(from_later, ((0, 0), (rows - LEFT, 0), (0, 0)))
        own = own + jnp.pad(from_earlier.astype(jnp.float32), ((0, 0), (0, rows - RIGHT), (0, 0)))
        return own.astype(jnp.bfloat16).reshape(clips * rows, width)

    parts = [grad_query.reshape(clips * rows, width), fold(grad_keys), fold(grad_values)]
    grad_qkv = reduce_gradient(entry, jnp.concatenate(parts, 1), False)
    grad_qkv = grad_qkv.reshape(-1, 3, width).transpose(1, 0, 2)
    grad_entry = sum(matmul_right_t(part, qkv[at]) for at, part in enumerate(parts))
    grad_in, grad_gain = norm_backward(grad_entry, normal, inverse, gain)
    return (grad_in, grad_gain, grad_qkv, grad_attn_out, grad_table)


def conv_forward(resid, gain_in, gain_mid, conv_in, depthwise, conv_out, shape):
    clips, rows, width = shape
    normed, normal, inverse = norm_forward(resid, gain_in)
    entry = normed.astype(jnp.bfloat16)
    joined = matmul(entry, conv_in)
    opened = jax.nn.sigmoid(joined[:, width:])
    glu = (joined[:, :width] * opened).astype(jnp.bfloat16).reshape(clips, rows, width)
    before = from_behind(glu[:, rows - (KERNEL - 1) :], "seq", 1)
    padded = jnp.concatenate([before, glu], 1).astype(jnp.float32)
    taps = depthwise.astype(jnp.float32)
    summed = jnp.zeros((clips, rows, width), jnp.float32)
    for tap in range(KERNEL):
        summed = summed + taps[tap] * padded[:, tap : tap + rows]
    middle, mid_normal, mid_inverse = norm_forward(summed.reshape(clips * rows, width), gain_mid)
    swished = (middle * jax.nn.sigmoid(middle)).astype(jnp.bfloat16)
    kept = (
        normal,
        inverse,
        entry,
        joined,
        opened,
        padded,
        middle,
        mid_normal,
        mid_inverse,
        swished,
    )
    return (matmul(swished, conv_out), kept)


def conv_back(grad_branch, kept, gain_in, gain_mid, conv_in, depthwise, conv_out, shape):
    clips, rows, width = shape
    normal, inverse, entry, joined, opened, padded, middle, mid_normal, mid_inverse, swished = kept
    taps = depthwise.astype(jnp.float32)
    grad_low = grad_branch.astype(jnp.bfloat16)
    grad_conv_out = reduce_gradient(swished, grad_low, False)
    grad_middle = matmul_right_t(grad_low, conv_out) * swish_grad(middle)
    grad_summed, grad_gain_mid = norm_backward(grad_middle, mid_normal, mid_inverse, gain_mid)
    grad_summed = grad_summed.reshape(clips, rows, width)
    grad_taps = jnp.stack(
        [jnp.sum(grad_summed * padded[:, tap : tap + rows], (0, 1)) for tap in range(KERNEL)]
    )
    grad_padded = jnp.zeros((clips, rows + KERNEL - 1, width), jnp.float32)
    for tap in range(KERNEL):
        grad_padded = grad_padded + jnp.pad(
            grad_summed * taps[tap], ((0, 0), (tap, KERNEL - 1 - tap), (0, 0))
        )
    from_later = from_behind(grad_padded[:, : KERNEL - 1].astype(jnp.bfloat16), "seq", -1).astype(
        jnp.float32
    )
    grad_glu = (
        grad_padded[:, KERNEL - 1 :]
        .at[:, rows - (KERNEL - 1) :]
        .add(from_later)
        .reshape(clips * rows, width)
    )
    value_part = joined[:, :width]
    grad_joined = jnp.concatenate(
        [grad_glu * opened, grad_glu * value_part * opened * (1.0 - opened)], 1
    )
    grad_joined = grad_joined.astype(jnp.bfloat16)
    grad_conv_in = reduce_gradient(entry, grad_joined, False)
    grad_in, grad_gain_in = norm_backward(
        matmul_right_t(grad_joined, conv_in), normal, inverse, gain_in
    )
    return (grad_in, grad_gain_in, grad_gain_mid, grad_conv_in, grad_taps, grad_conv_out)


def on_device(
    tokens,
    ffn_in,
    ffn_out,
    qkv,
    attn_out,
    conv_in,
    conv_out,
    depthwise,
    gains,
    rel_table,
    cotangent,
):
    clips, rows, width = tokens.shape
    shape = (clips, rows, width)
    flat_rows = clips * rows
    halve = lax.axis_size("seq") == 2
    norms, taps = (gains.shape[0], depthwise.shape[0])
    lines = -(-(norms + taps) // 16) * 16
    small = jnp.concatenate([gains, depthwise], 0)
    small = jnp.pad(small, ((0, lines - norms - taps), (0, 0)))[None]
    shards = (small, ffn_in, ffn_out, qkv, attn_out[None], conv_in[None], conv_out[None])
    cut = 2 if halve else 1
    plan = (
        (0, (0, 1), 0, 1),
        (1, (0, 1), cut, 2),
        (2, (0, 1), cut, 2),
        (3, (0, 3), 1, 1),
        (4, (0, 1), 1, 1),
        (5, (0, 1), 1, 1),
        (6, (0, 1), 1, 1),
        (1, (1, 1), cut, 2),
        (2, (1, 1), cut, 2),
    )
    gathered = gather_weights(shards, plan)
    small = gathered[0].reshape(-1, lines, gains.shape[1]).transpose(1, 0, 2).reshape(lines, width)
    gain_f = small[:norms].astype(jnp.float32)
    depth = small[norms : norms + taps]
    f_in = (gathered[1][0], gathered[7][0])
    f_out = (gathered[2][0], gathered[8][0])
    proj, a_out, c_in, c_out = (gathered[3], gathered[4][0], gathered[5][0], gathered[6][0])
    start = tokens.reshape(flat_rows, width).astype(jnp.float32)
    first_branch, first_kept = feed_forward(start, gain_f[0], f_in[0], f_out[0])
    after_first = start + 0.5 * first_branch
    attn_branch, attn_kept = attention_forward(
        after_first, gain_f[1], proj, a_out, rel_table, shape
    )
    after_attn = after_first + attn_branch
    conv_branch, conv_kept = conv_forward(
        after_attn, gain_f[2], gain_f[3], c_in, depth, c_out, shape
    )
    after_conv = after_attn + conv_branch
    second_branch, second_kept = feed_forward(after_conv, gain_f[4], f_in[1], f_out[1])
    final = after_conv + 0.5 * second_branch
    result, final_normal, final_inverse = norm_forward(final, gain_f[5])
    squares = jnp.stack(
        [
            jnp.sum(member * member)
            for member in (final, first_branch, attn_branch, conv_branch, second_branch)
        ]
    )
    grad = cotangent.reshape(flat_rows, width).astype(jnp.float32)
    grad, grad_gain_final = norm_backward(grad, final_normal, final_inverse, gain_f[5])
    back_in, grad_gain_second, grad_in_second, grad_out_second = feed_back(
        0.5 * grad, second_kept, gain_f[4], f_in[1], f_out[1], halve
    )
    grad = grad + back_in
    back_in, grad_gain_conv, grad_gain_mid, grad_conv_in, grad_taps, grad_conv_out = conv_back(
        grad, conv_kept, gain_f[2], gain_f[3], c_in, depth, c_out, shape
    )
    grad = grad + back_in
    back_in, grad_gain_attn, grad_qkv, grad_attn_out, grad_table = attention_back(
        grad, attn_kept, gain_f[1], proj, a_out, rel_table, shape
    )
    grad = grad + back_in
    back_in, grad_gain_first, grad_in_first, grad_out_first = feed_back(
        0.5 * grad, first_kept, gain_f[0], f_in[0], f_out[0], halve
    )
    grad = grad + back_in
    gain_grads = jnp.stack(
        [
            grad_gain_first,
            grad_gain_attn,
            grad_gain_conv,
            grad_gain_mid,
            grad_gain_second,
            grad_gain_final,
        ]
    )
    loose = jnp.concatenate([grad_table.reshape(-1), squares])
    lines = -(-loose.shape[0] // width)
    loose = jnp.pad(loose, (0, lines * width - loose.shape[0])).reshape(lines, width)
    totals = butterfly(jnp.concatenate([gain_grads, grad_taps, loose], 0))
    owned = lax.dynamic_slice_in_dim(
        totals[: norms + taps], lax.axis_index("group") * gains.shape[1], gains.shape[1], 1
    )
    loose = totals[norms + taps :].reshape(-1)
    table_size = rel_table.shape[0] * rel_table.shape[1]
    count = (
        flat_rows * width * lax.axis_size("seq") * lax.axis_size("group") * lax.axis_size("replica")
    )
    stats = jnp.sqrt(loose[table_size : table_size + 5] / count)
    return (
        result.astype(jnp.bfloat16).reshape(shape),
        grad.astype(jnp.bfloat16).reshape(shape),
        jnp.stack([grad_in_first, grad_in_second]),
        jnp.stack([grad_out_first, grad_out_second]),
        grad_qkv,
        grad_attn_out,
        grad_conv_in,
        grad_conv_out,
        owned[norms:],
        owned[:norms],
        loose[:table_size].reshape(rel_table.shape),
        stats,
    )


def solution(mesh):
    in_specs = (
        P(("group", "replica"), "seq", None),
        P(None, "group", None),
        P(None, "group", None),
        P(None, "group", None),
        P("group", None),
        P("group", None),
        P("group", None),
        P(None, "group"),
        P(None, "group"),
        P(),
        P(("group", "replica"), "seq", None),
    )
    out_specs = (
        P(("group", "replica"), "seq", None),
        P(("group", "replica"), "seq", None),
        P(None, "group", None),
        P(None, "group", None),
        P(None, "group", None),
        P("group", None),
        P("group", None),
        P("group", None),
        P(None, "group"),
        P(None, "group"),
        P(),
        P(),
    )
    return jax.shard_map(
        on_device, mesh=mesh, in_specs=in_specs, out_specs=out_specs, check_vma=False
    )
```

```python
import functools

import jax
import jax.numpy as jnp
from jax import lax
from jax.experimental import pallas as pl
from jax.experimental.pallas import tpu as pltpu
from jax.sharding import PartitionSpec as P

HEAD_DIM = 64
KERNEL = 31
LEFT = 64
RIGHT = 8
WIN = 73
LANES = 128
BLOCK = 128
SPAN = 256
BACK_PAD = 64


EPSILON = 1e-05
NEGATIVE = -1e30


MESH = pl.DeviceIdType.MESH


def from_behind(value, axis, steps):
    count = lax.axis_size(axis)
    initial, last = (max(0, -steps), min(count, count - steps))
    return lax.ppermute(value, axis, [(source, source + steps) for source in range(initial, last)])


def norm_forward(values, gain):
    centered = values - jnp.mean(values, -1, keepdims=True)
    inverse = lax.rsqrt(jnp.mean(centered * centered, -1, keepdims=True) + EPSILON)
    normal = centered * inverse
    return (normal * gain, normal, inverse)


def norm_backward(grad_out, normal, inverse, gain):
    grad_normal = grad_out * gain
    grad_in = inverse * (
        grad_normal
        - jnp.mean(grad_normal, -1, keepdims=True)
        - normal * jnp.mean(grad_normal * normal, -1, keepdims=True)
    )
    grad_gain = jnp.sum(grad_out * normal, 0)
    return (grad_in, grad_gain)


def matmul(left, right):
    return jnp.dot(left, right, preferred_element_type=jnp.float32)


def matmul_left_t(left, right):
    return lax.dot_general(
        left, right, (((0,), (0,)), ((), ())), preferred_element_type=jnp.float32
    )


def matmul_right_t(left, right):
    return lax.dot_general(
        left, right, (((1,), (1,)), ((), ())), preferred_element_type=jnp.float32
    )


def swish_grad(values):
    logistic = jax.nn.sigmoid(values)
    return logistic + values * logistic * (1.0 - logistic)


def nt(left,right):
    return lax.dot_general(left,right,(((1,),(1,)),((),())),preferred_element_type=jnp.float32)
def tn(left,right):
    return lax.dot_general(left,right,(((0,),(0,)),((),())),preferred_element_type=jnp.float32)
def nn(left,right):
    return jnp.dot(left,right,preferred_element_type=jnp.float32)

def block_mask(first, block, limit):
    rows=lax.broadcasted_iota(jnp.int32,(BLOCK,SPAN),0)
    cols=lax.broadcasted_iota(jnp.int32,(BLOCK,SPAN),1)
    offset=cols-rows
    place=first+block*BLOCK+cols-LEFT
    return (offset>=0)&(offset<WIN)&(place>=0)&(place<limit)

def head_lanes(head):
    lanes=lax.broadcasted_iota(jnp.int32,(BLOCK,LANES),1)
    return (lanes>=head*HEAD_DIM)&(lanes<(head+1)*HEAD_DIM)

def block_probs(query, keys, table, mask):
    relative=pltpu.roll(nt(query,table),0,1,stride=1,stride_axis=0)
    raw=jnp.where(mask,(nt(query,keys)+relative)*(HEAD_DIM**-0.5),NEGATIVE)
    expo=jnp.exp(raw-jnp.max(raw,-1,keepdims=True))
    return expo*(1.0/jnp.sum(expo,-1,keepdims=True))

def attend_kernel(limit, first_ref, q_ref, k_ref, v_ref, t_ref, c_ref):
    table=t_ref[...]
    zero=jnp.zeros((BLOCK,LANES),jnp.bfloat16)
    for block in range(q_ref.shape[1]//BLOCK):
        rows=pl.ds(block*BLOCK,BLOCK); span=pl.ds(block*BLOCK,SPAN)
        query=q_ref[0,rows,:]; keys=k_ref[0,span,:]; values=v_ref[0,span,:]
        mask=block_mask(first_ref[0],block,limit)
        mixed=[]
        for head in range(2):
            probs=block_probs(jnp.where(head_lanes(head),query,zero),keys,table,mask)
            mixed.append(nn(probs.astype(jnp.bfloat16),values))
        c_ref[0,rows,:]=jnp.where(head_lanes(0),mixed[0],mixed[1]).astype(jnp.bfloat16)

def attend_back_kernel(limit, first_ref, q_ref, k_ref, v_ref, t_ref, g_ref, dq_ref, dk_ref, dv_ref, dt_ref, dk_sum, dv_sum):
    table=t_ref[...]
    zero=jnp.zeros((BLOCK,LANES),jnp.bfloat16)
    flip=(lax.broadcasted_iota(jnp.int32,(BLOCK,BLOCK),0)+lax.broadcasted_iota(jnp.int32,(BLOCK,BLOCK),1)==BLOCK-1).astype(jnp.float32).astype(jnp.bfloat16)
    dk_sum[...]=jnp.zeros_like(dk_sum); dv_sum[...]=jnp.zeros_like(dv_sum)
    @pl.when((pl.program_id(0)==0)&(pl.program_id(1)==0))
    def _(): dt_ref[...]=jnp.zeros_like(dt_ref)
    for block in range(q_ref.shape[1]//BLOCK):
        rows=pl.ds(block*BLOCK,BLOCK); span=pl.ds(block*BLOCK,SPAN)
        keys=k_ref[0,span,:]; values=v_ref[0,span,:]
        mask=block_mask(first_ref[0],block,limit)
        grad_query=[]
        for head in range(2):
            query=jnp.where(head_lanes(head),q_ref[0,rows,:],zero)
            grad=jnp.where(head_lanes(head),g_ref[0,rows,:],zero)
            probs=block_probs(query,keys,table,mask)
            grad_probs=nt(grad,values)
            grad_raw=probs*(grad_probs-jnp.sum(probs*grad_probs,-1,keepdims=True))
            grad_raw=grad_raw.astype(jnp.bfloat16)
            turned=pltpu.roll(nn(flip,grad_raw),SPAN-BLOCK+1,1,stride=1,stride_axis=0)
            unskewed=nn(flip,turned.astype(jnp.bfloat16)).astype(jnp.bfloat16)
            dv_sum[span,:]+=tn(probs.astype(jnp.bfloat16),grad)
            dk_sum[span,:]+=tn(grad_raw,query)
            dt_ref[...]+=tn(unskewed,query)
            grad_query.append(nn(grad_raw,keys)+nn(unskewed,table))
        dq_ref[0,rows,:]=(jnp.where(head_lanes(0),grad_query[0],grad_query[1])*(HEAD_DIM**-0.5)).astype(jnp.bfloat16)
    dk_ref[0]=(dk_sum[...]*(HEAD_DIM**-0.5)).astype(jnp.bfloat16)
    dv_ref[0]=dv_sum[...].astype(jnp.bfloat16)

def wide_table(table):
    return jnp.tile(jnp.pad(table,((0,SPAN-table.shape[0]),(0,0))),(1,LANES//HEAD_DIM))

def specs(clips,rows,width):
    own=pl.BlockSpec((1,rows,LANES),lambda c,h:(c,0,h))
    ext=pl.BlockSpec((1,rows+LEFT+BACK_PAD,LANES),lambda c,h:(c,0,h))
    tab=pl.BlockSpec((SPAN,LANES),lambda c,h:(0,0))
    return (pl.BlockSpec(memory_space=pltpu.SMEM),own,ext,tab),(clips,width//LANES)

def attend(query,keys,values,table,rows):
    clips,_,width=query.shape
    first=lax.axis_index('seq').astype(jnp.int32)[None]*rows
    limit=rows*lax.axis_size('seq')
    (sc,own,ext,tab),grid=specs(clips,rows,width)
    return pl.pallas_call(functools.partial(attend_kernel,limit),grid=grid,
        in_specs=[sc,own,ext,ext,tab],out_specs=own,
        out_shape=jax.ShapeDtypeStruct(query.shape,jnp.bfloat16),name="attend",
    )(first,query,keys,values,wide_table(table))

def attend_back(query,keys,values,table,grad,rows):
    clips,_,width=query.shape
    first=lax.axis_index('seq').astype(jnp.int32)[None]*rows
    limit=rows*lax.axis_size('seq')
    (sc,own,ext,tab),grid=specs(clips,rows,width)
    dq,dk,dv,dt=pl.pallas_call(functools.partial(attend_back_kernel,limit),grid=grid,
        in_specs=[sc,own,ext,ext,tab,own],out_specs=[own,ext,ext,tab],
        out_shape=[jax.ShapeDtypeStruct(query.shape,jnp.bfloat16),jax.ShapeDtypeStruct(keys.shape,jnp.bfloat16),jax.ShapeDtypeStruct(keys.shape,jnp.bfloat16),jax.ShapeDtypeStruct((SPAN,LANES),jnp.float32)],
        scratch_shapes=[pltpu.VMEM((rows+LEFT+BACK_PAD,LANES),jnp.float32)]*2,name="attend_back",
    )(first,query,keys,values,wide_table(table),grad)
    return dq,dk,dv,(dt[:WIN,:HEAD_DIM]+dt[:WIN,HEAD_DIM:])*(HEAD_DIM**-0.5)
def depth_of():
    return lax.axis_size("group") // 2


def place():
    group = lax.axis_index("group")
    return (group // 2, group % 2, lax.axis_index("seq"), lax.axis_index("replica"))


def greet(peers):
    barrier = pltpu.get_barrier_semaphore()
    for peer in peers:
        pl.semaphore_signal(barrier, inc=1, device_id=peer, device_id_type=MESH)
    pl.semaphore_wait(barrier, len(peers))


def neighbours():
    z, x, seq, replica = place()
    depth = depth_of()
    deep = [{"group": (z + steps) % depth * 2 + x} for steps in range(1, depth)]
    across = {"group": z * 2 + 1 - x}
    beside = {"seq": 1 - seq}
    twin = {"replica": 1 - replica}
    return (deep, across, beside, twin)


class Gather:
    def __init__(self, source, target, cut, low, high, rows, sends, recvs, at):
        depth = depth_of()
        self.source, self.target, self.cut, self.low, self.rows = (source, target, cut, low, rows)
        self.piece = (high - low) // (1, 2, 4)[cut]
        self.sends, self.recvs, self.at = (sends, recvs, at)
        self.z, self.x, self.seq, self.replica = place()
        self.deep, self.across, self.beside, self.twin = neighbours()
        self.depth = depth
        self.firsts = (0, depth - 1, 2 * depth - 1, 4 * depth - 2)
        self.started = []

    def spot(self, ref, owner, dy, dc):
        part = 0
        if self.cut:
            part = (self.replica + dc) % 2
        if self.cut == 2:
            part = part + 2 * ((self.seq + dy) % 2)
        first = pl.multiple_of(owner * self.rows + self.low + part * self.piece, self.piece)
        return ref.at[:, pl.ds(first, self.piece)]

    def owner(self, steps, dx):
        return (self.z + self.depth - steps) % self.depth * 2 + (self.x + dx) % 2

    def copy(self, steps, dx, dy, dc, kind, index, peer):
        mine = steps == 0 and dx == 0
        slot = self.at + self.firsts[kind] + index
        spot = self.spot(self.target, self.owner(steps, dx), dy, dc)
        return pltpu.make_async_remote_copy(
            src_ref=self.spot(self.source, 0, dy, dc) if mine else spot,
            dst_ref=spot,
            send_sem=self.sends.at[slot],
            recv_sem=self.recvs.at[slot],
            device_id=peer,
            device_id_type=MESH,
        )

    def send(self, copy):
        copy.start()
        self.started.append(copy)

    def to_beside(self, steps, dx):
        if self.cut == 2:
            index = dx * self.depth + steps - 1
            self.send(self.copy(steps, dx, 0, 0, 2, index, self.beside))

    def to_twin(self, steps, dx, dy):
        if self.cut:
            index = dy * (2 * self.depth - 1) + dx * self.depth + steps - 1
            self.send(self.copy(steps, dx, dy, 0, 3, index, self.twin))

    def open(self):
        for steps, peer in enumerate(self.deep, 1):
            self.send(self.copy(0, 0, 0, 0, 0, steps - 1, peer))
        self.send(self.copy(0, 0, 0, 0, 1, 0, self.across))

    def got(self, steps, dx, dy, dc, kind, index):
        self.copy(steps or self.depth, dx, dy, dc, kind, index, self.twin).wait_recv()

    def forward_deep(self):
        for steps in range(1, self.depth):
            self.got(steps, 0, 0, 0, 0, steps - 1)
            self.send(self.copy(steps, 0, 0, 0, 1, steps, self.across))
            self.to_beside(steps, 0)
            self.to_twin(steps, 0, 0)

    def forward_across(self):
        for steps in range(self.depth):
            self.got(steps, 1, 0, 0, 1, steps)
            self.to_beside(steps, 1)
            self.to_twin(steps, 1, 0)

    def others(self):
        return [(steps, dx) for dx in range(2) for steps in range(self.depth) if steps or dx]

    def forward_beside(self):
        if self.cut == 2:
            for steps, dx in self.others():
                self.got(steps, dx, 1, 0, 2, dx * self.depth + steps - 1)
                self.to_twin(steps, dx, 1)

    def close(self):
        if self.cut:
            for dy in range(self.cut):
                for steps, dx in self.others():
                    index = dy * (2 * self.depth - 1) + dx * self.depth + steps - 1
                    self.got(steps, dx, dy, 1, 3, index)
        for copy in self.started:
            copy.wait_send()


def gather_kernel(plan, count, *refs):
    ins, outs = (refs[:count], refs[count : count + len(plan)])
    helds, (sends, recvs, local) = (refs[count + len(plan) : -3], refs[-3:])
    deep, across, beside, twin = neighbours()
    peers = deep + [across, twin]
    if any(cut == 2 for _, _, cut, _ in plan):
        peers.append(beside)
    greet(peers)
    loads = [
        pltpu.make_async_copy(ins[at], held, local.at[0, at]) for at, held in enumerate(helds)
    ]
    for load in loads:
        load.start()
    jobs, stores, at = ([], [], 0)
    for number, (source, layers, cut, chunks) in enumerate(plan):
        ref = ins[source].at[pl.ds(layers[0], layers[1])]
        rows = ins[source].shape[1]
        for chunk in range(chunks):
            low, high = (rows * chunk // chunks, rows * (chunk + 1) // chunks)
            jobs.append(Gather(ref, outs[number], cut, low, high, rows, sends, recvs, at))
            at += (2, 6, 8)[cut] * depth_of()
    z, x, _, _ = place()
    ready = set()
    for tick in range(len(jobs) + 4):
        if tick < len(jobs):
            jobs[tick].open()
        if 1 <= tick < len(jobs) + 1:
            jobs[tick - 1].forward_deep()
        if 2 <= tick < len(jobs) + 2:
            jobs[tick - 2].forward_across()
        if 3 <= tick < len(jobs) + 3:
            jobs[tick - 3].forward_beside()
        if 4 <= tick:
            jobs[tick - 4].close()
        if tick < len(plan):
            source, layers, _, _ = plan[tick]
            if source not in ready:
                loads[source].wait()
                ready.add(source)
            rows = ins[source].shape[1]
            first = pl.multiple_of((z * 2 + x) * rows, rows)
            store = pltpu.make_async_copy(
                helds[source].at[pl.ds(layers[0], layers[1])],
                outs[tick].at[:, pl.ds(first, rows)],
                local.at[1, tick],
            )
            store.start()
            stores.append(store)
    for store in stores:
        store.wait()


def gather_weights(shards, plan):
    groups = lax.axis_size("group")
    total = sum((2, 6, 8)[cut] * depth_of() * chunks for _, _, cut, chunks in plan)
    return pl.pallas_call(
        functools.partial(gather_kernel, plan, len(shards)),
        in_specs=[pl.BlockSpec(memory_space=pl.ANY)] * len(shards),
        out_specs=[pl.BlockSpec(memory_space=pl.ANY)] * len(plan),
        out_shape=[
            jax.ShapeDtypeStruct(
                (layers[1], groups * shards[source].shape[1], shards[source].shape[2]), jnp.bfloat16
            )
            for source, layers, _, _ in plan
        ],
        scratch_shapes=[pltpu.VMEM(shard.shape, jnp.bfloat16) for shard in shards]
        + [
            pltpu.SemaphoreType.DMA((total,)),
            pltpu.SemaphoreType.DMA((total,)),
            pltpu.SemaphoreType.DMA((2, len(plan))),
        ],
        compiler_params=pltpu.CompilerParams(
            collective_id=1, has_side_effects=True, vmem_limit_bytes=24 << 20
        ),
        name="gather_weights",
    )(*shards)


def swap(value, axis, bit=1):
    return lax.ppermute(value, axis, [(i, i ^ bit) for i in range(lax.axis_size(axis))])


def along_depth(value, steps):
    depth = depth_of()
    pairs = [(i, (i // 2 + steps) % depth * 2 + i % 2) for i in range(2 * depth)]
    return lax.ppermute(value, "group", pairs)


def butterfly(value):
    for axis in ("replica", "seq", "group"):
        bit = 1
        while bit < lax.axis_size(axis):
            value = value + swap(value, axis, bit)
            bit *= 2
    return value


def add_slabs(count, target, *sources):
    def body(at, carry):
        total = sources[0](at)[...].astype(jnp.float32)
        for source in sources[1:]:
            total = total + source(at)[...].astype(jnp.float32)
        target(at)[...] = total.astype(jnp.bfloat16)
        return carry

    lax.fori_loop(0, count, body, 0)


class Reduce:
    def __init__(self, source, target, low, left, cut, rows, width, buffers, sends, recvs, local):
        self.source, self.target, self.low, self.left, self.cut = (source, target, low, left, cut)
        self.piece, self.width = (rows // (2 * cut), width)
        self.buffers, self.sends, self.recvs, self.local = (buffers, sends, recvs, local)
        self.z, self.x, self.seq, self.replica = place()
        self.deep, self.across, self.beside, self.twin = neighbours()
        self.depth, self.span = (depth_of(), lax.axis_size("seq"))
        self.started, self.slots = ([], 0)
        self.stages = [
            self.exchange_twin,
            self.exchange_seq,
            self.exchange_across,
            self.exchange_deep,
            self.settle,
            self.hand_over,
            self.close,
        ]

    def row(self, dy, dc):
        part = (self.replica + dc) % 2
        if self.cut == 2:
            part = part + 2 * ((self.seq + dy) % 2)
        return pl.ds(pl.multiple_of(self.low + part * self.piece, self.piece), self.piece)

    def block(self, dy, dc):
        return self.source.at[:, :, self.row(dy, dc), pl.ds(self.left, self.width)]

    def send(self, source, target, slot, peer):
        copy = pltpu.make_async_remote_copy(
            src_ref=source,
            dst_ref=target,
            send_sem=self.sends.at[slot],
            recv_sem=self.recvs.at[slot],
            device_id=peer,
            device_id_type=MESH,
        )
        copy.start()
        self.started.append(copy)

    def wait(self, target, slot):
        pltpu.make_async_remote_copy(
            src_ref=target,
            dst_ref=target,
            send_sem=self.sends.at[slot],
            recv_sem=self.recvs.at[slot],
            device_id=self.twin,
            device_id_type=MESH,
        ).wait_recv()

    def exchange_twin(self):
        own, came = (self.buffers["own"], self.buffers["came"])
        self.loads = []
        for dy in reversed(range(self.cut)):
            self.send(self.block(dy, 1), came.at[dy], dy, self.twin)
            load = pltpu.make_async_copy(self.block(dy, 0), own.at[dy], self.local.at[dy])
            load.start()
            self.loads.append(load)

    def exchange_seq(self):
        if self.cut == 2:
            own, came, away = [self.buffers[name] for name in ("own", "came", "to_seq")]
            self.loads[0].wait()
            self.wait(came.at[1], 1)
            spot = lambda ref: lambda at: ref.at[at // 2, at % 2]
            add_slabs(2 * self.depth, spot(away), spot(own.at[1]), spot(came.at[1]))
            self.send(away, self.buffers["from_seq"], 2, self.beside)

    def parts(self, x):
        names = [self.buffers["own"].at[0], self.buffers["came"].at[0]]
        if self.cut == 2:
            names.append(self.buffers["from_seq"])
        return [lambda at, ref=ref: ref.at[at, x] for ref in names]

    def exchange_across(self):
        self.loads[-1].wait()
        self.wait(self.buffers["came"].at[0], 0)
        if self.cut == 2:
            self.wait(self.buffers["from_seq"], 2)
        away = self.buffers["to_x"]
        add_slabs(self.depth, lambda at: away.at[at], *self.parts(1 - self.x))
        self.send(away, self.buffers["from_x"], 3, self.across)

    def exchange_deep(self):
        mine, came, far = [self.buffers[name] for name in ("mine", "from_x", "from_z")]
        self.wait(came, 3)
        add_slabs(self.depth, lambda at: mine.at[at], lambda at: came.at[at], *self.parts(self.x))
        for steps, peer in enumerate(self.deep, 1):
            spot = mine.at[(self.z + steps) % self.depth]
            self.send(spot, far.at[steps - 1], 3 + steps, peer)

    def settle(self):
        mine, far = (self.buffers["mine"], self.buffers["from_z"])
        for steps in range(1, self.depth):
            self.wait(far.at[steps - 1], 3 + steps)
        sources = [lambda at: mine.at[self.z]]
        sources += [lambda at, steps=steps: far.at[steps - 1] for steps in range(1, self.depth)]
        done = self.buffers["done"]
        self.last = 4 + self.depth
        if self.cut == 2:
            add_slabs(1, lambda at: done, *sources)
            self.publish(done)
            self.send(done, self.spot(0, 0), self.last, self.beside)
        else:
            shared = self.buffers["shared"]
            add_slabs(1, lambda at: shared.at[self.seq], *sources)
            for steps in range(1, self.span):
                peer = {"seq": (self.seq + steps) % self.span}
                spot = shared.at[self.seq]
                self.send(spot, spot, self.last + 2 + steps, peer)

    def spot(self, dy, dc):
        return self.target.at[self.row(dy, dc), pl.ds(self.left, self.width)]

    def publish(self, done):
        self.store = pltpu.make_async_copy(done, self.spot(0, 0), self.local.at[2])
        self.store.start()
        self.send(done, self.spot(0, 0), self.last + 1, self.twin)

    def hand_over(self):
        if self.cut == 2:
            self.wait(self.spot(1, 0), self.last)
            self.send(self.spot(1, 0), self.spot(1, 0), self.last + 2, self.twin)
        else:
            shared = self.buffers["shared"]
            for steps in range(1, self.span):
                self.wait(shared.at[(self.seq + self.span - steps) % self.span], self.last + 2 + steps)
            done = self.buffers["done"]
            sources = [lambda at, turn=turn: shared.at[turn] for turn in range(self.span)]
            add_slabs(1, lambda at: done, *sources)
            self.publish(done)

    def close(self):
        self.wait(self.spot(0, 1), self.last + 1)
        if self.cut == 2:
            self.wait(self.spot(1, 1), self.last + 2)
        self.store.wait()
        for copy in self.started:
            copy.wait_send()


def reduce_shapes(cut, rows, width):
    depth, span = (depth_of(), lax.axis_size("seq"))
    piece = rows // (2 * cut)
    shapes = {
        "own": (cut, depth, 2, piece, width),
        "came": (cut, depth, 2, piece, width),
        "to_x": (depth, piece, width),
        "from_x": (depth, piece, width),
        "mine": (depth, piece, width),
        "from_z": (depth - 1, piece, width),
        "done": (piece, width),
    }
    if cut == 2:
        shapes["to_seq"] = shapes["from_seq"] = (depth, 2, piece, width)
    else:
        shapes["shared"] = (span, piece, width)
    return shapes


def reduce_plan(grads, rows, width, halve):
    plan = []
    for source, grad in enumerate(grads):
        for low in range(0, grad.shape[2], rows):
            for left in range(0, grad.shape[3], width):
                plan.append((source, low, left, 2 if halve and len(plan) % 2 == 0 else 1))
    return plan


def reduce_scratch(plan, rows, width):
    depth, span = (depth_of(), lax.axis_size("seq"))
    scratch = []
    for cut in (1, 2):
        count = sum(member[3] == cut for member in plan)
        if count:
            scratch += [
                pltpu.VMEM((count,) + shape, jnp.bfloat16)
                for shape in reduce_shapes(cut, rows, width).values()
            ]
    slots = 7 + depth + span
    return scratch + [
        pltpu.SemaphoreType.DMA((len(plan), slots)),
        pltpu.SemaphoreType.DMA((len(plan), slots)),
        pltpu.SemaphoreType.DMA((len(plan), 3)),
    ]


def reduce_ticks(plan, rows, width, sources, targets, scratch):
    held, (sends, recvs, local) = (list(scratch[:-3]), scratch[-3:])
    stacks = {}
    for cut in (1, 2):
        if any(member[3] == cut for member in plan):
            stacks[cut] = {name: held.pop(0) for name in reduce_shapes(cut, rows, width)}
    jobs, used = ([], {1: 0, 2: 0})
    for number, (source, low, left, cut) in enumerate(plan):
        buffers = {name: ref.at[used[cut]] for name, ref in stacks[cut].items()}
        used[cut] += 1
        sems = (sends.at[number], recvs.at[number], local.at[number])
        jobs.append(
            Reduce(sources[source], targets[source], low, left, cut, rows, width, buffers, *sems)
        )
    stages = len(jobs[0].stages)

    def tick(turn):
        for stage in range(stages):
            if 0 <= turn - stage < len(jobs):
                jobs[turn - stage].stages[stage]()

    return [functools.partial(tick, turn) for turn in range(len(jobs) + stages - 1)]


def reduce_greet():
    deep, across, _, twin = neighbours()
    span = lax.axis_size("seq")
    seq = lax.axis_index("seq")
    greet(deep + [across, twin] + [{"seq": (seq + steps) % span} for steps in range(1, span)])


def reduce_kernel(plan, rows, width, count, *refs):
    sources, targets, scratch = (refs[:count], refs[count : 2 * count], refs[2 * count :])
    reduce_greet()
    for tick in reduce_ticks(plan, rows, width, sources, targets, scratch):
        tick()


def reduce_gradients(grads, halve, number):
    groups = lax.axis_size("group")
    width = min(grad.shape[1] for grad in grads)
    rows = width // groups
    grads = [grad.reshape(groups // 2, 2, grad.shape[0] // groups, grad.shape[1]) for grad in grads]
    plan = reduce_plan(grads, rows, width, halve)
    return pl.pallas_call(
        functools.partial(reduce_kernel, plan, rows, width, len(grads)),
        in_specs=[pl.BlockSpec(memory_space=pl.ANY)] * len(grads),
        out_specs=[pl.BlockSpec(memory_space=pl.ANY)] * len(grads),
        out_shape=[jax.ShapeDtypeStruct(grad.shape[2:], jnp.bfloat16) for grad in grads],
        scratch_shapes=reduce_scratch(plan, rows, width),
        compiler_params=pltpu.CompilerParams(
            collective_id=number, has_side_effects=True, vmem_limit_bytes=48 << 20
        ),
        name="reduce_gradients",
    )(*grads)


def feed_forward(resid, gain, w_in, w_out):
    normed, normal, inverse = norm_forward(resid, gain)
    entry = normed.astype(jnp.bfloat16)
    hidden_pre = matmul(entry, w_in)
    hidden = (hidden_pre * jax.nn.sigmoid(hidden_pre)).astype(jnp.bfloat16)
    return (matmul(hidden, w_out), (normal, inverse, entry, hidden_pre, hidden))


def feed_back(grad_branch, kept, gain, w_in, w_out):
    normal, inverse, entry, hidden_pre, hidden = kept
    grad_low = grad_branch.astype(jnp.bfloat16)
    grad_w_out = matmul_left_t(hidden, grad_low).astype(jnp.bfloat16)
    grad_hidden = (matmul_right_t(grad_low, w_out) * swish_grad(hidden_pre)).astype(jnp.bfloat16)
    grad_w_in = matmul_left_t(entry, grad_hidden).astype(jnp.bfloat16)
    grad_in, grad_gain = norm_backward(matmul_right_t(grad_hidden, w_in), normal, inverse, gain)
    return (grad_in, grad_gain, grad_w_in, grad_w_out)


def attention_forward(resid, gain, qkv, attn_out, table, shape):
    clips, rows, width = shape
    normed, normal, inverse = norm_forward(resid, gain)
    entry = normed.astype(jnp.bfloat16)
    query, keys, values = [
        matmul(entry, qkv[part]).astype(jnp.bfloat16).reshape(shape) for part in range(3)
    ]
    tail = jnp.zeros((clips, BACK_PAD - RIGHT, width), jnp.bfloat16)

    def extend(value):
        before = from_behind(value[:, rows - LEFT :], "seq", 1)
        after = from_behind(value[:, :RIGHT], "seq", -1)
        return jnp.concatenate([before, value, after, tail], 1)

    keys, values = (extend(keys), extend(values))
    mixed = attend(query, keys, values, table, rows).reshape(clips * rows, width)
    return (matmul(mixed, attn_out), (normal, inverse, entry, query, keys, values, mixed))


def attention_back(grad_branch, kept, gain, qkv, attn_out, table, shape):
    clips, rows, width = shape
    normal, inverse, entry, query, keys, values, mixed = kept
    grad_low = grad_branch.astype(jnp.bfloat16)
    grad_attn_out = matmul_left_t(mixed, grad_low).astype(jnp.bfloat16)
    grad_mixed = matmul_right_t(grad_low, attn_out).astype(jnp.bfloat16).reshape(shape)
    grad_query, grad_keys, grad_values, grad_table = attend_back(
        query, keys, values, table, grad_mixed, rows
    )

    def fold(grad):
        from_later = from_behind(grad[:, :LEFT], "seq", -1).astype(jnp.float32)
        from_earlier = from_behind(grad[:, LEFT + rows : LEFT + rows + RIGHT], "seq", 1)
        own = grad[:, LEFT : LEFT + rows].astype(jnp.float32)
        own = own + jnp.pad(from_later, ((0, 0), (rows - LEFT, 0), (0, 0)))
        own = own + jnp.pad(from_earlier.astype(jnp.float32), ((0, 0), (0, rows - RIGHT), (0, 0)))
        return own.astype(jnp.bfloat16).reshape(clips * rows, width)

    parts = [grad_query.reshape(clips * rows, width), fold(grad_keys), fold(grad_values)]
    grad_qkv = [matmul_left_t(entry, part).astype(jnp.bfloat16) for part in parts]
    grad_entry = sum(matmul_right_t(part, qkv[at]) for at, part in enumerate(parts))
    grad_in, grad_gain = norm_backward(grad_entry, normal, inverse, gain)
    return (grad_in, grad_gain, grad_qkv, grad_attn_out, grad_table)


def conv_forward(resid, gain_in, gain_mid, conv_in, depthwise, conv_out, shape):
    clips, rows, width = shape
    normed, normal, inverse = norm_forward(resid, gain_in)
    entry = normed.astype(jnp.bfloat16)
    joined = matmul(entry, conv_in)
    opened = jax.nn.sigmoid(joined[:, width:])
    glu = (joined[:, :width] * opened).astype(jnp.bfloat16).reshape(clips, rows, width)
    before = from_behind(glu[:, rows - (KERNEL - 1) :], "seq", 1)
    padded = jnp.concatenate([before, glu], 1).astype(jnp.float32)
    taps = depthwise.astype(jnp.float32)
    summed = jnp.zeros((clips, rows, width), jnp.float32)
    for tap in range(KERNEL):
        summed = summed + taps[tap] * padded[:, tap : tap + rows]
    middle, mid_normal, mid_inverse = norm_forward(summed.reshape(clips * rows, width), gain_mid)
    swished = (middle * jax.nn.sigmoid(middle)).astype(jnp.bfloat16)
    kept = (
        normal,
        inverse,
        entry,
        joined,
        opened,
        padded,
        middle,
        mid_normal,
        mid_inverse,
        swished,
    )
    return (matmul(swished, conv_out), kept)


def conv_back(grad_branch, kept, gain_in, gain_mid, conv_in, depthwise, conv_out, shape):
    clips, rows, width = shape
    normal, inverse, entry, joined, opened, padded, middle, mid_normal, mid_inverse, swished = kept
    taps = depthwise.astype(jnp.float32)
    grad_low = grad_branch.astype(jnp.bfloat16)
    grad_conv_out = matmul_left_t(swished, grad_low).astype(jnp.bfloat16)
    grad_middle = matmul_right_t(grad_low, conv_out) * swish_grad(middle)
    grad_summed, grad_gain_mid = norm_backward(grad_middle, mid_normal, mid_inverse, gain_mid)
    grad_summed = grad_summed.reshape(clips, rows, width)
    grad_taps = jnp.stack(
        [jnp.sum(grad_summed * padded[:, tap : tap + rows], (0, 1)) for tap in range(KERNEL)]
    )
    grad_padded = jnp.zeros((clips, rows + KERNEL - 1, width), jnp.float32)
    for tap in range(KERNEL):
        grad_padded = grad_padded + jnp.pad(
            grad_summed * taps[tap], ((0, 0), (tap, KERNEL - 1 - tap), (0, 0))
        )
    from_later = from_behind(grad_padded[:, : KERNEL - 1].astype(jnp.bfloat16), "seq", -1).astype(
        jnp.float32
    )
    grad_glu = (
        grad_padded[:, KERNEL - 1 :]
        .at[:, rows - (KERNEL - 1) :]
        .add(from_later)
        .reshape(clips * rows, width)
    )
    value_part = joined[:, :width]
    grad_joined = jnp.concatenate(
        [grad_glu * opened, grad_glu * value_part * opened * (1.0 - opened)], 1
    )
    grad_joined = grad_joined.astype(jnp.bfloat16)
    grad_conv_in = matmul_left_t(entry, grad_joined).astype(jnp.bfloat16)
    grad_in, grad_gain_in = norm_backward(
        matmul_right_t(grad_joined, conv_in), normal, inverse, gain_in
    )
    return (grad_in, grad_gain_in, grad_gain_mid, grad_conv_in, grad_taps, grad_conv_out)


def on_device(
    tokens,
    ffn_in,
    ffn_out,
    qkv,
    attn_out,
    conv_in,
    conv_out,
    depthwise,
    gains,
    rel_table,
    cotangent,
):
    clips, rows, width = tokens.shape
    shape = (clips, rows, width)
    flat_rows = clips * rows
    halve = lax.axis_size("seq") == 2
    norms, taps = (gains.shape[0], depthwise.shape[0])
    lines = -(-(norms + taps) // 16) * 16
    small = jnp.concatenate([gains, depthwise], 0)
    small = jnp.pad(small, ((0, lines - norms - taps), (0, 0)))[None]
    shards = (small, ffn_in, ffn_out, qkv, attn_out[None], conv_in[None], conv_out[None])
    cut = 2 if halve else 1
    plan = (
        (0, (0, 1), 0, 1),
        (1, (0, 1), cut, 2),
        (2, (0, 1), cut, 2),
        (3, (0, 3), 1, 1),
        (4, (0, 1), 1, 1),
        (5, (0, 1), 1, 1),
        (6, (0, 1), 1, 1),
        (1, (1, 1), cut, 2),
        (2, (1, 1), cut, 2),
    )
    gathered = gather_weights(shards, plan)
    small = gathered[0].reshape(-1, lines, gains.shape[1]).transpose(1, 0, 2).reshape(lines, width)
    gain_f = small[:norms].astype(jnp.float32)
    depth = small[norms : norms + taps]
    f_in = (gathered[1][0], gathered[7][0])
    f_out = (gathered[2][0], gathered[8][0])
    proj, a_out, c_in, c_out = (gathered[3], gathered[4][0], gathered[5][0], gathered[6][0])
    start = tokens.reshape(flat_rows, width).astype(jnp.float32)
    first_branch, first_kept = feed_forward(start, gain_f[0], f_in[0], f_out[0])
    after_first = start + 0.5 * first_branch
    attn_branch, attn_kept = attention_forward(
        after_first, gain_f[1], proj, a_out, rel_table, shape
    )
    after_attn = after_first + attn_branch
    conv_branch, conv_kept = conv_forward(
        after_attn, gain_f[2], gain_f[3], c_in, depth, c_out, shape
    )
    after_conv = after_attn + conv_branch
    second_branch, second_kept = feed_forward(after_conv, gain_f[4], f_in[1], f_out[1])
    final = after_conv + 0.5 * second_branch
    result, final_normal, final_inverse = norm_forward(final, gain_f[5])
    squares = jnp.stack(
        [
            jnp.sum(member * member)
            for member in (final, first_branch, attn_branch, conv_branch, second_branch)
        ]
    )
    grad = cotangent.reshape(flat_rows, width).astype(jnp.float32)
    grad, grad_gain_final = norm_backward(grad, final_normal, final_inverse, gain_f[5])
    back_in, grad_gain_second, grad_in_second, grad_out_second = feed_back(
        0.5 * grad, second_kept, gain_f[4], f_in[1], f_out[1]
    )
    grad = grad + back_in
    back_in, grad_gain_conv, grad_gain_mid, grad_conv_in, grad_taps, grad_conv_out = conv_back(
        grad, conv_kept, gain_f[2], gain_f[3], c_in, depth, c_out, shape
    )
    grad = grad + back_in
    back_in, grad_gain_attn, grad_qkv, grad_attn_out, grad_table = attention_back(
        grad, attn_kept, gain_f[1], proj, a_out, rel_table, shape
    )
    grad = grad + back_in
    back_in, grad_gain_first, grad_in_first, grad_out_first = feed_back(
        0.5 * grad, first_kept, gain_f[0], f_in[0], f_out[0]
    )
    grad = grad + back_in
    wide = jnp.float32
    second = reduce_gradients([grad_out_second, grad_in_second], halve, 2)
    middle = [grad_conv_out, grad_conv_in, grad_attn_out] + grad_qkv
    middle = reduce_gradients(middle, halve, 3)
    first = reduce_gradients([grad_out_first, grad_in_first], halve, 4)
    gain_grads = jnp.stack(
        [
            grad_gain_first,
            grad_gain_attn,
            grad_gain_conv,
            grad_gain_mid,
            grad_gain_second,
            grad_gain_final,
        ]
    )
    loose = jnp.concatenate([grad_table.reshape(-1), squares])
    lines = -(-loose.shape[0] // width)
    loose = jnp.pad(loose, (0, lines * width - loose.shape[0])).reshape(lines, width)
    totals = butterfly(jnp.concatenate([gain_grads, grad_taps, loose], 0))
    owned = lax.dynamic_slice_in_dim(
        totals[: norms + taps], lax.axis_index("group") * gains.shape[1], gains.shape[1], 1
    )
    loose = totals[norms + taps :].reshape(-1)
    table_size = rel_table.shape[0] * rel_table.shape[1]
    count = (
        flat_rows * width * lax.axis_size("seq") * lax.axis_size("group") * lax.axis_size("replica")
    )
    stats = jnp.sqrt(loose[table_size : table_size + 5] / count)
    return (
        result.astype(jnp.bfloat16).reshape(shape),
        grad.astype(jnp.bfloat16).reshape(shape),
        jnp.stack([first[1], second[1]]).astype(wide),
        jnp.stack([first[0], second[0]]).astype(wide),
        jnp.stack(middle[3:]).astype(wide),
        middle[2].astype(wide),
        middle[1].astype(wide),
        middle[0].astype(wide),
        owned[norms:],
        owned[:norms],
        loose[:table_size].reshape(rel_table.shape),
        stats,
    )


def solution(mesh):
    in_specs = (
        P(("group", "replica"), "seq", None),
        P(None, "group", None),
        P(None, "group", None),
        P(None, "group", None),
        P("group", None),
        P("group", None),
        P("group", None),
        P(None, "group"),
        P(None, "group"),
        P(),
        P(("group", "replica"), "seq", None),
    )
    out_specs = (
        P(("group", "replica"), "seq", None),
        P(("group", "replica"), "seq", None),
        P(None, "group", None),
        P(None, "group", None),
        P(None, "group", None),
        P("group", None),
        P("group", None),
        P("group", None),
        P(None, "group"),
        P(None, "group"),
        P(),
        P(),
    )
    return jax.shard_map(
        on_device, mesh=mesh, in_specs=in_specs, out_specs=out_specs, check_vma=False
    )
```

```python
import functools

import jax
import jax.numpy as jnp
from jax import lax
from jax.experimental import pallas as pl
from jax.experimental.pallas import tpu as pltpu
from jax.sharding import PartitionSpec as P

HEAD_DIM = 64
KERNEL = 31
LEFT = 64
RIGHT = 8
WIN = 73
LANES = 128
BLOCK = 128
SPAN = 256
BACK_PAD = 64


EPSILON = 1e-05
NEGATIVE = -1e30


MESH = pl.DeviceIdType.MESH


def from_behind(value, axis, steps):
    count = lax.axis_size(axis)
    initial, last = (max(0, -steps), min(count, count - steps))
    return lax.ppermute(value, axis, [(source, source + steps) for source in range(initial, last)])


def norm_forward(values, gain):
    centered = values - jnp.mean(values, -1, keepdims=True)
    inverse = lax.rsqrt(jnp.mean(centered * centered, -1, keepdims=True) + EPSILON)
    normal = centered * inverse
    return (normal * gain, normal, inverse)


def norm_backward(grad_out, normal, inverse, gain):
    grad_normal = grad_out * gain
    grad_in = inverse * (
        grad_normal
        - jnp.mean(grad_normal, -1, keepdims=True)
        - normal * jnp.mean(grad_normal * normal, -1, keepdims=True)
    )
    grad_gain = jnp.sum(grad_out * normal, 0)
    return (grad_in, grad_gain)


def matmul(left, right):
    return jnp.dot(left, right, preferred_element_type=jnp.float32)


def matmul_left_t(left, right):
    return lax.dot_general(
        left, right, (((0,), (0,)), ((), ())), preferred_element_type=jnp.float32
    )


def matmul_right_t(left, right):
    return lax.dot_general(
        left, right, (((1,), (1,)), ((), ())), preferred_element_type=jnp.float32
    )


def swish_grad(values):
    logistic = jax.nn.sigmoid(values)
    return logistic + values * logistic * (1.0 - logistic)


def nt(left,right):
    return lax.dot_general(left,right,(((1,),(1,)),((),())),preferred_element_type=jnp.float32)
def tn(left,right):
    return lax.dot_general(left,right,(((0,),(0,)),((),())),preferred_element_type=jnp.float32)
def nn(left,right):
    return jnp.dot(left,right,preferred_element_type=jnp.float32)

def block_mask(first, block, limit):
    rows=lax.broadcasted_iota(jnp.int32,(BLOCK,SPAN),0)
    cols=lax.broadcasted_iota(jnp.int32,(BLOCK,SPAN),1)
    offset=cols-rows
    place=first+block*BLOCK+cols-LEFT
    return (offset>=0)&(offset<WIN)&(place>=0)&(place<limit)

def head_lanes(head):
    lanes=lax.broadcasted_iota(jnp.int32,(BLOCK,LANES),1)
    return (lanes>=head*HEAD_DIM)&(lanes<(head+1)*HEAD_DIM)

def block_probs(query, keys, table, mask):
    relative=pltpu.roll(nt(query,table),0,1,stride=1,stride_axis=0)
    raw=jnp.where(mask,(nt(query,keys)+relative)*(HEAD_DIM**-0.5),NEGATIVE)
    expo=jnp.exp(raw-jnp.max(raw,-1,keepdims=True))
    return expo*(1.0/jnp.sum(expo,-1,keepdims=True))

def attend_kernel(limit, first_ref, q_ref, k_ref, v_ref, t_ref, c_ref):
    table=t_ref[...]
    zero=jnp.zeros((BLOCK,LANES),jnp.bfloat16)
    for block in range(q_ref.shape[1]//BLOCK):
        rows=pl.ds(block*BLOCK,BLOCK); span=pl.ds(block*BLOCK,SPAN)
        query=q_ref[0,rows,:]; keys=k_ref[0,span,:]; values=v_ref[0,span,:]
        mask=block_mask(first_ref[0],block,limit)
        mixed=[]
        for head in range(2):
            probs=block_probs(jnp.where(head_lanes(head),query,zero),keys,table,mask)
            mixed.append(nn(probs.astype(jnp.bfloat16),values))
        c_ref[0,rows,:]=jnp.where(head_lanes(0),mixed[0],mixed[1]).astype(jnp.bfloat16)

def attend_back_kernel(limit, first_ref, q_ref, k_ref, v_ref, t_ref, g_ref, dq_ref, dk_ref, dv_ref, dt_ref, dk_sum, dv_sum):
    table=t_ref[...]
    zero=jnp.zeros((BLOCK,LANES),jnp.bfloat16)
    flip=(lax.broadcasted_iota(jnp.int32,(BLOCK,BLOCK),0)+lax.broadcasted_iota(jnp.int32,(BLOCK,BLOCK),1)==BLOCK-1).astype(jnp.float32).astype(jnp.bfloat16)
    dk_sum[...]=jnp.zeros_like(dk_sum); dv_sum[...]=jnp.zeros_like(dv_sum)
    @pl.when((pl.program_id(0)==0)&(pl.program_id(1)==0))
    def _(): dt_ref[...]=jnp.zeros_like(dt_ref)
    for block in range(q_ref.shape[1]//BLOCK):
        rows=pl.ds(block*BLOCK,BLOCK); span=pl.ds(block*BLOCK,SPAN)
        keys=k_ref[0,span,:]; values=v_ref[0,span,:]
        mask=block_mask(first_ref[0],block,limit)
        grad_query=[]
        for head in range(2):
            query=jnp.where(head_lanes(head),q_ref[0,rows,:],zero)
            grad=jnp.where(head_lanes(head),g_ref[0,rows,:],zero)
            probs=block_probs(query,keys,table,mask)
            grad_probs=nt(grad,values)
            grad_raw=probs*(grad_probs-jnp.sum(probs*grad_probs,-1,keepdims=True))
            grad_raw=grad_raw.astype(jnp.bfloat16)
            turned=pltpu.roll(nn(flip,grad_raw),SPAN-BLOCK+1,1,stride=1,stride_axis=0)
            unskewed=nn(flip,turned.astype(jnp.bfloat16)).astype(jnp.bfloat16)
            dv_sum[span,:]+=tn(probs.astype(jnp.bfloat16),grad)
            dk_sum[span,:]+=tn(grad_raw,query)
            dt_ref[...]+=tn(unskewed,query)
            grad_query.append(nn(grad_raw,keys)+nn(unskewed,table))
        dq_ref[0,rows,:]=(jnp.where(head_lanes(0),grad_query[0],grad_query[1])*(HEAD_DIM**-0.5)).astype(jnp.bfloat16)
    dk_ref[0]=(dk_sum[...]*(HEAD_DIM**-0.5)).astype(jnp.bfloat16)
    dv_ref[0]=dv_sum[...].astype(jnp.bfloat16)

def wide_table(table):
    return jnp.tile(jnp.pad(table,((0,SPAN-table.shape[0]),(0,0))),(1,LANES//HEAD_DIM))

def specs(clips,rows,width):
    own=pl.BlockSpec((1,rows,LANES),lambda c,h:(c,0,h))
    ext=pl.BlockSpec((1,rows+LEFT+BACK_PAD,LANES),lambda c,h:(c,0,h))
    tab=pl.BlockSpec((SPAN,LANES),lambda c,h:(0,0))
    return (pl.BlockSpec(memory_space=pltpu.SMEM),own,ext,tab),(clips,width//LANES)

def attend(query,keys,values,table,rows):
    clips,_,width=query.shape
    first=lax.axis_index('seq').astype(jnp.int32)[None]*rows
    limit=rows*lax.axis_size('seq')
    (sc,own,ext,tab),grid=specs(clips,rows,width)
    return pl.pallas_call(functools.partial(attend_kernel,limit),grid=grid,
        in_specs=[sc,own,ext,ext,tab],out_specs=own,
        out_shape=jax.ShapeDtypeStruct(query.shape,jnp.bfloat16),name="attend",
    )(first,query,keys,values,wide_table(table))

def attend_back(query,keys,values,table,grad,rows):
    clips,_,width=query.shape
    first=lax.axis_index('seq').astype(jnp.int32)[None]*rows
    limit=rows*lax.axis_size('seq')
    (sc,own,ext,tab),grid=specs(clips,rows,width)
    dq,dk,dv,dt=pl.pallas_call(functools.partial(attend_back_kernel,limit),grid=grid,
        in_specs=[sc,own,ext,ext,tab,own],out_specs=[own,ext,ext,tab],
        out_shape=[jax.ShapeDtypeStruct(query.shape,jnp.bfloat16),jax.ShapeDtypeStruct(keys.shape,jnp.bfloat16),jax.ShapeDtypeStruct(keys.shape,jnp.bfloat16),jax.ShapeDtypeStruct((SPAN,LANES),jnp.float32)],
        scratch_shapes=[pltpu.VMEM((rows+LEFT+BACK_PAD,LANES),jnp.float32)]*2,name="attend_back",
    )(first,query,keys,values,wide_table(table),grad)
    return dq,dk,dv,(dt[:WIN,:HEAD_DIM]+dt[:WIN,HEAD_DIM:])*(HEAD_DIM**-0.5)
def depth_of():
    return lax.axis_size("group") // 2


def place():
    group = lax.axis_index("group")
    return (group // 2, group % 2, lax.axis_index("seq"), lax.axis_index("replica"))


def greet(peers):
    barrier = pltpu.get_barrier_semaphore()
    for peer in peers:
        pl.semaphore_signal(barrier, inc=1, device_id=peer, device_id_type=MESH)
    pl.semaphore_wait(barrier, len(peers))


def neighbours():
    z, x, seq, replica = place()
    depth = depth_of()
    deep = [{"group": (z + steps) % depth * 2 + x} for steps in range(1, depth)]
    across = {"group": z * 2 + 1 - x}
    beside = {"seq": 1 - seq}
    twin = {"replica": 1 - replica}
    return (deep, across, beside, twin)


class Gather:
    def __init__(self, source, target, cut, low, high, rows, sends, recvs, at):
        depth = depth_of()
        self.source, self.target, self.cut, self.low, self.rows = (source, target, cut, low, rows)
        self.piece = (high - low) // (1, 2, 4)[cut]
        self.sends, self.recvs, self.at = (sends, recvs, at)
        self.z, self.x, self.seq, self.replica = place()
        self.deep, self.across, self.beside, self.twin = neighbours()
        self.depth = depth
        self.firsts = (0, depth - 1, 2 * depth - 1, 4 * depth - 2)
        self.started = []

    def spot(self, ref, owner, dy, dc):
        part = 0
        if self.cut:
            part = (self.replica + dc) % 2
        if self.cut == 2:
            part = part + 2 * ((self.seq + dy) % 2)
        first = pl.multiple_of(owner * self.rows + self.low + part * self.piece, self.piece)
        return ref.at[:, pl.ds(first, self.piece)]

    def owner(self, steps, dx):
        return (self.z + self.depth - steps) % self.depth * 2 + (self.x + dx) % 2

    def copy(self, steps, dx, dy, dc, kind, index, peer):
        mine = steps == 0 and dx == 0
        slot = self.at + self.firsts[kind] + index
        spot = self.spot(self.target, self.owner(steps, dx), dy, dc)
        return pltpu.make_async_remote_copy(
            src_ref=self.spot(self.source, 0, dy, dc) if mine else spot,
            dst_ref=spot,
            send_sem=self.sends.at[slot],
            recv_sem=self.recvs.at[slot],
            device_id=peer,
            device_id_type=MESH,
        )

    def send(self, copy):
        copy.start()
        self.started.append(copy)

    def to_beside(self, steps, dx):
        if self.cut == 2:
            index = dx * self.depth + steps - 1
            self.send(self.copy(steps, dx, 0, 0, 2, index, self.beside))

    def to_twin(self, steps, dx, dy):
        if self.cut:
            index = dy * (2 * self.depth - 1) + dx * self.depth + steps - 1
            self.send(self.copy(steps, dx, dy, 0, 3, index, self.twin))

    def open(self):
        for steps, peer in enumerate(self.deep, 1):
            self.send(self.copy(0, 0, 0, 0, 0, steps - 1, peer))
        self.send(self.copy(0, 0, 0, 0, 1, 0, self.across))

    def got(self, steps, dx, dy, dc, kind, index):
        self.copy(steps or self.depth, dx, dy, dc, kind, index, self.twin).wait_recv()

    def forward_deep(self):
        for steps in range(1, self.depth):
            self.got(steps, 0, 0, 0, 0, steps - 1)
            self.send(self.copy(steps, 0, 0, 0, 1, steps, self.across))
            self.to_beside(steps, 0)
            self.to_twin(steps, 0, 0)

    def forward_across(self):
        for steps in range(self.depth):
            self.got(steps, 1, 0, 0, 1, steps)
            self.to_beside(steps, 1)
            self.to_twin(steps, 1, 0)

    def others(self):
        return [(steps, dx) for dx in range(2) for steps in range(self.depth) if steps or dx]

    def forward_beside(self):
        if self.cut == 2:
            for steps, dx in self.others():
                self.got(steps, dx, 1, 0, 2, dx * self.depth + steps - 1)
                self.to_twin(steps, dx, 1)

    def close(self):
        if self.cut:
            for dy in range(self.cut):
                for steps, dx in self.others():
                    index = dy * (2 * self.depth - 1) + dx * self.depth + steps - 1
                    self.got(steps, dx, dy, 1, 3, index)
        for copy in self.started:
            copy.wait_send()


def gather_kernel(plan, count, *refs):
    ins, outs = (refs[:count], refs[count : count + len(plan)])
    helds, (sends, recvs, local) = (refs[count + len(plan) : -3], refs[-3:])
    deep, across, beside, twin = neighbours()
    peers = deep + [across, twin]
    if any(cut == 2 for _, _, cut, _ in plan):
        peers.append(beside)
    greet(peers)
    loads = [
        pltpu.make_async_copy(ins[at], held, local.at[0, at]) for at, held in enumerate(helds)
    ]
    for load in loads:
        load.start()
    jobs, stores, at = ([], [], 0)
    for number, (source, layers, cut, chunks) in enumerate(plan):
        ref = ins[source].at[pl.ds(layers[0], layers[1])]
        rows = ins[source].shape[1]
        for chunk in range(chunks):
            low, high = (rows * chunk // chunks, rows * (chunk + 1) // chunks)
            jobs.append(Gather(ref, outs[number], cut, low, high, rows, sends, recvs, at))
            at += (2, 6, 8)[cut] * depth_of()
    z, x, _, _ = place()
    ready = set()
    for tick in range(len(jobs) + 4):
        if tick < len(jobs):
            jobs[tick].open()
        if 1 <= tick < len(jobs) + 1:
            jobs[tick - 1].forward_deep()
        if 2 <= tick < len(jobs) + 2:
            jobs[tick - 2].forward_across()
        if 3 <= tick < len(jobs) + 3:
            jobs[tick - 3].forward_beside()
        if 4 <= tick:
            jobs[tick - 4].close()
        if tick < len(plan):
            source, layers, _, _ = plan[tick]
            if source not in ready:
                loads[source].wait()
                ready.add(source)
            rows = ins[source].shape[1]
            first = pl.multiple_of((z * 2 + x) * rows, rows)
            store = pltpu.make_async_copy(
                helds[source].at[pl.ds(layers[0], layers[1])],
                outs[tick].at[:, pl.ds(first, rows)],
                local.at[1, tick],
            )
            store.start()
            stores.append(store)
    for store in stores:
        store.wait()


def gather_weights(shards, plan):
    groups = lax.axis_size("group")
    total = sum((2, 6, 8)[cut] * depth_of() * chunks for _, _, cut, chunks in plan)
    return pl.pallas_call(
        functools.partial(gather_kernel, plan, len(shards)),
        in_specs=[pl.BlockSpec(memory_space=pl.ANY)] * len(shards),
        out_specs=[pl.BlockSpec(memory_space=pl.ANY)] * len(plan),
        out_shape=[
            jax.ShapeDtypeStruct(
                (layers[1], groups * shards[source].shape[1], shards[source].shape[2]), jnp.bfloat16
            )
            for source, layers, _, _ in plan
        ],
        scratch_shapes=[pltpu.VMEM(shard.shape, jnp.bfloat16) for shard in shards]
        + [
            pltpu.SemaphoreType.DMA((total,)),
            pltpu.SemaphoreType.DMA((total,)),
            pltpu.SemaphoreType.DMA((2, len(plan))),
        ],
        compiler_params=pltpu.CompilerParams(
            collective_id=1, has_side_effects=True, vmem_limit_bytes=24 << 20
        ),
        name="gather_weights",
    )(*shards)


def swap(value, axis, bit=1):
    return lax.ppermute(value, axis, [(i, i ^ bit) for i in range(lax.axis_size(axis))])


def along_depth(value, steps):
    depth = depth_of()
    pairs = [(i, (i // 2 + steps) % depth * 2 + i % 2) for i in range(2 * depth)]
    return lax.ppermute(value, "group", pairs)


def butterfly(value):
    for axis in ("replica", "seq", "group"):
        bit = 1
        while bit < lax.axis_size(axis):
            value = value + swap(value, axis, bit)
            bit *= 2
    return value


def add_slabs(count, target, *sources):
    def body(at, carry):
        total = sources[0](at)[...].astype(jnp.float32)
        for source in sources[1:]:
            total = total + source(at)[...].astype(jnp.float32)
        target(at)[...] = total.astype(jnp.bfloat16)
        return carry

    lax.fori_loop(0, count, body, 0)


class Reduce:
    def __init__(self, pool, number, source, target, low, left, cut):
        self.pool, self.number, self.cut = (pool, number, cut)
        self.source, self.target, self.low, self.left = (source, target, low, left)
        self.depth, self.span = (depth_of(), lax.axis_size("seq"))
        self.width = pool.width
        self.piece = pool.rows // (2 * cut)
        self.last = 4 + self.depth
        self.started = []
        self.stages = [
            self.exchange_twin,
            self.exchange_seq,
            self.exchange_across,
            self.exchange_deep,
            self.settle,
            self.hand_over,
            self.close,
        ]
        self.done_stages = 0
        self.ready = source is not None
        self.turn = pool.cuts.setdefault(cut, [])
        self.rank = len(self.turn)
        self.turn.append(self)
        self.own = pool.own.at[number % pool.ring]
        self.came = pool.came.at[number % pool.ring]
        self.from_x = pool.from_x.at[number % pool.ring, :, pl.ds(0, self.piece)]
        self.from_z = pool.from_z.at[number, :, pl.ds(0, self.piece)]
        self.finished = pool.finished.at[number % pool.ring, pl.ds(0, self.piece)]
        if cut == 2:
            self.from_seq = pool.from_seq.at[self.rank % pool.ring]
        else:
            self.shared = pool.shared.at[self.rank]

    def locate(self):
        self.z, self.x, self.seq, self.replica = place()
        self.deep, self.across, self.beside, self.twin = neighbours()

    def part(self, dy, dc):
        part = (self.replica + dc) % 2
        if self.cut == 2:
            part = part + 2 * ((self.seq + dy) % 2)
        return part

    def row(self, dy, dc, low=0):
        first = pl.multiple_of(low + self.part(dy, dc) * self.piece, self.piece)
        return pl.ds(first, self.piece)

    def half(self, dy):
        return pl.ds(dy * self.piece, self.piece)

    def remote(self, source, target, slot, peer):
        return pltpu.make_async_remote_copy(
            src_ref=source,
            dst_ref=target,
            send_sem=self.pool.sends.at[self.number, slot],
            recv_sem=self.pool.recvs.at[self.number, slot],
            device_id=peer,
            device_id_type=MESH,
        )

    def send(self, ends, slot, peer):
        make = lambda peer: self.remote(*ends(), slot, peer)
        make(peer).start()
        self.started.append(make)

    def wait(self, target, slot):
        self.remote(target, target, slot, self.twin).wait_recv()

    def load(self, dy):
        source = self.source.at[:, :, self.row(dy, 0, self.low), pl.ds(self.left, self.width)]
        target = self.own.at[:, :, self.row(dy, 0)]
        return pltpu.make_async_copy(source, target, self.pool.local.at[self.number, dy])

    def credit(self, kind, behind, peer):
        if behind >= self.pool.ring:
            pl.semaphore_wait(self.pool.credits.at[kind], 1)

    def release(self, kind, ahead, peer):
        if ahead:
            pl.semaphore_signal(
                self.pool.credits.at[kind], inc=1, device_id=peer, device_id_type=MESH
            )

    def exchange_twin(self):
        self.credit(0, self.number, self.twin)
        for dy in reversed(range(self.cut)):
            if self.source is None:
                ends = lambda dy=dy: (
                    self.own.at[:, :, self.row(dy, 1)],
                    self.came.at[:, :, self.half(dy)],
                )
            else:
                ends = lambda dy=dy: (
                    self.source.at[:, :, self.row(dy, 1, self.low), pl.ds(self.left, self.width)],
                    self.came.at[:, :, self.half(dy)],
                )
                self.load(dy).start()
            self.send(ends, dy, self.twin)

    def exchange_seq(self):
        if self.cut == 2:
            if self.source is not None:
                self.load(1).wait()
            self.wait(self.came.at[:, :, self.half(1)], 1)
            own = lambda at: self.own.at[at // 2, at % 2, self.row(1, 0)]
            came = lambda at: self.came.at[at // 2, at % 2, self.half(1)]
            add_slabs(2 * self.depth, own, own, came)
            self.credit(1, self.rank, self.beside)
            self.send(lambda: (self.own.at[:, :, self.row(1, 0)], self.from_seq), 2, self.beside)

    def spots(self, x):
        sources = [
            lambda at: self.own.at[at, x, self.row(0, 0)],
            lambda at: self.came.at[at, x, self.half(0)],
        ]
        if self.cut == 2:
            sources.append(lambda at: self.from_seq.at[at, x])
        return sources

    def exchange_across(self):
        if self.source is not None:
            self.load(0).wait()
        self.wait(self.came.at[:, :, self.half(0)], 0)
        if self.cut == 2:
            self.wait(self.from_seq, 2)
        sources = self.spots(1 - self.x)
        add_slabs(self.depth, sources[0], *sources)
        self.credit(2, self.number, self.across)
        ends = lambda: (self.own.at[:, 1 - self.x, self.row(0, 0)], self.from_x)
        self.send(ends, 3, self.across)

    def exchange_deep(self):
        self.wait(self.from_x, 3)
        sources = self.spots(self.x)
        add_slabs(self.depth, sources[0], lambda at: self.from_x.at[at], *sources)
        for steps, peer in enumerate(self.deep, 1):
            ends = lambda steps=steps: (
                self.own.at[(self.z + steps) % self.depth, self.x, self.row(0, 0)],
                self.from_z.at[steps - 1],
            )
            self.send(ends, 3 + steps, peer)
        total = self.pool.total
        self.release(0, self.number + self.pool.ring < total, self.twin)
        self.release(2, self.number + self.pool.ring < total, self.across)
        if self.cut == 2:
            self.release(1, self.rank + self.pool.ring < self.pool.pairs, self.beside)

    def settle(self):
        for steps in range(1, self.depth):
            self.wait(self.from_z.at[steps - 1], 3 + steps)
        self.flush()
        sources = [lambda at: self.own.at[self.z, self.x, self.row(0, 0)]]
        sources += [lambda at, steps=steps: self.from_z.at[steps - 1] for steps in range(1, self.depth)]
        if self.cut == 2:
            add_slabs(1, lambda at: self.finished, *sources)
            self.publish()
            self.send(lambda: (self.finished, self.spot(0, 0)), self.last, self.beside)
        else:
            add_slabs(1, lambda at: self.shared.at[self.seq], *sources)
            for steps in range(1, self.span):
                peer = {"seq": (self.seq + steps) % self.span}
                ends = lambda: (self.shared.at[self.seq], self.shared.at[self.seq])
                self.send(ends, self.last + 2 + steps, peer)

    def spot(self, dy, dc):
        return self.target.at[self.row(dy, dc, self.low), pl.ds(self.left, self.width)]

    def store(self):
        return pltpu.make_async_copy(
            self.finished, self.spot(0, 0), self.pool.local.at[self.number, 2]
        )

    def publish(self):
        self.store().start()
        self.send(lambda: (self.finished, self.spot(0, 0)), self.last + 1, self.twin)

    def hand_over(self):
        if self.cut == 2:
            self.wait(self.spot(1, 0), self.last)
            self.send(lambda: (self.spot(1, 0), self.spot(1, 0)), self.last + 2, self.twin)
        else:
            for steps in range(1, self.span):
                turn = (self.seq + self.span - steps) % self.span
                self.wait(self.shared.at[turn], self.last + 2 + steps)
            sources = [lambda at, turn=turn: self.shared.at[turn] for turn in range(self.span)]
            add_slabs(1, lambda at: self.finished, *sources)
            self.publish()

    def close(self):
        self.wait(self.spot(0, 1), self.last + 1)
        if self.cut == 2:
            self.wait(self.spot(1, 1), self.last + 2)
        self.store().wait()
        self.flush()

    def flush(self):
        for make in self.started:
            make(self.twin).wait_send()
        self.started = []

    def step(self):
        self.locate()
        self.stages[self.done_stages]()
        self.done_stages += 1


class Pool:
    def __init__(self, rows, width, plan, refs):
        self.ring = Pool.slots()
        self.rows, self.width, self.plan = (rows, width, plan)
        self.total = len(plan)
        self.pairs = sum(cut == 2 for cut in plan)
        names = list(Pool.shapes(rows, width, plan))
        for name, ref in zip(names, refs):
            setattr(self, name, ref)
        self.sends, self.recvs, self.local, self.credits = refs[len(names) :]
        self.cuts, self.jobs, self.next = ({}, [], 0)

    @staticmethod
    def slots():
        return 6 if lax.axis_size("seq") == 2 else 4

    @staticmethod
    def shapes(rows, width, plan):
        depth, span = (depth_of(), lax.axis_size("seq"))
        ring = min(Pool.slots(), len(plan))
        pairs = sum(cut == 2 for cut in plan)
        shapes = {
            "own": (ring, depth, 2, rows, width),
            "came": (ring, depth, 2, rows // 2, width),
            "from_x": (ring, depth, rows // 2, width),
            "from_z": (len(plan), depth - 1, rows // 2, width),
            "finished": (ring, rows // 2, width),
        }
        if pairs:
            shapes["from_seq"] = (min(ring, pairs), depth, 2, rows // 4, width)
        if pairs < len(plan):
            shapes["shared"] = (len(plan) - pairs, span, rows // 2, width)
        return shapes

    @staticmethod
    def scratch(rows, width, plan):
        slots = 7 + depth_of() + lax.axis_size("seq")
        shapes = Pool.shapes(rows, width, plan).values()
        return [pltpu.VMEM(shape, jnp.bfloat16) for shape in shapes] + [
            pltpu.SemaphoreType.DMA((len(plan), slots)),
            pltpu.SemaphoreType.DMA((len(plan), slots)),
            pltpu.SemaphoreType.DMA((len(plan), 3)),
            pltpu.SemaphoreType.REGULAR((3,)),
        ]

    def add(self, target, low, left, source=None):
        number = len(self.jobs)
        while number >= self.ring and self.jobs[number - self.ring].done_stages < 5:
            self.pump()
        job = Reduce(self, number, source, target, low, left, self.plan[number])
        self.jobs.append(job)
        return job

    def pump(self):
        active = [job for job in self.jobs if job.ready and 0 < job.done_stages < 7]
        fresh = [job for job in self.jobs if job.ready and job.done_stages == 0]
        for job in fresh[:1]:
            job.step()
        for job in reversed(active):
            job.step()

    def drain(self):
        while any(job.done_stages < 7 for job in self.jobs):
            self.pump()


def row_blocks(total, size, body):
    def step(at, carry):
        body(pl.ds(pl.multiple_of(at * size, size), size))
        return carry

    lax.fori_loop(0, total // size, step, 0)


def norm_parts(values):
    centered = values - jnp.mean(values, -1, keepdims=True)
    inverse = lax.rsqrt(jnp.mean(centered * centered, -1, keepdims=True) + EPSILON)
    return (centered * inverse, inverse)


def norm_rows(source, gain, target):
    def body(rows):
        normal, _ = norm_parts(source[rows, :].astype(jnp.float32))
        target[rows, :] = (normal * gain).astype(target.dtype)

    row_blocks(source.shape[0], 64, body)


def norm_back_rows(source, gain, grads, resid, sums, line):
    sums[pl.ds(line, 1), :] = jnp.zeros_like(sums[pl.ds(line, 1), :])

    def body(rows):
        normal, inverse = norm_parts(source[rows, :].astype(jnp.float32))
        grad = grads[rows, :]
        grad_normal = grad * gain
        resid[rows, :] += inverse * (
            grad_normal
            - jnp.mean(grad_normal, -1, keepdims=True)
            - normal * jnp.mean(grad_normal * normal, -1, keepdims=True)
        )
        sums[pl.ds(line, 1), :] += jnp.sum(grad * normal, 0, keepdims=True)

    row_blocks(source.shape[0], 64, body)


def cast_rows(source, target, scale=1.0):
    def body(rows):
        target[rows, :] = (source[rows, :] * scale).astype(jnp.bfloat16)

    row_blocks(source.shape[0], 64, body)


def transposed_rows(left, right, target, size=256):
    def body(cols):
        target[:, cols] = nt(left[...], right[cols, :]).astype(target.dtype)

    row_blocks(right.shape[0], size, body)


def add_transposed(left, right, target, size=256):
    def body(cols):
        target[:, cols] += nt(left[...], right[cols, :])

    row_blocks(right.shape[0], size, body)


def gradient_into(job, left, right):
    depth, _, rows, width = job.own.shape

    def step(z, carry):
        cols = pl.ds(pl.multiple_of(z * 2 * rows, 2 * rows), 2 * rows)
        value = tn(left[:, cols], right[...]).astype(jnp.bfloat16)
        job.own[z, 0] = value[:rows]
        job.own[z, 1] = value[rows:]
        return carry

    lax.fori_loop(0, depth, step, 0)
    job.ready = True


class Stream:
    def __init__(self, buffers, sems, copies):
        self.buffers, self.sems, self.copies = (buffers, sems, copies)
        self.issued = self.taken = 0
        for _ in range(len(buffers) - 1):
            self.issue()

    def parts(self, number):
        slot = number % len(self.buffers)
        made = self.copies[number](self.buffers[slot])
        return [
            pltpu.make_async_copy(source, target, self.sems.at[slot, at])
            for at, (source, target) in enumerate(made)
        ]

    def issue(self):
        if self.issued < len(self.copies):
            for copy in self.parts(self.issued):
                copy.start()
            self.issued += 1

    def take(self):
        for copy in self.parts(self.taken):
            copy.wait()
        self.taken += 1
        self.issue()
        return self.buffers[(self.taken - 1) % len(self.buffers)]


def module_copies(w_in, w_out, groups):
    chunks = w_out.shape[1]
    rows = w_out.shape[2]
    copies = []
    for chunk in range(chunks):
        copies.append(
            lambda slot, chunk=chunk: [
                (w_out.at[group, chunk], slot.at[pl.ds(group * rows, rows)])
                for group in range(groups)
            ]
        )
        copies.append(
            lambda slot, chunk=chunk: [
                (
                    w_in.at[:, pl.ds((group * chunks + chunk) * rows, rows)],
                    slot.at[:, pl.ds(group * rows, rows)],
                )
                for group in range(groups)
            ]
        )
    return copies


def saved_copies(saved, groups, rows):
    chunks = saved.shape[1] // (groups * rows)
    return [
        lambda slot, chunk=chunk: [
            (
                saved.at[:, pl.ds((group * chunks + chunk) * rows, rows)],
                slot.at[:, pl.ds(group * rows, rows)],
            )
            for group in range(groups)
        ]
        for chunk in range(chunks)
    ]


def module_back(pool, pump, weights, saved, buffers, chunks, outs):
    entry, low, hidden, grad_hidden, total = buffers
    grad_in, grad_out = outs
    width = total.shape[1]
    total[...] = jnp.zeros_like(total)
    for chunk in range(chunks):
        before = saved.take()
        w_out = weights.take()

        def body(cols):
            value = before[:, cols].astype(jnp.float32)
            logistic = jax.nn.sigmoid(value)
            hidden[:, cols] = (value * logistic).astype(jnp.bfloat16)
            slope = logistic * (1.0 + value * (1.0 - logistic))
            grad = nt(low[...], w_out[cols, :]) * slope
            grad_hidden[:, cols] = grad.astype(jnp.bfloat16)

        row_blocks(width, 256, body)
        job = pool.add(grad_out, chunk * pool.rows, 0)
        gradient_into(job, hidden, low)
        pump()
        job = pool.add(grad_in, 0, chunk * width)
        gradient_into(job, entry, grad_hidden)
        pump()
        add_transposed(grad_hidden, weights.take(), total)
        pump()
def late_back_kernel(settings, *refs):
    plan, early, count, clips, rows, limit = settings
    first_ref, table_ref, gains = refs[:3]
    grad, x1, x0, u0, mixed, query, keys, values, a_out, qkv, w_in, w_out = refs[3:15]
    refs = refs[15:]
    sources, refs = (refs[:count], refs[count:])
    grad_x, gain_sums, dt_ref, to_attn, to_q, to_k, to_v, to_out, to_in = refs[:9]
    refs = refs[9:]
    targets, refs = (refs[:count], refs[count:])
    resid, total, resid_in, low, entry, mixed_grad, q_ref, dq_ref = refs[:8]
    k_ref, v_ref, dk_ref, dv_ref, later, earlier, dk_sum, dv_sum, slots = refs[8:17]
    local, slot_sems, saved_sems, halo_sems = refs[17:21]
    width = total.shape[1]
    groups = lax.axis_size("group")
    part = width // groups
    span = lax.axis_size("seq")
    chunks = w_out.shape[1]
    reduce_greet()
    pool = Pool(part, width, plan, refs[21:])
    loads = [
        pltpu.make_async_copy(source, target, local.at[at])
        for at, (source, target) in enumerate(
            (
                (grad, resid),
                (mixed, entry),
                (query, q_ref),
                (keys, k_ref),
                (values, v_ref),
                (x1, resid_in),
            )
        )
    ]
    for load in loads:
        load.start()
    copies = [lambda slot: [(a_out, slot)]]
    copies += [lambda slot, at=at: [(qkv.at[at], slot)] for at in range(3)]
    copies += module_copies(w_in, w_out, groups)
    weights = Stream([slots.at[at] for at in range(3)], slot_sems, copies)
    waiting = list(early)

    def feed():
        number = len(pool.jobs)
        free = number < pool.ring or pool.jobs[number - pool.ring].done_stages >= 5
        if waiting and free and not any(job.done_stages == 0 for job in pool.jobs):
            source, low_row, left = waiting.pop(0)
            pool.add(targets[source], low_row, left, sources[source])

    def pump():
        feed()
        pool.pump()

    pump()
    loads[0].wait()
    cast_rows(resid, low)
    loads[1].wait()
    job = pool.add(to_attn, 0, 0)
    gradient_into(job, entry, low)
    pump()
    transposed_rows(low, weights.take(), mixed_grad)
    pump()
    for load in loads[2:]:
        load.wait()
    table = table_ref[...]
    zero = jnp.zeros((BLOCK, LANES), jnp.bfloat16)
    across = lax.broadcasted_iota(jnp.int32, (BLOCK, BLOCK), 0)
    across = across + lax.broadcasted_iota(jnp.int32, (BLOCK, BLOCK), 1)
    flip = (across == BLOCK - 1).astype(jnp.float32).astype(jnp.bfloat16)
    dt_ref[...] = jnp.zeros_like(dt_ref)
    blocks = rows // BLOCK
    for pair in range(width // LANES):
        lanes = pl.ds(pair * LANES, LANES)
        dk_sum[...] = jnp.zeros_like(dk_sum)
        dv_sum[...] = jnp.zeros_like(dv_sum)

        def attend_block(at, carry):
            clip, block = (at // blocks, at % blocks)
            here = pl.ds(pl.multiple_of(at * BLOCK, BLOCK), BLOCK)
            near = pl.ds(pl.multiple_of(block * BLOCK, BLOCK), SPAN)
            key = k_ref[clip, near, lanes]
            value = v_ref[clip, near, lanes]
            mask = block_mask(first_ref[0], block, limit)
            grad_query = []
            for head in range(2):
                q = jnp.where(head_lanes(head), q_ref[here, lanes], zero)
                g = jnp.where(head_lanes(head), mixed_grad[here, lanes], zero)
                probs = block_probs(q, key, table, mask)
                grad_probs = nt(g, value)
                grad_raw = probs * (grad_probs - jnp.sum(probs * grad_probs, -1, keepdims=True))
                grad_raw = grad_raw.astype(jnp.bfloat16)
                turned = pltpu.roll(
                    nn(flip, grad_raw), SPAN - BLOCK + 1, 1, stride=1, stride_axis=0
                )
                unskewed = nn(flip, turned.astype(jnp.bfloat16)).astype(jnp.bfloat16)
                dv_sum[clip, near, :] += tn(probs.astype(jnp.bfloat16), g)
                dk_sum[clip, near, :] += tn(grad_raw, q)
                dt_ref[...] += tn(unskewed, q)
                grad_query.append(nn(grad_raw, key) + nn(unskewed, table))
            both = jnp.where(head_lanes(0), grad_query[0], grad_query[1])
            dq_ref[here, lanes] = (both * HEAD_DIM**-0.5).astype(jnp.bfloat16)
            return carry

        lax.fori_loop(0, clips * blocks, attend_block, 0)
        dk_ref[:, :, lanes] = (dk_sum[...] * HEAD_DIM**-0.5).astype(jnp.bfloat16)
        dv_ref[:, :, lanes] = dv_sum[...].astype(jnp.bfloat16)
        pump()

    _, _, seq, _ = place()
    free = [ref.at[0, pl.ds(0, rows)] for ref in (k_ref, v_ref)]
    saved = Stream(free, saved_sems, saved_copies(u0, groups, part))
    edges = []
    for at, ref in enumerate((dk_ref, dv_ref)):
        for way, (target, low_row, size, step) in enumerate(
            ((later, 0, LEFT, span - 1), (earlier, LEFT + rows, 2 * RIGHT, 1))
        ):
            edges.append(
                pltpu.make_async_remote_copy(
                    src_ref=ref.at[:, pl.ds(low_row, size)],
                    dst_ref=target.at[at],
                    send_sem=halo_sems.at[0, 2 * at + way],
                    recv_sem=halo_sems.at[1, 2 * at + way],
                    device_id={"seq": (seq + step) % span},
                    device_id_type=MESH,
                )
            )
    for edge in edges:
        edge.start()
    gain = gains[pl.ds(1, 1), :]
    norm_rows(resid_in, gain, entry)
    job = pool.add(to_q, 0, 0)
    gradient_into(job, entry, dq_ref)
    total[...] = jnp.zeros_like(total)
    add_transposed(dq_ref, weights.take(), total)
    pump()
    for edge in edges:
        edge.wait()
    for at, (ref, flat) in enumerate(((dk_ref, mixed_grad), (dv_ref, q_ref))):
        for clip in range(clips):
            base = clip * rows
            flat[pl.ds(base, rows), :] = ref[clip, pl.ds(LEFT, rows), :]
            tail = pl.ds(base + rows - LEFT, LEFT)
            zero_tail = jnp.zeros((LEFT, width), jnp.float32)
            came = jnp.where(seq < span - 1, later[at, clip].astype(jnp.float32), zero_tail)
            flat[tail, :] = (flat[tail, :].astype(jnp.float32) + came).astype(jnp.bfloat16)
            head = pl.ds(base, 2 * RIGHT)
            zero_head = jnp.zeros((2 * RIGHT, width), jnp.float32)
            came = jnp.where(seq > 0, earlier[at, clip].astype(jnp.float32), zero_head)
            flat[head, :] = (flat[head, :].astype(jnp.float32) + came).astype(jnp.bfloat16)
    for target, flat in ((to_k, mixed_grad), (to_v, q_ref)):
        job = pool.add(target, 0, 0)
        gradient_into(job, entry, flat)
        pump()
        add_transposed(flat, weights.take(), total)
        pump()
    norm_back_rows(resid_in, gain, total, resid, gain_sums, 1)
    load = pltpu.make_async_copy(x0, dq_ref, local.at[0])
    load.start()
    cast_rows(resid, low, 0.5)
    load.wait()
    gain = gains[pl.ds(0, 1), :]
    norm_rows(dq_ref, gain, entry)
    buffers = (entry, low, mixed_grad, q_ref, total)
    module_back(pool, pump, weights, saved, buffers, chunks, (to_in, to_out))
    while waiting:
        pump()
    norm_back_rows(dq_ref, gain, total, resid, gain_sums, 0)
    cast_rows(resid, low)
    store = pltpu.make_async_copy(low, grad_x, local.at[1])
    store.start()
    pool.drain()
    store.wait()


def reduce_views(grads):
    groups = lax.axis_size("group")
    return [grad.reshape(groups // 2, 2, grad.shape[0] // groups, grad.shape[1]) for grad in grads]


def early_list(views, rows, width):
    return [
        (source, low, left)
        for source, view in enumerate(views)
        for low in range(0, view.shape[2], rows)
        for left in range(0, view.shape[3], width)
    ]


def reduce_greet():
    deep, across, _, twin = neighbours()
    span = lax.axis_size("seq")
    seq = lax.axis_index("seq")
    greet(deep + [across, twin] + [{"seq": (seq + steps) % span} for steps in range(1, span)])


def late_back(grad, x1, x0, u0, kept, table, gains, weights, grads, rows, halve):
    query, keys, values, mixed = kept
    a_out, qkv, w_in, w_out = weights
    clips, ext, width = keys.shape
    flat = clips * rows
    groups = lax.axis_size("group")
    part = width // groups
    chunks = w_out.shape[0] // width
    views = reduce_views(grads)
    early = early_list(views, part, width)
    count = len(early) + 4 + 2 * chunks
    plan = [2 if halve and at % 2 == 0 else 1 for at in range(count)]
    first = lax.axis_index("seq").astype(jnp.int32)[None] * rows
    limit = rows * lax.axis_size("seq")
    hbm = pl.BlockSpec(memory_space=pl.ANY)
    vmem = pl.BlockSpec(memory_space=pltpu.VMEM)
    low = lambda *shape: jax.ShapeDtypeStruct(shape, jnp.bfloat16)
    wide = lambda *shape: jax.ShapeDtypeStruct(shape, jnp.float32)
    holds = [pltpu.VMEM((flat, width), jnp.float32)] * 3
    holds += [pltpu.VMEM((flat, width), jnp.bfloat16)] * 5
    holds += [pltpu.VMEM((clips, ext, width), jnp.bfloat16)] * 4
    holds += [
        pltpu.VMEM((2, clips, LEFT, width), jnp.bfloat16),
        pltpu.VMEM((2, clips, 2 * RIGHT, width), jnp.bfloat16),
        pltpu.VMEM((clips, ext, LANES), jnp.float32),
        pltpu.VMEM((clips, ext, LANES), jnp.float32),
        pltpu.VMEM((3, width, width), jnp.bfloat16),
        pltpu.SemaphoreType.DMA((6,)),
        pltpu.SemaphoreType.DMA((3, groups)),
        pltpu.SemaphoreType.DMA((2, groups)),
        pltpu.SemaphoreType.DMA((2, 4)),
    ]
    results = pl.pallas_call(
        functools.partial(late_back_kernel, (plan, early, len(views), clips, rows, limit)),
        in_specs=[pl.BlockSpec(memory_space=pltpu.SMEM), vmem, vmem] + [hbm] * (12 + len(views)),
        out_specs=[hbm, vmem, vmem] + [hbm] * (6 + len(views)),
        out_shape=[low(flat, width), wide(8, width), wide(SPAN, LANES)]
        + [low(part, width)] * 4
        + [low(chunks * part, width), low(part, chunks * width)]
        + [low(*view.shape[2:]) for view in views],
        scratch_shapes=holds + Pool.scratch(part, width, plan),
        compiler_params=pltpu.CompilerParams(
            collective_id=3, has_side_effects=True, vmem_limit_bytes=62 << 20
        ),
        name="late_back",
    )(
        first,
        wide_table(table),
        gains,
        grad,
        x1,
        x0,
        u0,
        mixed,
        query.reshape(flat, width),
        keys,
        values,
        a_out,
        qkv,
        w_in,
        w_out.reshape(groups, chunks, part, width),
        *views,
    )
    grad_x, gain_sums, dt = results[:3]
    dt = (dt[:WIN, :HEAD_DIM] + dt[:WIN, HEAD_DIM:]) * HEAD_DIM**-0.5
    return grad_x, gain_sums, dt, results[3:9], results[9:]


def unmix(grad, groups):
    rows, width = grad.shape
    chunks = width // (rows * groups)
    return grad.reshape(rows, chunks, groups, rows).transpose(0, 2, 1, 3).reshape(rows, width)


def feed_forward(resid, gain, w_in, w_out):
    normed, normal, inverse = norm_forward(resid, gain)
    entry = normed.astype(jnp.bfloat16)
    hidden_pre = matmul(entry, w_in)
    hidden = (hidden_pre * jax.nn.sigmoid(hidden_pre)).astype(jnp.bfloat16)
    return (matmul(hidden, w_out), (normal, inverse, entry, hidden_pre, hidden))


def feed_back(grad_branch, kept, gain, w_in, w_out):
    normal, inverse, entry, hidden_pre, hidden = kept
    grad_low = grad_branch.astype(jnp.bfloat16)
    grad_w_out = matmul_left_t(hidden, grad_low).astype(jnp.bfloat16)
    grad_hidden = (matmul_right_t(grad_low, w_out) * swish_grad(hidden_pre)).astype(jnp.bfloat16)
    grad_w_in = matmul_left_t(entry, grad_hidden).astype(jnp.bfloat16)
    grad_in, grad_gain = norm_backward(matmul_right_t(grad_hidden, w_in), normal, inverse, gain)
    return (grad_in, grad_gain, grad_w_in, grad_w_out)


def attention_forward(resid, gain, qkv, attn_out, table, shape):
    clips, rows, width = shape
    normed, normal, inverse = norm_forward(resid, gain)
    entry = normed.astype(jnp.bfloat16)
    query, keys, values = [
        matmul(entry, qkv[part]).astype(jnp.bfloat16).reshape(shape) for part in range(3)
    ]
    tail = jnp.zeros((clips, BACK_PAD - RIGHT, width), jnp.bfloat16)

    def extend(value):
        before = from_behind(value[:, rows - LEFT :], "seq", 1)
        after = from_behind(value[:, :RIGHT], "seq", -1)
        return jnp.concatenate([before, value, after, tail], 1)

    keys, values = (extend(keys), extend(values))
    mixed = attend(query, keys, values, table, rows).reshape(clips * rows, width)
    return (matmul(mixed, attn_out), (normal, inverse, entry, query, keys, values, mixed))


def attention_back(grad_branch, kept, gain, qkv, attn_out, table, shape):
    clips, rows, width = shape
    normal, inverse, entry, query, keys, values, mixed = kept
    grad_low = grad_branch.astype(jnp.bfloat16)
    grad_attn_out = matmul_left_t(mixed, grad_low).astype(jnp.bfloat16)
    grad_mixed = matmul_right_t(grad_low, attn_out).astype(jnp.bfloat16).reshape(shape)
    grad_query, grad_keys, grad_values, grad_table = attend_back(
        query, keys, values, table, grad_mixed, rows
    )

    def fold(grad):
        from_later = from_behind(grad[:, :LEFT], "seq", -1).astype(jnp.float32)
        from_earlier = from_behind(grad[:, LEFT + rows : LEFT + rows + RIGHT], "seq", 1)
        own = grad[:, LEFT : LEFT + rows].astype(jnp.float32)
        own = own + jnp.pad(from_later, ((0, 0), (rows - LEFT, 0), (0, 0)))
        own = own + jnp.pad(from_earlier.astype(jnp.float32), ((0, 0), (0, rows - RIGHT), (0, 0)))
        return own.astype(jnp.bfloat16).reshape(clips * rows, width)

    parts = [grad_query.reshape(clips * rows, width), fold(grad_keys), fold(grad_values)]
    grad_qkv = [matmul_left_t(entry, part).astype(jnp.bfloat16) for part in parts]
    grad_entry = sum(matmul_right_t(part, qkv[at]) for at, part in enumerate(parts))
    grad_in, grad_gain = norm_backward(grad_entry, normal, inverse, gain)
    return (grad_in, grad_gain, grad_qkv, grad_attn_out, grad_table)


def conv_forward(resid, gain_in, gain_mid, conv_in, depthwise, conv_out, shape):
    clips, rows, width = shape
    normed, normal, inverse = norm_forward(resid, gain_in)
    entry = normed.astype(jnp.bfloat16)
    joined = matmul(entry, conv_in)
    opened = jax.nn.sigmoid(joined[:, width:])
    glu = (joined[:, :width] * opened).astype(jnp.bfloat16).reshape(clips, rows, width)
    before = from_behind(glu[:, rows - (KERNEL - 1) :], "seq", 1)
    padded = jnp.concatenate([before, glu], 1).astype(jnp.float32)
    taps = depthwise.astype(jnp.float32)
    summed = jnp.zeros((clips, rows, width), jnp.float32)
    for tap in range(KERNEL):
        summed = summed + taps[tap] * padded[:, tap : tap + rows]
    middle, mid_normal, mid_inverse = norm_forward(summed.reshape(clips * rows, width), gain_mid)
    swished = (middle * jax.nn.sigmoid(middle)).astype(jnp.bfloat16)
    kept = (
        normal,
        inverse,
        entry,
        joined,
        opened,
        padded,
        middle,
        mid_normal,
        mid_inverse,
        swished,
    )
    return (matmul(swished, conv_out), kept)


def conv_back(grad_branch, kept, gain_in, gain_mid, conv_in, depthwise, conv_out, shape):
    clips, rows, width = shape
    normal, inverse, entry, joined, opened, padded, middle, mid_normal, mid_inverse, swished = kept
    taps = depthwise.astype(jnp.float32)
    grad_low = grad_branch.astype(jnp.bfloat16)
    grad_conv_out = matmul_left_t(swished, grad_low).astype(jnp.bfloat16)
    grad_middle = matmul_right_t(grad_low, conv_out) * swish_grad(middle)
    grad_summed, grad_gain_mid = norm_backward(grad_middle, mid_normal, mid_inverse, gain_mid)
    grad_summed = grad_summed.reshape(clips, rows, width)
    grad_taps = jnp.stack(
        [jnp.sum(grad_summed * padded[:, tap : tap + rows], (0, 1)) for tap in range(KERNEL)]
    )
    grad_padded = jnp.zeros((clips, rows + KERNEL - 1, width), jnp.float32)
    for tap in range(KERNEL):
        grad_padded = grad_padded + jnp.pad(
            grad_summed * taps[tap], ((0, 0), (tap, KERNEL - 1 - tap), (0, 0))
        )
    from_later = from_behind(grad_padded[:, : KERNEL - 1].astype(jnp.bfloat16), "seq", -1).astype(
        jnp.float32
    )
    grad_glu = (
        grad_padded[:, KERNEL - 1 :]
        .at[:, rows - (KERNEL - 1) :]
        .add(from_later)
        .reshape(clips * rows, width)
    )
    value_part = joined[:, :width]
    grad_joined = jnp.concatenate(
        [grad_glu * opened, grad_glu * value_part * opened * (1.0 - opened)], 1
    )
    grad_joined = grad_joined.astype(jnp.bfloat16)
    grad_conv_in = matmul_left_t(entry, grad_joined).astype(jnp.bfloat16)
    grad_in, grad_gain_in = norm_backward(
        matmul_right_t(grad_joined, conv_in), normal, inverse, gain_in
    )
    return (grad_in, grad_gain_in, grad_gain_mid, grad_conv_in, grad_taps, grad_conv_out)


def on_device(
    tokens,
    ffn_in,
    ffn_out,
    qkv,
    attn_out,
    conv_in,
    conv_out,
    depthwise,
    gains,
    rel_table,
    cotangent,
):
    clips, rows, width = tokens.shape
    shape = (clips, rows, width)
    flat_rows = clips * rows
    halve = lax.axis_size("seq") == 2
    norms, taps = (gains.shape[0], depthwise.shape[0])
    lines = -(-(norms + taps) // 16) * 16
    small = jnp.concatenate([gains, depthwise], 0)
    small = jnp.pad(small, ((0, lines - norms - taps), (0, 0)))[None]
    shards = (small, ffn_in, ffn_out, qkv, attn_out[None], conv_in[None], conv_out[None])
    cut = 2 if halve else 1
    plan = (
        (0, (0, 1), 0, 1),
        (1, (0, 1), cut, 2),
        (2, (0, 1), cut, 2),
        (3, (0, 3), 1, 1),
        (4, (0, 1), 1, 1),
        (5, (0, 1), 1, 1),
        (6, (0, 1), 1, 1),
        (1, (1, 1), cut, 2),
        (2, (1, 1), cut, 2),
    )
    gathered = gather_weights(shards, plan)
    small = gathered[0].reshape(-1, lines, gains.shape[1]).transpose(1, 0, 2).reshape(lines, width)
    gain_f = small[:norms].astype(jnp.float32)
    depth = small[norms : norms + taps]
    f_in = (gathered[1][0], gathered[7][0])
    f_out = (gathered[2][0], gathered[8][0])
    proj, a_out, c_in, c_out = (gathered[3], gathered[4][0], gathered[5][0], gathered[6][0])
    start = tokens.reshape(flat_rows, width).astype(jnp.float32)
    first_branch, first_kept = feed_forward(start, gain_f[0], f_in[0], f_out[0])
    after_first = start + 0.5 * first_branch
    attn_branch, attn_kept = attention_forward(
        after_first, gain_f[1], proj, a_out, rel_table, shape
    )
    after_attn = after_first + attn_branch
    conv_branch, conv_kept = conv_forward(
        after_attn, gain_f[2], gain_f[3], c_in, depth, c_out, shape
    )
    after_conv = after_attn + conv_branch
    second_branch, second_kept = feed_forward(after_conv, gain_f[4], f_in[1], f_out[1])
    final = after_conv + 0.5 * second_branch
    result, final_normal, final_inverse = norm_forward(final, gain_f[5])
    squares = jnp.stack(
        [
            jnp.sum(member * member)
            for member in (final, first_branch, attn_branch, conv_branch, second_branch)
        ]
    )
    grad = cotangent.reshape(flat_rows, width).astype(jnp.float32)
    grad, grad_gain_final = norm_backward(grad, final_normal, final_inverse, gain_f[5])
    back_in, grad_gain_second, grad_in_second, grad_out_second = feed_back(
        0.5 * grad, second_kept, gain_f[4], f_in[1], f_out[1]
    )
    grad = grad + back_in
    back_in, grad_gain_conv, grad_gain_mid, grad_conv_in, grad_taps, grad_conv_out = conv_back(
        grad, conv_kept, gain_f[2], gain_f[3], c_in, depth, c_out, shape
    )
    grad = grad + back_in
    if halve and clips == 1 and gains.shape[1] % LANES == 0:
        early = [grad_out_second, grad_in_second, grad_conv_out, grad_conv_in]
        grad, gain_sums, grad_table, mine, early = late_back(
            grad,
            after_first,
            tokens.reshape(flat_rows, width),
            first_kept[3].astype(jnp.bfloat16),
            attn_kept[3:],
            rel_table,
            small[:8].astype(jnp.float32),
            (a_out, proj, f_in[0], f_out[0]),
            early,
            rows,
            halve,
        )
        grad_gain_first, grad_gain_attn = (gain_sums[0], gain_sums[1])
        grad_attn_out, grad_out_first = (mine[0], mine[4])
        grad_qkv, grad_in_first = (mine[1:4], unmix(mine[5], lax.axis_size("group")))
        grad_out_second, grad_in_second, grad_conv_out, grad_conv_in = early
    else:
        back_in, grad_gain_attn, grad_qkv, grad_attn_out, grad_table = attention_back(
            grad, attn_kept, gain_f[1], proj, a_out, rel_table, shape
        )
        grad = grad + back_in
        back_in, grad_gain_first, grad_in_first, grad_out_first = feed_back(
            0.5 * grad, first_kept, gain_f[0], f_in[0], f_out[0]
        )
        grad = grad + back_in
        matrices = [grad_in_first, grad_in_second, grad_out_first, grad_out_second]
        matrices += [grad_attn_out, grad_conv_in, grad_conv_out] + grad_qkv
        matrices = [
            lax.psum(lax.psum_scatter(member, "group", tiled=True), ("seq", "replica"))
            for member in matrices
        ]
        grad_in_first, grad_in_second, grad_out_first, grad_out_second = matrices[:4]
        grad_attn_out, grad_conv_in, grad_conv_out = matrices[4:7]
        grad_qkv = matrices[7:]
    gain_grads = jnp.stack(
        [
            grad_gain_first,
            grad_gain_attn,
            grad_gain_conv,
            grad_gain_mid,
            grad_gain_second,
            grad_gain_final,
        ]
    )
    loose = jnp.concatenate([grad_table.reshape(-1), squares])
    lines = -(-loose.shape[0] // width)
    loose = jnp.pad(loose, (0, lines * width - loose.shape[0])).reshape(lines, width)
    totals = butterfly(jnp.concatenate([gain_grads, grad_taps, loose], 0))
    owned = lax.dynamic_slice_in_dim(
        totals[: norms + taps], lax.axis_index("group") * gains.shape[1], gains.shape[1], 1
    )
    loose = totals[norms + taps :].reshape(-1)
    table_size = rel_table.shape[0] * rel_table.shape[1]
    count = (
        flat_rows * width * lax.axis_size("seq") * lax.axis_size("group") * lax.axis_size("replica")
    )
    stats = jnp.sqrt(loose[table_size : table_size + 5] / count)
    return (
        result.astype(jnp.bfloat16).reshape(shape),
        grad.astype(jnp.bfloat16).reshape(shape),
        jnp.stack([grad_in_first, grad_in_second]).astype(jnp.float32),
        jnp.stack([grad_out_first, grad_out_second]).astype(jnp.float32),
        jnp.stack(grad_qkv).astype(jnp.float32),
        grad_attn_out.astype(jnp.float32),
        grad_conv_in.astype(jnp.float32),
        grad_conv_out.astype(jnp.float32),
        owned[norms:],
        owned[:norms],
        loose[:table_size].reshape(rel_table.shape),
        stats,
    )


def solution(mesh):
    in_specs = (
        P(("group", "replica"), "seq", None),
        P(None, "group", None),
        P(None, "group", None),
        P(None, "group", None),
        P("group", None),
        P("group", None),
        P("group", None),
        P(None, "group"),
        P(None, "group"),
        P(),
        P(("group", "replica"), "seq", None),
    )
    out_specs = (
        P(("group", "replica"), "seq", None),
        P(("group", "replica"), "seq", None),
        P(None, "group", None),
        P(None, "group", None),
        P(None, "group", None),
        P("group", None),
        P("group", None),
        P("group", None),
        P(None, "group"),
        P(None, "group"),
        P(),
        P(),
    )
    return jax.shard_map(
        on_device, mesh=mesh, in_specs=in_specs, out_specs=out_specs, check_vma=False
    )
```

```python
import functools

import jax
import jax.numpy as jnp
from jax import lax
from jax.experimental import pallas as pl
from jax.experimental.pallas import tpu as pltpu
from jax.sharding import PartitionSpec as P

HEAD_DIM = 64
KERNEL = 31
LEFT = 64
RIGHT = 8
WIN = 73
LANES = 128
BLOCK = 128
SPAN = 256
BACK_PAD = 64


EPSILON = 1e-05
NEGATIVE = -1e30


MESH = pl.DeviceIdType.MESH


def from_behind(value, axis, steps):
    count = lax.axis_size(axis)
    initial, last = (max(0, -steps), min(count, count - steps))
    return lax.ppermute(value, axis, [(source, source + steps) for source in range(initial, last)])


def norm_forward(values, gain):
    centered = values - jnp.mean(values, -1, keepdims=True)
    inverse = lax.rsqrt(jnp.mean(centered * centered, -1, keepdims=True) + EPSILON)
    normal = centered * inverse
    return (normal * gain, normal, inverse)


def norm_backward(grad_out, normal, inverse, gain):
    grad_normal = grad_out * gain
    grad_in = inverse * (
        grad_normal
        - jnp.mean(grad_normal, -1, keepdims=True)
        - normal * jnp.mean(grad_normal * normal, -1, keepdims=True)
    )
    grad_gain = jnp.sum(grad_out * normal, 0)
    return (grad_in, grad_gain)


def matmul(left, right):
    return jnp.dot(left, right, preferred_element_type=jnp.float32)


def matmul_left_t(left, right):
    return lax.dot_general(
        left, right, (((0,), (0,)), ((), ())), preferred_element_type=jnp.float32
    )


def matmul_right_t(left, right):
    return lax.dot_general(
        left, right, (((1,), (1,)), ((), ())), preferred_element_type=jnp.float32
    )


def swish_grad(values):
    logistic = jax.nn.sigmoid(values)
    return logistic + values * logistic * (1.0 - logistic)


def nt(left,right):
    return lax.dot_general(left,right,(((1,),(1,)),((),())),preferred_element_type=jnp.float32)
def tn(left,right):
    return lax.dot_general(left,right,(((0,),(0,)),((),())),preferred_element_type=jnp.float32)
def nn(left,right):
    return jnp.dot(left,right,preferred_element_type=jnp.float32)

def block_mask(first, block, limit):
    rows=lax.broadcasted_iota(jnp.int32,(BLOCK,SPAN),0)
    cols=lax.broadcasted_iota(jnp.int32,(BLOCK,SPAN),1)
    offset=cols-rows
    place=first+block*BLOCK+cols-LEFT
    return (offset>=0)&(offset<WIN)&(place>=0)&(place<limit)

def head_lanes(head):
    lanes=lax.broadcasted_iota(jnp.int32,(BLOCK,LANES),1)
    return (lanes>=head*HEAD_DIM)&(lanes<(head+1)*HEAD_DIM)

def block_probs(query, keys, table, mask):
    relative=pltpu.roll(nt(query,table),0,1,stride=1,stride_axis=0)
    raw=jnp.where(mask,(nt(query,keys)+relative)*(HEAD_DIM**-0.5),NEGATIVE)
    expo=jnp.exp(raw-jnp.max(raw,-1,keepdims=True))
    return expo*(1.0/jnp.sum(expo,-1,keepdims=True))

def attend_kernel(limit, first_ref, q_ref, k_ref, v_ref, t_ref, c_ref):
    table=t_ref[...]
    zero=jnp.zeros((BLOCK,LANES),jnp.bfloat16)
    for block in range(q_ref.shape[1]//BLOCK):
        rows=pl.ds(block*BLOCK,BLOCK); span=pl.ds(block*BLOCK,SPAN)
        query=q_ref[0,rows,:]; keys=k_ref[0,span,:]; values=v_ref[0,span,:]
        mask=block_mask(first_ref[0],block,limit)
        mixed=[]
        for head in range(2):
            probs=block_probs(jnp.where(head_lanes(head),query,zero),keys,table,mask)
            mixed.append(nn(probs.astype(jnp.bfloat16),values))
        c_ref[0,rows,:]=jnp.where(head_lanes(0),mixed[0],mixed[1]).astype(jnp.bfloat16)

def attend_back_kernel(limit, first_ref, q_ref, k_ref, v_ref, t_ref, g_ref, dq_ref, dk_ref, dv_ref, dt_ref, dk_sum, dv_sum):
    table=t_ref[...]
    zero=jnp.zeros((BLOCK,LANES),jnp.bfloat16)
    flip=(lax.broadcasted_iota(jnp.int32,(BLOCK,BLOCK),0)+lax.broadcasted_iota(jnp.int32,(BLOCK,BLOCK),1)==BLOCK-1).astype(jnp.float32).astype(jnp.bfloat16)
    dk_sum[...]=jnp.zeros_like(dk_sum); dv_sum[...]=jnp.zeros_like(dv_sum)
    @pl.when((pl.program_id(0)==0)&(pl.program_id(1)==0))
    def _(): dt_ref[...]=jnp.zeros_like(dt_ref)
    for block in range(q_ref.shape[1]//BLOCK):
        rows=pl.ds(block*BLOCK,BLOCK); span=pl.ds(block*BLOCK,SPAN)
        keys=k_ref[0,span,:]; values=v_ref[0,span,:]
        mask=block_mask(first_ref[0],block,limit)
        grad_query=[]
        for head in range(2):
            query=jnp.where(head_lanes(head),q_ref[0,rows,:],zero)
            grad=jnp.where(head_lanes(head),g_ref[0,rows,:],zero)
            probs=block_probs(query,keys,table,mask)
            grad_probs=nt(grad,values)
            grad_raw=probs*(grad_probs-jnp.sum(probs*grad_probs,-1,keepdims=True))
            grad_raw=grad_raw.astype(jnp.bfloat16)
            turned=pltpu.roll(nn(flip,grad_raw),SPAN-BLOCK+1,1,stride=1,stride_axis=0)
            unskewed=nn(flip,turned.astype(jnp.bfloat16)).astype(jnp.bfloat16)
            dv_sum[span,:]+=tn(probs.astype(jnp.bfloat16),grad)
            dk_sum[span,:]+=tn(grad_raw,query)
            dt_ref[...]+=tn(unskewed,query)
            grad_query.append(nn(grad_raw,keys)+nn(unskewed,table))
        dq_ref[0,rows,:]=(jnp.where(head_lanes(0),grad_query[0],grad_query[1])*(HEAD_DIM**-0.5)).astype(jnp.bfloat16)
    dk_ref[0]=(dk_sum[...]*(HEAD_DIM**-0.5)).astype(jnp.bfloat16)
    dv_ref[0]=dv_sum[...].astype(jnp.bfloat16)

def wide_table(table):
    return jnp.tile(jnp.pad(table,((0,SPAN-table.shape[0]),(0,0))),(1,LANES//HEAD_DIM))

def specs(clips,rows,width):
    own=pl.BlockSpec((1,rows,LANES),lambda c,h:(c,0,h))
    ext=pl.BlockSpec((1,rows+LEFT+BACK_PAD,LANES),lambda c,h:(c,0,h))
    tab=pl.BlockSpec((SPAN,LANES),lambda c,h:(0,0))
    return (pl.BlockSpec(memory_space=pltpu.SMEM),own,ext,tab),(clips,width//LANES)

def attend(query,keys,values,table,rows):
    clips,_,width=query.shape
    first=lax.axis_index('seq').astype(jnp.int32)[None]*rows
    limit=rows*lax.axis_size('seq')
    (sc,own,ext,tab),grid=specs(clips,rows,width)
    return pl.pallas_call(functools.partial(attend_kernel,limit),grid=grid,
        in_specs=[sc,own,ext,ext,tab],out_specs=own,
        out_shape=jax.ShapeDtypeStruct(query.shape,jnp.bfloat16),name="attend",
    )(first,query,keys,values,wide_table(table))

def attend_back(query,keys,values,table,grad,rows):
    clips,_,width=query.shape
    first=lax.axis_index('seq').astype(jnp.int32)[None]*rows
    limit=rows*lax.axis_size('seq')
    (sc,own,ext,tab),grid=specs(clips,rows,width)
    dq,dk,dv,dt=pl.pallas_call(functools.partial(attend_back_kernel,limit),grid=grid,
        in_specs=[sc,own,ext,ext,tab,own],out_specs=[own,ext,ext,tab],
        out_shape=[jax.ShapeDtypeStruct(query.shape,jnp.bfloat16),jax.ShapeDtypeStruct(keys.shape,jnp.bfloat16),jax.ShapeDtypeStruct(keys.shape,jnp.bfloat16),jax.ShapeDtypeStruct((SPAN,LANES),jnp.float32)],
        scratch_shapes=[pltpu.VMEM((rows+LEFT+BACK_PAD,LANES),jnp.float32)]*2,name="attend_back",
    )(first,query,keys,values,wide_table(table),grad)
    return dq,dk,dv,(dt[:WIN,:HEAD_DIM]+dt[:WIN,HEAD_DIM:])*(HEAD_DIM**-0.5)
def depth_of():
    return lax.axis_size("group") // 2


def place():
    group = lax.axis_index("group")
    return (group // 2, group % 2, lax.axis_index("seq"), lax.axis_index("replica"))


def greet(peers):
    barrier = pltpu.get_barrier_semaphore()
    for peer in peers:
        pl.semaphore_signal(barrier, inc=1, device_id=peer, device_id_type=MESH)
    pl.semaphore_wait(barrier, len(peers))


def neighbours():
    z, x, seq, replica = place()
    depth = depth_of()
    deep = [{"group": (z + steps) % depth * 2 + x} for steps in range(1, depth)]
    across = {"group": z * 2 + 1 - x}
    beside = {"seq": 1 - seq}
    twin = {"replica": 1 - replica}
    return (deep, across, beside, twin)


class Gather:
    def __init__(self, source, target, cut, low, left, rows, size, sends, recvs, at):
        depth = depth_of()
        self.source, self.target, self.cut, self.low, self.rows = (source, target, cut, low, rows)
        self.piece = size[0] // (1, 2, 4)[cut]
        self.columns = pl.ds(left, size[1])
        self.sends, self.recvs, self.at = (sends, recvs, at)
        self.z, self.x, self.seq, self.replica = place()
        self.deep, self.across, self.beside, self.twin = neighbours()
        self.depth = depth
        self.firsts = (0, depth - 1, 2 * depth - 1, 4 * depth - 2)
        self.started = []

    def spot(self, ref, owner, dy, dc):
        part = 0
        if self.cut:
            part = (self.replica + dc) % 2
        if self.cut == 2:
            part = part + 2 * ((self.seq + dy) % 2)
        first = pl.multiple_of(owner * self.rows + self.low + part * self.piece, self.piece)
        return ref.at[pl.ds(first, self.piece), self.columns]

    def owner(self, steps, dx):
        return (self.z + self.depth - steps) % self.depth * 2 + (self.x + dx) % 2

    def copy(self, steps, dx, dy, dc, kind, index, peer):
        mine = steps == 0 and dx == 0
        slot = self.at + self.firsts[kind] + index
        spot = self.spot(self.target, self.owner(steps, dx), dy, dc)
        return pltpu.make_async_remote_copy(
            src_ref=self.spot(self.source, 0, dy, dc) if mine else spot,
            dst_ref=spot,
            send_sem=self.sends.at[slot],
            recv_sem=self.recvs.at[slot],
            device_id=peer,
            device_id_type=MESH,
        )

    def send(self, copy):
        copy.start()
        self.started.append(copy)

    def to_beside(self, steps, dx):
        if self.cut == 2:
            index = dx * self.depth + steps - 1
            self.send(self.copy(steps, dx, 0, 0, 2, index, self.beside))

    def to_twin(self, steps, dx, dy):
        if self.cut:
            index = dy * (2 * self.depth - 1) + dx * self.depth + steps - 1
            self.send(self.copy(steps, dx, dy, 0, 3, index, self.twin))

    def open(self):
        for steps, peer in enumerate(self.deep, 1):
            self.send(self.copy(0, 0, 0, 0, 0, steps - 1, peer))
        self.send(self.copy(0, 0, 0, 0, 1, 0, self.across))

    def got(self, steps, dx, dy, dc, kind, index):
        self.copy(steps or self.depth, dx, dy, dc, kind, index, self.twin).wait_recv()

    def forward_deep(self):
        for steps in range(1, self.depth):
            self.got(steps, 0, 0, 0, 0, steps - 1)
            self.send(self.copy(steps, 0, 0, 0, 1, steps, self.across))
            self.to_beside(steps, 0)
            self.to_twin(steps, 0, 0)

    def forward_across(self):
        for steps in range(self.depth):
            self.got(steps, 1, 0, 0, 1, steps)
            self.to_beside(steps, 1)
            self.to_twin(steps, 1, 0)

    def others(self):
        return [(steps, dx) for dx in range(2) for steps in range(self.depth) if steps or dx]

    def forward_beside(self):
        if self.cut == 2:
            for steps, dx in self.others():
                self.got(steps, dx, 1, 0, 2, dx * self.depth + steps - 1)
                self.to_twin(steps, dx, 1)

    def close(self):
        if self.cut:
            for dy in range(self.cut):
                for steps, dx in self.others():
                    index = dy * (2 * self.depth - 1) + dx * self.depth + steps - 1
                    self.got(steps, dx, dy, 1, 3, index)
        for copy in self.started:
            copy.wait_send()


def gather_kernel(plan, sources, count, *refs):
    ins, outs = (refs[:count], refs[count : count + len(sources)])
    helds, (sends, recvs, local) = (refs[count + len(sources) : -3], refs[-3:])
    deep, across, beside, twin = neighbours()
    peers = deep + [across, twin]
    if any(member[-1] == 2 for member in plan):
        peers.append(beside)
    greet(peers)
    loads = [
        pltpu.make_async_copy(ins[at], held, local.at[0, at]) for at, held in enumerate(helds)
    ]
    for load in loads:
        load.start()
    jobs, at = ([], 0)
    for number, layer, low, left, size, cut in plan:
        source, first = sources[number]
        ref = ins[source].at[first + layer]
        rows = ins[source].shape[1]
        target = outs[number].at[layer]
        jobs.append(Gather(ref, target, cut, low, left, rows, size, sends, recvs, at))
        at += (2, 6, 8)[cut] * depth_of()
    z, x, _, _ = place()
    ready, stores = (set(), [])
    for tick in range(len(jobs) + 8):
        for lag, name in enumerate(
            ("open", "forward_deep", "forward_across", "forward_beside", "close")
        ):
            if 0 <= tick - 2 * lag < len(jobs):
                getattr(jobs[tick - 2 * lag], name)()
        if tick < len(sources):
            source, first = sources[tick]
            if source not in ready:
                loads[source].wait()
                ready.add(source)
            rows = ins[source].shape[1]
            start = pl.multiple_of((z * 2 + x) * rows, rows)
            store = pltpu.make_async_copy(
                helds[source].at[pl.ds(first, outs[tick].shape[0])],
                outs[tick].at[:, pl.ds(start, rows)],
                local.at[1, tick],
            )
            store.start()
            stores.append(store)
    for store in stores:
        store.wait()


def gather_weights(shards, sources, halve):
    groups = lax.axis_size("group")
    width = shards[1].shape[1] * groups
    part = width // groups
    plan = [(0, 0, 0, 0, shards[0].shape[1:], 0)]
    for number, (source, first, layers) in enumerate(sources):
        for layer in range(layers if source else 0):
            for low in range(0, shards[source].shape[1], part):
                for left in range(0, shards[source].shape[2], width):
                    cut = 2 if halve and len(plan) % 3 else 1
                    plan.append((number, layer, low, left, (part, width), cut))
    total = sum((2, 6, 8)[member[-1]] * depth_of() for member in plan)
    return pl.pallas_call(
        functools.partial(
            gather_kernel, plan, [(source, first) for source, first, _ in sources], len(shards)
        ),
        in_specs=[pl.BlockSpec(memory_space=pl.ANY)] * len(shards),
        out_specs=[pl.BlockSpec(memory_space=pl.ANY)] * len(sources),
        out_shape=[
            jax.ShapeDtypeStruct(
                (layers, groups * shards[source].shape[1], shards[source].shape[2]), jnp.bfloat16
            )
            for source, _, layers in sources
        ],
        scratch_shapes=[pltpu.VMEM(shard.shape, jnp.bfloat16) for shard in shards]
        + [
            pltpu.SemaphoreType.DMA((total,)),
            pltpu.SemaphoreType.DMA((total,)),
            pltpu.SemaphoreType.DMA((2, len(sources))),
        ],
        compiler_params=pltpu.CompilerParams(
            collective_id=1, has_side_effects=True, vmem_limit_bytes=24 << 20
        ),
        name="gather_weights",
    )(*shards)


def swap(value, axis, bit=1):
    return lax.ppermute(value, axis, [(i, i ^ bit) for i in range(lax.axis_size(axis))])


def butterfly(value):
    for axis in ("replica", "seq", "group"):
        bit = 1
        while bit < lax.axis_size(axis):
            value = value + swap(value, axis, bit)
            bit *= 2
    return value


def add_slabs(count, target, *sources):
    def body(at, carry):
        total = sources[0](at)[...].astype(jnp.float32)
        for source in sources[1:]:
            total = total + source(at)[...].astype(jnp.float32)
        target(at)[...] = total.astype(jnp.bfloat16)
        return carry

    lax.fori_loop(0, count, body, 0)


class Reduce:
    def __init__(self, pool, number, target, low, left):
        self.pool, self.number = (pool, number)
        self.target, self.low, self.left = (target, low, left)
        self.source = pool.kept.at[number]
        self.stage = pool.stage.at[number % 2]
        self.kept = False
        self.depth, self.width = (depth_of(), pool.width)
        self.half, self.unit = (pool.rows // 2, pool.rows // 8)
        self.started = []
        self.stages = [
            self.exchange_twin,
            self.exchange_seq,
            self.exchange_across,
            self.exchange_deep,
            self.settle,
            self.hand_over,
            self.close,
        ]
        self.done_stages = 0
        slot = number % pool.ring
        self.own, self.came = (pool.own.at[slot], pool.came.at[slot])
        self.from_x, self.from_seq = (pool.from_x.at[slot], pool.from_seq.at[slot])
        self.from_z, self.shared = (pool.from_z.at[number], pool.shared.at[number])
        self.alone = pool.finished.at[slot, pl.ds(0, self.unit)]
        self.joint = pool.finished.at[slot, pl.ds(self.unit, 2 * self.unit)]

    def locate(self):
        self.z, self.x, self.seq, self.replica = place()
        self.deep, self.across, self.beside, self.twin = neighbours()

    def rows(self, first, count):
        return pl.ds(pl.multiple_of(first, self.unit), count * self.unit)

    def near(self):
        return self.rows(self.seq * self.unit, 3)

    def lone(self):
        return self.rows(3 * self.unit * self.seq, 1)

    def far(self):
        return self.rows(3 * self.unit * (1 - self.seq), 1)

    def both(self):
        return pl.ds(self.unit, 2 * self.unit)

    def side(self, replica):
        return pl.ds(pl.multiple_of(replica * self.half, self.half), self.half)

    def remote(self, source, target, slot, peer):
        return pltpu.make_async_remote_copy(
            src_ref=source,
            dst_ref=target,
            send_sem=self.pool.sends.at[self.number, slot],
            recv_sem=self.pool.recvs.at[self.number, slot],
            device_id=peer,
            device_id_type=MESH,
        )

    def send(self, ends, slot, peer):
        make = lambda peer: self.remote(*ends(), slot, peer)
        make(peer).start()
        self.started.append(make)

    def wait(self, target, slot):
        self.remote(target, target, slot, self.twin).wait_recv()

    def keep(self):
        return pltpu.make_async_copy(self.stage, self.source, self.pool.local.at[self.number, 0])

    def await_kept(self):
        if not self.kept:
            self.keep().wait()
            self.kept = True

    def load(self):
        source = self.source.at[:, :, self.side(self.replica)]
        return pltpu.make_async_copy(source, self.own, self.pool.local.at[self.number, 1])

    def credit(self, kind):
        if self.number >= self.pool.ring:
            pl.semaphore_wait(self.pool.credits.at[kind], 1)

    def release(self, kind, peer):
        if self.number + self.pool.ring < self.pool.total:
            pl.semaphore_signal(
                self.pool.credits.at[kind], inc=1, device_id=peer, device_id_type=MESH
            )

    def exchange_twin(self):
        self.await_kept()
        self.credit(0)
        self.load().start()
        ends = lambda: (self.source.at[:, :, self.side(1 - self.replica)], self.came)
        self.send(ends, 0, self.twin)

    def exchange_seq(self):
        self.load().wait()
        self.wait(self.came, 0)
        far = self.far()
        own = lambda at: self.own.at[at // 2, at % 2, far]
        add_slabs(2 * self.depth, own, own, lambda at: self.came.at[at // 2, at % 2, far])
        self.credit(1)
        self.send(lambda: (self.own.at[:, :, self.far()], self.from_seq), 1, self.beside)

    def gather(self, x, arrived):
        both, lone = (self.both(), self.lone())
        refs = [self.own.at[:, x], self.came.at[:, x]]
        pick = lambda rows: [lambda at, ref=ref: ref.at[at, rows] for ref in refs]
        shared, alone = (pick(both), pick(lone))
        alone.append(lambda at: self.from_seq.at[at, x])
        if arrived:
            both_here = self.rows(self.unit * (1 - self.seq), 2)
            lone_here = self.rows(2 * self.unit * self.seq, 1)
            shared.append(lambda at: self.from_x.at[at, both_here])
            alone.append(lambda at: self.from_x.at[at, lone_here])
        add_slabs(self.depth, shared[0], *shared)
        add_slabs(self.depth, alone[0], *alone)

    def exchange_across(self):
        self.wait(self.from_seq, 1)
        self.gather(1 - self.x, False)
        self.credit(2)
        self.send(lambda: (self.own.at[:, 1 - self.x, self.near()], self.from_x), 2, self.across)

    def exchange_deep(self):
        self.wait(self.from_x, 2)
        self.gather(self.x, True)
        for steps, peer in enumerate(self.deep, 1):
            ends = lambda steps=steps: (
                self.own.at[(self.z + steps) % self.depth, self.x, self.near()],
                self.from_z.at[steps - 1],
            )
            self.send(ends, 2 + steps, peer)
        self.release(0, self.twin)
        self.release(1, self.beside)
        self.release(2, self.across)

    def settle(self):
        for steps in range(1, self.depth):
            self.wait(self.from_z.at[steps - 1], 2 + steps)
        self.flush()
        both_here = self.rows(self.unit * (1 - self.seq), 2)
        lone_here = self.rows(2 * self.unit * self.seq, 1)
        for target, own, here in (
            (self.shared.at[self.seq], self.both(), both_here),
            (self.alone, self.lone(), lone_here),
        ):
            sources = [lambda at, own=own: self.own.at[self.z, self.x, own]]
            sources += [
                lambda at, steps=steps, here=here: self.from_z.at[steps, here]
                for steps in range(self.depth - 1)
            ]
            add_slabs(1, lambda at, target=target: target, *sources)
        self.last = 2 + self.depth
        ends = lambda: (self.shared.at[self.seq], self.shared.at[self.seq])
        self.send(ends, self.last, self.beside)
        self.store(0).start()
        self.send(lambda: (self.alone, self.spot(self.lone_out())), self.last + 1, self.beside)
        self.send(lambda: (self.alone, self.spot(self.lone_out())), self.last + 2, self.twin)

    def spot(self, first, count=1):
        return self.target.at[self.rows(first, count), pl.ds(self.left, self.width)]

    def lone_out(self, dy=0, dc=0):
        seq = self.seq if dy == 0 else 1 - self.seq
        replica = self.replica if dc == 0 else 1 - self.replica
        return self.low + replica * self.half + 3 * self.unit * seq

    def both_out(self, dc=0):
        replica = self.replica if dc == 0 else 1 - self.replica
        return self.low + replica * self.half + self.unit

    def store(self, kind):
        source = self.joint if kind else self.alone
        target = self.spot(self.both_out(), 2) if kind else self.spot(self.lone_out())
        return pltpu.make_async_copy(source, target, self.pool.local.at[self.number, 2 + kind])

    def hand_over(self):
        self.wait(self.spot(self.lone_out(1)), self.last + 1)
        spot = lambda: self.spot(self.lone_out(1))
        self.send(lambda: (spot(), spot()), self.last + 3, self.twin)
        self.wait(self.shared.at[1 - self.seq], self.last)
        sources = [lambda at, turn=turn: self.shared.at[turn] for turn in range(2)]
        add_slabs(1, lambda at: self.joint, *sources)
        self.store(1).start()
        self.send(lambda: (self.joint, self.spot(self.both_out(), 2)), self.last + 4, self.twin)

    def close(self):
        self.wait(self.spot(self.lone_out(0, 1)), self.last + 2)
        self.wait(self.spot(self.lone_out(1, 1)), self.last + 3)
        self.wait(self.spot(self.both_out(1), 2), self.last + 4)
        self.store(0).wait()
        self.store(1).wait()
        self.flush()

    def flush(self):
        for make in self.started:
            make(self.twin).wait_send()
        self.started = []

    def step(self):
        self.locate()
        self.stages[self.done_stages]()
        self.done_stages += 1


class Pool:
    ring = 7

    def __init__(self, rows, width, total, kept, refs):
        self.rows, self.width, self.total, self.kept = (rows, width, total, kept)
        names = list(Pool.shapes(rows, width, total))
        for name, ref in zip(names, refs):
            setattr(self, name, ref)
        self.sends, self.recvs, self.local, self.credits = refs[len(names) :]
        self.jobs = []

    @staticmethod
    def shapes(rows, width, total):
        depth, ring = (depth_of(), Pool.ring)
        unit = rows // 8
        return {
            "own": (ring, depth, 2, rows // 2, width),
            "came": (ring, depth, 2, rows // 2, width),
            "from_x": (ring, depth, 3 * unit, width),
            "from_seq": (ring, depth, 2, unit, width),
            "from_z": (total, depth - 1, 3 * unit, width),
            "shared": (total, 2, 2 * unit, width),
            "finished": (ring, 3 * unit, width),
            "stage": (2, depth, 2, rows, width),
        }

    @staticmethod
    def scratch(rows, width, total):
        slots = 7 + depth_of()
        return [pltpu.VMEM(shape, jnp.bfloat16) for shape in Pool.shapes(rows, width, total).values()] + [
            pltpu.SemaphoreType.DMA((total, slots)),
            pltpu.SemaphoreType.DMA((total, slots)),
            pltpu.SemaphoreType.DMA((total, 4)),
            pltpu.SemaphoreType.REGULAR((3,)),
        ]

    def add(self, target, low, left):
        number = len(self.jobs)
        if number >= 2:
            self.jobs[number - 2].await_kept()
        job = Reduce(self, number, target, low, left)
        self.jobs.append(job)
        return job

    def free(self, number):
        return number < self.ring or self.jobs[number - self.ring].done_stages >= 5

    def pump(self):
        active = [job for job in self.jobs if 0 < job.done_stages < 7]
        fresh = [job for job in self.jobs if job.done_stages == 0][:1]
        for job in fresh:
            if self.free(job.number):
                job.step()
        for job in reversed(active):
            job.step()

    def drain(self):
        while any(job.done_stages < 7 for job in self.jobs):
            self.pump()


def row_blocks(total, size, body):
    def step(at, carry):
        body(pl.ds(pl.multiple_of(at * size, size), size))
        return carry

    lax.fori_loop(0, total // size, step, 0)


def norm_parts(values):
    centered = values - jnp.mean(values, -1, keepdims=True)
    inverse = lax.rsqrt(jnp.mean(centered * centered, -1, keepdims=True) + EPSILON)
    return (centered * inverse, inverse)


def norm_rows(source, gain, target):
    def body(rows):
        normal, _ = norm_parts(source[rows, :].astype(jnp.float32))
        target[rows, :] = (normal * gain).astype(target.dtype)

    row_blocks(source.shape[0], 64, body)


def norm_back_rows(source, gain, grads, resid, sums, line):
    sums[pl.ds(line, 1), :] = jnp.zeros_like(sums[pl.ds(line, 1), :])

    def body(rows):
        normal, inverse = norm_parts(source[rows, :].astype(jnp.float32))
        grad = grads[rows, :]
        grad_normal = grad * gain
        resid[rows, :] += inverse * (
            grad_normal
            - jnp.mean(grad_normal, -1, keepdims=True)
            - normal * jnp.mean(grad_normal * normal, -1, keepdims=True)
        )
        sums[pl.ds(line, 1), :] += jnp.sum(grad * normal, 0, keepdims=True)

    row_blocks(source.shape[0], 64, body)


def cast_rows(source, target, scale=1.0):
    def body(rows):
        target[rows, :] = (source[rows, :] * scale).astype(jnp.bfloat16)

    row_blocks(source.shape[0], 64, body)


def transposed_rows(left, right, target, size=256):
    def body(cols):
        target[:, cols] = nt(left[...], right[cols, :]).astype(target.dtype)

    row_blocks(right.shape[0], size, body)


def add_transposed(left, right, target, size=256):
    def body(cols):
        target[:, cols] += nt(left[...], right[cols, :])

    row_blocks(right.shape[0], size, body)


def gradient_into(job, left, right):
    depth, _, rows, width = job.stage.shape

    def step(z, carry):
        cols = pl.ds(pl.multiple_of(z * 2 * rows, 2 * rows), 2 * rows)
        value = tn(left[:, cols], right[...]).astype(jnp.bfloat16)
        job.stage[z, 0] = value[:rows]
        job.stage[z, 1] = value[rows:]
        return carry

    lax.fori_loop(0, depth, step, 0)
    job.keep().start()


class Stream:
    def __init__(self, buffers, sems, copies):
        self.buffers, self.sems, self.copies = (buffers, sems, copies)
        self.issued = self.taken = 0
        for _ in range(len(buffers) - 1):
            self.issue()

    def parts(self, number):
        slot = number % len(self.buffers)
        made = self.copies[number](self.buffers[slot])
        return [
            pltpu.make_async_copy(source, target, self.sems.at[slot, at])
            for at, (source, target) in enumerate(made)
        ]

    def issue(self):
        if self.issued < len(self.copies):
            for copy in self.parts(self.issued):
                copy.start()
            self.issued += 1

    def take(self):
        for copy in self.parts(self.taken):
            copy.wait()
        self.taken += 1
        self.issue()
        return self.buffers[(self.taken - 1) % len(self.buffers)]


def module_copies(w_in, w_out, groups):
    chunks = w_out.shape[1]
    rows = w_out.shape[2]
    copies = []
    for chunk in range(chunks):
        copies.append(
            lambda slot, chunk=chunk: [
                (w_out.at[group, chunk], slot.at[pl.ds(group * rows, rows)])
                for group in range(groups)
            ]
        )
        copies.append(
            lambda slot, chunk=chunk: [
                (
                    w_in.at[:, pl.ds((group * chunks + chunk) * rows, rows)],
                    slot.at[:, pl.ds(group * rows, rows)],
                )
                for group in range(groups)
            ]
        )
    return copies


def saved_copies(saved, groups, rows):
    chunks = saved.shape[1] // (groups * rows)
    return [
        lambda slot, chunk=chunk: [
            (
                saved.at[:, pl.ds((group * chunks + chunk) * rows, rows)],
                slot.at[:, pl.ds(group * rows, rows)],
            )
            for group in range(groups)
        ]
        for chunk in range(chunks)
    ]


def module_back(pool, weights, saved, buffers, chunks, outs, often):
    pump = pool.pump
    entry, low, hidden, grad_hidden, total = buffers
    grad_in, grad_out = outs
    width = total.shape[1]
    total[...] = jnp.zeros_like(total)
    for chunk in range(chunks):
        before = saved.take()
        w_out = weights.take()

        def body(cols):
            value = before[:, cols].astype(jnp.float32)
            logistic = jax.nn.sigmoid(value)
            hidden[:, cols] = (value * logistic).astype(jnp.bfloat16)
            slope = logistic * (1.0 + value * (1.0 - logistic))
            grad = nt(low[...], w_out[cols, :]) * slope
            grad_hidden[:, cols] = grad.astype(jnp.bfloat16)

        row_blocks(width, 256, body)
        job = pool.add(grad_out, chunk * pool.rows, 0)
        gradient_into(job, hidden, low)
        job = pool.add(grad_in, 0, chunk * width)
        gradient_into(job, entry, grad_hidden)
        if often:
            pump()
        add_transposed(grad_hidden, weights.take(), total)
        pump()
def middle_rows(source, gain, grads, entry, sums, line):
    sums[pl.ds(line, 1), :] = jnp.zeros_like(sums[pl.ds(line, 1), :])

    def body(rows):
        normal, inverse = norm_parts(source[rows, :])
        middle = normal * gain
        logistic = jax.nn.sigmoid(middle)
        entry[rows, :] = (middle * logistic).astype(jnp.bfloat16)
        grad = grads[rows, :] * (logistic + middle * logistic * (1.0 - logistic))
        grad_normal = grad * gain
        grads[rows, :] = inverse * (
            grad_normal
            - jnp.mean(grad_normal, -1, keepdims=True)
            - normal * jnp.mean(grad_normal * normal, -1, keepdims=True)
        )
        sums[pl.ds(line, 1), :] += jnp.sum(grad * normal, 0, keepdims=True)

    row_blocks(source.shape[0], 64, body)


def depthwise_back(grads, taps, value, gate, grad_value, grad_gate, tap_sums, pump):
    total, width = value.shape
    tap_sums[...] = jnp.zeros_like(tap_sums)
    for column in range(width // LANES):
        lanes = pl.ds(column * LANES, LANES)

        def body(at, carry):
            first = pl.multiple_of(at * LANES, LANES)
            rows = pl.ds(first, LANES)
            held = value[rows, lanes].astype(jnp.float32)
            opened = jax.nn.sigmoid(gate[rows, lanes].astype(jnp.float32))
            glu = (held * opened).astype(jnp.bfloat16).astype(jnp.float32)
            grad = jnp.zeros((LANES, LANES), jnp.float32)
            window = grads[pl.ds(first, LANES + 32), lanes]
            for tap in range(KERNEL):
                ahead = KERNEL - 1 - tap
                moved = window[ahead : ahead + LANES]
                grad = grad + moved * taps[pl.ds(tap, 1), lanes]
                tap_sums[pl.ds(tap, 1), lanes] += jnp.sum(glu * moved, 0, keepdims=True)
            grad_value[rows, lanes] = (grad * opened).astype(jnp.bfloat16)
            grad_gate[rows, lanes] = (grad * held * opened * (1.0 - opened)).astype(jnp.bfloat16)
            return carry

        lax.fori_loop(0, total // LANES, body, 0)
        if column % 2:
            pump()


def fetch(source, target, sem):
    copy = pltpu.make_async_copy(source, target, sem)
    copy.start()
    return copy


def back_kernel(settings, *refs):
    count, clips, rows, limit = settings
    first_ref, table_ref, gains, taps = refs[:4]
    cot, x4, x3, x2, x1, x0, u1, u0, joined, summed = refs[4:14]
    mixed, query, keys, values, c_in, c_out, a_out, qkv = refs[14:22]
    second_in, second_out, w_in, w_out = refs[22:26]
    grad_x, gain_sums, dt_ref, tap_sums = refs[26:30]
    to_second_out, to_second_in, to_conv_out, to_conv_in = refs[30:34]
    to_attn, to_q, to_k, to_v, to_out, to_in, kept = refs[34:41]
    refs = refs[41:]
    resid, total_ext, resid_in, low, entry, mixed_grad, q_ref, dq_ref = refs[:8]
    k_ref, v_ref, dk_ref, dv_ref, later, earlier, dk_sum, dv_sum, slots = refs[8:17]
    local, slot_sems, saved_sems, halo_sems = refs[17:21]
    width = resid.shape[1]
    total = total_ext.at[pl.ds(0, rows)]
    groups = lax.axis_size("group")
    part = width // groups
    span = lax.axis_size("seq")
    chunks = w_out.shape[1]
    reduce_greet()
    pool = Pool(part, width, count, kept, refs[21:])
    pump = pool.pump
    copies = module_copies(second_in, second_out, groups)
    copies += [lambda slot: [(c_out, slot)]]
    copies += [
        lambda slot, at=at: [(c_in.at[:, pl.ds(at * width, width)], slot)] for at in range(2)
    ]
    copies += [lambda slot: [(a_out, slot)]]
    copies += [lambda slot, at=at: [(qkv.at[at], slot)] for at in range(3)]
    copies += module_copies(w_in, w_out, groups)
    load = fetch(x4, resid_in, local.at[0])
    arrival = fetch(cot, low, local.at[1])
    weights = Stream([slots.at[at] for at in range(3)], slot_sems, copies)
    free = [ref.at[0, pl.ds(0, rows)] for ref in (k_ref, v_ref)]
    saved = Stream(free, saved_sems, saved_copies(u1, groups, part))
    halves = [ref.at[0, pl.ds(0, rows)] for ref in (dk_ref, dv_ref)]
    opening = [
        fetch(joined.at[:, pl.ds(at * width, width)], half, local.at[2 + at])
        for at, half in enumerate(halves)
    ]
    resid[...] = jnp.zeros_like(resid)
    arrival.wait()
    load.wait()

    def widen(at):
        total[at, :] = low[at, :].astype(jnp.float32)

    row_blocks(rows, 64, widen)
    norm_back_rows(resid_in, gains[pl.ds(5, 1), :], total, resid, gain_sums, 5)
    load = fetch(x3, resid_in, local.at[0])
    cast_rows(resid, low, 0.5)
    load.wait()
    norm_rows(resid_in, gains[pl.ds(4, 1), :], entry)
    buffers = (entry, low, mixed_grad, q_ref, total)
    module_back(
        pool, weights, saved, buffers, chunks, (to_second_in, to_second_out), False
    )
    norm_back_rows(resid_in, gains[pl.ds(4, 1), :], total, resid, gain_sums, 4)
    load = fetch(summed, resid_in, local.at[0])
    cast_rows(resid, low)
    transposed_rows(low, weights.take(), total)
    load.wait()
    middle_rows(resid_in, gains[pl.ds(3, 1), :], total, entry, gain_sums, 3)
    _, _, seq, _ = place()
    halo = pltpu.make_async_remote_copy(
        src_ref=total_ext.at[pl.ds(0, 32)],
        dst_ref=total_ext.at[pl.ds(rows, 32)],
        send_sem=halo_sems.at[0, 4],
        recv_sem=halo_sems.at[1, 4],
        device_id={"seq": (seq + span - 1) % span},
        device_id_type=MESH,
    )
    halo.start()
    load = fetch(x2, resid_in, local.at[0])
    job = pool.add(to_conv_out, 0, 0)
    gradient_into(job, entry, low)
    pump()
    for copy in opening:
        copy.wait()
    load.wait()
    norm_rows(resid_in, gains[pl.ds(2, 1), :], entry)
    halo.wait()
    beyond = pl.ds(rows, 32)
    nothing = jnp.zeros((32, width), jnp.float32)
    total_ext[beyond, :] = jnp.where(seq < span - 1, total_ext[beyond, :], nothing)
    depthwise_back(total_ext, taps, *halves, mixed_grad, q_ref, tap_sums, pump)
    total[...] = jnp.zeros_like(total)
    for at, flat in enumerate((mixed_grad, q_ref)):
        job = pool.add(to_conv_in, 0, at * width)
        gradient_into(job, entry, flat)
        pump()
        add_transposed(flat, weights.take(), total)
        pump()
    norm_back_rows(resid_in, gains[pl.ds(2, 1), :], total, resid, gain_sums, 2)
    loads = [
        fetch(source, target, local.at[at])
        for at, (source, target) in enumerate(
            ((mixed, entry), (query, q_ref), (keys, k_ref), (values, v_ref), (x1, resid_in))
        )
    ]
    cast_rows(resid, low)
    transposed_rows(low, weights.take(), mixed_grad)
    loads[0].wait()
    job = pool.add(to_attn, 0, 0)
    gradient_into(job, entry, low)
    pump()
    for load in loads[1:]:
        load.wait()
    table = table_ref[...]
    zero = jnp.zeros((BLOCK, LANES), jnp.bfloat16)
    across = lax.broadcasted_iota(jnp.int32, (BLOCK, BLOCK), 0)
    across = across + lax.broadcasted_iota(jnp.int32, (BLOCK, BLOCK), 1)
    flip = (across == BLOCK - 1).astype(jnp.float32).astype(jnp.bfloat16)
    dt_ref[...] = jnp.zeros_like(dt_ref)
    blocks = rows // BLOCK
    for pair in range(width // LANES):
        lanes = pl.ds(pair * LANES, LANES)
        dk_sum[...] = jnp.zeros_like(dk_sum)
        dv_sum[...] = jnp.zeros_like(dv_sum)

        def attend_block(at, carry):
            clip, block = (at // blocks, at % blocks)
            here = pl.ds(pl.multiple_of(at * BLOCK, BLOCK), BLOCK)
            near = pl.ds(pl.multiple_of(block * BLOCK, BLOCK), SPAN)
            key = k_ref[clip, near, lanes]
            value = v_ref[clip, near, lanes]
            mask = block_mask(first_ref[0], block, limit)
            grad_query = []
            for head in range(2):
                q = jnp.where(head_lanes(head), q_ref[here, lanes], zero)
                g = jnp.where(head_lanes(head), mixed_grad[here, lanes], zero)
                probs = block_probs(q, key, table, mask)
                grad_probs = nt(g, value)
                grad_raw = probs * (grad_probs - jnp.sum(probs * grad_probs, -1, keepdims=True))
                grad_raw = grad_raw.astype(jnp.bfloat16)
                turned = pltpu.roll(
                    nn(flip, grad_raw), SPAN - BLOCK + 1, 1, stride=1, stride_axis=0
                )
                unskewed = nn(flip, turned.astype(jnp.bfloat16)).astype(jnp.bfloat16)
                dv_sum[clip, near, :] += tn(probs.astype(jnp.bfloat16), g)
                dk_sum[clip, near, :] += tn(grad_raw, q)
                dt_ref[...] += tn(unskewed, q)
                grad_query.append(nn(grad_raw, key) + nn(unskewed, table))
            both = jnp.where(head_lanes(0), grad_query[0], grad_query[1])
            dq_ref[here, lanes] = (both * HEAD_DIM**-0.5).astype(jnp.bfloat16)
            return carry

        lax.fori_loop(0, clips * blocks, attend_block, 0, unroll=2)
        dk_ref[:, :, lanes] = (dk_sum[...] * HEAD_DIM**-0.5).astype(jnp.bfloat16)
        dv_ref[:, :, lanes] = dv_sum[...].astype(jnp.bfloat16)
        pump()

    saved = Stream(free, saved_sems, saved_copies(u0, groups, part))
    edges = []
    for at, ref in enumerate((dk_ref, dv_ref)):
        for way, (target, low_row, size, step) in enumerate(
            ((later, 0, LEFT, span - 1), (earlier, LEFT + rows, 2 * RIGHT, 1))
        ):
            edges.append(
                pltpu.make_async_remote_copy(
                    src_ref=ref.at[:, pl.ds(low_row, size)],
                    dst_ref=target.at[at],
                    send_sem=halo_sems.at[0, 2 * at + way],
                    recv_sem=halo_sems.at[1, 2 * at + way],
                    device_id={"seq": (seq + step) % span},
                    device_id_type=MESH,
                )
            )
    for edge in edges:
        edge.start()
    gain = gains[pl.ds(1, 1), :]
    norm_rows(resid_in, gain, entry)
    job = pool.add(to_q, 0, 0)
    gradient_into(job, entry, dq_ref)
    total[...] = jnp.zeros_like(total)
    add_transposed(dq_ref, weights.take(), total)
    pump()
    for edge in edges:
        edge.wait()
    for at, (ref, flat) in enumerate(((dk_ref, mixed_grad), (dv_ref, q_ref))):
        for clip in range(clips):
            base = clip * rows
            flat[pl.ds(base, rows), :] = ref[clip, pl.ds(LEFT, rows), :]
            tail = pl.ds(base + rows - LEFT, LEFT)
            zero_tail = jnp.zeros((LEFT, width), jnp.float32)
            came = jnp.where(seq < span - 1, later[at, clip].astype(jnp.float32), zero_tail)
            flat[tail, :] = (flat[tail, :].astype(jnp.float32) + came).astype(jnp.bfloat16)
            head = pl.ds(base, 2 * RIGHT)
            zero_head = jnp.zeros((2 * RIGHT, width), jnp.float32)
            came = jnp.where(seq > 0, earlier[at, clip].astype(jnp.float32), zero_head)
            flat[head, :] = (flat[head, :].astype(jnp.float32) + came).astype(jnp.bfloat16)
    for target, flat in ((to_k, mixed_grad), (to_v, q_ref)):
        job = pool.add(target, 0, 0)
        gradient_into(job, entry, flat)
        pump()
        add_transposed(flat, weights.take(), total)
        pump()
    norm_back_rows(resid_in, gain, total, resid, gain_sums, 1)
    load = pltpu.make_async_copy(x0, dq_ref, local.at[0])
    load.start()
    cast_rows(resid, low, 0.5)
    load.wait()
    gain = gains[pl.ds(0, 1), :]
    norm_rows(dq_ref, gain, entry)
    buffers = (entry, low, mixed_grad, q_ref, total)
    module_back(pool, weights, saved, buffers, chunks, (to_in, to_out), True)
    norm_back_rows(dq_ref, gain, total, resid, gain_sums, 0)
    cast_rows(resid, low)
    store = pltpu.make_async_copy(low, grad_x, local.at[1])
    store.start()
    pool.drain()
    store.wait()


def reduce_greet():
    deep, across, _, twin = neighbours()
    span = lax.axis_size("seq")
    seq = lax.axis_index("seq")
    greet(deep + [across, twin] + [{"seq": (seq + steps) % span} for steps in range(1, span)])


def back(cot, resids, saved, kept, table, gains, taps, weights, rows):
    joined, summed, u1, u0 = saved
    query, keys, values, mixed = kept
    c_in, c_out, a_out, qkv, second_in, second_out, w_in, w_out = weights
    clips, ext, width = keys.shape
    groups = lax.axis_size("group")
    part = width // groups
    chunks = w_out.shape[0] // width
    count = 7 + 4 * chunks
    first = lax.axis_index("seq").astype(jnp.int32)[None] * rows
    limit = rows * lax.axis_size("seq")
    hbm = pl.BlockSpec(memory_space=pl.ANY)
    vmem = pl.BlockSpec(memory_space=pltpu.VMEM)
    low = lambda *shape: jax.ShapeDtypeStruct(shape, jnp.bfloat16)
    wide = lambda *shape: jax.ShapeDtypeStruct(shape, jnp.float32)
    holds = [pltpu.VMEM((rows + more, width), jnp.float32) for more in (0, 32, 0)]
    holds += [pltpu.VMEM((rows, width), jnp.bfloat16)] * 5
    holds += [pltpu.VMEM((clips, ext, width), jnp.bfloat16)] * 4
    holds += [
        pltpu.VMEM((2, clips, LEFT, width), jnp.bfloat16),
        pltpu.VMEM((2, clips, 2 * RIGHT, width), jnp.bfloat16),
        pltpu.VMEM((clips, ext, LANES), jnp.float32),
        pltpu.VMEM((clips, ext, LANES), jnp.float32),
        pltpu.VMEM((3, width, width), jnp.bfloat16),
        pltpu.SemaphoreType.DMA((6,)),
        pltpu.SemaphoreType.DMA((3, groups)),
        pltpu.SemaphoreType.DMA((2, groups)),
        pltpu.SemaphoreType.DMA((2, 5)),
    ]
    grad_out = low(chunks * part, width)
    grad_in = low(part, chunks * width)
    by_chunk = lambda weight: weight.reshape(groups, chunks, part, width)
    results = pl.pallas_call(
        functools.partial(back_kernel, (count, clips, rows, limit)),
        in_specs=[pl.BlockSpec(memory_space=pltpu.SMEM)] + [vmem] * 3 + [hbm] * 22,
        out_specs=[hbm] + [vmem] * 3 + [hbm] * 11,
        out_shape=[low(rows, width), wide(8, width), wide(SPAN, LANES), wide(32, width)]
        + [grad_out, grad_in, low(part, width), low(part, 2 * width)]
        + [low(part, width)] * 4
        + [grad_out, grad_in, low(count, groups // 2, 2, part, width)],
        scratch_shapes=holds + Pool.scratch(part, width, count),
        compiler_params=pltpu.CompilerParams(
            collective_id=3, has_side_effects=True, vmem_limit_bytes=63 << 20
        ),
        name="back",
    )(
        first,
        wide_table(table),
        gains,
        taps,
        cot,
        *resids,
        u1,
        u0,
        joined,
        summed,
        mixed,
        query.reshape(rows, width),
        keys,
        values,
        c_in,
        c_out,
        a_out,
        qkv,
        second_in,
        by_chunk(second_out),
        w_in,
        by_chunk(w_out),
    )
    grad_x, gain_sums, dt, tap_sums = results[:4]
    dt = (dt[:WIN, :HEAD_DIM] + dt[:WIN, HEAD_DIM:]) * HEAD_DIM**-0.5
    return grad_x, gain_sums, dt, tap_sums, results[4:]


def unmix(grad, groups):
    rows, width = grad.shape
    chunks = width // (rows * groups)
    return grad.reshape(rows, chunks, groups, rows).transpose(0, 2, 1, 3).reshape(rows, width)


def feed_forward(resid, gain, w_in, w_out):
    normed, normal, inverse = norm_forward(resid, gain)
    entry = normed.astype(jnp.bfloat16)
    hidden_pre = matmul(entry, w_in)
    hidden = (hidden_pre * jax.nn.sigmoid(hidden_pre)).astype(jnp.bfloat16)
    return (matmul(hidden, w_out), (normal, inverse, entry, hidden_pre, hidden))


def feed_back(grad_branch, kept, gain, w_in, w_out):
    normal, inverse, entry, hidden_pre, hidden = kept
    grad_low = grad_branch.astype(jnp.bfloat16)
    grad_w_out = matmul_left_t(hidden, grad_low).astype(jnp.bfloat16)
    grad_hidden = (matmul_right_t(grad_low, w_out) * swish_grad(hidden_pre)).astype(jnp.bfloat16)
    grad_w_in = matmul_left_t(entry, grad_hidden).astype(jnp.bfloat16)
    grad_in, grad_gain = norm_backward(matmul_right_t(grad_hidden, w_in), normal, inverse, gain)
    return (grad_in, grad_gain, grad_w_in, grad_w_out)


def attention_forward(resid, gain, qkv, attn_out, table, shape):
    clips, rows, width = shape
    normed, normal, inverse = norm_forward(resid, gain)
    entry = normed.astype(jnp.bfloat16)
    query, keys, values = [
        matmul(entry, qkv[part]).astype(jnp.bfloat16).reshape(shape) for part in range(3)
    ]
    tail = jnp.zeros((clips, BACK_PAD - RIGHT, width), jnp.bfloat16)

    def extend(value):
        before = from_behind(value[:, rows - LEFT :], "seq", 1)
        after = from_behind(value[:, :RIGHT], "seq", -1)
        return jnp.concatenate([before, value, after, tail], 1)

    keys, values = (extend(keys), extend(values))
    mixed = attend(query, keys, values, table, rows).reshape(clips * rows, width)
    return (matmul(mixed, attn_out), (normal, inverse, entry, query, keys, values, mixed))


def attention_back(grad_branch, kept, gain, qkv, attn_out, table, shape):
    clips, rows, width = shape
    normal, inverse, entry, query, keys, values, mixed = kept
    grad_low = grad_branch.astype(jnp.bfloat16)
    grad_attn_out = matmul_left_t(mixed, grad_low).astype(jnp.bfloat16)
    grad_mixed = matmul_right_t(grad_low, attn_out).astype(jnp.bfloat16).reshape(shape)
    grad_query, grad_keys, grad_values, grad_table = attend_back(
        query, keys, values, table, grad_mixed, rows
    )

    def fold(grad):
        from_later = from_behind(grad[:, :LEFT], "seq", -1).astype(jnp.float32)
        from_earlier = from_behind(grad[:, LEFT + rows : LEFT + rows + RIGHT], "seq", 1)
        own = grad[:, LEFT : LEFT + rows].astype(jnp.float32)
        own = own + jnp.pad(from_later, ((0, 0), (rows - LEFT, 0), (0, 0)))
        own = own + jnp.pad(from_earlier.astype(jnp.float32), ((0, 0), (0, rows - RIGHT), (0, 0)))
        return own.astype(jnp.bfloat16).reshape(clips * rows, width)

    parts = [grad_query.reshape(clips * rows, width), fold(grad_keys), fold(grad_values)]
    grad_qkv = [matmul_left_t(entry, part).astype(jnp.bfloat16) for part in parts]
    grad_entry = sum(matmul_right_t(part, qkv[at]) for at, part in enumerate(parts))
    grad_in, grad_gain = norm_backward(grad_entry, normal, inverse, gain)
    return (grad_in, grad_gain, grad_qkv, grad_attn_out, grad_table)


def conv_forward(resid, gain_in, gain_mid, conv_in, depthwise, conv_out, shape):
    clips, rows, width = shape
    normed, normal, inverse = norm_forward(resid, gain_in)
    entry = normed.astype(jnp.bfloat16)
    joined = matmul(entry, conv_in)
    opened = jax.nn.sigmoid(joined[:, width:])
    glu = (joined[:, :width] * opened).astype(jnp.bfloat16).reshape(clips, rows, width)
    before = from_behind(glu[:, rows - (KERNEL - 1) :], "seq", 1)
    padded = jnp.concatenate([before, glu], 1).astype(jnp.float32)
    taps = depthwise.astype(jnp.float32)
    summed = jnp.zeros((clips, rows, width), jnp.float32)
    for tap in range(KERNEL):
        summed = summed + taps[tap] * padded[:, tap : tap + rows]
    middle, mid_normal, mid_inverse = norm_forward(summed.reshape(clips * rows, width), gain_mid)
    swished = (middle * jax.nn.sigmoid(middle)).astype(jnp.bfloat16)
    kept = (
        normal,
        inverse,
        entry,
        joined,
        opened,
        padded,
        middle,
        mid_normal,
        mid_inverse,
        swished,
    )
    return (matmul(swished, conv_out), summed.reshape(clips * rows, width), kept)


def conv_back(grad_branch, kept, gain_in, gain_mid, conv_in, depthwise, conv_out, shape):
    clips, rows, width = shape
    normal, inverse, entry, joined, opened, padded, middle, mid_normal, mid_inverse, swished = kept
    taps = depthwise.astype(jnp.float32)
    grad_low = grad_branch.astype(jnp.bfloat16)
    grad_conv_out = matmul_left_t(swished, grad_low).astype(jnp.bfloat16)
    grad_middle = matmul_right_t(grad_low, conv_out) * swish_grad(middle)
    grad_summed, grad_gain_mid = norm_backward(grad_middle, mid_normal, mid_inverse, gain_mid)
    grad_summed = grad_summed.reshape(clips, rows, width)
    grad_taps = jnp.stack(
        [jnp.sum(grad_summed * padded[:, tap : tap + rows], (0, 1)) for tap in range(KERNEL)]
    )
    grad_padded = jnp.zeros((clips, rows + KERNEL - 1, width), jnp.float32)
    for tap in range(KERNEL):
        grad_padded = grad_padded + jnp.pad(
            grad_summed * taps[tap], ((0, 0), (tap, KERNEL - 1 - tap), (0, 0))
        )
    from_later = from_behind(grad_padded[:, : KERNEL - 1].astype(jnp.bfloat16), "seq", -1).astype(
        jnp.float32
    )
    grad_glu = (
        grad_padded[:, KERNEL - 1 :]
        .at[:, rows - (KERNEL - 1) :]
        .add(from_later)
        .reshape(clips * rows, width)
    )
    value_part = joined[:, :width]
    grad_joined = jnp.concatenate(
        [grad_glu * opened, grad_glu * value_part * opened * (1.0 - opened)], 1
    )
    grad_joined = grad_joined.astype(jnp.bfloat16)
    grad_conv_in = matmul_left_t(entry, grad_joined).astype(jnp.bfloat16)
    grad_in, grad_gain_in = norm_backward(
        matmul_right_t(grad_joined, conv_in), normal, inverse, gain_in
    )
    return (grad_in, grad_gain_in, grad_gain_mid, grad_conv_in, grad_taps, grad_conv_out)


def on_device(
    tokens,
    ffn_in,
    ffn_out,
    qkv,
    attn_out,
    conv_in,
    conv_out,
    depthwise,
    gains,
    rel_table,
    cotangent,
):
    clips, rows, width = tokens.shape
    shape = (clips, rows, width)
    flat_rows = clips * rows
    halve = lax.axis_size("seq") == 2
    norms, taps = (gains.shape[0], depthwise.shape[0])
    lines = -(-(norms + taps) // 16) * 16
    small = jnp.concatenate([gains, depthwise], 0)
    small = jnp.pad(small, ((0, lines - norms - taps), (0, 0)))[None]
    shards = (small, ffn_in, ffn_out, qkv, attn_out[None], conv_in[None], conv_out[None])
    sources = (
        (0, 0, 1),
        (1, 0, 1),
        (2, 0, 1),
        (3, 0, 3),
        (4, 0, 1),
        (5, 0, 1),
        (6, 0, 1),
        (1, 1, 1),
        (2, 1, 1),
    )
    gathered = gather_weights(shards, sources, halve)
    small = gathered[0].reshape(-1, lines, gains.shape[1]).transpose(1, 0, 2).reshape(lines, width)
    gain_f = small[:norms].astype(jnp.float32)
    depth = small[norms : norms + taps]
    f_in = (gathered[1][0], gathered[7][0])
    f_out = (gathered[2][0], gathered[8][0])
    proj, a_out, c_in, c_out = (gathered[3], gathered[4][0], gathered[5][0], gathered[6][0])
    start = tokens.reshape(flat_rows, width).astype(jnp.float32)
    first_branch, first_kept = feed_forward(start, gain_f[0], f_in[0], f_out[0])
    after_first = start + 0.5 * first_branch
    attn_branch, attn_kept = attention_forward(
        after_first, gain_f[1], proj, a_out, rel_table, shape
    )
    after_attn = after_first + attn_branch
    conv_branch, summed, conv_kept = conv_forward(
        after_attn, gain_f[2], gain_f[3], c_in, depth, c_out, shape
    )
    after_conv = after_attn + conv_branch
    second_branch, second_kept = feed_forward(after_conv, gain_f[4], f_in[1], f_out[1])
    final = after_conv + 0.5 * second_branch
    result, final_normal, final_inverse = norm_forward(final, gain_f[5])
    squares = jnp.stack(
        [
            jnp.sum(member * member)
            for member in (final, first_branch, attn_branch, conv_branch, second_branch)
        ]
    )
    if halve and clips == 1 and gains.shape[1] % LANES == 0:
        grad, gain_sums, grad_table, grad_taps, shares = back(
            cotangent.reshape(flat_rows, width),
            (final, after_conv, after_attn, after_first, tokens.reshape(flat_rows, width)),
            (
                conv_kept[3].astype(jnp.bfloat16),
                summed,
                second_kept[3].astype(jnp.bfloat16),
                first_kept[3].astype(jnp.bfloat16),
            ),
            attn_kept[3:],
            rel_table,
            small[:8].astype(jnp.float32),
            jnp.pad(depth.astype(jnp.float32), ((0, 32 - taps), (0, 0))),
            (c_in, c_out, a_out, proj, f_in[1], f_out[1], f_in[0], f_out[0]),
            rows,
        )
        gain_grads = gain_sums[:norms]
        grad_taps = grad_taps[:taps]
        groups = lax.axis_size("group")
        grad_in_first, grad_in_second = (unmix(shares[9], groups), unmix(shares[1], groups))
        grad_out_first, grad_out_second = (shares[8], shares[0])
        grad_conv_out, grad_conv_in, grad_attn_out = shares[2:5]
        grad_qkv = shares[5:8]
    else:
        grad = cotangent.reshape(flat_rows, width).astype(jnp.float32)
        grad, grad_gain_final = norm_backward(grad, final_normal, final_inverse, gain_f[5])
        back_in, grad_gain_second, grad_in_second, grad_out_second = feed_back(
            0.5 * grad, second_kept, gain_f[4], f_in[1], f_out[1]
        )
        grad = grad + back_in
        back_in, grad_gain_conv, grad_gain_mid, grad_conv_in, grad_taps, grad_conv_out = conv_back(
            grad, conv_kept, gain_f[2], gain_f[3], c_in, depth, c_out, shape
        )
        grad = grad + back_in
        back_in, grad_gain_attn, grad_qkv, grad_attn_out, grad_table = attention_back(
            grad, attn_kept, gain_f[1], proj, a_out, rel_table, shape
        )
        grad = grad + back_in
        back_in, grad_gain_first, grad_in_first, grad_out_first = feed_back(
            0.5 * grad, first_kept, gain_f[0], f_in[0], f_out[0]
        )
        grad = grad + back_in
        matrices = [grad_in_first, grad_in_second, grad_out_first, grad_out_second]
        matrices += [grad_attn_out, grad_conv_in, grad_conv_out] + grad_qkv
        matrices = [
            lax.psum(lax.psum_scatter(member, "group", tiled=True), ("seq", "replica"))
            for member in matrices
        ]
        grad_in_first, grad_in_second, grad_out_first, grad_out_second = matrices[:4]
        grad_attn_out, grad_conv_in, grad_conv_out = matrices[4:7]
        grad_qkv = matrices[7:]
        gain_grads = jnp.stack(
            [
                grad_gain_first,
                grad_gain_attn,
                grad_gain_conv,
                grad_gain_mid,
                grad_gain_second,
                grad_gain_final,
            ]
        )
    loose = jnp.concatenate([grad_table.reshape(-1), squares])
    lines = -(-loose.shape[0] // width)
    loose = jnp.pad(loose, (0, lines * width - loose.shape[0])).reshape(lines, width)
    totals = butterfly(jnp.concatenate([gain_grads, grad_taps, loose], 0))
    owned = lax.dynamic_slice_in_dim(
        totals[: norms + taps], lax.axis_index("group") * gains.shape[1], gains.shape[1], 1
    )
    loose = totals[norms + taps :].reshape(-1)
    table_size = rel_table.shape[0] * rel_table.shape[1]
    count = (
        flat_rows * width * lax.axis_size("seq") * lax.axis_size("group") * lax.axis_size("replica")
    )
    stats = jnp.sqrt(loose[table_size : table_size + 5] / count)
    return (
        result.astype(jnp.bfloat16).reshape(shape),
        grad.astype(jnp.bfloat16).reshape(shape),
        jnp.stack([grad_in_first, grad_in_second]).astype(jnp.float32),
        jnp.stack([grad_out_first, grad_out_second]).astype(jnp.float32),
        jnp.stack(grad_qkv).astype(jnp.float32),
        grad_attn_out.astype(jnp.float32),
        grad_conv_in.astype(jnp.float32),
        grad_conv_out.astype(jnp.float32),
        owned[norms:],
        owned[:norms],
        loose[:table_size].reshape(rel_table.shape),
        stats,
    )


def solution(mesh):
    in_specs = (
        P(("group", "replica"), "seq", None),
        P(None, "group", None),
        P(None, "group", None),
        P(None, "group", None),
        P("group", None),
        P("group", None),
        P("group", None),
        P(None, "group"),
        P(None, "group"),
        P(),
        P(("group", "replica"), "seq", None),
    )
    out_specs = (
        P(("group", "replica"), "seq", None),
        P(("group", "replica"), "seq", None),
        P(None, "group", None),
        P(None, "group", None),
        P(None, "group", None),
        P("group", None),
        P("group", None),
        P("group", None),
        P(None, "group"),
        P(None, "group"),
        P(),
        P(),
    )
    return jax.shard_map(
        on_device, mesh=mesh, in_specs=in_specs, out_specs=out_specs, check_vma=False
    )
```

```python
import functools

import jax
import jax.numpy as jnp
from jax import lax
from jax.experimental import pallas as pl
from jax.experimental.pallas import tpu as pltpu
from jax.sharding import PartitionSpec as P

HEAD_DIM = 64
KERNEL = 31
LEFT = 64
RIGHT = 8
WIN = 73
LANES = 128
BLOCK = 128
SPAN = 256
BACK_PAD = 64


EPSILON = 1e-05
NEGATIVE = -1e30


MESH = pl.DeviceIdType.MESH


def from_behind(value, axis, steps):
    count = lax.axis_size(axis)
    initial, last = (max(0, -steps), min(count, count - steps))
    return lax.ppermute(value, axis, [(source, source + steps) for source in range(initial, last)])


def norm_forward(values, gain):
    centered = values - jnp.mean(values, -1, keepdims=True)
    inverse = lax.rsqrt(jnp.mean(centered * centered, -1, keepdims=True) + EPSILON)
    normal = centered * inverse
    return (normal * gain, normal, inverse)


def norm_backward(grad_out, normal, inverse, gain):
    grad_normal = grad_out * gain
    grad_in = inverse * (
        grad_normal
        - jnp.mean(grad_normal, -1, keepdims=True)
        - normal * jnp.mean(grad_normal * normal, -1, keepdims=True)
    )
    grad_gain = jnp.sum(grad_out * normal, 0)
    return (grad_in, grad_gain)


def matmul(left, right):
    return jnp.dot(left, right, preferred_element_type=jnp.float32)


def matmul_left_t(left, right):
    return lax.dot_general(
        left, right, (((0,), (0,)), ((), ())), preferred_element_type=jnp.float32
    )


def matmul_right_t(left, right):
    return lax.dot_general(
        left, right, (((1,), (1,)), ((), ())), preferred_element_type=jnp.float32
    )


def swish_grad(values):
    logistic = jax.nn.sigmoid(values)
    return logistic + values * logistic * (1.0 - logistic)


def nt(left,right):
    return lax.dot_general(left,right,(((1,),(1,)),((),())),preferred_element_type=jnp.float32)
def tn(left,right):
    return lax.dot_general(left,right,(((0,),(0,)),((),())),preferred_element_type=jnp.float32)
def nn(left,right):
    return jnp.dot(left,right,preferred_element_type=jnp.float32)

def block_mask(first, block, limit):
    rows=lax.broadcasted_iota(jnp.int32,(BLOCK,SPAN),0)
    cols=lax.broadcasted_iota(jnp.int32,(BLOCK,SPAN),1)
    offset=cols-rows
    place=first+block*BLOCK+cols-LEFT
    return (offset>=0)&(offset<WIN)&(place>=0)&(place<limit)

def head_lanes(head):
    lanes=lax.broadcasted_iota(jnp.int32,(BLOCK,LANES),1)
    return (lanes>=head*HEAD_DIM)&(lanes<(head+1)*HEAD_DIM)

def block_probs(query, keys, table, mask):
    relative=pltpu.roll(nt(query,table),0,1,stride=1,stride_axis=0)
    raw=jnp.where(mask,(nt(query,keys)+relative)*(HEAD_DIM**-0.5),NEGATIVE)
    expo=jnp.exp(raw-jnp.max(raw,-1,keepdims=True))
    return expo*(1.0/jnp.sum(expo,-1,keepdims=True))

def attend_kernel(limit, first_ref, q_ref, k_ref, v_ref, t_ref, c_ref):
    table=t_ref[...]
    zero=jnp.zeros((BLOCK,LANES),jnp.bfloat16)
    for block in range(q_ref.shape[1]//BLOCK):
        rows=pl.ds(block*BLOCK,BLOCK); span=pl.ds(block*BLOCK,SPAN)
        query=q_ref[0,rows,:]; keys=k_ref[0,span,:]; values=v_ref[0,span,:]
        mask=block_mask(first_ref[0],block,limit)
        mixed=[]
        for head in range(2):
            probs=block_probs(jnp.where(head_lanes(head),query,zero),keys,table,mask)
            mixed.append(nn(probs.astype(jnp.bfloat16),values))
        c_ref[0,rows,:]=jnp.where(head_lanes(0),mixed[0],mixed[1]).astype(jnp.bfloat16)

def attend_back_kernel(limit, first_ref, q_ref, k_ref, v_ref, t_ref, g_ref, dq_ref, dk_ref, dv_ref, dt_ref, dk_sum, dv_sum):
    table=t_ref[...]
    zero=jnp.zeros((BLOCK,LANES),jnp.bfloat16)
    flip=(lax.broadcasted_iota(jnp.int32,(BLOCK,BLOCK),0)+lax.broadcasted_iota(jnp.int32,(BLOCK,BLOCK),1)==BLOCK-1).astype(jnp.float32).astype(jnp.bfloat16)
    dk_sum[...]=jnp.zeros_like(dk_sum); dv_sum[...]=jnp.zeros_like(dv_sum)
    @pl.when((pl.program_id(0)==0)&(pl.program_id(1)==0))
    def _(): dt_ref[...]=jnp.zeros_like(dt_ref)
    for block in range(q_ref.shape[1]//BLOCK):
        rows=pl.ds(block*BLOCK,BLOCK); span=pl.ds(block*BLOCK,SPAN)
        keys=k_ref[0,span,:]; values=v_ref[0,span,:]
        mask=block_mask(first_ref[0],block,limit)
        grad_query=[]
        for head in range(2):
            query=jnp.where(head_lanes(head),q_ref[0,rows,:],zero)
            grad=jnp.where(head_lanes(head),g_ref[0,rows,:],zero)
            probs=block_probs(query,keys,table,mask)
            grad_probs=nt(grad,values)
            grad_raw=probs*(grad_probs-jnp.sum(probs*grad_probs,-1,keepdims=True))
            grad_raw=grad_raw.astype(jnp.bfloat16)
            turned=pltpu.roll(nn(flip,grad_raw),SPAN-BLOCK+1,1,stride=1,stride_axis=0)
            unskewed=nn(flip,turned.astype(jnp.bfloat16)).astype(jnp.bfloat16)
            dv_sum[span,:]+=tn(probs.astype(jnp.bfloat16),grad)
            dk_sum[span,:]+=tn(grad_raw,query)
            dt_ref[...]+=tn(unskewed,query)
            grad_query.append(nn(grad_raw,keys)+nn(unskewed,table))
        dq_ref[0,rows,:]=(jnp.where(head_lanes(0),grad_query[0],grad_query[1])*(HEAD_DIM**-0.5)).astype(jnp.bfloat16)
    dk_ref[0]=(dk_sum[...]*(HEAD_DIM**-0.5)).astype(jnp.bfloat16)
    dv_ref[0]=dv_sum[...].astype(jnp.bfloat16)

def wide_table(table):
    return jnp.tile(jnp.pad(table,((0,SPAN-table.shape[0]),(0,0))),(1,LANES//HEAD_DIM))

def specs(clips,rows,width):
    own=pl.BlockSpec((1,rows,LANES),lambda c,h:(c,0,h))
    ext=pl.BlockSpec((1,rows+LEFT+BACK_PAD,LANES),lambda c,h:(c,0,h))
    tab=pl.BlockSpec((SPAN,LANES),lambda c,h:(0,0))
    return (pl.BlockSpec(memory_space=pltpu.SMEM),own,ext,tab),(clips,width//LANES)

def attend(query,keys,values,table,rows):
    clips,_,width=query.shape
    first=lax.axis_index('seq').astype(jnp.int32)[None]*rows
    limit=rows*lax.axis_size('seq')
    (sc,own,ext,tab),grid=specs(clips,rows,width)
    return pl.pallas_call(functools.partial(attend_kernel,limit),grid=grid,
        in_specs=[sc,own,ext,ext,tab],out_specs=own,
        out_shape=jax.ShapeDtypeStruct(query.shape,jnp.bfloat16),name="attend",
    )(first,query,keys,values,wide_table(table))

def attend_back(query,keys,values,table,grad,rows):
    clips,_,width=query.shape
    first=lax.axis_index('seq').astype(jnp.int32)[None]*rows
    limit=rows*lax.axis_size('seq')
    (sc,own,ext,tab),grid=specs(clips,rows,width)
    dq,dk,dv,dt=pl.pallas_call(functools.partial(attend_back_kernel,limit),grid=grid,
        in_specs=[sc,own,ext,ext,tab,own],out_specs=[own,ext,ext,tab],
        out_shape=[jax.ShapeDtypeStruct(query.shape,jnp.bfloat16),jax.ShapeDtypeStruct(keys.shape,jnp.bfloat16),jax.ShapeDtypeStruct(keys.shape,jnp.bfloat16),jax.ShapeDtypeStruct((SPAN,LANES),jnp.float32)],
        scratch_shapes=[pltpu.VMEM((rows+LEFT+BACK_PAD,LANES),jnp.float32)]*2,name="attend_back",
    )(first,query,keys,values,wide_table(table),grad)
    return dq,dk,dv,(dt[:WIN,:HEAD_DIM]+dt[:WIN,HEAD_DIM:])*(HEAD_DIM**-0.5)
def depth_of():
    return lax.axis_size("group") // 2


def place():
    group = lax.axis_index("group")
    return (group // 2, group % 2, lax.axis_index("seq"), lax.axis_index("replica"))


def greet(peers):
    barrier = pltpu.get_barrier_semaphore()
    for peer in peers:
        pl.semaphore_signal(barrier, inc=1, device_id=peer, device_id_type=MESH)
    pl.semaphore_wait(barrier, len(peers))


def neighbours():
    z, x, seq, replica = place()
    depth = depth_of()
    deep = [{"group": (z + steps) % depth * 2 + x} for steps in range(1, depth)]
    across = {"group": z * 2 + 1 - x}
    beside = {"seq": 1 - seq}
    twin = {"replica": 1 - replica}
    return (deep, across, beside, twin)


class Gather:
    def __init__(self, source, target, cut, low, left, rows, size, sends, recvs, at):
        depth = depth_of()
        self.source, self.target, self.cut, self.low, self.rows = (source, target, cut, low, rows)
        self.piece = size[0] // (1, 2, 4)[cut]
        self.columns = pl.ds(left, size[1])
        self.sends, self.recvs, self.at = (sends, recvs, at)
        self.z, self.x, self.seq, self.replica = place()
        self.deep, self.across, self.beside, self.twin = neighbours()
        self.depth = depth
        self.firsts = (0, depth - 1, 2 * depth - 1, 4 * depth - 2)
        self.started = []

    def spot(self, ref, owner, dy, dc):
        part = 0
        if self.cut:
            part = (self.replica + dc) % 2
        if self.cut == 2:
            part = part + 2 * ((self.seq + dy) % 2)
        first = pl.multiple_of(owner * self.rows + self.low + part * self.piece, self.piece)
        return ref.at[pl.ds(first, self.piece), self.columns]

    def owner(self, steps, dx):
        return (self.z + self.depth - steps) % self.depth * 2 + (self.x + dx) % 2

    def copy(self, steps, dx, dy, dc, kind, index, peer):
        mine = steps == 0 and dx == 0
        slot = self.at + self.firsts[kind] + index
        spot = self.spot(self.target, self.owner(steps, dx), dy, dc)
        return pltpu.make_async_remote_copy(
            src_ref=self.spot(self.source, 0, dy, dc) if mine else spot,
            dst_ref=spot,
            send_sem=self.sends.at[slot],
            recv_sem=self.recvs.at[slot],
            device_id=peer,
            device_id_type=MESH,
        )

    def send(self, copy):
        copy.start()
        self.started.append(copy)

    def to_beside(self, steps, dx):
        if self.cut == 2:
            index = dx * self.depth + steps - 1
            self.send(self.copy(steps, dx, 0, 0, 2, index, self.beside))

    def to_twin(self, steps, dx, dy):
        if self.cut:
            index = dy * (2 * self.depth - 1) + dx * self.depth + steps - 1
            self.send(self.copy(steps, dx, dy, 0, 3, index, self.twin))

    def open(self):
        for steps, peer in enumerate(self.deep, 1):
            self.send(self.copy(0, 0, 0, 0, 0, steps - 1, peer))
        self.send(self.copy(0, 0, 0, 0, 1, 0, self.across))

    def got(self, steps, dx, dy, dc, kind, index):
        self.copy(steps or self.depth, dx, dy, dc, kind, index, self.twin).wait_recv()

    def forward_deep(self):
        for steps in range(1, self.depth):
            self.got(steps, 0, 0, 0, 0, steps - 1)
            self.send(self.copy(steps, 0, 0, 0, 1, steps, self.across))
            self.to_beside(steps, 0)
            self.to_twin(steps, 0, 0)

    def forward_across(self):
        for steps in range(self.depth):
            self.got(steps, 1, 0, 0, 1, steps)
            self.to_beside(steps, 1)
            self.to_twin(steps, 1, 0)

    def others(self):
        return [(steps, dx) for dx in range(2) for steps in range(self.depth) if steps or dx]

    def forward_beside(self):
        if self.cut == 2:
            for steps, dx in self.others():
                self.got(steps, dx, 1, 0, 2, dx * self.depth + steps - 1)
                self.to_twin(steps, dx, 1)

    def close(self):
        if self.cut:
            for dy in range(self.cut):
                for steps, dx in self.others():
                    index = dy * (2 * self.depth - 1) + dx * self.depth + steps - 1
                    self.got(steps, dx, dy, 1, 3, index)
        for copy in self.started:
            copy.wait_send()


class Ticker:
    def __init__(self, jobs, numbers, stores, loads):
        self.jobs, self.numbers, self.stores, self.loads = (jobs, numbers, stores, loads)
        self.tick, self.stored, self.loaded = (0, set(), set())

    def advance(self):
        names = ("open", "forward_deep", "forward_across", "forward_beside", "close")
        if self.tick >= len(self.jobs) + 8:
            return
        for lag, name in enumerate(names):
            if 0 <= self.tick - 2 * lag < len(self.jobs):
                getattr(self.jobs[self.tick - 2 * lag], name)()
        if self.tick < len(self.stores):
            source, store = self.stores[self.tick]
            if source not in self.loaded:
                self.loads[source].wait()
                self.loaded.add(source)
            store.start()
        self.tick += 1

    def until(self, number):
        last = max(at for at, owner in enumerate(self.numbers) if owner == number)
        while self.tick <= max(last + 8, number):
            self.advance()
        if number not in self.stored:
            self.stores[number][1].wait()
            self.stored.add(number)

    def finish(self):
        while self.tick < len(self.jobs) + 8:
            self.advance()
        for number in range(len(self.stores)):
            self.until(number)


def gather_ticker(plan, sources, ins, outs, helds, sems):
    sends, recvs, local = sems
    deep, across, beside, twin = neighbours()
    peers = deep + [across, twin]
    if any(member[-1] == 2 for member in plan):
        peers.append(beside)
    greet(peers)
    loads = [
        pltpu.make_async_copy(ins[at], held, local.at[0, at]) for at, held in enumerate(helds)
    ]
    for load in loads:
        load.start()
    jobs, at = ([], 0)
    for number, layer, low, left, size, cut in plan:
        source, first = sources[number]
        ref = ins[source].at[first + layer]
        rows = ins[source].shape[1]
        target = outs[number].at[layer]
        jobs.append(Gather(ref, target, cut, low, left, rows, size, sends, recvs, at))
        at += (2, 6, 8)[cut] * depth_of()
    z, x, _, _ = place()
    stores = []
    for number, (source, first) in enumerate(sources):
        rows = ins[source].shape[1]
        start = pl.multiple_of((z * 2 + x) * rows, rows)
        store = pltpu.make_async_copy(
            helds[source].at[pl.ds(first, outs[number].shape[0])],
            outs[number].at[:, pl.ds(start, rows)],
            local.at[1, number],
        )
        stores.append((source, store))
    return Ticker(jobs, [member[0] for member in plan], stores, loads)


def gather_kernel(plan, sources, count, *refs):
    ins, outs = (refs[:count], refs[count : count + len(sources)])
    ticker = gather_ticker(
        plan, sources, ins, outs, refs[count + len(sources) : -3], refs[-3:]
    )
    ticker.finish()


def product_rows(left, right, target, size=256):
    def body(cols):
        target[:, cols] = nn(left[...], right[:, cols]).astype(target.dtype)

    row_blocks(right.shape[1], size, body)


def join_rows(resid, branch, scale, squares, line):
    squares[pl.ds(line, 1), :] = jnp.zeros_like(squares[pl.ds(line, 1), :])

    def body(rows):
        value = branch[rows, :]
        resid[rows, :] += scale * value
        squares[pl.ds(line, 1), :] += jnp.sum(value * value, 0, keepdims=True)

    row_blocks(resid.shape[0], 64, body)


def module_forward(ticker, weights, entry, hidden, total, helds, saved, sems, chunks):
    width = total.shape[1]
    total[...] = jnp.zeros_like(total)
    stores = []
    for chunk in range(chunks):
        before = helds[chunk % 2]
        if chunk > 1:
            stores[chunk - 2].wait()
        w_in = weights.take()

        def body(cols):
            value = nn(entry[...], w_in[:, cols])
            before[:, cols] = value.astype(jnp.bfloat16)
            hidden[:, cols] = (value * jax.nn.sigmoid(value)).astype(jnp.bfloat16)

        row_blocks(width, 256, body)
        target = saved.at[:, pl.ds(chunk * width, width)]
        stores.append(fetch(before, target, sems.at[chunk]))
        w_out = weights.take()

        def gather(cols):
            total[:, cols] += nn(hidden[...], w_out[:, cols])

        row_blocks(width, 256, gather)
        ticker.advance()
    for store in stores[-2:]:
        store.wait()


def depthwise_rows(glu, taps, skip, target, ticker):
    total, width = target.shape
    for column in range(width // LANES):
        lanes = pl.ds(column * LANES, LANES)

        def body(at, carry):
            first = pl.multiple_of(at * LANES, LANES)
            window = glu[pl.ds(first, LANES + 32), lanes]
            summed = jnp.zeros((LANES, LANES), jnp.float32)
            for tap in range(KERNEL):
                moved = window[tap + 2 : tap + 2 + LANES]
                summed = summed + moved * taps[pl.ds(skip + tap, 1), lanes]
            target[pl.ds(first, LANES), lanes] = summed
            return carry

        lax.fori_loop(0, total // LANES, body, 0)
        if column % 4 == 3:
            ticker.advance()


def swish_rows(source, gain, target):
    def body(rows):
        normal, _ = norm_parts(source[rows, :])
        middle = normal * gain
        target[rows, :] = (middle * jax.nn.sigmoid(middle)).astype(jnp.bfloat16)

    row_blocks(source.shape[0], 64, body)


def forward_kernel(settings, *refs):
    plan, sources, count, norms, rows, limit = settings
    first_ref, table_ref, tokens = refs[:3]
    ins, refs = (refs[3 : 3 + count], refs[3 + count :])
    outs, refs = (refs[: len(sources)], refs[len(sources) :])
    out, squares, x1, x2, x3, x4, u0, u1, q_out, k_out, v_out, mixed_out, joined, summed = refs[:14]
    helds, refs = (refs[14 : 14 + count], refs[14 + count :])
    resid, total, glu, low_gains, gains, entry, hidden, held_a, held_b, q_ref = refs[:10]
    k_ref, v_ref, mixed, slots = refs[10:14]
    local, slot_sems, saved_sems, halo_sems = refs[14:18]
    ticker = gather_ticker(plan, sources, ins, outs, helds, refs[18:])
    width = resid.shape[1]
    chunks = u0.shape[1] // width
    groups = lax.axis_size("group")
    part = width // groups
    lines = low_gains.shape[0]
    load = fetch(tokens, entry, local.at[0])
    spaces = [slots.at[at] for at in range(3)]

    def stream(*weights):
        return Stream(spaces, slot_sems, [lambda slot, ref=ref: [(ref, slot)] for ref in weights])

    def module_stream(w_in, w_out):
        parts = []
        for chunk in range(chunks):
            here = pl.ds(chunk * width, width)
            parts += [w_in.at[0, :, here], w_out.at[0, here]]
        return stream(*parts)

    for _ in range(5):
        ticker.advance()
    ticker.until(0)
    small = [
        fetch(
            outs[0].at[0, pl.ds(group * lines, lines)],
            low_gains.at[:, pl.ds(group * part, part)],
            slot_sems.at[0, group],
        )
        for group in range(groups)
    ]
    for copy in small:
        copy.wait()
    gains[...] = low_gains[...].astype(jnp.float32)
    load.wait()

    def widen(at):
        resid[at, :] = entry[at, :].astype(jnp.float32)

    row_blocks(rows, 64, widen)
    norm_rows(resid, gains[pl.ds(0, 1), :], entry)
    ticker.until(1)
    ticker.until(2)
    pair = (held_a, held_b)
    weights = module_stream(outs[1], outs[2])
    module_forward(ticker, weights, entry, hidden, total, pair, u0, saved_sems, chunks)
    join_rows(resid, total, 0.5, squares, 1)
    stored = fetch(resid, x1, local.at[0])
    norm_rows(resid, gains[pl.ds(1, 1), :], entry)
    ticker.until(3)
    weights = stream(*[outs[3].at[at] for at in range(3)])
    own = pl.ds(LEFT, rows)
    spare = BACK_PAD - 2 * RIGHT
    for ref in (k_ref, v_ref):
        ref[0, pl.ds(LEFT + rows + 2 * RIGHT, spare), :] = jnp.zeros((spare, width), jnp.bfloat16)
    product_rows(entry, weights.take(), q_ref)
    product_rows(entry, weights.take(), k_ref.at[0, own])
    product_rows(entry, weights.take(), v_ref.at[0, own])
    _, _, seq, _ = place()
    span = lax.axis_size("seq")
    edges = []
    for at, ref in enumerate((k_ref, v_ref)):
        for way, (source, target, size, step) in enumerate(
            ((rows, 0, LEFT, 1), (LEFT, LEFT + rows, 2 * RIGHT, span - 1))
        ):
            edges.append(
                pltpu.make_async_remote_copy(
                    src_ref=ref.at[0, pl.ds(source, size)],
                    dst_ref=ref.at[0, pl.ds(target, size)],
                    send_sem=halo_sems.at[0, 2 * at + way],
                    recv_sem=halo_sems.at[1, 2 * at + way],
                    device_id={"seq": (seq + step) % span},
                    device_id_type=MESH,
                )
            )
    for edge in edges:
        edge.start()
    ticker.advance()
    for edge in edges:
        edge.wait()
    table = table_ref[...]
    zero = jnp.zeros((BLOCK, LANES), jnp.bfloat16)
    for pair_at in range(width // LANES):
        lanes = pl.ds(pair_at * LANES, LANES)

        def attend_block(block, carry):
            here = pl.ds(pl.multiple_of(block * BLOCK, BLOCK), BLOCK)
            near = pl.ds(pl.multiple_of(block * BLOCK, BLOCK), SPAN)
            key, value = (k_ref[0, near, lanes], v_ref[0, near, lanes])
            mask = block_mask(first_ref[0], block, limit)
            both = []
            for head in range(2):
                query = jnp.where(head_lanes(head), q_ref[here, lanes], zero)
                probs = block_probs(query, key, table, mask)
                both.append(nn(probs.astype(jnp.bfloat16), value))
            mixed[here, lanes] = jnp.where(head_lanes(0), both[0], both[1]).astype(jnp.bfloat16)
            return carry

        lax.fori_loop(0, rows // BLOCK, attend_block, 0)
        if pair_at % 2:
            ticker.advance()
    keeps = [
        fetch(source, target, local.at[1 + at])
        for at, (source, target) in enumerate(
            ((q_ref, q_out), (k_ref, k_out), (v_ref, v_out), (mixed, mixed_out))
        )
    ]
    ticker.until(4)
    product_rows(mixed, stream(outs[4].at[0]).take(), total)
    stored.wait()
    join_rows(resid, total, 1.0, squares, 2)
    stored = fetch(resid, x2, local.at[0])
    norm_rows(resid, gains[pl.ds(2, 1), :], entry)
    ticker.until(5)
    weights = stream(*[outs[5].at[0, :, pl.ds(at * width, width)] for at in range(2)])
    value_part, gate_part = (weights.take(), weights.take())

    def open_columns(cols):
        value = nn(entry[...], value_part[:, cols])
        gate = nn(entry[...], gate_part[:, cols])
        held_a[:, cols] = value.astype(jnp.bfloat16)
        held_b[:, cols] = gate.astype(jnp.bfloat16)
        opened = (value * jax.nn.sigmoid(gate)).astype(jnp.bfloat16)
        glu[pl.ds(32, rows), cols] = opened.astype(jnp.float32)

    row_blocks(width, 256, open_columns)
    halo = pltpu.make_async_remote_copy(
        src_ref=glu.at[pl.ds(rows, 32)],
        dst_ref=glu.at[pl.ds(0, 32)],
        send_sem=halo_sems.at[0, 4],
        recv_sem=halo_sems.at[1, 4],
        device_id={"seq": (seq + 1) % span},
        device_id_type=MESH,
    )
    halo.start()
    keeps += [
        fetch(held, joined.at[:, pl.ds(at * width, width)], local.at[5 + at])
        for at, held in enumerate(pair)
    ]
    ticker.advance()
    halo.wait()
    ahead = pl.ds(0, 32)
    glu[ahead, :] = jnp.where(seq > 0, glu[ahead, :], jnp.zeros((32, width), jnp.float32))
    depthwise_rows(glu, gains, norms, total, ticker)
    kept = fetch(total, summed, local.at[7])
    swish_rows(total, gains[pl.ds(3, 1), :], entry)
    ticker.until(6)
    conv = glu.at[pl.ds(0, rows)]
    product_rows(entry, stream(outs[6].at[0]).take(), conv)
    stored.wait()
    join_rows(resid, conv, 1.0, squares, 3)
    stored = fetch(resid, x3, local.at[0])
    norm_rows(resid, gains[pl.ds(4, 1), :], entry)
    kept.wait()
    for keep in keeps:
        keep.wait()
    ticker.until(7)
    ticker.until(8)
    weights = module_stream(outs[7], outs[8])
    module_forward(ticker, weights, entry, hidden, total, pair, u1, saved_sems, chunks)
    stored.wait()
    join_rows(resid, total, 0.5, squares, 4)
    stored = fetch(resid, x4, local.at[0])
    squares[pl.ds(0, 1), :] = jnp.zeros((1, width), jnp.float32)

    def tally(at):
        squares[pl.ds(0, 1), :] += jnp.sum(resid[at, :] * resid[at, :], 0, keepdims=True)

    row_blocks(rows, 64, tally)
    norm_rows(resid, gains[pl.ds(5, 1), :], entry)
    last = fetch(entry, out, local.at[1])
    ticker.finish()
    stored.wait()
    last.wait()


def gather_plan(shards, sources, halve):
    groups = lax.axis_size("group")
    width = shards[1].shape[1] * groups
    part = width // groups
    plan = [(0, 0, 0, 0, shards[0].shape[1:], 0)]
    for number, (source, first, layers) in enumerate(sources):
        for layer in range(layers if source else 0):
            for low in range(0, shards[source].shape[1], part):
                for left in range(0, shards[source].shape[2], width):
                    cut = 2 if halve and len(plan) % 3 else 1
                    plan.append((number, layer, low, left, (part, width), cut))
    return plan


def gather_outputs(shards, sources):
    groups = lax.axis_size("group")
    return [
        jax.ShapeDtypeStruct(
            (layers, groups * shards[source].shape[1], shards[source].shape[2]), jnp.bfloat16
        )
        for source, _, layers in sources
    ]


def gather_scratch(plan, sources):
    total = sum((2, 6, 8)[member[-1]] * depth_of() for member in plan)
    return [
        pltpu.SemaphoreType.DMA((total,)),
        pltpu.SemaphoreType.DMA((total,)),
        pltpu.SemaphoreType.DMA((2, len(sources))),
    ]


def gather_weights(shards, sources, halve):
    plan = gather_plan(shards, sources, halve)
    return pl.pallas_call(
        functools.partial(
            gather_kernel, plan, [(source, first) for source, first, _ in sources], len(shards)
        ),
        in_specs=[pl.BlockSpec(memory_space=pl.ANY)] * len(shards),
        out_specs=[pl.BlockSpec(memory_space=pl.ANY)] * len(sources),
        out_shape=gather_outputs(shards, sources),
        scratch_shapes=[pltpu.VMEM(shard.shape, jnp.bfloat16) for shard in shards]
        + gather_scratch(plan, sources),
        compiler_params=pltpu.CompilerParams(
            collective_id=1, has_side_effects=True, vmem_limit_bytes=24 << 20
        ),
        name="gather_weights",
    )(*shards)


def forward(tokens, shards, sources, norms, table, halve):
    rows, width = tokens.shape
    plan = gather_plan(shards, sources, halve)
    groups = lax.axis_size("group")
    first = lax.axis_index("seq").astype(jnp.int32)[None] * rows
    limit = rows * lax.axis_size("seq")
    ext = rows + LEFT + BACK_PAD
    inner = shards[1].shape[2]
    lines = shards[0].shape[1]
    hbm = pl.BlockSpec(memory_space=pl.ANY)
    vmem = pl.BlockSpec(memory_space=pltpu.VMEM)
    low = lambda *shape: jax.ShapeDtypeStruct(shape, jnp.bfloat16)
    wide = lambda *shape: jax.ShapeDtypeStruct(shape, jnp.float32)
    settings = (plan, [member[:2] for member in sources], len(shards), norms, rows, limit)
    results = pl.pallas_call(
        functools.partial(forward_kernel, settings),
        in_specs=[pl.BlockSpec(memory_space=pltpu.SMEM), vmem] + [hbm] * (1 + len(shards)),
        out_specs=[hbm] * len(sources) + [hbm, vmem] + [hbm] * 12,
        out_shape=gather_outputs(shards, sources)
        + [low(rows, width), wide(8, width)]
        + [wide(rows, width)] * 4
        + [low(rows, inner)] * 2
        + [low(rows, width), low(1, ext, width), low(1, ext, width), low(rows, width)]
        + [low(rows, 2 * width), wide(rows, width)],
        scratch_shapes=[pltpu.VMEM(shard.shape, jnp.bfloat16) for shard in shards]
        + [
            pltpu.VMEM((rows, width), jnp.float32),
            pltpu.VMEM((rows, width), jnp.float32),
            pltpu.VMEM((rows + 32, width), jnp.float32),
            pltpu.VMEM((lines, width), jnp.bfloat16),
            pltpu.VMEM((lines, width), jnp.float32),
        ]
        + [pltpu.VMEM((rows, width), jnp.bfloat16)] * 5
        + [
            pltpu.VMEM((1, ext, width), jnp.bfloat16),
            pltpu.VMEM((1, ext, width), jnp.bfloat16),
            pltpu.VMEM((rows, width), jnp.bfloat16),
            pltpu.VMEM((3, width, width), jnp.bfloat16),
            pltpu.SemaphoreType.DMA((8,)),
            pltpu.SemaphoreType.DMA((3, groups)),
            pltpu.SemaphoreType.DMA((inner // width,)),
            pltpu.SemaphoreType.DMA((2, 5)),
        ]
        + gather_scratch(plan, sources),
        compiler_params=pltpu.CompilerParams(
            collective_id=5, has_side_effects=True, vmem_limit_bytes=56 << 20
        ),
        name="forward",
    )(first, wide_table(table), tokens, *shards)
    return results[: len(sources)], results[len(sources) :]


def swap(value, axis, bit=1):
    return lax.ppermute(value, axis, [(i, i ^ bit) for i in range(lax.axis_size(axis))])


def butterfly(value):
    for axis in ("replica", "seq", "group"):
        bit = 1
        while bit < lax.axis_size(axis):
            value = value + swap(value, axis, bit)
            bit *= 2
    return value


def add_slabs(count, target, *sources):
    def body(at, carry):
        total = sources[0](at)[...].astype(jnp.float32)
        for source in sources[1:]:
            total = total + source(at)[...].astype(jnp.float32)
        target(at)[...] = total.astype(jnp.bfloat16)
        return carry

    lax.fori_loop(0, count, body, 0)


class Reduce:
    def __init__(self, pool, number, target, low, left):
        self.pool, self.number = (pool, number)
        self.target, self.low, self.left = (target, low, left)
        self.source = pool.kept.at[number]
        self.stage = pool.stage.at[number % 2]
        self.kept = False
        self.depth, self.width = (depth_of(), pool.width)
        self.half, self.unit = (pool.rows // 2, pool.rows // 8)
        self.started = []
        self.stages = [
            self.exchange_twin,
            self.exchange_seq,
            self.exchange_across,
            self.exchange_deep,
            self.settle,
            self.hand_over,
            self.close,
        ]
        self.done_stages = 0
        slot = number % pool.ring
        self.own, self.came = (pool.own.at[slot], pool.came.at[slot])
        self.from_x, self.from_seq = (pool.from_x.at[slot], pool.from_seq.at[slot])
        self.from_z, self.shared = (pool.from_z.at[number], pool.shared.at[number])
        self.alone = pool.finished.at[slot, pl.ds(0, self.unit)]
        self.joint = pool.finished.at[slot, pl.ds(self.unit, 2 * self.unit)]

    def locate(self):
        self.z, self.x, self.seq, self.replica = place()
        self.deep, self.across, self.beside, self.twin = neighbours()

    def rows(self, first, count):
        return pl.ds(pl.multiple_of(first, self.unit), count * self.unit)

    def near(self):
        return self.rows(self.seq * self.unit, 3)

    def lone(self):
        return self.rows(3 * self.unit * self.seq, 1)

    def far(self):
        return self.rows(3 * self.unit * (1 - self.seq), 1)

    def both(self):
        return pl.ds(self.unit, 2 * self.unit)

    def side(self, replica):
        return pl.ds(pl.multiple_of(replica * self.half, self.half), self.half)

    def remote(self, source, target, slot, peer):
        return pltpu.make_async_remote_copy(
            src_ref=source,
            dst_ref=target,
            send_sem=self.pool.sends.at[self.number, slot],
            recv_sem=self.pool.recvs.at[self.number, slot],
            device_id=peer,
            device_id_type=MESH,
        )

    def send(self, ends, slot, peer):
        make = lambda peer: self.remote(*ends(), slot, peer)
        make(peer).start()
        self.started.append(make)

    def wait(self, target, slot):
        self.remote(target, target, slot, self.twin).wait_recv()

    def keep(self):
        return pltpu.make_async_copy(self.stage, self.source, self.pool.local.at[self.number, 0])

    def await_kept(self):
        if not self.kept:
            self.keep().wait()
            self.kept = True

    def load(self):
        source = self.source.at[:, :, self.side(self.replica)]
        return pltpu.make_async_copy(source, self.own, self.pool.local.at[self.number, 1])

    def credit(self, kind):
        if self.number >= self.pool.ring:
            pl.semaphore_wait(self.pool.credits.at[kind], 1)

    def release(self, kind, peer):
        if self.number + self.pool.ring < self.pool.total:
            pl.semaphore_signal(
                self.pool.credits.at[kind], inc=1, device_id=peer, device_id_type=MESH
            )

    def exchange_twin(self):
        self.await_kept()
        self.credit(0)
        self.load().start()
        ends = lambda: (self.source.at[:, :, self.side(1 - self.replica)], self.came)
        self.send(ends, 0, self.twin)

    def exchange_seq(self):
        self.load().wait()
        self.wait(self.came, 0)
        far = self.far()
        own = lambda at: self.own.at[at // 2, at % 2, far]
        add_slabs(2 * self.depth, own, own, lambda at: self.came.at[at // 2, at % 2, far])
        self.credit(1)
        self.send(lambda: (self.own.at[:, :, self.far()], self.from_seq), 1, self.beside)

    def gather(self, x, arrived):
        both, lone = (self.both(), self.lone())
        refs = [self.own.at[:, x], self.came.at[:, x]]
        pick = lambda rows: [lambda at, ref=ref: ref.at[at, rows] for ref in refs]
        shared, alone = (pick(both), pick(lone))
        alone.append(lambda at: self.from_seq.at[at, x])
        if arrived:
            both_here = self.rows(self.unit * (1 - self.seq), 2)
            lone_here = self.rows(2 * self.unit * self.seq, 1)
            shared.append(lambda at: self.from_x.at[at, both_here])
            alone.append(lambda at: self.from_x.at[at, lone_here])
        add_slabs(self.depth, shared[0], *shared)
        add_slabs(self.depth, alone[0], *alone)

    def exchange_across(self):
        self.wait(self.from_seq, 1)
        self.gather(1 - self.x, False)
        self.credit(2)
        self.send(lambda: (self.own.at[:, 1 - self.x, self.near()], self.from_x), 2, self.across)

    def exchange_deep(self):
        self.wait(self.from_x, 2)
        self.gather(self.x, True)
        for steps, peer in enumerate(self.deep, 1):
            ends = lambda steps=steps: (
                self.own.at[(self.z + steps) % self.depth, self.x, self.near()],
                self.from_z.at[steps - 1],
            )
            self.send(ends, 2 + steps, peer)
        self.release(0, self.twin)
        self.release(1, self.beside)
        self.release(2, self.across)

    def settle(self):
        for steps in range(1, self.depth):
            self.wait(self.from_z.at[steps - 1], 2 + steps)
        self.flush()
        both_here = self.rows(self.unit * (1 - self.seq), 2)
        lone_here = self.rows(2 * self.unit * self.seq, 1)
        for target, own, here in (
            (self.shared.at[self.seq], self.both(), both_here),
            (self.alone, self.lone(), lone_here),
        ):
            sources = [lambda at, own=own: self.own.at[self.z, self.x, own]]
            sources += [
                lambda at, steps=steps, here=here: self.from_z.at[steps, here]
                for steps in range(self.depth - 1)
            ]
            add_slabs(1, lambda at, target=target: target, *sources)
        self.last = 2 + self.depth
        ends = lambda: (self.shared.at[self.seq], self.shared.at[self.seq])
        self.send(ends, self.last, self.beside)
        self.store(0).start()
        self.send(lambda: (self.alone, self.spot(self.lone_out())), self.last + 1, self.beside)
        self.send(lambda: (self.alone, self.spot(self.lone_out())), self.last + 2, self.twin)

    def spot(self, first, count=1):
        return self.target.at[self.rows(first, count), pl.ds(self.left, self.width)]

    def lone_out(self, dy=0, dc=0):
        seq = self.seq if dy == 0 else 1 - self.seq
        replica = self.replica if dc == 0 else 1 - self.replica
        return self.low + replica * self.half + 3 * self.unit * seq

    def both_out(self, dc=0):
        replica = self.replica if dc == 0 else 1 - self.replica
        return self.low + replica * self.half + self.unit

    def store(self, kind):
        source = self.joint if kind else self.alone
        target = self.spot(self.both_out(), 2) if kind else self.spot(self.lone_out())
        return pltpu.make_async_copy(source, target, self.pool.local.at[self.number, 2 + kind])

    def hand_over(self):
        self.wait(self.spot(self.lone_out(1)), self.last + 1)
        spot = lambda: self.spot(self.lone_out(1))
        self.send(lambda: (spot(), spot()), self.last + 3, self.twin)
        self.wait(self.shared.at[1 - self.seq], self.last)
        sources = [lambda at, turn=turn: self.shared.at[turn] for turn in range(2)]
        add_slabs(1, lambda at: self.joint, *sources)
        self.store(1).start()
        self.send(lambda: (self.joint, self.spot(self.both_out(), 2)), self.last + 4, self.twin)

    def close(self):
        self.wait(self.spot(self.lone_out(0, 1)), self.last + 2)
        self.wait(self.spot(self.lone_out(1, 1)), self.last + 3)
        self.wait(self.spot(self.both_out(1), 2), self.last + 4)
        self.store(0).wait()
        self.store(1).wait()
        self.flush()

    def flush(self):
        for make in self.started:
            make(self.twin).wait_send()
        self.started = []

    def step(self):
        self.locate()
        self.stages[self.done_stages]()
        self.done_stages += 1


class Pool:
    ring = 7

    def __init__(self, rows, width, total, kept, refs):
        self.rows, self.width, self.total, self.kept = (rows, width, total, kept)
        names = list(Pool.shapes(rows, width, total))
        for name, ref in zip(names, refs):
            setattr(self, name, ref)
        self.sends, self.recvs, self.local, self.credits = refs[len(names) :]
        self.jobs = []

    @staticmethod
    def shapes(rows, width, total):
        depth, ring = (depth_of(), Pool.ring)
        unit = rows // 8
        return {
            "own": (ring, depth, 2, rows // 2, width),
            "came": (ring, depth, 2, rows // 2, width),
            "from_x": (ring, depth, 3 * unit, width),
            "from_seq": (ring, depth, 2, unit, width),
            "from_z": (total, depth - 1, 3 * unit, width),
            "shared": (total, 2, 2 * unit, width),
            "finished": (ring, 3 * unit, width),
            "stage": (2, depth, 2, rows, width),
        }

    @staticmethod
    def scratch(rows, width, total):
        slots = 7 + depth_of()
        return [pltpu.VMEM(shape, jnp.bfloat16) for shape in Pool.shapes(rows, width, total).values()] + [
            pltpu.SemaphoreType.DMA((total, slots)),
            pltpu.SemaphoreType.DMA((total, slots)),
            pltpu.SemaphoreType.DMA((total, 4)),
            pltpu.SemaphoreType.REGULAR((3,)),
        ]

    def add(self, target, low, left):
        number = len(self.jobs)
        if number >= 2:
            self.jobs[number - 2].await_kept()
        job = Reduce(self, number, target, low, left)
        self.jobs.append(job)
        return job

    def free(self, number):
        return number < self.ring or self.jobs[number - self.ring].done_stages >= 5

    def pump(self):
        active = [job for job in self.jobs if 0 < job.done_stages < 7]
        fresh = [job for job in self.jobs if job.done_stages == 0][:1]
        for job in fresh:
            if self.free(job.number):
                job.step()
        for job in reversed(active):
            job.step()

    def drain(self):
        while any(job.done_stages < 7 for job in self.jobs):
            self.pump()


def row_blocks(total, size, body):
    def step(at, carry):
        body(pl.ds(pl.multiple_of(at * size, size), size))
        return carry

    lax.fori_loop(0, total // size, step, 0)


def norm_parts(values):
    centered = values - jnp.mean(values, -1, keepdims=True)
    inverse = lax.rsqrt(jnp.mean(centered * centered, -1, keepdims=True) + EPSILON)
    return (centered * inverse, inverse)


def norm_rows(source, gain, target):
    def body(rows):
        normal, _ = norm_parts(source[rows, :].astype(jnp.float32))
        target[rows, :] = (normal * gain).astype(target.dtype)

    row_blocks(source.shape[0], 64, body)


def norm_back_rows(source, gain, grads, resid, sums, line):
    sums[pl.ds(line, 1), :] = jnp.zeros_like(sums[pl.ds(line, 1), :])

    def body(rows):
        normal, inverse = norm_parts(source[rows, :].astype(jnp.float32))
        grad = grads[rows, :]
        grad_normal = grad * gain
        resid[rows, :] += inverse * (
            grad_normal
            - jnp.mean(grad_normal, -1, keepdims=True)
            - normal * jnp.mean(grad_normal * normal, -1, keepdims=True)
        )
        sums[pl.ds(line, 1), :] += jnp.sum(grad * normal, 0, keepdims=True)

    row_blocks(source.shape[0], 64, body)


def cast_rows(source, target, scale=1.0):
    def body(rows):
        target[rows, :] = (source[rows, :] * scale).astype(jnp.bfloat16)

    row_blocks(source.shape[0], 64, body)


def transposed_rows(left, right, target, size=256):
    def body(cols):
        target[:, cols] = nt(left[...], right[cols, :]).astype(target.dtype)

    row_blocks(right.shape[0], size, body)


def add_transposed(left, right, target, size=256):
    def body(cols):
        target[:, cols] += nt(left[...], right[cols, :])

    row_blocks(right.shape[0], size, body)


def gradient_into(job, left, right):
    depth, _, rows, width = job.stage.shape

    def step(z, carry):
        cols = pl.ds(pl.multiple_of(z * 2 * rows, 2 * rows), 2 * rows)
        value = tn(left[:, cols], right[...]).astype(jnp.bfloat16)
        job.stage[z, 0] = value[:rows]
        job.stage[z, 1] = value[rows:]
        return carry

    lax.fori_loop(0, depth, step, 0)
    job.keep().start()


class Stream:
    def __init__(self, buffers, sems, copies):
        self.buffers, self.sems, self.copies = (buffers, sems, copies)
        self.issued = self.taken = 0
        for _ in range(len(buffers) - 1):
            self.issue()

    def parts(self, number):
        slot = number % len(self.buffers)
        made = self.copies[number](self.buffers[slot])
        return [
            pltpu.make_async_copy(source, target, self.sems.at[slot, at])
            for at, (source, target) in enumerate(made)
        ]

    def issue(self):
        if self.issued < len(self.copies):
            for copy in self.parts(self.issued):
                copy.start()
            self.issued += 1

    def take(self):
        for copy in self.parts(self.taken):
            copy.wait()
        self.taken += 1
        self.issue()
        return self.buffers[(self.taken - 1) % len(self.buffers)]


def module_copies(w_in, w_out, groups):
    chunks = w_out.shape[1]
    rows = w_out.shape[2]
    copies = []
    for chunk in range(chunks):
        copies.append(
            lambda slot, chunk=chunk: [
                (w_out.at[group, chunk], slot.at[pl.ds(group * rows, rows)])
                for group in range(groups)
            ]
        )
        copies.append(
            lambda slot, chunk=chunk: [
                (
                    w_in.at[:, pl.ds((group * chunks + chunk) * rows, rows)],
                    slot.at[:, pl.ds(group * rows, rows)],
                )
                for group in range(groups)
            ]
        )
    return copies


def saved_copies(saved, groups, rows):
    chunks = saved.shape[1] // (groups * rows)
    return [
        lambda slot, chunk=chunk: [
            (
                saved.at[:, pl.ds((group * chunks + chunk) * rows, rows)],
                slot.at[:, pl.ds(group * rows, rows)],
            )
            for group in range(groups)
        ]
        for chunk in range(chunks)
    ]


def module_back(pool, weights, saved, buffers, chunks, outs, often):
    pump = pool.pump
    entry, low, hidden, grad_hidden, total = buffers
    grad_in, grad_out = outs
    width = total.shape[1]
    total[...] = jnp.zeros_like(total)
    for chunk in range(chunks):
        before = saved.take()
        w_out = weights.take()

        def body(cols):
            value = before[:, cols].astype(jnp.float32)
            logistic = jax.nn.sigmoid(value)
            hidden[:, cols] = (value * logistic).astype(jnp.bfloat16)
            slope = logistic * (1.0 + value * (1.0 - logistic))
            grad = nt(low[...], w_out[cols, :]) * slope
            grad_hidden[:, cols] = grad.astype(jnp.bfloat16)

        row_blocks(width, 256, body)
        job = pool.add(grad_out, chunk * pool.rows, 0)
        gradient_into(job, hidden, low)
        job = pool.add(grad_in, 0, chunk * width)
        gradient_into(job, entry, grad_hidden)
        if often:
            pump()
        add_transposed(grad_hidden, weights.take(), total)
        if often or chunk % 2:
            pump()
def middle_rows(source, gain, grads, entry, sums, line):
    sums[pl.ds(line, 1), :] = jnp.zeros_like(sums[pl.ds(line, 1), :])

    def body(rows):
        normal, inverse = norm_parts(source[rows, :])
        middle = normal * gain
        logistic = jax.nn.sigmoid(middle)
        entry[rows, :] = (middle * logistic).astype(jnp.bfloat16)
        grad = grads[rows, :] * (logistic + middle * logistic * (1.0 - logistic))
        grad_normal = grad * gain
        grads[rows, :] = inverse * (
            grad_normal
            - jnp.mean(grad_normal, -1, keepdims=True)
            - normal * jnp.mean(grad_normal * normal, -1, keepdims=True)
        )
        sums[pl.ds(line, 1), :] += jnp.sum(grad * normal, 0, keepdims=True)

    row_blocks(source.shape[0], 64, body)


def depthwise_back(grads, taps, value, gate, grad_value, grad_gate, tap_sums, pump):
    total, width = value.shape
    tap_sums[...] = jnp.zeros_like(tap_sums)
    for column in range(width // LANES):
        lanes = pl.ds(column * LANES, LANES)

        def body(at, carry):
            first = pl.multiple_of(at * LANES, LANES)
            rows = pl.ds(first, LANES)
            held = value[rows, lanes].astype(jnp.float32)
            opened = jax.nn.sigmoid(gate[rows, lanes].astype(jnp.float32))
            glu = (held * opened).astype(jnp.bfloat16).astype(jnp.float32)
            grad = jnp.zeros((LANES, LANES), jnp.float32)
            window = grads[pl.ds(first, LANES + 32), lanes]
            for tap in range(KERNEL):
                ahead = KERNEL - 1 - tap
                moved = window[ahead : ahead + LANES]
                grad = grad + moved * taps[pl.ds(tap, 1), lanes]
                tap_sums[pl.ds(tap, 1), lanes] += jnp.sum(glu * moved, 0, keepdims=True)
            grad_value[rows, lanes] = (grad * opened).astype(jnp.bfloat16)
            grad_gate[rows, lanes] = (grad * held * opened * (1.0 - opened)).astype(jnp.bfloat16)
            return carry

        lax.fori_loop(0, total // LANES, body, 0)
        if column % 4 == 3:
            pump()


def fetch(source, target, sem):
    copy = pltpu.make_async_copy(source, target, sem)
    copy.start()
    return copy


def back_kernel(settings, *refs):
    count, clips, rows, limit = settings
    first_ref, table_ref, gains, taps = refs[:4]
    cot, x4, x3, x2, x1, x0, u1, u0, joined, summed = refs[4:14]
    mixed, query, keys, values, c_in, c_out, a_out, qkv = refs[14:22]
    second_in, second_out, w_in, w_out = refs[22:26]
    grad_x, gain_sums, dt_ref, tap_sums = refs[26:30]
    to_second_out, to_second_in, to_conv_out, to_conv_in = refs[30:34]
    to_attn, to_q, to_k, to_v, to_out, to_in, kept = refs[34:41]
    refs = refs[41:]
    resid, total_ext, resid_in, low, entry, mixed_grad, q_ref, dq_ref = refs[:8]
    k_ref, v_ref, dk_ref, dv_ref, later, earlier, dk_sum, dv_sum, slots = refs[8:17]
    local, slot_sems, saved_sems, halo_sems = refs[17:21]
    width = resid.shape[1]
    total = total_ext.at[pl.ds(0, rows)]
    groups = lax.axis_size("group")
    part = width // groups
    span = lax.axis_size("seq")
    chunks = w_out.shape[1]
    reduce_greet()
    pool = Pool(part, width, count, kept, refs[21:])
    pump = pool.pump
    copies = module_copies(second_in, second_out, groups)
    copies += [lambda slot: [(c_out, slot)]]
    copies += [
        lambda slot, at=at: [(c_in.at[:, pl.ds(at * width, width)], slot)] for at in range(2)
    ]
    copies += [lambda slot: [(a_out, slot)]]
    copies += [lambda slot, at=at: [(qkv.at[at], slot)] for at in range(3)]
    copies += module_copies(w_in, w_out, groups)
    load = fetch(x4, resid_in, local.at[0])
    arrival = fetch(cot, low, local.at[1])
    weights = Stream([slots.at[at] for at in range(3)], slot_sems, copies)
    free = [ref.at[0, pl.ds(0, rows)] for ref in (k_ref, v_ref)]
    saved = Stream(free, saved_sems, saved_copies(u1, groups, part))
    halves = [ref.at[0, pl.ds(0, rows)] for ref in (dk_ref, dv_ref)]
    opening = [
        fetch(joined.at[:, pl.ds(at * width, width)], half, local.at[2 + at])
        for at, half in enumerate(halves)
    ]
    resid[...] = jnp.zeros_like(resid)
    arrival.wait()
    load.wait()

    def widen(at):
        total[at, :] = low[at, :].astype(jnp.float32)

    row_blocks(rows, 64, widen)
    norm_back_rows(resid_in, gains[pl.ds(5, 1), :], total, resid, gain_sums, 5)
    load = fetch(x3, resid_in, local.at[0])
    cast_rows(resid, low, 0.5)
    load.wait()
    norm_rows(resid_in, gains[pl.ds(4, 1), :], entry)
    buffers = (entry, low, mixed_grad, q_ref, total)
    module_back(
        pool, weights, saved, buffers, chunks, (to_second_in, to_second_out), False
    )
    norm_back_rows(resid_in, gains[pl.ds(4, 1), :], total, resid, gain_sums, 4)
    load = fetch(summed, resid_in, local.at[0])
    cast_rows(resid, low)
    transposed_rows(low, weights.take(), total)
    load.wait()
    middle_rows(resid_in, gains[pl.ds(3, 1), :], total, entry, gain_sums, 3)
    _, _, seq, _ = place()
    halo = pltpu.make_async_remote_copy(
        src_ref=total_ext.at[pl.ds(0, 32)],
        dst_ref=total_ext.at[pl.ds(rows, 32)],
        send_sem=halo_sems.at[0, 4],
        recv_sem=halo_sems.at[1, 4],
        device_id={"seq": (seq + span - 1) % span},
        device_id_type=MESH,
    )
    halo.start()
    load = fetch(x2, resid_in, local.at[0])
    job = pool.add(to_conv_out, 0, 0)
    gradient_into(job, entry, low)
    pump()
    for copy in opening:
        copy.wait()
    load.wait()
    norm_rows(resid_in, gains[pl.ds(2, 1), :], entry)
    halo.wait()
    beyond = pl.ds(rows, 32)
    nothing = jnp.zeros((32, width), jnp.float32)
    total_ext[beyond, :] = jnp.where(seq < span - 1, total_ext[beyond, :], nothing)
    depthwise_back(total_ext, taps, *halves, mixed_grad, q_ref, tap_sums, pump)
    total[...] = jnp.zeros_like(total)
    for at, flat in enumerate((mixed_grad, q_ref)):
        job = pool.add(to_conv_in, 0, at * width)
        gradient_into(job, entry, flat)
        add_transposed(flat, weights.take(), total)
        pump()
    norm_back_rows(resid_in, gains[pl.ds(2, 1), :], total, resid, gain_sums, 2)
    loads = [
        fetch(source, target, local.at[at])
        for at, (source, target) in enumerate(
            ((mixed, entry), (query, q_ref), (keys, k_ref), (values, v_ref), (x1, resid_in))
        )
    ]
    cast_rows(resid, low)
    transposed_rows(low, weights.take(), mixed_grad)
    loads[0].wait()
    job = pool.add(to_attn, 0, 0)
    gradient_into(job, entry, low)
    pump()
    for load in loads[1:]:
        load.wait()
    table = table_ref[...]
    zero = jnp.zeros((BLOCK, LANES), jnp.bfloat16)
    across = lax.broadcasted_iota(jnp.int32, (BLOCK, BLOCK), 0)
    across = across + lax.broadcasted_iota(jnp.int32, (BLOCK, BLOCK), 1)
    flip = (across == BLOCK - 1).astype(jnp.float32).astype(jnp.bfloat16)
    dt_ref[...] = jnp.zeros_like(dt_ref)
    blocks = rows // BLOCK
    for pair in range(width // LANES):
        lanes = pl.ds(pair * LANES, LANES)
        dk_sum[...] = jnp.zeros_like(dk_sum)
        dv_sum[...] = jnp.zeros_like(dv_sum)

        def attend_block(at, carry):
            clip, block = (at // blocks, at % blocks)
            here = pl.ds(pl.multiple_of(at * BLOCK, BLOCK), BLOCK)
            near = pl.ds(pl.multiple_of(block * BLOCK, BLOCK), SPAN)
            key = k_ref[clip, near, lanes]
            value = v_ref[clip, near, lanes]
            mask = block_mask(first_ref[0], block, limit)
            grad_query = []
            for head in range(2):
                q = jnp.where(head_lanes(head), q_ref[here, lanes], zero)
                g = jnp.where(head_lanes(head), mixed_grad[here, lanes], zero)
                probs = block_probs(q, key, table, mask)
                grad_probs = nt(g, value)
                grad_raw = probs * (grad_probs - jnp.sum(probs * grad_probs, -1, keepdims=True))
                grad_raw = grad_raw.astype(jnp.bfloat16)
                turned = pltpu.roll(
                    nn(flip, grad_raw), SPAN - BLOCK + 1, 1, stride=1, stride_axis=0
                )
                unskewed = nn(flip, turned.astype(jnp.bfloat16)).astype(jnp.bfloat16)
                dv_sum[clip, near, :] += tn(probs.astype(jnp.bfloat16), g)
                dk_sum[clip, near, :] += tn(grad_raw, q)
                dt_ref[...] += tn(unskewed, q)
                grad_query.append(nn(grad_raw, key) + nn(unskewed, table))
            both = jnp.where(head_lanes(0), grad_query[0], grad_query[1])
            dq_ref[here, lanes] = (both * HEAD_DIM**-0.5).astype(jnp.bfloat16)
            return carry

        lax.fori_loop(0, clips * blocks, attend_block, 0, unroll=2)
        dk_ref[:, :, lanes] = (dk_sum[...] * HEAD_DIM**-0.5).astype(jnp.bfloat16)
        dv_ref[:, :, lanes] = dv_sum[...].astype(jnp.bfloat16)
        pump()

    saved = Stream(free, saved_sems, saved_copies(u0, groups, part))
    edges = []
    for at, ref in enumerate((dk_ref, dv_ref)):
        for way, (target, low_row, size, step) in enumerate(
            ((later, 0, LEFT, span - 1), (earlier, LEFT + rows, 2 * RIGHT, 1))
        ):
            edges.append(
                pltpu.make_async_remote_copy(
                    src_ref=ref.at[:, pl.ds(low_row, size)],
                    dst_ref=target.at[at],
                    send_sem=halo_sems.at[0, 2 * at + way],
                    recv_sem=halo_sems.at[1, 2 * at + way],
                    device_id={"seq": (seq + step) % span},
                    device_id_type=MESH,
                )
            )
    for edge in edges:
        edge.start()
    gain = gains[pl.ds(1, 1), :]
    norm_rows(resid_in, gain, entry)
    job = pool.add(to_q, 0, 0)
    gradient_into(job, entry, dq_ref)
    total[...] = jnp.zeros_like(total)
    add_transposed(dq_ref, weights.take(), total)
    pump()
    for edge in edges:
        edge.wait()
    for at, (ref, flat) in enumerate(((dk_ref, mixed_grad), (dv_ref, q_ref))):
        for clip in range(clips):
            base = clip * rows
            flat[pl.ds(base, rows), :] = ref[clip, pl.ds(LEFT, rows), :]
            tail = pl.ds(base + rows - LEFT, LEFT)
            zero_tail = jnp.zeros((LEFT, width), jnp.float32)
            came = jnp.where(seq < span - 1, later[at, clip].astype(jnp.float32), zero_tail)
            flat[tail, :] = (flat[tail, :].astype(jnp.float32) + came).astype(jnp.bfloat16)
            head = pl.ds(base, 2 * RIGHT)
            zero_head = jnp.zeros((2 * RIGHT, width), jnp.float32)
            came = jnp.where(seq > 0, earlier[at, clip].astype(jnp.float32), zero_head)
            flat[head, :] = (flat[head, :].astype(jnp.float32) + came).astype(jnp.bfloat16)
    for target, flat in ((to_k, mixed_grad), (to_v, q_ref)):
        job = pool.add(target, 0, 0)
        gradient_into(job, entry, flat)
        pump()
        add_transposed(flat, weights.take(), total)
        pump()
    norm_back_rows(resid_in, gain, total, resid, gain_sums, 1)
    load = pltpu.make_async_copy(x0, dq_ref, local.at[0])
    load.start()
    cast_rows(resid, low, 0.5)
    load.wait()
    gain = gains[pl.ds(0, 1), :]
    norm_rows(dq_ref, gain, entry)
    buffers = (entry, low, mixed_grad, q_ref, total)
    module_back(pool, weights, saved, buffers, chunks, (to_in, to_out), True)
    norm_back_rows(dq_ref, gain, total, resid, gain_sums, 0)
    cast_rows(resid, low)
    store = pltpu.make_async_copy(low, grad_x, local.at[1])
    store.start()
    pool.drain()
    store.wait()


def reduce_greet():
    deep, across, _, twin = neighbours()
    span = lax.axis_size("seq")
    seq = lax.axis_index("seq")
    greet(deep + [across, twin] + [{"seq": (seq + steps) % span} for steps in range(1, span)])


def back(cot, resids, saved, kept, table, gains, taps, weights, rows):
    joined, summed, u1, u0 = saved
    query, keys, values, mixed = kept
    c_in, c_out, a_out, qkv, second_in, second_out, w_in, w_out = weights
    clips, ext, width = keys.shape
    groups = lax.axis_size("group")
    part = width // groups
    chunks = w_out.shape[0] // width
    count = 7 + 4 * chunks
    first = lax.axis_index("seq").astype(jnp.int32)[None] * rows
    limit = rows * lax.axis_size("seq")
    hbm = pl.BlockSpec(memory_space=pl.ANY)
    vmem = pl.BlockSpec(memory_space=pltpu.VMEM)
    low = lambda *shape: jax.ShapeDtypeStruct(shape, jnp.bfloat16)
    wide = lambda *shape: jax.ShapeDtypeStruct(shape, jnp.float32)
    holds = [pltpu.VMEM((rows + more, width), jnp.float32) for more in (0, 32, 0)]
    holds += [pltpu.VMEM((rows, width), jnp.bfloat16)] * 5
    holds += [pltpu.VMEM((clips, ext, width), jnp.bfloat16)] * 4
    holds += [
        pltpu.VMEM((2, clips, LEFT, width), jnp.bfloat16),
        pltpu.VMEM((2, clips, 2 * RIGHT, width), jnp.bfloat16),
        pltpu.VMEM((clips, ext, LANES), jnp.float32),
        pltpu.VMEM((clips, ext, LANES), jnp.float32),
        pltpu.VMEM((3, width, width), jnp.bfloat16),
        pltpu.SemaphoreType.DMA((6,)),
        pltpu.SemaphoreType.DMA((3, groups)),
        pltpu.SemaphoreType.DMA((2, groups)),
        pltpu.SemaphoreType.DMA((2, 5)),
    ]
    grad_out = low(chunks * part, width)
    grad_in = low(part, chunks * width)
    by_chunk = lambda weight: weight.reshape(groups, chunks, part, width)
    results = pl.pallas_call(
        functools.partial(back_kernel, (count, clips, rows, limit)),
        in_specs=[pl.BlockSpec(memory_space=pltpu.SMEM)] + [vmem] * 3 + [hbm] * 22,
        out_specs=[hbm] + [vmem] * 3 + [hbm] * 11,
        out_shape=[low(rows, width), wide(8, width), wide(SPAN, LANES), wide(32, width)]
        + [grad_out, grad_in, low(part, width), low(part, 2 * width)]
        + [low(part, width)] * 4
        + [grad_out, grad_in, low(count, groups // 2, 2, part, width)],
        scratch_shapes=holds + Pool.scratch(part, width, count),
        compiler_params=pltpu.CompilerParams(
            collective_id=3, has_side_effects=True, vmem_limit_bytes=63 << 20
        ),
        name="back",
    )(
        first,
        wide_table(table),
        gains,
        taps,
        cot,
        *resids,
        u1,
        u0,
        joined,
        summed,
        mixed,
        query.reshape(rows, width),
        keys,
        values,
        c_in,
        c_out,
        a_out,
        qkv,
        second_in,
        by_chunk(second_out),
        w_in,
        by_chunk(w_out),
    )
    grad_x, gain_sums, dt, tap_sums = results[:4]
    dt = (dt[:WIN, :HEAD_DIM] + dt[:WIN, HEAD_DIM:]) * HEAD_DIM**-0.5
    return grad_x, gain_sums, dt, tap_sums, results[4:]


def unmix(grad, groups):
    rows, width = grad.shape
    chunks = width // (rows * groups)
    return grad.reshape(rows, chunks, groups, rows).transpose(0, 2, 1, 3).reshape(rows, width)


def feed_forward(resid, gain, w_in, w_out):
    normed, normal, inverse = norm_forward(resid, gain)
    entry = normed.astype(jnp.bfloat16)
    hidden_pre = matmul(entry, w_in)
    hidden = (hidden_pre * jax.nn.sigmoid(hidden_pre)).astype(jnp.bfloat16)
    return (matmul(hidden, w_out), (normal, inverse, entry, hidden_pre, hidden))


def feed_back(grad_branch, kept, gain, w_in, w_out):
    normal, inverse, entry, hidden_pre, hidden = kept
    grad_low = grad_branch.astype(jnp.bfloat16)
    grad_w_out = matmul_left_t(hidden, grad_low).astype(jnp.bfloat16)
    grad_hidden = (matmul_right_t(grad_low, w_out) * swish_grad(hidden_pre)).astype(jnp.bfloat16)
    grad_w_in = matmul_left_t(entry, grad_hidden).astype(jnp.bfloat16)
    grad_in, grad_gain = norm_backward(matmul_right_t(grad_hidden, w_in), normal, inverse, gain)
    return (grad_in, grad_gain, grad_w_in, grad_w_out)


def attention_forward(resid, gain, qkv, attn_out, table, shape):
    clips, rows, width = shape
    normed, normal, inverse = norm_forward(resid, gain)
    entry = normed.astype(jnp.bfloat16)
    query, keys, values = [
        matmul(entry, qkv[part]).astype(jnp.bfloat16).reshape(shape) for part in range(3)
    ]
    tail = jnp.zeros((clips, BACK_PAD - RIGHT, width), jnp.bfloat16)

    def extend(value):
        before = from_behind(value[:, rows - LEFT :], "seq", 1)
        after = from_behind(value[:, :RIGHT], "seq", -1)
        return jnp.concatenate([before, value, after, tail], 1)

    keys, values = (extend(keys), extend(values))
    mixed = attend(query, keys, values, table, rows).reshape(clips * rows, width)
    return (matmul(mixed, attn_out), (normal, inverse, entry, query, keys, values, mixed))


def attention_back(grad_branch, kept, gain, qkv, attn_out, table, shape):
    clips, rows, width = shape
    normal, inverse, entry, query, keys, values, mixed = kept
    grad_low = grad_branch.astype(jnp.bfloat16)
    grad_attn_out = matmul_left_t(mixed, grad_low).astype(jnp.bfloat16)
    grad_mixed = matmul_right_t(grad_low, attn_out).astype(jnp.bfloat16).reshape(shape)
    grad_query, grad_keys, grad_values, grad_table = attend_back(
        query, keys, values, table, grad_mixed, rows
    )

    def fold(grad):
        from_later = from_behind(grad[:, :LEFT], "seq", -1).astype(jnp.float32)
        from_earlier = from_behind(grad[:, LEFT + rows : LEFT + rows + RIGHT], "seq", 1)
        own = grad[:, LEFT : LEFT + rows].astype(jnp.float32)
        own = own + jnp.pad(from_later, ((0, 0), (rows - LEFT, 0), (0, 0)))
        own = own + jnp.pad(from_earlier.astype(jnp.float32), ((0, 0), (0, rows - RIGHT), (0, 0)))
        return own.astype(jnp.bfloat16).reshape(clips * rows, width)

    parts = [grad_query.reshape(clips * rows, width), fold(grad_keys), fold(grad_values)]
    grad_qkv = [matmul_left_t(entry, part).astype(jnp.bfloat16) for part in parts]
    grad_entry = sum(matmul_right_t(part, qkv[at]) for at, part in enumerate(parts))
    grad_in, grad_gain = norm_backward(grad_entry, normal, inverse, gain)
    return (grad_in, grad_gain, grad_qkv, grad_attn_out, grad_table)


def conv_forward(resid, gain_in, gain_mid, conv_in, depthwise, conv_out, shape):
    clips, rows, width = shape
    normed, normal, inverse = norm_forward(resid, gain_in)
    entry = normed.astype(jnp.bfloat16)
    joined = matmul(entry, conv_in)
    opened = jax.nn.sigmoid(joined[:, width:])
    glu = (joined[:, :width] * opened).astype(jnp.bfloat16).reshape(clips, rows, width)
    before = from_behind(glu[:, rows - (KERNEL - 1) :], "seq", 1)
    padded = jnp.concatenate([before, glu], 1).astype(jnp.float32)
    taps = depthwise.astype(jnp.float32)
    summed = jnp.zeros((clips, rows, width), jnp.float32)
    for tap in range(KERNEL):
        summed = summed + taps[tap] * padded[:, tap : tap + rows]
    middle, mid_normal, mid_inverse = norm_forward(summed.reshape(clips * rows, width), gain_mid)
    swished = (middle * jax.nn.sigmoid(middle)).astype(jnp.bfloat16)
    kept = (
        normal,
        inverse,
        entry,
        joined,
        opened,
        padded,
        middle,
        mid_normal,
        mid_inverse,
        swished,
    )
    return (matmul(swished, conv_out), summed.reshape(clips * rows, width), kept)


def conv_back(grad_branch, kept, gain_in, gain_mid, conv_in, depthwise, conv_out, shape):
    clips, rows, width = shape
    normal, inverse, entry, joined, opened, padded, middle, mid_normal, mid_inverse, swished = kept
    taps = depthwise.astype(jnp.float32)
    grad_low = grad_branch.astype(jnp.bfloat16)
    grad_conv_out = matmul_left_t(swished, grad_low).astype(jnp.bfloat16)
    grad_middle = matmul_right_t(grad_low, conv_out) * swish_grad(middle)
    grad_summed, grad_gain_mid = norm_backward(grad_middle, mid_normal, mid_inverse, gain_mid)
    grad_summed = grad_summed.reshape(clips, rows, width)
    grad_taps = jnp.stack(
        [jnp.sum(grad_summed * padded[:, tap : tap + rows], (0, 1)) for tap in range(KERNEL)]
    )
    grad_padded = jnp.zeros((clips, rows + KERNEL - 1, width), jnp.float32)
    for tap in range(KERNEL):
        grad_padded = grad_padded + jnp.pad(
            grad_summed * taps[tap], ((0, 0), (tap, KERNEL - 1 - tap), (0, 0))
        )
    from_later = from_behind(grad_padded[:, : KERNEL - 1].astype(jnp.bfloat16), "seq", -1).astype(
        jnp.float32
    )
    grad_glu = (
        grad_padded[:, KERNEL - 1 :]
        .at[:, rows - (KERNEL - 1) :]
        .add(from_later)
        .reshape(clips * rows, width)
    )
    value_part = joined[:, :width]
    grad_joined = jnp.concatenate(
        [grad_glu * opened, grad_glu * value_part * opened * (1.0 - opened)], 1
    )
    grad_joined = grad_joined.astype(jnp.bfloat16)
    grad_conv_in = matmul_left_t(entry, grad_joined).astype(jnp.bfloat16)
    grad_in, grad_gain_in = norm_backward(
        matmul_right_t(grad_joined, conv_in), normal, inverse, gain_in
    )
    return (grad_in, grad_gain_in, grad_gain_mid, grad_conv_in, grad_taps, grad_conv_out)


def on_device(
    tokens,
    ffn_in,
    ffn_out,
    qkv,
    attn_out,
    conv_in,
    conv_out,
    depthwise,
    gains,
    rel_table,
    cotangent,
):
    clips, rows, width = tokens.shape
    shape = (clips, rows, width)
    flat_rows = clips * rows
    halve = lax.axis_size("seq") == 2
    norms, taps = (gains.shape[0], depthwise.shape[0])
    lines = -(-(norms + taps) // 16) * 16
    small = jnp.concatenate([gains, depthwise], 0)
    small = jnp.pad(small, ((0, lines - norms - taps), (0, 0)))[None]
    shards = (small, ffn_in, ffn_out, qkv, attn_out[None], conv_in[None], conv_out[None])
    sources = (
        (0, 0, 1),
        (1, 0, 1),
        (2, 0, 1),
        (3, 0, 3),
        (4, 0, 1),
        (5, 0, 1),
        (6, 0, 1),
        (1, 1, 1),
        (2, 1, 1),
    )
    quick = halve and clips == 1 and gains.shape[1] % LANES == 0
    if quick:
        flat = tokens.reshape(flat_rows, width)
        gathered, saved = forward(flat, shards, sources, norms, rel_table, halve)
    else:
        gathered = gather_weights(shards, sources, halve)
    small = gathered[0].reshape(-1, lines, gains.shape[1]).transpose(1, 0, 2).reshape(lines, width)
    gain_f = small[:norms].astype(jnp.float32)
    depth = small[norms : norms + taps]
    f_in = (gathered[1][0], gathered[7][0])
    f_out = (gathered[2][0], gathered[8][0])
    proj, a_out, c_in, c_out = (gathered[3], gathered[4][0], gathered[5][0], gathered[6][0])
    if quick:
        result, squares, x1, x2, x3, x4, u0, u1, query, keys, values, mixed, joined, summed = saved
        squares = jnp.sum(squares[:5], 1)
        grad, gain_sums, grad_table, grad_taps, shares = back(
            cotangent.reshape(flat_rows, width),
            (x4, x3, x2, x1, flat),
            (joined, summed, u1, u0),
            (query, keys, values, mixed),
            rel_table,
            small[:8].astype(jnp.float32),
            jnp.pad(depth.astype(jnp.float32), ((0, 32 - taps), (0, 0))),
            (c_in, c_out, a_out, proj, f_in[1], f_out[1], f_in[0], f_out[0]),
            rows,
        )
        gain_grads = gain_sums[:norms]
        grad_taps = grad_taps[:taps]
        groups = lax.axis_size("group")
        grad_in_first, grad_in_second = (unmix(shares[9], groups), unmix(shares[1], groups))
        grad_out_first, grad_out_second = (shares[8], shares[0])
        grad_conv_out, grad_conv_in, grad_attn_out = shares[2:5]
        grad_qkv = shares[5:8]
    else:
        start = tokens.reshape(flat_rows, width).astype(jnp.float32)
        first_branch, first_kept = feed_forward(start, gain_f[0], f_in[0], f_out[0])
        after_first = start + 0.5 * first_branch
        attn_branch, attn_kept = attention_forward(
            after_first, gain_f[1], proj, a_out, rel_table, shape
        )
        after_attn = after_first + attn_branch
        conv_branch, summed, conv_kept = conv_forward(
            after_attn, gain_f[2], gain_f[3], c_in, depth, c_out, shape
        )
        after_conv = after_attn + conv_branch
        second_branch, second_kept = feed_forward(after_conv, gain_f[4], f_in[1], f_out[1])
        final = after_conv + 0.5 * second_branch
        result, final_normal, final_inverse = norm_forward(final, gain_f[5])
        squares = jnp.stack(
            [
                jnp.sum(member * member)
                for member in (final, first_branch, attn_branch, conv_branch, second_branch)
            ]
        )
        grad = cotangent.reshape(flat_rows, width).astype(jnp.float32)
        grad, grad_gain_final = norm_backward(grad, final_normal, final_inverse, gain_f[5])
        back_in, grad_gain_second, grad_in_second, grad_out_second = feed_back(
            0.5 * grad, second_kept, gain_f[4], f_in[1], f_out[1]
        )
        grad = grad + back_in
        back_in, grad_gain_conv, grad_gain_mid, grad_conv_in, grad_taps, grad_conv_out = conv_back(
            grad, conv_kept, gain_f[2], gain_f[3], c_in, depth, c_out, shape
        )
        grad = grad + back_in
        back_in, grad_gain_attn, grad_qkv, grad_attn_out, grad_table = attention_back(
            grad, attn_kept, gain_f[1], proj, a_out, rel_table, shape
        )
        grad = grad + back_in
        back_in, grad_gain_first, grad_in_first, grad_out_first = feed_back(
            0.5 * grad, first_kept, gain_f[0], f_in[0], f_out[0]
        )
        grad = grad + back_in
        matrices = [grad_in_first, grad_in_second, grad_out_first, grad_out_second]
        matrices += [grad_attn_out, grad_conv_in, grad_conv_out] + grad_qkv
        matrices = [
            lax.psum(lax.psum_scatter(member, "group", tiled=True), ("seq", "replica"))
            for member in matrices
        ]
        grad_in_first, grad_in_second, grad_out_first, grad_out_second = matrices[:4]
        grad_attn_out, grad_conv_in, grad_conv_out = matrices[4:7]
        grad_qkv = matrices[7:]
        gain_grads = jnp.stack(
            [
                grad_gain_first,
                grad_gain_attn,
                grad_gain_conv,
                grad_gain_mid,
                grad_gain_second,
                grad_gain_final,
            ]
        )
    loose = jnp.concatenate([grad_table.reshape(-1), squares])
    lines = -(-loose.shape[0] // width)
    loose = jnp.pad(loose, (0, lines * width - loose.shape[0])).reshape(lines, width)
    totals = butterfly(jnp.concatenate([gain_grads, grad_taps, loose], 0))
    owned = lax.dynamic_slice_in_dim(
        totals[: norms + taps], lax.axis_index("group") * gains.shape[1], gains.shape[1], 1
    )
    loose = totals[norms + taps :].reshape(-1)
    table_size = rel_table.shape[0] * rel_table.shape[1]
    count = (
        flat_rows * width * lax.axis_size("seq") * lax.axis_size("group") * lax.axis_size("replica")
    )
    stats = jnp.sqrt(loose[table_size : table_size + 5] / count)
    return (
        result.astype(jnp.bfloat16).reshape(shape),
        grad.astype(jnp.bfloat16).reshape(shape),
        jnp.stack([grad_in_first, grad_in_second]).astype(jnp.float32),
        jnp.stack([grad_out_first, grad_out_second]).astype(jnp.float32),
        jnp.stack(grad_qkv).astype(jnp.float32),
        grad_attn_out.astype(jnp.float32),
        grad_conv_in.astype(jnp.float32),
        grad_conv_out.astype(jnp.float32),
        owned[norms:],
        owned[:norms],
        loose[:table_size].reshape(rel_table.shape),
        stats,
    )


def solution(mesh):
    in_specs = (
        P(("group", "replica"), "seq", None),
        P(None, "group", None),
        P(None, "group", None),
        P(None, "group", None),
        P("group", None),
        P("group", None),
        P("group", None),
        P(None, "group"),
        P(None, "group"),
        P(),
        P(("group", "replica"), "seq", None),
    )
    out_specs = (
        P(("group", "replica"), "seq", None),
        P(("group", "replica"), "seq", None),
        P(None, "group", None),
        P(None, "group", None),
        P(None, "group", None),
        P("group", None),
        P("group", None),
        P("group", None),
        P(None, "group"),
        P(None, "group"),
        P(),
        P(),
    )
    return jax.shard_map(
        on_device, mesh=mesh, in_specs=in_specs, out_specs=out_specs, check_vma=False
    )
```

```python
import functools

import jax
import jax.numpy as jnp
from jax import lax
from jax.experimental import pallas as pl
from jax.experimental.pallas import tpu as pltpu
from jax.sharding import PartitionSpec as P

HEAD_DIM = 64
KERNEL = 31
LEFT = 64
RIGHT = 8
WIN = 73
LANES = 128
BLOCK = 128
SPAN = 256
BACK_PAD = 64


EPSILON = 1e-05
NEGATIVE = -1e30


MESH = pl.DeviceIdType.MESH


def from_behind(value, axis, steps):
    count = lax.axis_size(axis)
    initial, last = (max(0, -steps), min(count, count - steps))
    return lax.ppermute(value, axis, [(source, source + steps) for source in range(initial, last)])


def norm_forward(values, gain):
    centered = values - jnp.mean(values, -1, keepdims=True)
    inverse = lax.rsqrt(jnp.mean(centered * centered, -1, keepdims=True) + EPSILON)
    normal = centered * inverse
    return (normal * gain, normal, inverse)


def norm_backward(grad_out, normal, inverse, gain):
    grad_normal = grad_out * gain
    grad_in = inverse * (
        grad_normal
        - jnp.mean(grad_normal, -1, keepdims=True)
        - normal * jnp.mean(grad_normal * normal, -1, keepdims=True)
    )
    grad_gain = jnp.sum(grad_out * normal, 0)
    return (grad_in, grad_gain)


def matmul(left, right):
    return jnp.dot(left, right, preferred_element_type=jnp.float32)


def matmul_left_t(left, right):
    return lax.dot_general(
        left, right, (((0,), (0,)), ((), ())), preferred_element_type=jnp.float32
    )


def matmul_right_t(left, right):
    return lax.dot_general(
        left, right, (((1,), (1,)), ((), ())), preferred_element_type=jnp.float32
    )


def swish_grad(values):
    logistic = jax.nn.sigmoid(values)
    return logistic + values * logistic * (1.0 - logistic)


def nt(left,right):
    return lax.dot_general(left,right,(((1,),(1,)),((),())),preferred_element_type=jnp.float32)
def tn(left,right):
    return lax.dot_general(left,right,(((0,),(0,)),((),())),preferred_element_type=jnp.float32)
def nn(left,right):
    return jnp.dot(left,right,preferred_element_type=jnp.float32)

def block_mask(first, block, limit, lines=BLOCK):
    rows=lax.broadcasted_iota(jnp.int32,(lines,SPAN),0)%BLOCK
    cols=lax.broadcasted_iota(jnp.int32,(lines,SPAN),1)
    offset=cols-rows
    place=first+block*BLOCK+cols-LEFT
    return (offset>=0)&(offset<WIN)&(place>=0)&(place<limit)

def head_lanes(head):
    lanes=lax.broadcasted_iota(jnp.int32,(BLOCK,LANES),1)
    return (lanes>=head*HEAD_DIM)&(lanes<(head+1)*HEAD_DIM)

def block_probs(query, keys, table, mask):
    relative=pltpu.roll(nt(query,table),0,1,stride=1,stride_axis=0)
    raw=jnp.where(mask,(nt(query,keys)+relative)*(HEAD_DIM**-0.5),NEGATIVE)
    expo=jnp.exp(raw-jnp.max(raw,-1,keepdims=True))
    return expo*(1.0/jnp.sum(expo,-1,keepdims=True))

def attend_kernel(limit, first_ref, q_ref, k_ref, v_ref, t_ref, c_ref):
    table=t_ref[...]
    zero=jnp.zeros((BLOCK,LANES),jnp.bfloat16)
    for block in range(q_ref.shape[1]//BLOCK):
        rows=pl.ds(block*BLOCK,BLOCK); span=pl.ds(block*BLOCK,SPAN)
        query=q_ref[0,rows,:]; keys=k_ref[0,span,:]; values=v_ref[0,span,:]
        mask=block_mask(first_ref[0],block,limit)
        mixed=[]
        for head in range(2):
            probs=block_probs(jnp.where(head_lanes(head),query,zero),keys,table,mask)
            mixed.append(nn(probs.astype(jnp.bfloat16),values))
        c_ref[0,rows,:]=jnp.where(head_lanes(0),mixed[0],mixed[1]).astype(jnp.bfloat16)

def attend_back_kernel(limit, first_ref, q_ref, k_ref, v_ref, t_ref, g_ref, dq_ref, dk_ref, dv_ref, dt_ref, dk_sum, dv_sum):
    table=t_ref[...]
    zero=jnp.zeros((BLOCK,LANES),jnp.bfloat16)
    flip=(lax.broadcasted_iota(jnp.int32,(BLOCK,BLOCK),0)+lax.broadcasted_iota(jnp.int32,(BLOCK,BLOCK),1)==BLOCK-1).astype(jnp.float32).astype(jnp.bfloat16)
    dk_sum[...]=jnp.zeros_like(dk_sum); dv_sum[...]=jnp.zeros_like(dv_sum)
    @pl.when((pl.program_id(0)==0)&(pl.program_id(1)==0))
    def _(): dt_ref[...]=jnp.zeros_like(dt_ref)
    for block in range(q_ref.shape[1]//BLOCK):
        rows=pl.ds(block*BLOCK,BLOCK); span=pl.ds(block*BLOCK,SPAN)
        keys=k_ref[0,span,:]; values=v_ref[0,span,:]
        mask=block_mask(first_ref[0],block,limit)
        grad_query=[]
        for head in range(2):
            query=jnp.where(head_lanes(head),q_ref[0,rows,:],zero)
            grad=jnp.where(head_lanes(head),g_ref[0,rows,:],zero)
            probs=block_probs(query,keys,table,mask)
            grad_probs=nt(grad,values)
            grad_raw=probs*(grad_probs-jnp.sum(probs*grad_probs,-1,keepdims=True))
            grad_raw=grad_raw.astype(jnp.bfloat16)
            turned=pltpu.roll(nn(flip,grad_raw),SPAN-BLOCK+1,1,stride=1,stride_axis=0)
            unskewed=nn(flip,turned.astype(jnp.bfloat16)).astype(jnp.bfloat16)
            dv_sum[span,:]+=tn(probs.astype(jnp.bfloat16),grad)
            dk_sum[span,:]+=tn(grad_raw,query)
            dt_ref[...]+=tn(unskewed,query)
            grad_query.append(nn(grad_raw,keys)+nn(unskewed,table))
        dq_ref[0,rows,:]=(jnp.where(head_lanes(0),grad_query[0],grad_query[1])*(HEAD_DIM**-0.5)).astype(jnp.bfloat16)
    dk_ref[0]=(dk_sum[...]*(HEAD_DIM**-0.5)).astype(jnp.bfloat16)
    dv_ref[0]=dv_sum[...].astype(jnp.bfloat16)

def wide_table(table):
    return jnp.tile(jnp.pad(table,((0,SPAN-table.shape[0]),(0,0))),(1,LANES//HEAD_DIM))

def specs(clips,rows,width):
    own=pl.BlockSpec((1,rows,LANES),lambda c,h:(c,0,h))
    ext=pl.BlockSpec((1,rows+LEFT+BACK_PAD,LANES),lambda c,h:(c,0,h))
    tab=pl.BlockSpec((SPAN,LANES),lambda c,h:(0,0))
    return (pl.BlockSpec(memory_space=pltpu.SMEM),own,ext,tab),(clips,width//LANES)

def attend(query,keys,values,table,rows):
    clips,_,width=query.shape
    first=lax.axis_index('seq').astype(jnp.int32)[None]*rows
    limit=rows*lax.axis_size('seq')
    (sc,own,ext,tab),grid=specs(clips,rows,width)
    return pl.pallas_call(functools.partial(attend_kernel,limit),grid=grid,
        in_specs=[sc,own,ext,ext,tab],out_specs=own,
        out_shape=jax.ShapeDtypeStruct(query.shape,jnp.bfloat16),name="attend",
    )(first,query,keys,values,wide_table(table))

def attend_back(query,keys,values,table,grad,rows):
    clips,_,width=query.shape
    first=lax.axis_index('seq').astype(jnp.int32)[None]*rows
    limit=rows*lax.axis_size('seq')
    (sc,own,ext,tab),grid=specs(clips,rows,width)
    dq,dk,dv,dt=pl.pallas_call(functools.partial(attend_back_kernel,limit),grid=grid,
        in_specs=[sc,own,ext,ext,tab,own],out_specs=[own,ext,ext,tab],
        out_shape=[jax.ShapeDtypeStruct(query.shape,jnp.bfloat16),jax.ShapeDtypeStruct(keys.shape,jnp.bfloat16),jax.ShapeDtypeStruct(keys.shape,jnp.bfloat16),jax.ShapeDtypeStruct((SPAN,LANES),jnp.float32)],
        scratch_shapes=[pltpu.VMEM((rows+LEFT+BACK_PAD,LANES),jnp.float32)]*2,name="attend_back",
    )(first,query,keys,values,wide_table(table),grad)
    return dq,dk,dv,(dt[:WIN,:HEAD_DIM]+dt[:WIN,HEAD_DIM:])*(HEAD_DIM**-0.5)
def depth_of():
    return lax.axis_size("group") // 2


def place():
    group = lax.axis_index("group")
    return (group // 2, group % 2, lax.axis_index("seq"), lax.axis_index("replica"))


def greet(peers):
    barrier = pltpu.get_barrier_semaphore()
    for peer in peers:
        pl.semaphore_signal(barrier, inc=1, device_id=peer, device_id_type=MESH)
    pl.semaphore_wait(barrier, len(peers))


def neighbours():
    z, x, seq, replica = place()
    depth = depth_of()
    deep = [{"group": (z + steps) % depth * 2 + x} for steps in range(1, depth)]
    across = {"group": z * 2 + 1 - x}
    beside = {"seq": 1 - seq}
    twin = {"replica": 1 - replica}
    return (deep, across, beside, twin)


class Gather:
    def __init__(self, source, target, cut, low, left, rows, size, sends, recvs, at):
        depth = depth_of()
        self.source, self.target, self.cut, self.low, self.rows = (source, target, cut, low, rows)
        self.piece = size[0] // (1, 2, 4)[cut]
        self.columns = pl.ds(left, size[1])
        self.sends, self.recvs, self.at = (sends, recvs, at)
        self.z, self.x, self.seq, self.replica = place()
        self.deep, self.across, self.beside, self.twin = neighbours()
        self.depth = depth
        self.firsts = (0, depth - 1, 2 * depth - 1, 4 * depth - 2)
        self.started = []

    def spot(self, ref, owner, dy, dc):
        part = 0
        if self.cut:
            part = (self.replica + dc) % 2
        if self.cut == 2:
            part = part + 2 * ((self.seq + dy) % 2)
        first = pl.multiple_of(owner * self.rows + self.low + part * self.piece, self.piece)
        return ref.at[pl.ds(first, self.piece), self.columns]

    def owner(self, steps, dx):
        return (self.z + self.depth - steps) % self.depth * 2 + (self.x + dx) % 2

    def copy(self, steps, dx, dy, dc, kind, index, peer):
        mine = steps == 0 and dx == 0
        slot = self.at + self.firsts[kind] + index
        spot = self.spot(self.target, self.owner(steps, dx), dy, dc)
        return pltpu.make_async_remote_copy(
            src_ref=self.spot(self.source, 0, dy, dc) if mine else spot,
            dst_ref=spot,
            send_sem=self.sends.at[slot],
            recv_sem=self.recvs.at[slot],
            device_id=peer,
            device_id_type=MESH,
        )

    def send(self, copy):
        copy.start()
        self.started.append(copy)

    def to_beside(self, steps, dx):
        if self.cut == 2:
            index = dx * self.depth + steps - 1
            self.send(self.copy(steps, dx, 0, 0, 2, index, self.beside))

    def to_twin(self, steps, dx, dy):
        if self.cut:
            index = dy * (2 * self.depth - 1) + dx * self.depth + steps - 1
            self.send(self.copy(steps, dx, dy, 0, 3, index, self.twin))

    def open(self):
        for steps, peer in enumerate(self.deep, 1):
            self.send(self.copy(0, 0, 0, 0, 0, steps - 1, peer))
        self.send(self.copy(0, 0, 0, 0, 1, 0, self.across))

    def got(self, steps, dx, dy, dc, kind, index):
        self.copy(steps or self.depth, dx, dy, dc, kind, index, self.twin).wait_recv()

    def forward_deep(self):
        for steps in range(1, self.depth):
            self.got(steps, 0, 0, 0, 0, steps - 1)
            self.send(self.copy(steps, 0, 0, 0, 1, steps, self.across))
            self.to_beside(steps, 0)
            self.to_twin(steps, 0, 0)

    def forward_across(self):
        for steps in range(self.depth):
            self.got(steps, 1, 0, 0, 1, steps)
            self.to_beside(steps, 1)
            self.to_twin(steps, 1, 0)

    def others(self):
        return [(steps, dx) for dx in range(2) for steps in range(self.depth) if steps or dx]

    def forward_beside(self):
        if self.cut == 2:
            for steps, dx in self.others():
                self.got(steps, dx, 1, 0, 2, dx * self.depth + steps - 1)
                self.to_twin(steps, dx, 1)

    def close(self):
        if self.cut:
            for dy in range(self.cut):
                for steps, dx in self.others():
                    index = dy * (2 * self.depth - 1) + dx * self.depth + steps - 1
                    self.got(steps, dx, dy, 1, 3, index)
        for copy in self.started:
            copy.wait_send()


def stack_heads(values):
    zero = jnp.zeros((BLOCK, LANES), jnp.bfloat16)
    return jnp.concatenate([jnp.where(head_lanes(head), values, zero) for head in range(2)], 0)


def roll_halves(values, shift):
    halves = [values[:BLOCK], values[BLOCK:]]
    rolled = [pltpu.roll(half, shift, 1, stride=1, stride_axis=0) for half in halves]
    return jnp.concatenate(rolled, 0)


def stacked_probs(query, keys, table, mask):
    relative = roll_halves(nt(query, table), 0)
    raw = jnp.where(mask, (nt(query, keys) + relative) * HEAD_DIM**-0.5, NEGATIVE)
    expo = jnp.exp(raw - jnp.max(raw, -1, keepdims=True))
    return expo * (1.0 / jnp.sum(expo, -1, keepdims=True))


class Ticker:
    def __init__(self, jobs, numbers, stores, loads):
        self.jobs, self.numbers, self.stores, self.loads = (jobs, numbers, stores, loads)
        self.tick, self.stored, self.loaded = (0, set(), set())

    def advance(self):
        names = ("open", "forward_deep", "forward_across", "forward_beside", "close")
        if self.tick >= len(self.jobs) + 8:
            return
        for lag, name in enumerate(names):
            if 0 <= self.tick - 2 * lag < len(self.jobs):
                getattr(self.jobs[self.tick - 2 * lag], name)()
        if self.tick < len(self.stores):
            source, store = self.stores[self.tick]
            if source not in self.loaded:
                self.loads[source].wait()
                self.loaded.add(source)
            store.start()
        self.tick += 1

    def until(self, number):
        last = max(at for at, owner in enumerate(self.numbers) if owner == number)
        while self.tick <= max(last + 8, number):
            self.advance()
        if number not in self.stored:
            self.stores[number][1].wait()
            self.stored.add(number)

    def finish(self):
        while self.tick < len(self.jobs) + 8:
            self.advance()
        for number in range(len(self.stores)):
            self.until(number)


def gather_ticker(plan, sources, ins, outs, helds, sems):
    sends, recvs, local = sems
    deep, across, beside, twin = neighbours()
    peers = deep + [across, twin]
    if any(member[-1] == 2 for member in plan):
        peers.append(beside)
    greet(peers)
    loads = [
        pltpu.make_async_copy(ins[at], held, local.at[0, at]) for at, held in enumerate(helds)
    ]
    for load in loads:
        load.start()
    jobs, at = ([], 0)
    for number, layer, low, left, size, cut in plan:
        source, first = sources[number]
        ref = ins[source].at[first + layer]
        rows = ins[source].shape[1]
        target = outs[number].at[layer]
        jobs.append(Gather(ref, target, cut, low, left, rows, size, sends, recvs, at))
        at += (2, 6, 8)[cut] * depth_of()
    z, x, _, _ = place()
    stores = []
    for number, (source, first) in enumerate(sources):
        rows = ins[source].shape[1]
        start = pl.multiple_of((z * 2 + x) * rows, rows)
        store = pltpu.make_async_copy(
            helds[source].at[pl.ds(first, outs[number].shape[0])],
            outs[number].at[:, pl.ds(start, rows)],
            local.at[1, number],
        )
        stores.append((source, store))
    return Ticker(jobs, [member[0] for member in plan], stores, loads)


def gather_kernel(plan, sources, count, *refs):
    ins, outs = (refs[:count], refs[count : count + len(sources)])
    ticker = gather_ticker(
        plan, sources, ins, outs, refs[count + len(sources) : -3], refs[-3:]
    )
    ticker.finish()


def product_rows(left, right, target, size=256):
    def body(cols):
        target[:, cols] = nn(left[...], right[:, cols]).astype(target.dtype)

    row_blocks(right.shape[1], size, body)


def join_rows(resid, branch, scale, squares, line):
    squares[pl.ds(line, 1), :] = jnp.zeros_like(squares[pl.ds(line, 1), :])

    def body(rows):
        value = branch[rows, :]
        resid[rows, :] += scale * value
        squares[pl.ds(line, 1), :] += jnp.sum(value * value, 0, keepdims=True)

    row_blocks(resid.shape[0], 64, body)


def module_forward(ticker, weights, entry, hidden, total, helds, saved, sems, ready):
    width = total.shape[1]
    chunks = hidden.shape[0]
    stores = []
    for chunk in range(chunks):
        before = helds[chunk % 2]
        if chunk > 1:
            stores[chunk - 2].wait()
        w_in = weights[0].take()

        def body(cols):
            value = nn(entry[...], w_in[:, cols])
            before[:, cols] = value.astype(jnp.bfloat16)
            hidden[chunk, :, cols] = (value * jax.nn.sigmoid(value)).astype(jnp.bfloat16)

        row_blocks(width, 256, body)
        target = saved.at[:, pl.ds(chunk * width, width)]
        stores.append(fetch(before, target, sems.at[chunk]))
        if ready == 2 or chunk % 2:
            ticker.advance()
    total[...] = jnp.zeros_like(total)
    ticker.until(ready)
    weights = weights[1]()
    for chunk in range(chunks):
        w_out = weights.take()

        def gather(cols):
            total[:, cols] += nn(hidden[chunk], w_out[:, cols])

        row_blocks(width, 256, gather)
        if chunk % 2:
            ticker.advance()
    for store in stores[-2:]:
        store.wait()


def depthwise_rows(glu, taps, skip, target, ticker):
    total, width = target.shape
    for column in range(width // LANES):
        lanes = pl.ds(column * LANES, LANES)

        def body(at, carry):
            first = pl.multiple_of(at * LANES, LANES)
            window = glu[pl.ds(first, LANES + 32), lanes]
            summed = jnp.zeros((LANES, LANES), jnp.float32)
            for tap in range(KERNEL):
                moved = window[tap + 2 : tap + 2 + LANES]
                summed = summed + moved * taps[pl.ds(skip + tap, 1), lanes]
            target[pl.ds(first, LANES), lanes] = summed
            return carry

        lax.fori_loop(0, total // LANES, body, 0)
        if column % 4 == 3:
            ticker.advance()


def swish_rows(source, gain, target):
    def body(rows):
        normal, _ = norm_parts(source[rows, :])
        middle = normal * gain
        target[rows, :] = (middle * jax.nn.sigmoid(middle)).astype(jnp.bfloat16)

    row_blocks(source.shape[0], 64, body)


def forward_kernel(settings, *refs):
    plan, sources, count, norms, rows, limit = settings
    first_ref, table_ref, tokens = refs[:3]
    ins, refs = (refs[3 : 3 + count], refs[3 + count :])
    outs, refs = (refs[: len(sources)], refs[len(sources) :])
    out, squares, x1, x2, x3, x4, u0, u1, q_out, k_out, v_out, mixed_out, joined, summed = refs[:14]
    helds, refs = (refs[14 : 14 + count], refs[14 + count :])
    resid, total, glu, low_gains, gains, entry, hidden, held_a, held_b, q_ref = refs[:10]
    k_ref, v_ref, mixed, slots = refs[10:14]
    local, slot_sems, saved_sems, halo_sems = refs[14:18]
    ticker = gather_ticker(plan, sources, ins, outs, helds, refs[18:])
    width = resid.shape[1]
    chunks = u0.shape[1] // width
    groups = lax.axis_size("group")
    part = width // groups
    lines = low_gains.shape[0]
    load = fetch(tokens, entry, local.at[0])
    spaces = [slots.at[at] for at in range(3)]

    def stream(*weights):
        return Stream(spaces, slot_sems, [lambda slot, ref=ref: [(ref, slot)] for ref in weights])

    def module_streams(w_in, w_out):
        heres = [pl.ds(chunk * width, width) for chunk in range(chunks)]
        first = stream(*[w_in.at[0, :, here] for here in heres])
        return (first, lambda: stream(*[w_out.at[0, here] for here in heres]))

    for _ in range(5):
        ticker.advance()
    ticker.until(0)
    small = [
        fetch(
            outs[0].at[0, pl.ds(group * lines, lines)],
            low_gains.at[:, pl.ds(group * part, part)],
            slot_sems.at[0, group],
        )
        for group in range(groups)
    ]
    for copy in small:
        copy.wait()
    gains[...] = low_gains[...].astype(jnp.float32)
    load.wait()

    def widen(at):
        resid[at, :] = entry[at, :].astype(jnp.float32)

    row_blocks(rows, 64, widen)
    norm_rows(resid, gains[pl.ds(0, 1), :], entry)
    ticker.until(1)
    pair = (held_a, held_b)
    weights = module_streams(outs[1], outs[2])
    module_forward(ticker, weights, entry, hidden, total, pair, u0, saved_sems, 2)
    join_rows(resid, total, 0.5, squares, 1)
    stored = fetch(resid, x1, local.at[0])
    norm_rows(resid, gains[pl.ds(1, 1), :], entry)
    ticker.until(3)
    weights = stream(*[outs[3].at[at] for at in range(3)])
    own = pl.ds(LEFT, rows)
    spare = BACK_PAD - 2 * RIGHT
    for ref in (k_ref, v_ref):
        ref[0, pl.ds(LEFT + rows + 2 * RIGHT, spare), :] = jnp.zeros((spare, width), jnp.bfloat16)
    product_rows(entry, weights.take(), q_ref)
    product_rows(entry, weights.take(), k_ref.at[0, own])
    product_rows(entry, weights.take(), v_ref.at[0, own])
    _, _, seq, _ = place()
    span = lax.axis_size("seq")
    edges = []
    for at, ref in enumerate((k_ref, v_ref)):
        for way, (source, target, size, step) in enumerate(
            ((rows, 0, LEFT, 1), (LEFT, LEFT + rows, 2 * RIGHT, span - 1))
        ):
            edges.append(
                pltpu.make_async_remote_copy(
                    src_ref=ref.at[0, pl.ds(source, size)],
                    dst_ref=ref.at[0, pl.ds(target, size)],
                    send_sem=halo_sems.at[0, 2 * at + way],
                    recv_sem=halo_sems.at[1, 2 * at + way],
                    device_id={"seq": (seq + step) % span},
                    device_id_type=MESH,
                )
            )
    for edge in edges:
        edge.start()
    ticker.advance()
    for edge in edges:
        edge.wait()
    table = table_ref[...]
    for pair_at in range(width // LANES):
        lanes = pl.ds(pair_at * LANES, LANES)

        def attend_block(block, carry):
            here = pl.ds(pl.multiple_of(block * BLOCK, BLOCK), BLOCK)
            near = pl.ds(pl.multiple_of(block * BLOCK, BLOCK), SPAN)
            key, value = (k_ref[0, near, lanes], v_ref[0, near, lanes])
            mask = block_mask(first_ref[0], block, limit, 2 * BLOCK)
            probs = stacked_probs(stack_heads(q_ref[here, lanes]), key, table, mask)
            both = nn(probs.astype(jnp.bfloat16), value)
            both = jnp.where(head_lanes(0), both[:BLOCK], both[BLOCK:])
            mixed[here, lanes] = both.astype(jnp.bfloat16)
            return carry

        lax.fori_loop(0, rows // BLOCK, attend_block, 0)
        if pair_at % 2:
            ticker.advance()
    keeps = [
        fetch(source, target, local.at[1 + at])
        for at, (source, target) in enumerate(
            ((q_ref, q_out), (k_ref, k_out), (v_ref, v_out), (mixed, mixed_out))
        )
    ]
    ticker.until(4)
    ticker.advance()
    product_rows(mixed, stream(outs[4].at[0]).take(), total)
    stored.wait()
    join_rows(resid, total, 1.0, squares, 2)
    stored = fetch(resid, x2, local.at[0])
    norm_rows(resid, gains[pl.ds(2, 1), :], entry)
    ticker.until(5)
    weights = stream(*[outs[5].at[0, :, pl.ds(at * width, width)] for at in range(2)])
    value_part, gate_part = (weights.take(), weights.take())

    def open_columns(cols):
        value = nn(entry[...], value_part[:, cols])
        gate = nn(entry[...], gate_part[:, cols])
        held_a[:, cols] = value.astype(jnp.bfloat16)
        held_b[:, cols] = gate.astype(jnp.bfloat16)
        opened = (value * jax.nn.sigmoid(gate)).astype(jnp.bfloat16)
        glu[pl.ds(32, rows), cols] = opened.astype(jnp.float32)

    ticker.advance()
    row_blocks(width, 256, open_columns)
    halo = pltpu.make_async_remote_copy(
        src_ref=glu.at[pl.ds(rows, 32)],
        dst_ref=glu.at[pl.ds(0, 32)],
        send_sem=halo_sems.at[0, 4],
        recv_sem=halo_sems.at[1, 4],
        device_id={"seq": (seq + 1) % span},
        device_id_type=MESH,
    )
    halo.start()
    keeps += [
        fetch(held, joined.at[:, pl.ds(at * width, width)], local.at[5 + at])
        for at, held in enumerate(pair)
    ]
    ticker.advance()
    halo.wait()
    ahead = pl.ds(0, 32)
    glu[ahead, :] = jnp.where(seq > 0, glu[ahead, :], jnp.zeros((32, width), jnp.float32))
    depthwise_rows(glu, gains, norms, total, ticker)
    kept = fetch(total, summed, local.at[7])
    swish_rows(total, gains[pl.ds(3, 1), :], entry)
    ticker.until(6)
    ticker.advance()
    conv = glu.at[pl.ds(0, rows)]
    product_rows(entry, stream(outs[6].at[0]).take(), conv)
    stored.wait()
    join_rows(resid, conv, 1.0, squares, 3)
    stored = fetch(resid, x3, local.at[0])
    norm_rows(resid, gains[pl.ds(4, 1), :], entry)
    kept.wait()
    for keep in keeps:
        keep.wait()
    ticker.until(7)
    weights = module_streams(outs[7], outs[8])
    module_forward(ticker, weights, entry, hidden, total, pair, u1, saved_sems, 8)
    stored.wait()
    join_rows(resid, total, 0.5, squares, 4)
    stored = fetch(resid, x4, local.at[0])
    squares[pl.ds(0, 1), :] = jnp.zeros((1, width), jnp.float32)

    def tally(at):
        squares[pl.ds(0, 1), :] += jnp.sum(resid[at, :] * resid[at, :], 0, keepdims=True)

    row_blocks(rows, 64, tally)
    norm_rows(resid, gains[pl.ds(5, 1), :], entry)
    last = fetch(entry, out, local.at[1])
    ticker.finish()
    stored.wait()
    last.wait()


def gather_plan(shards, sources, halve):
    groups = lax.axis_size("group")
    width = shards[1].shape[1] * groups
    part = width // groups
    plan = [(0, 0, 0, 0, shards[0].shape[1:], 0)]
    for number, (source, first, layers) in enumerate(sources):
        for layer in range(layers if source else 0):
            for low in range(0, shards[source].shape[1], part):
                for left in range(0, shards[source].shape[2], width):
                    cut = 2 if halve and len(plan) % 3 else 1
                    plan.append((number, layer, low, left, (part, width), cut))
    return plan


def gather_outputs(shards, sources):
    groups = lax.axis_size("group")
    return [
        jax.ShapeDtypeStruct(
            (layers, groups * shards[source].shape[1], shards[source].shape[2]), jnp.bfloat16
        )
        for source, _, layers in sources
    ]


def gather_scratch(plan, sources):
    total = sum((2, 6, 8)[member[-1]] * depth_of() for member in plan)
    return [
        pltpu.SemaphoreType.DMA((total,)),
        pltpu.SemaphoreType.DMA((total,)),
        pltpu.SemaphoreType.DMA((2, len(sources))),
    ]


def gather_weights(shards, sources, halve):
    plan = gather_plan(shards, sources, halve)
    return pl.pallas_call(
        functools.partial(
            gather_kernel, plan, [(source, first) for source, first, _ in sources], len(shards)
        ),
        in_specs=[pl.BlockSpec(memory_space=pl.ANY)] * len(shards),
        out_specs=[pl.BlockSpec(memory_space=pl.ANY)] * len(sources),
        out_shape=gather_outputs(shards, sources),
        scratch_shapes=[pltpu.VMEM(shard.shape, jnp.bfloat16) for shard in shards]
        + gather_scratch(plan, sources),
        compiler_params=pltpu.CompilerParams(
            collective_id=1, has_side_effects=True, vmem_limit_bytes=24 << 20
        ),
        name="gather_weights",
    )(*shards)


def forward(tokens, shards, sources, norms, table, halve):
    rows, width = tokens.shape
    plan = gather_plan(shards, sources, halve)
    groups = lax.axis_size("group")
    first = lax.axis_index("seq").astype(jnp.int32)[None] * rows
    limit = rows * lax.axis_size("seq")
    ext = rows + LEFT + BACK_PAD
    inner = shards[1].shape[2]
    lines = shards[0].shape[1]
    hbm = pl.BlockSpec(memory_space=pl.ANY)
    vmem = pl.BlockSpec(memory_space=pltpu.VMEM)
    low = lambda *shape: jax.ShapeDtypeStruct(shape, jnp.bfloat16)
    wide = lambda *shape: jax.ShapeDtypeStruct(shape, jnp.float32)
    settings = (plan, [member[:2] for member in sources], len(shards), norms, rows, limit)
    results = pl.pallas_call(
        functools.partial(forward_kernel, settings),
        in_specs=[pl.BlockSpec(memory_space=pltpu.SMEM), vmem] + [hbm] * (1 + len(shards)),
        out_specs=[hbm] * len(sources) + [hbm, vmem] + [hbm] * 12,
        out_shape=gather_outputs(shards, sources)
        + [low(rows, width), wide(8, width)]
        + [wide(rows, width)] * 4
        + [low(rows, inner)] * 2
        + [low(rows, width), low(1, ext, width), low(1, ext, width), low(rows, width)]
        + [low(rows, 2 * width), wide(rows, width)],
        scratch_shapes=[pltpu.VMEM(shard.shape, jnp.bfloat16) for shard in shards]
        + [
            pltpu.VMEM((rows, width), jnp.float32),
            pltpu.VMEM((rows, width), jnp.float32),
            pltpu.VMEM((rows + 32, width), jnp.float32),
            pltpu.VMEM((lines, width), jnp.bfloat16),
            pltpu.VMEM((lines, width), jnp.float32),
        ]
        + [
            pltpu.VMEM((rows, width), jnp.bfloat16),
            pltpu.VMEM((inner // width, rows, width), jnp.bfloat16),
        ]
        + [pltpu.VMEM((rows, width), jnp.bfloat16)] * 3
        + [
            pltpu.VMEM((1, ext, width), jnp.bfloat16),
            pltpu.VMEM((1, ext, width), jnp.bfloat16),
            pltpu.VMEM((rows, width), jnp.bfloat16),
            pltpu.VMEM((3, width, width), jnp.bfloat16),
            pltpu.SemaphoreType.DMA((8,)),
            pltpu.SemaphoreType.DMA((3, groups)),
            pltpu.SemaphoreType.DMA((inner // width,)),
            pltpu.SemaphoreType.DMA((2, 5)),
        ]
        + gather_scratch(plan, sources),
        compiler_params=pltpu.CompilerParams(
            collective_id=5, has_side_effects=True, vmem_limit_bytes=56 << 20
        ),
        name="forward",
    )(first, wide_table(table), tokens, *shards)
    return results[: len(sources)], results[len(sources) :]


def swap(value, axis, bit=1):
    return lax.ppermute(value, axis, [(i, i ^ bit) for i in range(lax.axis_size(axis))])


def butterfly(value):
    for axis in ("replica", "seq", "group"):
        bit = 1
        while bit < lax.axis_size(axis):
            value = value + swap(value, axis, bit)
            bit *= 2
    return value


def add_slabs(count, target, *sources):
    def body(at, carry):
        total = sources[0](at)[...].astype(jnp.float32)
        for source in sources[1:]:
            total = total + source(at)[...].astype(jnp.float32)
        target(at)[...] = total.astype(jnp.bfloat16)
        return carry

    lax.fori_loop(0, count, body, 0)


class Reduce:
    def __init__(self, pool, number, target, low, left):
        self.pool, self.number = (pool, number)
        self.target, self.low, self.left = (target, low, left)
        self.source = pool.kept.at[number]
        self.stage = pool.stage.at[number % 2]
        self.kept = False
        self.depth, self.width = (depth_of(), pool.width)
        self.half, self.unit = (pool.rows // 2, pool.rows // 8)
        self.started = []
        self.stages = [
            self.exchange_twin,
            self.exchange_seq,
            self.exchange_across,
            self.exchange_deep,
            self.settle,
            self.hand_over,
            self.close,
        ]
        self.done_stages = 0
        slot = number % pool.ring
        self.own, self.came = (pool.own.at[slot], pool.came.at[slot])
        self.from_x, self.from_seq = (pool.from_x.at[slot], pool.from_seq.at[slot])
        self.from_z, self.shared = (pool.from_z.at[number], pool.shared.at[number])
        self.alone = pool.finished.at[slot, pl.ds(0, self.unit)]
        self.joint = pool.finished.at[slot, pl.ds(self.unit, 2 * self.unit)]

    def locate(self):
        self.z, self.x, self.seq, self.replica = place()
        self.deep, self.across, self.beside, self.twin = neighbours()

    def rows(self, first, count):
        return pl.ds(pl.multiple_of(first, self.unit), count * self.unit)

    def near(self):
        return self.rows(self.seq * self.unit, 3)

    def lone(self):
        return self.rows(3 * self.unit * self.seq, 1)

    def far(self):
        return self.rows(3 * self.unit * (1 - self.seq), 1)

    def both(self):
        return pl.ds(self.unit, 2 * self.unit)

    def side(self, replica):
        return pl.ds(pl.multiple_of(replica * self.half, self.half), self.half)

    def remote(self, source, target, slot, peer):
        return pltpu.make_async_remote_copy(
            src_ref=source,
            dst_ref=target,
            send_sem=self.pool.sends.at[self.number, slot],
            recv_sem=self.pool.recvs.at[self.number, slot],
            device_id=peer,
            device_id_type=MESH,
        )

    def send(self, ends, slot, peer):
        make = lambda peer: self.remote(*ends(), slot, peer)
        make(peer).start()
        self.started.append(make)

    def wait(self, target, slot):
        self.remote(target, target, slot, self.twin).wait_recv()

    def keep(self):
        return pltpu.make_async_copy(self.stage, self.source, self.pool.local.at[self.number, 0])

    def await_kept(self):
        if not self.kept:
            self.keep().wait()
            self.kept = True

    def load(self):
        source = self.source.at[:, :, self.side(self.replica)]
        return pltpu.make_async_copy(source, self.own, self.pool.local.at[self.number, 1])

    def credit(self, kind):
        if self.number >= self.pool.ring:
            pl.semaphore_wait(self.pool.credits.at[kind], 1)

    def release(self, kind, peer):
        if self.number + self.pool.ring < self.pool.total:
            pl.semaphore_signal(
                self.pool.credits.at[kind], inc=1, device_id=peer, device_id_type=MESH
            )

    def exchange_twin(self):
        self.await_kept()
        self.credit(0)
        self.load().start()
        ends = lambda: (self.source.at[:, :, self.side(1 - self.replica)], self.came)
        self.send(ends, 0, self.twin)

    def exchange_seq(self):
        self.load().wait()
        self.wait(self.came, 0)
        far = self.far()
        own = lambda at: self.own.at[at // 2, at % 2, far]
        add_slabs(2 * self.depth, own, own, lambda at: self.came.at[at // 2, at % 2, far])
        self.credit(1)
        self.send(lambda: (self.own.at[:, :, self.far()], self.from_seq), 1, self.beside)

    def gather(self, x, arrived):
        both, lone = (self.both(), self.lone())
        refs = [self.own.at[:, x], self.came.at[:, x]]
        pick = lambda rows: [lambda at, ref=ref: ref.at[at, rows] for ref in refs]
        shared, alone = (pick(both), pick(lone))
        alone.append(lambda at: self.from_seq.at[at, x])
        if arrived:
            both_here = self.rows(self.unit * (1 - self.seq), 2)
            lone_here = self.rows(2 * self.unit * self.seq, 1)
            shared.append(lambda at: self.from_x.at[at, both_here])
            alone.append(lambda at: self.from_x.at[at, lone_here])
        add_slabs(self.depth, shared[0], *shared)
        add_slabs(self.depth, alone[0], *alone)

    def exchange_across(self):
        self.wait(self.from_seq, 1)
        self.gather(1 - self.x, False)
        self.credit(2)
        self.send(lambda: (self.own.at[:, 1 - self.x, self.near()], self.from_x), 2, self.across)

    def exchange_deep(self):
        self.wait(self.from_x, 2)
        self.gather(self.x, True)
        for steps, peer in enumerate(self.deep, 1):
            ends = lambda steps=steps: (
                self.own.at[(self.z + steps) % self.depth, self.x, self.near()],
                self.from_z.at[steps - 1],
            )
            self.send(ends, 2 + steps, peer)
        self.release(0, self.twin)
        self.release(1, self.beside)
        self.release(2, self.across)

    def settle(self):
        for steps in range(1, self.depth):
            self.wait(self.from_z.at[steps - 1], 2 + steps)
        self.flush()
        both_here = self.rows(self.unit * (1 - self.seq), 2)
        lone_here = self.rows(2 * self.unit * self.seq, 1)
        for target, own, here in (
            (self.shared.at[self.seq], self.both(), both_here),
            (self.alone, self.lone(), lone_here),
        ):
            sources = [lambda at, own=own: self.own.at[self.z, self.x, own]]
            sources += [
                lambda at, steps=steps, here=here: self.from_z.at[steps, here]
                for steps in range(self.depth - 1)
            ]
            add_slabs(1, lambda at, target=target: target, *sources)
        self.last = 2 + self.depth
        ends = lambda: (self.shared.at[self.seq], self.shared.at[self.seq])
        self.send(ends, self.last, self.beside)
        self.store(0).start()
        self.send(lambda: (self.alone, self.spot(self.lone_out())), self.last + 1, self.beside)
        self.send(lambda: (self.alone, self.spot(self.lone_out())), self.last + 2, self.twin)

    def spot(self, first, count=1):
        return self.target.at[self.rows(first, count), pl.ds(self.left, self.width)]

    def lone_out(self, dy=0, dc=0):
        seq = self.seq if dy == 0 else 1 - self.seq
        replica = self.replica if dc == 0 else 1 - self.replica
        return self.low + replica * self.half + 3 * self.unit * seq

    def both_out(self, dc=0):
        replica = self.replica if dc == 0 else 1 - self.replica
        return self.low + replica * self.half + self.unit

    def store(self, kind):
        source = self.joint if kind else self.alone
        target = self.spot(self.both_out(), 2) if kind else self.spot(self.lone_out())
        return pltpu.make_async_copy(source, target, self.pool.local.at[self.number, 2 + kind])

    def hand_over(self):
        self.wait(self.spot(self.lone_out(1)), self.last + 1)
        spot = lambda: self.spot(self.lone_out(1))
        self.send(lambda: (spot(), spot()), self.last + 3, self.twin)
        self.wait(self.shared.at[1 - self.seq], self.last)
        sources = [lambda at, turn=turn: self.shared.at[turn] for turn in range(2)]
        add_slabs(1, lambda at: self.joint, *sources)
        self.store(1).start()
        self.send(lambda: (self.joint, self.spot(self.both_out(), 2)), self.last + 4, self.twin)

    def close(self):
        self.wait(self.spot(self.lone_out(0, 1)), self.last + 2)
        self.wait(self.spot(self.lone_out(1, 1)), self.last + 3)
        self.wait(self.spot(self.both_out(1), 2), self.last + 4)
        self.store(0).wait()
        self.store(1).wait()
        self.flush()

    def flush(self):
        for make in self.started:
            make(self.twin).wait_send()
        self.started = []

    def step(self):
        self.locate()
        self.stages[self.done_stages]()
        self.done_stages += 1


class Pool:
    ring = 7

    def __init__(self, rows, width, total, kept, refs):
        self.rows, self.width, self.total, self.kept = (rows, width, total, kept)
        names = list(Pool.shapes(rows, width, total))
        for name, ref in zip(names, refs):
            setattr(self, name, ref)
        self.sends, self.recvs, self.local, self.credits = refs[len(names) :]
        self.jobs = []

    @staticmethod
    def shapes(rows, width, total):
        depth, ring = (depth_of(), Pool.ring)
        unit = rows // 8
        return {
            "own": (ring, depth, 2, rows // 2, width),
            "came": (ring, depth, 2, rows // 2, width),
            "from_x": (ring, depth, 3 * unit, width),
            "from_seq": (ring, depth, 2, unit, width),
            "from_z": (total, depth - 1, 3 * unit, width),
            "shared": (total, 2, 2 * unit, width),
            "finished": (ring, 3 * unit, width),
            "stage": (2, depth, 2, rows, width),
        }

    @staticmethod
    def scratch(rows, width, total):
        slots = 7 + depth_of()
        return [pltpu.VMEM(shape, jnp.bfloat16) for shape in Pool.shapes(rows, width, total).values()] + [
            pltpu.SemaphoreType.DMA((total, slots)),
            pltpu.SemaphoreType.DMA((total, slots)),
            pltpu.SemaphoreType.DMA((total, 4)),
            pltpu.SemaphoreType.REGULAR((3,)),
        ]

    def add(self, target, low, left):
        number = len(self.jobs)
        if number >= 2:
            self.jobs[number - 2].await_kept()
        job = Reduce(self, number, target, low, left)
        self.jobs.append(job)
        return job

    def free(self, number):
        return number < self.ring or self.jobs[number - self.ring].done_stages >= 5

    def pump(self):
        active = [job for job in self.jobs if 0 < job.done_stages < 7]
        fresh = [job for job in self.jobs if job.done_stages == 0][:1]
        for job in fresh:
            if self.free(job.number):
                job.step()
        for job in reversed(active):
            job.step()

    def drain(self):
        while any(job.done_stages < 7 for job in self.jobs):
            self.pump()


def row_blocks(total, size, body):
    def step(at, carry):
        body(pl.ds(pl.multiple_of(at * size, size), size))
        return carry

    lax.fori_loop(0, total // size, step, 0)


def norm_parts(values):
    centered = values - jnp.mean(values, -1, keepdims=True)
    inverse = lax.rsqrt(jnp.mean(centered * centered, -1, keepdims=True) + EPSILON)
    return (centered * inverse, inverse)


def norm_rows(source, gain, target):
    def body(rows):
        normal, _ = norm_parts(source[rows, :].astype(jnp.float32))
        target[rows, :] = (normal * gain).astype(target.dtype)

    row_blocks(source.shape[0], 64, body)


def norm_back_rows(source, gain, grads, resid, sums, line):
    sums[pl.ds(line, 1), :] = jnp.zeros_like(sums[pl.ds(line, 1), :])

    def body(rows):
        normal, inverse = norm_parts(source[rows, :].astype(jnp.float32))
        grad = grads[rows, :]
        grad_normal = grad * gain
        resid[rows, :] += inverse * (
            grad_normal
            - jnp.mean(grad_normal, -1, keepdims=True)
            - normal * jnp.mean(grad_normal * normal, -1, keepdims=True)
        )
        sums[pl.ds(line, 1), :] += jnp.sum(grad * normal, 0, keepdims=True)

    row_blocks(source.shape[0], 64, body)


def cast_rows(source, target, scale=1.0):
    def body(rows):
        target[rows, :] = (source[rows, :] * scale).astype(jnp.bfloat16)

    row_blocks(source.shape[0], 64, body)


def transposed_rows(left, right, target, size=256):
    def body(cols):
        target[:, cols] = nt(left[...], right[cols, :]).astype(target.dtype)

    row_blocks(right.shape[0], size, body)


def add_transposed(left, right, target, size=256):
    def body(cols):
        target[:, cols] += nt(left[...], right[cols, :])

    row_blocks(right.shape[0], size, body)


def gradient_into(job, left, right):
    depth, _, rows, width = job.stage.shape

    def step(z, carry):
        cols = pl.ds(pl.multiple_of(z * 2 * rows, 2 * rows), 2 * rows)
        value = tn(left[:, cols], right[...]).astype(jnp.bfloat16)
        job.stage[z, 0] = value[:rows]
        job.stage[z, 1] = value[rows:]
        return carry

    lax.fori_loop(0, depth, step, 0)
    job.keep().start()


class Stream:
    def __init__(self, buffers, sems, copies):
        self.buffers, self.sems, self.copies = (buffers, sems, copies)
        self.issued = self.taken = 0
        for _ in range(len(buffers) - 1):
            self.issue()

    def parts(self, number):
        slot = number % len(self.buffers)
        made = self.copies[number](self.buffers[slot])
        return [
            pltpu.make_async_copy(source, target, self.sems.at[slot, at])
            for at, (source, target) in enumerate(made)
        ]

    def issue(self):
        if self.issued < len(self.copies):
            for copy in self.parts(self.issued):
                copy.start()
            self.issued += 1

    def take(self):
        for copy in self.parts(self.taken):
            copy.wait()
        self.taken += 1
        self.issue()
        return self.buffers[(self.taken - 1) % len(self.buffers)]


def module_copies(w_in, w_out, groups):
    chunks = w_out.shape[1]
    rows = w_out.shape[2]
    copies = []
    for chunk in range(chunks):
        copies.append(
            lambda slot, chunk=chunk: [
                (w_out.at[group, chunk], slot.at[pl.ds(group * rows, rows)])
                for group in range(groups)
            ]
        )
        copies.append(
            lambda slot, chunk=chunk: [
                (
                    w_in.at[:, pl.ds((group * chunks + chunk) * rows, rows)],
                    slot.at[:, pl.ds(group * rows, rows)],
                )
                for group in range(groups)
            ]
        )
    return copies


def saved_copies(saved, groups, rows):
    chunks = saved.shape[1] // (groups * rows)
    return [
        lambda slot, chunk=chunk: [
            (
                saved.at[:, pl.ds((group * chunks + chunk) * rows, rows)],
                slot.at[:, pl.ds(group * rows, rows)],
            )
            for group in range(groups)
        ]
        for chunk in range(chunks)
    ]


def module_back(pool, weights, saved, buffers, chunks, outs, often):
    pump = pool.pump
    entry, low, hidden, grad_hidden, total = buffers
    grad_in, grad_out = outs
    width = total.shape[1]
    total[...] = jnp.zeros_like(total)
    for chunk in range(chunks):
        before = saved.take()
        w_out = weights.take()

        def body(cols):
            value = before[:, cols].astype(jnp.float32)
            logistic = jax.nn.sigmoid(value)
            hidden[:, cols] = (value * logistic).astype(jnp.bfloat16)
            slope = logistic * (1.0 + value * (1.0 - logistic))
            grad = nt(low[...], w_out[cols, :]) * slope
            grad_hidden[:, cols] = grad.astype(jnp.bfloat16)

        row_blocks(width, 256, body)
        job = pool.add(grad_out, chunk * pool.rows, 0)
        gradient_into(job, hidden, low)
        job = pool.add(grad_in, 0, chunk * width)
        gradient_into(job, entry, grad_hidden)
        if often:
            pump()
        add_transposed(grad_hidden, weights.take(), total)
        if often or chunk % 2:
            pump()
def middle_rows(source, gain, grads, entry, sums, line):
    sums[pl.ds(line, 1), :] = jnp.zeros_like(sums[pl.ds(line, 1), :])

    def body(rows):
        normal, inverse = norm_parts(source[rows, :])
        middle = normal * gain
        logistic = jax.nn.sigmoid(middle)
        entry[rows, :] = (middle * logistic).astype(jnp.bfloat16)
        grad = grads[rows, :] * (logistic + middle * logistic * (1.0 - logistic))
        grad_normal = grad * gain
        grads[rows, :] = inverse * (
            grad_normal
            - jnp.mean(grad_normal, -1, keepdims=True)
            - normal * jnp.mean(grad_normal * normal, -1, keepdims=True)
        )
        sums[pl.ds(line, 1), :] += jnp.sum(grad * normal, 0, keepdims=True)

    row_blocks(source.shape[0], 64, body)


def depthwise_back(grads, taps, value, gate, grad_value, grad_gate, tap_sums, pump):
    total, width = value.shape
    tap_sums[...] = jnp.zeros_like(tap_sums)
    for column in range(width // LANES):
        lanes = pl.ds(column * LANES, LANES)

        def body(at, carry):
            first = pl.multiple_of(at * LANES, LANES)
            rows = pl.ds(first, LANES)
            held = value[rows, lanes].astype(jnp.float32)
            opened = jax.nn.sigmoid(gate[rows, lanes].astype(jnp.float32))
            glu = (held * opened).astype(jnp.bfloat16).astype(jnp.float32)
            grad = jnp.zeros((LANES, LANES), jnp.float32)
            window = grads[pl.ds(first, LANES + 32), lanes]
            for tap in range(KERNEL):
                ahead = KERNEL - 1 - tap
                moved = window[ahead : ahead + LANES]
                grad = grad + moved * taps[pl.ds(tap, 1), lanes]
                tap_sums[pl.ds(tap, 1), lanes] += jnp.sum(glu * moved, 0, keepdims=True)
            grad_value[rows, lanes] = (grad * opened).astype(jnp.bfloat16)
            grad_gate[rows, lanes] = (grad * held * opened * (1.0 - opened)).astype(jnp.bfloat16)
            return carry

        lax.fori_loop(0, total // LANES, body, 0)
        if column % 4 == 3:
            pump()


def fetch(source, target, sem):
    copy = pltpu.make_async_copy(source, target, sem)
    copy.start()
    return copy


def back_kernel(settings, *refs):
    count, clips, rows, limit = settings
    first_ref, table_ref, gains, taps, squares = refs[:5]
    refs = refs[1:]
    cot, x4, x3, x2, x1, x0, u1, u0, joined, summed = refs[4:14]
    mixed, query, keys, values, c_in, c_out, a_out, qkv = refs[14:22]
    second_in, second_out, w_in, w_out = refs[22:26]
    grad_x, tally = refs[26:28]
    refs = refs[:26] + (None, None) + refs[26:]
    to_second_out, to_second_in, to_conv_out, to_conv_in = refs[30:34]
    to_attn, to_q, to_k, to_v, to_out, to_in, kept = refs[34:41]
    refs = refs[41:]
    resid, total_ext, resid_in, low, entry, mixed_grad, q_ref, dq_ref = refs[:8]
    k_ref, v_ref, dk_ref, dv_ref, later, earlier, dk_sum, dv_sum, slots = refs[8:17]
    local, slot_sems, saved_sems, halo_sems, arrivals, tally_sems, dt_ref = refs[17:24]
    gain_sums, tap_sums = (tally.at[pl.ds(0, 8)], tally.at[pl.ds(8, 32)])
    width = resid.shape[1]
    total = total_ext.at[pl.ds(0, rows)]
    groups = lax.axis_size("group")
    part = width // groups
    span = lax.axis_size("seq")
    chunks = w_out.shape[1]
    reduce_greet()
    pool = Pool(part, width, count, kept, refs[24:])
    pump = pool.pump
    copies = module_copies(second_in, second_out, groups)
    copies += [lambda slot: [(c_out, slot)]]
    copies += [
        lambda slot, at=at: [(c_in.at[:, pl.ds(at * width, width)], slot)] for at in range(2)
    ]
    copies += [lambda slot: [(a_out, slot)]]
    copies += [lambda slot, at=at: [(qkv.at[at], slot)] for at in range(3)]
    copies += module_copies(w_in, w_out, groups)
    load = fetch(x4, resid_in, local.at[0])
    arrival = fetch(cot, low, local.at[1])
    weights = Stream([slots.at[at] for at in range(3)], slot_sems, copies)
    free = [ref.at[0, pl.ds(0, rows)] for ref in (k_ref, v_ref)]
    saved = Stream(free, saved_sems, saved_copies(u1, groups, part))
    halves = [ref.at[0, pl.ds(0, rows)] for ref in (dk_ref, dv_ref)]
    opening = [
        fetch(joined.at[:, pl.ds(at * width, width)], half, local.at[2 + at])
        for at, half in enumerate(halves)
    ]
    resid[...] = jnp.zeros_like(resid)
    arrival.wait()
    load.wait()

    def widen(at):
        total[at, :] = low[at, :].astype(jnp.float32)

    row_blocks(rows, 64, widen)
    norm_back_rows(resid_in, gains[pl.ds(5, 1), :], total, resid, gain_sums, 5)
    load = fetch(x3, resid_in, local.at[0])
    cast_rows(resid, low, 0.5)
    load.wait()
    norm_rows(resid_in, gains[pl.ds(4, 1), :], entry)
    buffers = (entry, low, mixed_grad, q_ref, total)
    module_back(
        pool, weights, saved, buffers, chunks, (to_second_in, to_second_out), False
    )
    norm_back_rows(resid_in, gains[pl.ds(4, 1), :], total, resid, gain_sums, 4)
    load = fetch(summed, resid_in, local.at[0])
    cast_rows(resid, low)
    transposed_rows(low, weights.take(), total)
    load.wait()
    middle_rows(resid_in, gains[pl.ds(3, 1), :], total, entry, gain_sums, 3)
    _, _, seq, _ = place()
    halo = pltpu.make_async_remote_copy(
        src_ref=total_ext.at[pl.ds(0, 32)],
        dst_ref=total_ext.at[pl.ds(rows, 32)],
        send_sem=halo_sems.at[0, 4],
        recv_sem=halo_sems.at[1, 4],
        device_id={"seq": (seq + span - 1) % span},
        device_id_type=MESH,
    )
    halo.start()
    load = fetch(x2, resid_in, local.at[0])
    job = pool.add(to_conv_out, 0, 0)
    gradient_into(job, entry, low)
    pump()
    for copy in opening:
        copy.wait()
    load.wait()
    norm_rows(resid_in, gains[pl.ds(2, 1), :], entry)
    halo.wait()
    beyond = pl.ds(rows, 32)
    nothing = jnp.zeros((32, width), jnp.float32)
    total_ext[beyond, :] = jnp.where(seq < span - 1, total_ext[beyond, :], nothing)
    depthwise_back(total_ext, taps, *halves, mixed_grad, q_ref, tap_sums, pump)
    total[...] = jnp.zeros_like(total)
    for at, flat in enumerate((mixed_grad, q_ref)):
        job = pool.add(to_conv_in, 0, at * width)
        gradient_into(job, entry, flat)
        add_transposed(flat, weights.take(), total)
        pump()
    norm_back_rows(resid_in, gains[pl.ds(2, 1), :], total, resid, gain_sums, 2)
    loads = [
        fetch(source, target, local.at[at])
        for at, (source, target) in enumerate(
            ((mixed, entry), (query, q_ref), (keys, k_ref), (values, v_ref), (x1, resid_in))
        )
    ]
    cast_rows(resid, low)
    transposed_rows(low, weights.take(), mixed_grad)
    loads[0].wait()
    job = pool.add(to_attn, 0, 0)
    gradient_into(job, entry, low)
    pump()
    for load in loads[1:]:
        load.wait()
    table = table_ref[...]
    across = lax.broadcasted_iota(jnp.int32, (2 * BLOCK, 2 * BLOCK), 0)
    across = across + lax.broadcasted_iota(jnp.int32, (2 * BLOCK, 2 * BLOCK), 1)
    flip = (across == 2 * BLOCK - 1).astype(jnp.float32).astype(jnp.bfloat16)
    dt_ref[...] = jnp.zeros_like(dt_ref)
    blocks = rows // BLOCK
    for pair in range(width // LANES):
        lanes = pl.ds(pair * LANES, LANES)
        dk_sum[...] = jnp.zeros_like(dk_sum)
        dv_sum[...] = jnp.zeros_like(dv_sum)

        def attend_block(at, carry):
            clip, block = (at // blocks, at % blocks)
            here = pl.ds(pl.multiple_of(at * BLOCK, BLOCK), BLOCK)
            near = pl.ds(pl.multiple_of(block * BLOCK, BLOCK), SPAN)
            key = k_ref[clip, near, lanes]
            value = v_ref[clip, near, lanes]
            mask = block_mask(first_ref[0], block, limit, 2 * BLOCK)
            q = stack_heads(q_ref[here, lanes])
            g = stack_heads(mixed_grad[here, lanes])
            probs = stacked_probs(q, key, table, mask)
            grad_probs = nt(g, value)
            grad_raw = probs * (grad_probs - jnp.sum(probs * grad_probs, -1, keepdims=True))
            grad_raw = grad_raw.astype(jnp.bfloat16)
            dv_sum[clip, near, :] += tn(probs.astype(jnp.bfloat16), g)
            dk_sum[clip, near, :] += tn(grad_raw, q)
            turned = roll_halves(nn(flip, grad_raw), SPAN - BLOCK + 1).astype(jnp.bfloat16)
            dt_ref[...] += tn(turned, nn(flip, q).astype(jnp.bfloat16))
            relative = nn(turned, table)
            relative = jnp.where(head_lanes(0), relative[BLOCK:], relative[:BLOCK])
            relative = nn(flip[:BLOCK, BLOCK:], relative.astype(jnp.bfloat16))
            direct = nn(grad_raw, key)
            direct = jnp.where(head_lanes(0), direct[:BLOCK], direct[BLOCK:])
            dq_ref[here, lanes] = ((direct + relative) * HEAD_DIM**-0.5).astype(jnp.bfloat16)
            return carry

        lax.fori_loop(0, clips * blocks, attend_block, 0, unroll=2)
        dk_ref[:, :, lanes] = (dk_sum[...] * HEAD_DIM**-0.5).astype(jnp.bfloat16)
        dv_ref[:, :, lanes] = dv_sum[...].astype(jnp.bfloat16)
        pump()

    saved = Stream(free, saved_sems, saved_copies(u0, groups, part))
    edges = []
    for at, ref in enumerate((dk_ref, dv_ref)):
        for way, (target, low_row, size, step) in enumerate(
            ((later, 0, LEFT, span - 1), (earlier, LEFT + rows, 2 * RIGHT, 1))
        ):
            edges.append(
                pltpu.make_async_remote_copy(
                    src_ref=ref.at[:, pl.ds(low_row, size)],
                    dst_ref=target.at[at],
                    send_sem=halo_sems.at[0, 2 * at + way],
                    recv_sem=halo_sems.at[1, 2 * at + way],
                    device_id={"seq": (seq + step) % span},
                    device_id_type=MESH,
                )
            )
    for edge in edges:
        edge.start()
    gain = gains[pl.ds(1, 1), :]
    norm_rows(resid_in, gain, entry)
    job = pool.add(to_q, 0, 0)
    gradient_into(job, entry, dq_ref)
    total[...] = jnp.zeros_like(total)
    add_transposed(dq_ref, weights.take(), total)
    pump()
    for edge in edges:
        edge.wait()
    for at, (ref, flat) in enumerate(((dk_ref, mixed_grad), (dv_ref, q_ref))):
        for clip in range(clips):
            base = clip * rows
            flat[pl.ds(base, rows), :] = ref[clip, pl.ds(LEFT, rows), :]
            tail = pl.ds(base + rows - LEFT, LEFT)
            zero_tail = jnp.zeros((LEFT, width), jnp.float32)
            came = jnp.where(seq < span - 1, later[at, clip].astype(jnp.float32), zero_tail)
            flat[tail, :] = (flat[tail, :].astype(jnp.float32) + came).astype(jnp.bfloat16)
            head = pl.ds(base, 2 * RIGHT)
            zero_head = jnp.zeros((2 * RIGHT, width), jnp.float32)
            came = jnp.where(seq > 0, earlier[at, clip].astype(jnp.float32), zero_head)
            flat[head, :] = (flat[head, :].astype(jnp.float32) + came).astype(jnp.bfloat16)
    for target, flat in ((to_k, mixed_grad), (to_v, q_ref)):
        job = pool.add(target, 0, 0)
        gradient_into(job, entry, flat)
        pump()
        add_transposed(flat, weights.take(), total)
        pump()
    norm_back_rows(resid_in, gain, total, resid, gain_sums, 1)
    load = pltpu.make_async_copy(x0, dq_ref, local.at[0])
    load.start()
    cast_rows(resid, low, 0.5)
    load.wait()
    gain = gains[pl.ds(0, 1), :]
    norm_rows(dq_ref, gain, entry)
    buffers = (entry, low, mixed_grad, q_ref, total)
    module_back(pool, weights, saved, buffers, chunks, (to_in, to_out), True)
    norm_back_rows(dq_ref, gain, total, resid, gain_sums, 0)
    cast_rows(resid, low)
    store = pltpu.make_async_copy(low, grad_x, local.at[1])
    store.start()
    for block in range(10):
        spot = pl.ds(40 + block // 8 * 8, 8)
        tally[spot, pl.ds(block % 8 * LANES, LANES)] = dt_ref[pl.ds(block * 8, 8), :]
    tally[pl.ds(48, 8), pl.ds(2 * LANES, width - 2 * LANES)] = jnp.zeros(
        (8, width - 2 * LANES), jnp.float32
    )
    tally[pl.ds(56, 8), :] = squares[...]
    for turn, peer in enumerate(partners()):
        copy = pltpu.make_async_remote_copy(
            src_ref=tally,
            dst_ref=arrivals.at[turn],
            send_sem=tally_sems.at[0, turn],
            recv_sem=tally_sems.at[1, turn],
            device_id=peer,
            device_id_type=MESH,
        )
        copy.start()
        pool.pump()
        copy.wait()
        tally[...] += arrivals[turn]
    pool.drain()
    store.wait()


def partners():
    group = lax.axis_index("group")
    peers = [{"replica": 1 - lax.axis_index("replica")}, {"seq": 1 - lax.axis_index("seq")}]
    bit = 1
    while bit < lax.axis_size("group"):
        peers.append({"group": group + bit * (1 - 2 * (group // bit % 2))})
        bit *= 2
    return peers


def reduce_greet():
    deep, across, _, twin = neighbours()
    span = lax.axis_size("seq")
    seq = lax.axis_index("seq")
    greet(deep + [across, twin] + [{"seq": (seq + steps) % span} for steps in range(1, span)])


def back(cot, resids, saved, kept, table, gains, taps, squares, weights, rows):
    joined, summed, u1, u0 = saved
    query, keys, values, mixed = kept
    c_in, c_out, a_out, qkv, second_in, second_out, w_in, w_out = weights
    clips, ext, width = keys.shape
    groups = lax.axis_size("group")
    part = width // groups
    chunks = w_out.shape[0] // width
    count = 7 + 4 * chunks
    first = lax.axis_index("seq").astype(jnp.int32)[None] * rows
    limit = rows * lax.axis_size("seq")
    hbm = pl.BlockSpec(memory_space=pl.ANY)
    vmem = pl.BlockSpec(memory_space=pltpu.VMEM)
    low = lambda *shape: jax.ShapeDtypeStruct(shape, jnp.bfloat16)
    wide = lambda *shape: jax.ShapeDtypeStruct(shape, jnp.float32)
    turns = 2 + (groups - 1).bit_length()
    holds = [pltpu.VMEM((rows + more, width), jnp.float32) for more in (0, 32, 0)]
    holds += [pltpu.VMEM((rows, width), jnp.bfloat16)] * 5
    holds += [pltpu.VMEM((clips, ext, width), jnp.bfloat16)] * 4
    holds += [
        pltpu.VMEM((2, clips, LEFT, width), jnp.bfloat16),
        pltpu.VMEM((2, clips, 2 * RIGHT, width), jnp.bfloat16),
        pltpu.VMEM((clips, ext, LANES), jnp.float32),
        pltpu.VMEM((clips, ext, LANES), jnp.float32),
        pltpu.VMEM((3, width, width), jnp.bfloat16),
        pltpu.SemaphoreType.DMA((6,)),
        pltpu.SemaphoreType.DMA((3, groups)),
        pltpu.SemaphoreType.DMA((2, groups)),
        pltpu.SemaphoreType.DMA((2, 5)),
        pltpu.VMEM((turns, 64, width), jnp.float32),
        pltpu.SemaphoreType.DMA((2, turns)),
        pltpu.VMEM((SPAN, LANES), jnp.float32),
    ]
    grad_out = low(chunks * part, width)
    grad_in = low(part, chunks * width)
    by_chunk = lambda weight: weight.reshape(groups, chunks, part, width)
    results = pl.pallas_call(
        functools.partial(back_kernel, (count, clips, rows, limit)),
        in_specs=[pl.BlockSpec(memory_space=pltpu.SMEM)] + [vmem] * 4 + [hbm] * 22,
        out_specs=[hbm, vmem] + [hbm] * 11,
        out_shape=[low(rows, width), wide(64, width)]
        + [grad_out, grad_in, low(part, width), low(part, 2 * width)]
        + [low(part, width)] * 4
        + [grad_out, grad_in, low(count, groups // 2, 2, part, width)],
        scratch_shapes=holds + Pool.scratch(part, width, count),
        compiler_params=pltpu.CompilerParams(
            collective_id=3, has_side_effects=True, vmem_limit_bytes=63 << 20
        ),
        name="back",
    )(
        first,
        wide_table(table),
        gains,
        taps,
        squares,
        cot,
        *resids,
        u1,
        u0,
        joined,
        summed,
        mixed,
        query.reshape(rows, width),
        keys,
        values,
        c_in,
        c_out,
        a_out,
        qkv,
        second_in,
        by_chunk(second_out),
        w_in,
        by_chunk(w_out),
    )
    grad_x, tally = results[:2]
    tables = tally[40:56].reshape(2, 8, width // LANES, LANES).transpose(0, 2, 1, 3)
    dt = tables.reshape(-1, LANES)
    dt = (dt[:WIN, :HEAD_DIM] + dt[:WIN, HEAD_DIM:]) * HEAD_DIM**-0.5
    return grad_x, tally, dt, results[2:]


def unmix(grad, groups):
    rows, width = grad.shape
    chunks = width // (rows * groups)
    return grad.reshape(rows, chunks, groups, rows).transpose(0, 2, 1, 3).reshape(rows, width)


def feed_forward(resid, gain, w_in, w_out):
    normed, normal, inverse = norm_forward(resid, gain)
    entry = normed.astype(jnp.bfloat16)
    hidden_pre = matmul(entry, w_in)
    hidden = (hidden_pre * jax.nn.sigmoid(hidden_pre)).astype(jnp.bfloat16)
    return (matmul(hidden, w_out), (normal, inverse, entry, hidden_pre, hidden))


def feed_back(grad_branch, kept, gain, w_in, w_out):
    normal, inverse, entry, hidden_pre, hidden = kept
    grad_low = grad_branch.astype(jnp.bfloat16)
    grad_w_out = matmul_left_t(hidden, grad_low).astype(jnp.bfloat16)
    grad_hidden = (matmul_right_t(grad_low, w_out) * swish_grad(hidden_pre)).astype(jnp.bfloat16)
    grad_w_in = matmul_left_t(entry, grad_hidden).astype(jnp.bfloat16)
    grad_in, grad_gain = norm_backward(matmul_right_t(grad_hidden, w_in), normal, inverse, gain)
    return (grad_in, grad_gain, grad_w_in, grad_w_out)


def attention_forward(resid, gain, qkv, attn_out, table, shape):
    clips, rows, width = shape
    normed, normal, inverse = norm_forward(resid, gain)
    entry = normed.astype(jnp.bfloat16)
    query, keys, values = [
        matmul(entry, qkv[part]).astype(jnp.bfloat16).reshape(shape) for part in range(3)
    ]
    tail = jnp.zeros((clips, BACK_PAD - RIGHT, width), jnp.bfloat16)

    def extend(value):
        before = from_behind(value[:, rows - LEFT :], "seq", 1)
        after = from_behind(value[:, :RIGHT], "seq", -1)
        return jnp.concatenate([before, value, after, tail], 1)

    keys, values = (extend(keys), extend(values))
    mixed = attend(query, keys, values, table, rows).reshape(clips * rows, width)
    return (matmul(mixed, attn_out), (normal, inverse, entry, query, keys, values, mixed))


def attention_back(grad_branch, kept, gain, qkv, attn_out, table, shape):
    clips, rows, width = shape
    normal, inverse, entry, query, keys, values, mixed = kept
    grad_low = grad_branch.astype(jnp.bfloat16)
    grad_attn_out = matmul_left_t(mixed, grad_low).astype(jnp.bfloat16)
    grad_mixed = matmul_right_t(grad_low, attn_out).astype(jnp.bfloat16).reshape(shape)
    grad_query, grad_keys, grad_values, grad_table = attend_back(
        query, keys, values, table, grad_mixed, rows
    )

    def fold(grad):
        from_later = from_behind(grad[:, :LEFT], "seq", -1).astype(jnp.float32)
        from_earlier = from_behind(grad[:, LEFT + rows : LEFT + rows + RIGHT], "seq", 1)
        own = grad[:, LEFT : LEFT + rows].astype(jnp.float32)
        own = own + jnp.pad(from_later, ((0, 0), (rows - LEFT, 0), (0, 0)))
        own = own + jnp.pad(from_earlier.astype(jnp.float32), ((0, 0), (0, rows - RIGHT), (0, 0)))
        return own.astype(jnp.bfloat16).reshape(clips * rows, width)

    parts = [grad_query.reshape(clips * rows, width), fold(grad_keys), fold(grad_values)]
    grad_qkv = [matmul_left_t(entry, part).astype(jnp.bfloat16) for part in parts]
    grad_entry = sum(matmul_right_t(part, qkv[at]) for at, part in enumerate(parts))
    grad_in, grad_gain = norm_backward(grad_entry, normal, inverse, gain)
    return (grad_in, grad_gain, grad_qkv, grad_attn_out, grad_table)


def conv_forward(resid, gain_in, gain_mid, conv_in, depthwise, conv_out, shape):
    clips, rows, width = shape
    normed, normal, inverse = norm_forward(resid, gain_in)
    entry = normed.astype(jnp.bfloat16)
    joined = matmul(entry, conv_in)
    opened = jax.nn.sigmoid(joined[:, width:])
    glu = (joined[:, :width] * opened).astype(jnp.bfloat16).reshape(clips, rows, width)
    before = from_behind(glu[:, rows - (KERNEL - 1) :], "seq", 1)
    padded = jnp.concatenate([before, glu], 1).astype(jnp.float32)
    taps = depthwise.astype(jnp.float32)
    summed = jnp.zeros((clips, rows, width), jnp.float32)
    for tap in range(KERNEL):
        summed = summed + taps[tap] * padded[:, tap : tap + rows]
    middle, mid_normal, mid_inverse = norm_forward(summed.reshape(clips * rows, width), gain_mid)
    swished = (middle * jax.nn.sigmoid(middle)).astype(jnp.bfloat16)
    kept = (
        normal,
        inverse,
        entry,
        joined,
        opened,
        padded,
        middle,
        mid_normal,
        mid_inverse,
        swished,
    )
    return (matmul(swished, conv_out), summed.reshape(clips * rows, width), kept)


def conv_back(grad_branch, kept, gain_in, gain_mid, conv_in, depthwise, conv_out, shape):
    clips, rows, width = shape
    normal, inverse, entry, joined, opened, padded, middle, mid_normal, mid_inverse, swished = kept
    taps = depthwise.astype(jnp.float32)
    grad_low = grad_branch.astype(jnp.bfloat16)
    grad_conv_out = matmul_left_t(swished, grad_low).astype(jnp.bfloat16)
    grad_middle = matmul_right_t(grad_low, conv_out) * swish_grad(middle)
    grad_summed, grad_gain_mid = norm_backward(grad_middle, mid_normal, mid_inverse, gain_mid)
    grad_summed = grad_summed.reshape(clips, rows, width)
    grad_taps = jnp.stack(
        [jnp.sum(grad_summed * padded[:, tap : tap + rows], (0, 1)) for tap in range(KERNEL)]
    )
    grad_padded = jnp.zeros((clips, rows + KERNEL - 1, width), jnp.float32)
    for tap in range(KERNEL):
        grad_padded = grad_padded + jnp.pad(
            grad_summed * taps[tap], ((0, 0), (tap, KERNEL - 1 - tap), (0, 0))
        )
    from_later = from_behind(grad_padded[:, : KERNEL - 1].astype(jnp.bfloat16), "seq", -1).astype(
        jnp.float32
    )
    grad_glu = (
        grad_padded[:, KERNEL - 1 :]
        .at[:, rows - (KERNEL - 1) :]
        .add(from_later)
        .reshape(clips * rows, width)
    )
    value_part = joined[:, :width]
    grad_joined = jnp.concatenate(
        [grad_glu * opened, grad_glu * value_part * opened * (1.0 - opened)], 1
    )
    grad_joined = grad_joined.astype(jnp.bfloat16)
    grad_conv_in = matmul_left_t(entry, grad_joined).astype(jnp.bfloat16)
    grad_in, grad_gain_in = norm_backward(
        matmul_right_t(grad_joined, conv_in), normal, inverse, gain_in
    )
    return (grad_in, grad_gain_in, grad_gain_mid, grad_conv_in, grad_taps, grad_conv_out)


def on_device(
    tokens,
    ffn_in,
    ffn_out,
    qkv,
    attn_out,
    conv_in,
    conv_out,
    depthwise,
    gains,
    rel_table,
    cotangent,
):
    clips, rows, width = tokens.shape
    shape = (clips, rows, width)
    flat_rows = clips * rows
    halve = lax.axis_size("seq") == 2
    norms, taps = (gains.shape[0], depthwise.shape[0])
    lines = -(-(norms + taps) // 16) * 16
    small = jnp.concatenate([gains, depthwise], 0)
    small = jnp.pad(small, ((0, lines - norms - taps), (0, 0)))[None]
    shards = (small, ffn_in, ffn_out, qkv, attn_out[None], conv_in[None], conv_out[None])
    sources = (
        (0, 0, 1),
        (1, 0, 1),
        (2, 0, 1),
        (3, 0, 3),
        (4, 0, 1),
        (5, 0, 1),
        (6, 0, 1),
        (1, 1, 1),
        (2, 1, 1),
    )
    quick = halve and clips == 1 and gains.shape[1] % LANES == 0
    if quick:
        flat = tokens.reshape(flat_rows, width)
        gathered, saved = forward(flat, shards, sources, norms, rel_table, halve)
    else:
        gathered = gather_weights(shards, sources, halve)
    small = gathered[0].reshape(-1, lines, gains.shape[1]).transpose(1, 0, 2).reshape(lines, width)
    gain_f = small[:norms].astype(jnp.float32)
    depth = small[norms : norms + taps]
    f_in = (gathered[1][0], gathered[7][0])
    f_out = (gathered[2][0], gathered[8][0])
    proj, a_out, c_in, c_out = (gathered[3], gathered[4][0], gathered[5][0], gathered[6][0])
    if quick:
        result, squares, x1, x2, x3, x4, u0, u1, query, keys, values, mixed, joined, summed = saved
        grad, totals, total_table, shares = back(
            cotangent.reshape(flat_rows, width),
            (x4, x3, x2, x1, flat),
            (joined, summed, u1, u0),
            (query, keys, values, mixed),
            rel_table,
            small[:8].astype(jnp.float32),
            jnp.pad(depth.astype(jnp.float32), ((0, 32 - taps), (0, 0))),
            squares,
            (c_in, c_out, a_out, proj, f_in[1], f_out[1], f_in[0], f_out[0]),
            rows,
        )
        sums = jnp.sum(totals[56:61], 1)
        totals = jnp.concatenate([totals[:norms], totals[8 : 8 + taps]], 0)
        groups = lax.axis_size("group")
        grad_in_first, grad_in_second = (unmix(shares[9], groups), unmix(shares[1], groups))
        grad_out_first, grad_out_second = (shares[8], shares[0])
        grad_conv_out, grad_conv_in, grad_attn_out = shares[2:5]
        grad_qkv = shares[5:8]
    else:
        start = tokens.reshape(flat_rows, width).astype(jnp.float32)
        first_branch, first_kept = feed_forward(start, gain_f[0], f_in[0], f_out[0])
        after_first = start + 0.5 * first_branch
        attn_branch, attn_kept = attention_forward(
            after_first, gain_f[1], proj, a_out, rel_table, shape
        )
        after_attn = after_first + attn_branch
        conv_branch, summed, conv_kept = conv_forward(
            after_attn, gain_f[2], gain_f[3], c_in, depth, c_out, shape
        )
        after_conv = after_attn + conv_branch
        second_branch, second_kept = feed_forward(after_conv, gain_f[4], f_in[1], f_out[1])
        final = after_conv + 0.5 * second_branch
        result, final_normal, final_inverse = norm_forward(final, gain_f[5])
        squares = jnp.stack(
            [
                jnp.sum(member * member)
                for member in (final, first_branch, attn_branch, conv_branch, second_branch)
            ]
        )
        grad = cotangent.reshape(flat_rows, width).astype(jnp.float32)
        grad, grad_gain_final = norm_backward(grad, final_normal, final_inverse, gain_f[5])
        back_in, grad_gain_second, grad_in_second, grad_out_second = feed_back(
            0.5 * grad, second_kept, gain_f[4], f_in[1], f_out[1]
        )
        grad = grad + back_in
        back_in, grad_gain_conv, grad_gain_mid, grad_conv_in, grad_taps, grad_conv_out = conv_back(
            grad, conv_kept, gain_f[2], gain_f[3], c_in, depth, c_out, shape
        )
        grad = grad + back_in
        back_in, grad_gain_attn, grad_qkv, grad_attn_out, grad_table = attention_back(
            grad, attn_kept, gain_f[1], proj, a_out, rel_table, shape
        )
        grad = grad + back_in
        back_in, grad_gain_first, grad_in_first, grad_out_first = feed_back(
            0.5 * grad, first_kept, gain_f[0], f_in[0], f_out[0]
        )
        grad = grad + back_in
        matrices = [grad_in_first, grad_in_second, grad_out_first, grad_out_second]
        matrices += [grad_attn_out, grad_conv_in, grad_conv_out] + grad_qkv
        matrices = [
            lax.psum(lax.psum_scatter(member, "group", tiled=True), ("seq", "replica"))
            for member in matrices
        ]
        grad_in_first, grad_in_second, grad_out_first, grad_out_second = matrices[:4]
        grad_attn_out, grad_conv_in, grad_conv_out = matrices[4:7]
        grad_qkv = matrices[7:]
        gain_grads = jnp.stack(
            [
                grad_gain_first,
                grad_gain_attn,
                grad_gain_conv,
                grad_gain_mid,
                grad_gain_second,
                grad_gain_final,
            ]
        )
        loose = jnp.concatenate([grad_table.reshape(-1), squares])
        lines = -(-loose.shape[0] // width)
        loose = jnp.pad(loose, (0, lines * width - loose.shape[0])).reshape(lines, width)
        totals = butterfly(jnp.concatenate([gain_grads, grad_taps, loose], 0))
        loose = totals[norms + taps :].reshape(-1)
        totals = totals[: norms + taps]
        table_size = rel_table.shape[0] * rel_table.shape[1]
        total_table = loose[:table_size].reshape(rel_table.shape)
        sums = loose[table_size : table_size + 5]
    owned = lax.dynamic_slice_in_dim(
        totals, lax.axis_index("group") * gains.shape[1], gains.shape[1], 1
    )
    count = (
        flat_rows * width * lax.axis_size("seq") * lax.axis_size("group") * lax.axis_size("replica")
    )
    stats = jnp.sqrt(sums / count)
    return (
        result.astype(jnp.bfloat16).reshape(shape),
        grad.astype(jnp.bfloat16).reshape(shape),
        jnp.stack([grad_in_first, grad_in_second]).astype(jnp.float32),
        jnp.stack([grad_out_first, grad_out_second]).astype(jnp.float32),
        jnp.stack(grad_qkv).astype(jnp.float32),
        grad_attn_out.astype(jnp.float32),
        grad_conv_in.astype(jnp.float32),
        grad_conv_out.astype(jnp.float32),
        owned[norms:],
        owned[:norms],
        total_table,
        stats,
    )


def solution(mesh):
    in_specs = (
        P(("group", "replica"), "seq", None),
        P(None, "group", None),
        P(None, "group", None),
        P(None, "group", None),
        P("group", None),
        P("group", None),
        P("group", None),
        P(None, "group"),
        P(None, "group"),
        P(),
        P(("group", "replica"), "seq", None),
    )
    out_specs = (
        P(("group", "replica"), "seq", None),
        P(("group", "replica"), "seq", None),
        P(None, "group", None),
        P(None, "group", None),
        P(None, "group", None),
        P("group", None),
        P("group", None),
        P("group", None),
        P(None, "group"),
        P(None, "group"),
        P(),
        P(),
    )
    return jax.shard_map(
        on_device, mesh=mesh, in_specs=in_specs, out_specs=out_specs, check_vma=False
    )
```

```python
import functools

import jax
import jax.numpy as jnp
from jax import lax
from jax.experimental import pallas as pl
from jax.experimental.pallas import tpu as pltpu
from jax.sharding import PartitionSpec as P

HEAD_DIM = 64
KERNEL = 31
LEFT = 64
RIGHT = 8
WIN = 73
LANES = 128
BLOCK = 128
SPAN = 256
BACK_PAD = 64


EPSILON = 1e-05
NEGATIVE = -1e30


MESH = pl.DeviceIdType.MESH


def from_behind(value, axis, steps):
    count = lax.axis_size(axis)
    initial, last = (max(0, -steps), min(count, count - steps))
    return lax.ppermute(value, axis, [(source, source + steps) for source in range(initial, last)])


def norm_forward(values, gain):
    centered = values - jnp.mean(values, -1, keepdims=True)
    inverse = lax.rsqrt(jnp.mean(centered * centered, -1, keepdims=True) + EPSILON)
    normal = centered * inverse
    return (normal * gain, normal, inverse)


def norm_backward(grad_out, normal, inverse, gain):
    grad_normal = grad_out * gain
    grad_in = inverse * (
        grad_normal
        - jnp.mean(grad_normal, -1, keepdims=True)
        - normal * jnp.mean(grad_normal * normal, -1, keepdims=True)
    )
    grad_gain = jnp.sum(grad_out * normal, 0)
    return (grad_in, grad_gain)


def matmul(left, right):
    return jnp.dot(left, right, preferred_element_type=jnp.float32)


def matmul_left_t(left, right):
    return lax.dot_general(
        left, right, (((0,), (0,)), ((), ())), preferred_element_type=jnp.float32
    )


def matmul_right_t(left, right):
    return lax.dot_general(
        left, right, (((1,), (1,)), ((), ())), preferred_element_type=jnp.float32
    )


def swish_grad(values):
    logistic = jax.nn.sigmoid(values)
    return logistic + values * logistic * (1.0 - logistic)


def nt(left,right):
    return lax.dot_general(left,right,(((1,),(1,)),((),())),preferred_element_type=jnp.float32)
def tn(left,right):
    return lax.dot_general(left,right,(((0,),(0,)),((),())),preferred_element_type=jnp.float32)
def nn(left,right):
    return jnp.dot(left,right,preferred_element_type=jnp.float32)

def block_mask(first, block, limit, lines=BLOCK):
    rows=lax.broadcasted_iota(jnp.int32,(lines,SPAN),0)%BLOCK
    cols=lax.broadcasted_iota(jnp.int32,(lines,SPAN),1)
    offset=cols-rows
    place=first+block*BLOCK+cols-LEFT
    return (offset>=0)&(offset<WIN)&(place>=0)&(place<limit)

def head_lanes(head):
    lanes=lax.broadcasted_iota(jnp.int32,(BLOCK,LANES),1)
    return (lanes>=head*HEAD_DIM)&(lanes<(head+1)*HEAD_DIM)

def block_probs(query, keys, table, mask):
    relative=pltpu.roll(nt(query,table),0,1,stride=1,stride_axis=0)
    raw=jnp.where(mask,(nt(query,keys)+relative)*(HEAD_DIM**-0.5),NEGATIVE)
    expo=jnp.exp(raw-jnp.max(raw,-1,keepdims=True))
    return expo*(1.0/jnp.sum(expo,-1,keepdims=True))

def attend_kernel(limit, first_ref, q_ref, k_ref, v_ref, t_ref, c_ref):
    table=t_ref[...]
    zero=jnp.zeros((BLOCK,LANES),jnp.bfloat16)
    for block in range(q_ref.shape[1]//BLOCK):
        rows=pl.ds(block*BLOCK,BLOCK); span=pl.ds(block*BLOCK,SPAN)
        query=q_ref[0,rows,:]; keys=k_ref[0,span,:]; values=v_ref[0,span,:]
        mask=block_mask(first_ref[0],block,limit)
        mixed=[]
        for head in range(2):
            probs=block_probs(jnp.where(head_lanes(head),query,zero),keys,table,mask)
            mixed.append(nn(probs.astype(jnp.bfloat16),values))
        c_ref[0,rows,:]=jnp.where(head_lanes(0),mixed[0],mixed[1]).astype(jnp.bfloat16)

def attend_back_kernel(limit, first_ref, q_ref, k_ref, v_ref, t_ref, g_ref, dq_ref, dk_ref, dv_ref, dt_ref, dk_sum, dv_sum):
    table=t_ref[...]
    zero=jnp.zeros((BLOCK,LANES),jnp.bfloat16)
    flip=(lax.broadcasted_iota(jnp.int32,(BLOCK,BLOCK),0)+lax.broadcasted_iota(jnp.int32,(BLOCK,BLOCK),1)==BLOCK-1).astype(jnp.float32).astype(jnp.bfloat16)
    dk_sum[...]=jnp.zeros_like(dk_sum); dv_sum[...]=jnp.zeros_like(dv_sum)
    @pl.when((pl.program_id(0)==0)&(pl.program_id(1)==0))
    def _(): dt_ref[...]=jnp.zeros_like(dt_ref)
    for block in range(q_ref.shape[1]//BLOCK):
        rows=pl.ds(block*BLOCK,BLOCK); span=pl.ds(block*BLOCK,SPAN)
        keys=k_ref[0,span,:]; values=v_ref[0,span,:]
        mask=block_mask(first_ref[0],block,limit)
        grad_query=[]
        for head in range(2):
            query=jnp.where(head_lanes(head),q_ref[0,rows,:],zero)
            grad=jnp.where(head_lanes(head),g_ref[0,rows,:],zero)
            probs=block_probs(query,keys,table,mask)
            grad_probs=nt(grad,values)
            grad_raw=probs*(grad_probs-jnp.sum(probs*grad_probs,-1,keepdims=True))
            grad_raw=grad_raw.astype(jnp.bfloat16)
            turned=pltpu.roll(nn(flip,grad_raw),SPAN-BLOCK+1,1,stride=1,stride_axis=0)
            unskewed=nn(flip,turned.astype(jnp.bfloat16)).astype(jnp.bfloat16)
            dv_sum[span,:]+=tn(probs.astype(jnp.bfloat16),grad)
            dk_sum[span,:]+=tn(grad_raw,query)
            dt_ref[...]+=tn(unskewed,query)
            grad_query.append(nn(grad_raw,keys)+nn(unskewed,table))
        dq_ref[0,rows,:]=(jnp.where(head_lanes(0),grad_query[0],grad_query[1])*(HEAD_DIM**-0.5)).astype(jnp.bfloat16)
    dk_ref[0]=(dk_sum[...]*(HEAD_DIM**-0.5)).astype(jnp.bfloat16)
    dv_ref[0]=dv_sum[...].astype(jnp.bfloat16)

def wide_table(table):
    return jnp.tile(jnp.pad(table,((0,SPAN-table.shape[0]),(0,0))),(1,LANES//HEAD_DIM))

def specs(clips,rows,width):
    own=pl.BlockSpec((1,rows,LANES),lambda c,h:(c,0,h))
    ext=pl.BlockSpec((1,rows+LEFT+BACK_PAD,LANES),lambda c,h:(c,0,h))
    tab=pl.BlockSpec((SPAN,LANES),lambda c,h:(0,0))
    return (pl.BlockSpec(memory_space=pltpu.SMEM),own,ext,tab),(clips,width//LANES)

def attend(query,keys,values,table,rows):
    clips,_,width=query.shape
    first=lax.axis_index('seq').astype(jnp.int32)[None]*rows
    limit=rows*lax.axis_size('seq')
    (sc,own,ext,tab),grid=specs(clips,rows,width)
    return pl.pallas_call(functools.partial(attend_kernel,limit),grid=grid,
        in_specs=[sc,own,ext,ext,tab],out_specs=own,
        out_shape=jax.ShapeDtypeStruct(query.shape,jnp.bfloat16),name="attend",
    )(first,query,keys,values,wide_table(table))

def attend_back(query,keys,values,table,grad,rows):
    clips,_,width=query.shape
    first=lax.axis_index('seq').astype(jnp.int32)[None]*rows
    limit=rows*lax.axis_size('seq')
    (sc,own,ext,tab),grid=specs(clips,rows,width)
    dq,dk,dv,dt=pl.pallas_call(functools.partial(attend_back_kernel,limit),grid=grid,
        in_specs=[sc,own,ext,ext,tab,own],out_specs=[own,ext,ext,tab],
        out_shape=[jax.ShapeDtypeStruct(query.shape,jnp.bfloat16),jax.ShapeDtypeStruct(keys.shape,jnp.bfloat16),jax.ShapeDtypeStruct(keys.shape,jnp.bfloat16),jax.ShapeDtypeStruct((SPAN,LANES),jnp.float32)],
        scratch_shapes=[pltpu.VMEM((rows+LEFT+BACK_PAD,LANES),jnp.float32)]*2,name="attend_back",
    )(first,query,keys,values,wide_table(table),grad)
    return dq,dk,dv,(dt[:WIN,:HEAD_DIM]+dt[:WIN,HEAD_DIM:])*(HEAD_DIM**-0.5)
def depth_of():
    return lax.axis_size("group") // 2


def place():
    group = lax.axis_index("group")
    return (group // 2, group % 2, lax.axis_index("seq"), lax.axis_index("replica"))


def greet(peers):
    barrier = pltpu.get_barrier_semaphore()
    for peer in peers:
        pl.semaphore_signal(barrier, inc=1, device_id=peer, device_id_type=MESH)
    pl.semaphore_wait(barrier, len(peers))


def neighbours():
    z, x, seq, replica = place()
    depth = depth_of()
    deep = [{"group": (z + steps) % depth * 2 + x} for steps in range(1, depth)]
    across = {"group": z * 2 + 1 - x}
    beside = {"seq": 1 - seq}
    twin = {"replica": 1 - replica}
    return (deep, across, beside, twin)


class Gather:
    def __init__(self, source, target, cut, low, left, rows, size, sends, recvs, at):
        depth = depth_of()
        self.source, self.target, self.cut, self.low, self.rows = (source, target, cut, low, rows)
        self.piece = size[0] // (1, 2, 4)[cut]
        self.columns = pl.ds(left, size[1])
        self.sends, self.recvs, self.at = (sends, recvs, at)
        self.z, self.x, self.seq, self.replica = place()
        self.deep, self.across, self.beside, self.twin = neighbours()
        self.depth = depth
        self.firsts = (0, depth - 1, 2 * depth - 1, 4 * depth - 2)
        self.started = []

    def spot(self, ref, owner, dy, dc):
        part = 0
        if self.cut:
            part = (self.replica + dc) % 2
        if self.cut == 2:
            part = part + 2 * ((self.seq + dy) % 2)
        first = pl.multiple_of(owner * self.rows + self.low + part * self.piece, self.piece)
        return ref.at[pl.ds(first, self.piece), self.columns]

    def owner(self, steps, dx):
        return (self.z + self.depth - steps) % self.depth * 2 + (self.x + dx) % 2

    def copy(self, steps, dx, dy, dc, kind, index, peer):
        mine = steps == 0 and dx == 0
        slot = self.at + self.firsts[kind] + index
        spot = self.spot(self.target, self.owner(steps, dx), dy, dc)
        return pltpu.make_async_remote_copy(
            src_ref=self.spot(self.source, 0, dy, dc) if mine else spot,
            dst_ref=spot,
            send_sem=self.sends.at[slot],
            recv_sem=self.recvs.at[slot],
            device_id=peer,
            device_id_type=MESH,
        )

    def send(self, copy):
        copy.start()
        self.started.append(copy)

    def to_beside(self, steps, dx):
        if self.cut == 2:
            index = dx * self.depth + steps - 1
            self.send(self.copy(steps, dx, 0, 0, 2, index, self.beside))

    def to_twin(self, steps, dx, dy):
        if self.cut:
            index = dy * (2 * self.depth - 1) + dx * self.depth + steps - 1
            self.send(self.copy(steps, dx, dy, 0, 3, index, self.twin))

    def open(self):
        for steps, peer in enumerate(self.deep, 1):
            self.send(self.copy(0, 0, 0, 0, 0, steps - 1, peer))
        self.send(self.copy(0, 0, 0, 0, 1, 0, self.across))

    def got(self, steps, dx, dy, dc, kind, index):
        self.copy(steps or self.depth, dx, dy, dc, kind, index, self.twin).wait_recv()

    def forward_deep(self):
        for steps in range(1, self.depth):
            self.got(steps, 0, 0, 0, 0, steps - 1)
            self.send(self.copy(steps, 0, 0, 0, 1, steps, self.across))
            self.to_beside(steps, 0)
            self.to_twin(steps, 0, 0)

    def forward_across(self):
        for steps in range(self.depth):
            self.got(steps, 1, 0, 0, 1, steps)
            self.to_beside(steps, 1)
            self.to_twin(steps, 1, 0)

    def others(self):
        return [(steps, dx) for dx in range(2) for steps in range(self.depth) if steps or dx]

    def forward_beside(self):
        if self.cut == 2:
            for steps, dx in self.others():
                self.got(steps, dx, 1, 0, 2, dx * self.depth + steps - 1)
                self.to_twin(steps, dx, 1)

    def close(self):
        if self.cut:
            for dy in range(self.cut):
                for steps, dx in self.others():
                    index = dy * (2 * self.depth - 1) + dx * self.depth + steps - 1
                    self.got(steps, dx, dy, 1, 3, index)
        for copy in self.started:
            copy.wait_send()


def stack_heads(values):
    zero = jnp.zeros((BLOCK, LANES), jnp.bfloat16)
    return jnp.concatenate([jnp.where(head_lanes(head), values, zero) for head in range(2)], 0)


def roll_halves(values, shift):
    halves = [values[:BLOCK], values[BLOCK:]]
    rolled = [pltpu.roll(half, shift, 1, stride=1, stride_axis=0) for half in halves]
    return jnp.concatenate(rolled, 0)


def stacked_probs(query, keys, table, mask):
    relative = roll_halves(nt(query, table), 0)
    raw = jnp.where(mask, (nt(query, keys) + relative) * HEAD_DIM**-0.5, NEGATIVE)
    expo = jnp.exp(raw - jnp.max(raw, -1, keepdims=True))
    return expo * (1.0 / jnp.sum(expo, -1, keepdims=True))


class Ticker:
    def __init__(self, jobs, numbers, stores, loads):
        self.jobs, self.numbers, self.stores, self.loads = (jobs, numbers, stores, loads)
        self.tick, self.stored, self.loaded = (0, set(), set())

    def advance(self):
        names = ("open", "forward_deep", "forward_across", "forward_beside", "close")
        if self.tick >= len(self.jobs) + 8:
            return
        for lag, name in enumerate(names):
            if 0 <= self.tick - 2 * lag < len(self.jobs):
                getattr(self.jobs[self.tick - 2 * lag], name)()
        if self.tick < len(self.stores):
            source, store = self.stores[self.tick]
            if source not in self.loaded:
                self.loads[source].wait()
                self.loaded.add(source)
            store.start()
        self.tick += 1

    def until(self, number):
        last = max(at for at, owner in enumerate(self.numbers) if owner == number)
        while self.tick <= max(last + 8, number):
            self.advance()
        if number not in self.stored:
            self.stores[number][1].wait()
            self.stored.add(number)

    def finish(self):
        while self.tick < len(self.jobs) + 8:
            self.advance()
        for number in range(len(self.stores)):
            self.until(number)


def gather_ticker(plan, sources, ins, outs, helds, sems):
    sends, recvs, local = sems
    deep, across, beside, twin = neighbours()
    peers = deep + [across, twin]
    if any(member[-1] == 2 for member in plan):
        peers.append(beside)
    greet(peers)
    loads = [
        pltpu.make_async_copy(ins[at], held, local.at[0, at]) for at, held in enumerate(helds)
    ]
    for load in loads:
        load.start()
    jobs, at = ([], 0)
    for number, layer, low, left, size, cut in plan:
        source, first = sources[number]
        ref = ins[source].at[first + layer]
        rows = ins[source].shape[1]
        target = outs[number].at[layer]
        jobs.append(Gather(ref, target, cut, low, left, rows, size, sends, recvs, at))
        at += (2, 6, 8)[cut] * depth_of()
    z, x, _, _ = place()
    stores = []
    for number, (source, first) in enumerate(sources):
        rows = ins[source].shape[1]
        start = pl.multiple_of((z * 2 + x) * rows, rows)
        store = pltpu.make_async_copy(
            helds[source].at[pl.ds(first, outs[number].shape[0])],
            outs[number].at[:, pl.ds(start, rows)],
            local.at[1, number],
        )
        stores.append((source, store))
    return Ticker(jobs, [member[0] for member in plan], stores, loads)


def gather_kernel(plan, sources, count, *refs):
    ins, outs = (refs[:count], refs[count : count + len(sources)])
    ticker = gather_ticker(
        plan, sources, ins, outs, refs[count + len(sources) : -3], refs[-3:]
    )
    ticker.finish()


def product_rows(left, right, target, size=256):
    def body(cols):
        target[:, cols] = nn(left[...], right[:, cols]).astype(target.dtype)

    row_blocks(right.shape[1], size, body)


def join_rows(resid, branch, scale, squares, line):
    squares[pl.ds(line, 1), :] = jnp.zeros_like(squares[pl.ds(line, 1), :])

    def body(rows):
        value = branch[rows, :]
        resid[rows, :] += scale * value
        squares[pl.ds(line, 1), :] += jnp.sum(value * value, 0, keepdims=True)

    row_blocks(resid.shape[0], 128, body)


def module_forward(ticker, weights, entry, hidden, total, helds, saved, sems, ready):
    width = total.shape[1]
    chunks = hidden.shape[0]
    stores = []
    for chunk in range(chunks):
        before = helds[chunk % 2]
        if chunk > 1:
            stores[chunk - 2].wait()
        w_in = weights[0].take()

        def body(cols):
            value = nn(entry[...], w_in[:, cols])
            before[:, cols] = value.astype(jnp.bfloat16)
            hidden[chunk, :, cols] = (value * jax.nn.sigmoid(value)).astype(jnp.bfloat16)

        row_blocks(width, 256, body)
        target = saved.at[:, pl.ds(chunk * width, width)]
        stores.append(fetch(before, target, sems.at[chunk]))
        if ready == 2 or chunk % 2:
            ticker.advance()
    total[...] = jnp.zeros_like(total)
    ticker.until(ready)
    weights = weights[1]()
    for chunk in range(chunks):
        w_out = weights.take()

        def gather(cols):
            total[:, cols] += nn(hidden[chunk], w_out[:, cols])

        row_blocks(width, 256, gather)
        if chunk % 2:
            ticker.advance()
    for store in stores[-2:]:
        store.wait()


def depthwise_rows(glu, taps, skip, target, ticker):
    total, width = target.shape
    for column in range(width // LANES):
        lanes = pl.ds(column * LANES, LANES)

        def body(at, carry):
            first = pl.multiple_of(at * LANES, LANES)
            window = glu[pl.ds(first, LANES + 32), lanes]
            summed = jnp.zeros((LANES, LANES), jnp.float32)
            for tap in range(KERNEL):
                moved = window[tap + 2 : tap + 2 + LANES]
                summed = summed + moved * taps[pl.ds(skip + tap, 1), lanes]
            target[pl.ds(first, LANES), lanes] = summed
            return carry

        lax.fori_loop(0, total // LANES, body, 0)
        if column % 4 == 3:
            ticker.advance()


def swish_rows(source, gain, target):
    def body(rows):
        normal, _ = norm_parts(source[rows, :])
        middle = normal * gain
        target[rows, :] = (middle * jax.nn.sigmoid(middle)).astype(jnp.bfloat16)

    row_blocks(source.shape[0], 128, body)


def forward_kernel(settings, *refs):
    plan, sources, count, norms, rows, limit = settings
    first_ref, table_ref, tokens = refs[:3]
    ins, refs = (refs[3 : 3 + count], refs[3 + count :])
    outs, refs = (refs[: len(sources)], refs[len(sources) :])
    out, squares, x1, x2, x3, x4, u0, u1, q_out, k_out, v_out, mixed_out, joined, summed = refs[:14]
    helds, refs = (refs[14 : 14 + count], refs[14 + count :])
    resid, total, glu, low_gains, gains, entry, hidden, held_a, held_b, q_ref = refs[:10]
    k_ref, v_ref, mixed, slots = refs[10:14]
    local, slot_sems, saved_sems, halo_sems = refs[14:18]
    ticker = gather_ticker(plan, sources, ins, outs, helds, refs[18:])
    width = resid.shape[1]
    chunks = u0.shape[1] // width
    groups = lax.axis_size("group")
    part = width // groups
    lines = low_gains.shape[0]
    load = fetch(tokens, entry, local.at[0])
    spaces = [slots.at[at] for at in range(3)]

    def stream(*weights):
        return Stream(spaces, slot_sems, [lambda slot, ref=ref: [(ref, slot)] for ref in weights])

    def module_streams(w_in, w_out):
        heres = [pl.ds(chunk * width, width) for chunk in range(chunks)]
        first = stream(*[w_in.at[0, :, here] for here in heres])
        return (first, lambda: stream(*[w_out.at[0, here] for here in heres]))

    for _ in range(5):
        ticker.advance()
    ticker.until(0)
    small = [
        fetch(
            outs[0].at[0, pl.ds(group * lines, lines)],
            low_gains.at[:, pl.ds(group * part, part)],
            slot_sems.at[0, group],
        )
        for group in range(groups)
    ]
    for copy in small:
        copy.wait()
    gains[...] = low_gains[...].astype(jnp.float32)
    load.wait()

    def widen(at):
        resid[at, :] = entry[at, :].astype(jnp.float32)

    row_blocks(rows, 128, widen)
    norm_rows(resid, gains[pl.ds(0, 1), :], entry)
    ticker.until(1)
    pair = (held_a, held_b)
    weights = module_streams(outs[1], outs[2])
    module_forward(ticker, weights, entry, hidden, total, pair, u0, saved_sems, 2)
    join_rows(resid, total, 0.5, squares, 1)
    stored = fetch(resid, x1, local.at[0])
    norm_rows(resid, gains[pl.ds(1, 1), :], entry)
    ticker.until(3)
    weights = stream(*[outs[3].at[at] for at in range(3)])
    own = pl.ds(LEFT, rows)
    spare = BACK_PAD - 2 * RIGHT
    for ref in (k_ref, v_ref):
        ref[0, pl.ds(LEFT + rows + 2 * RIGHT, spare), :] = jnp.zeros((spare, width), jnp.bfloat16)
    product_rows(entry, weights.take(), q_ref)
    product_rows(entry, weights.take(), k_ref.at[0, own])
    product_rows(entry, weights.take(), v_ref.at[0, own])
    _, _, seq, _ = place()
    span = lax.axis_size("seq")
    edges = []
    for at, ref in enumerate((k_ref, v_ref)):
        for way, (source, target, size, step) in enumerate(
            ((rows, 0, LEFT, 1), (LEFT, LEFT + rows, 2 * RIGHT, span - 1))
        ):
            edges.append(
                pltpu.make_async_remote_copy(
                    src_ref=ref.at[0, pl.ds(source, size)],
                    dst_ref=ref.at[0, pl.ds(target, size)],
                    send_sem=halo_sems.at[0, 2 * at + way],
                    recv_sem=halo_sems.at[1, 2 * at + way],
                    device_id={"seq": (seq + step) % span},
                    device_id_type=MESH,
                )
            )
    for edge in edges:
        edge.start()
    ticker.advance()
    for edge in edges:
        edge.wait()
    table = table_ref[...]
    for pair_at in range(width // LANES):
        lanes = pl.ds(pair_at * LANES, LANES)

        def attend_block(block, carry):
            here = pl.ds(pl.multiple_of(block * BLOCK, BLOCK), BLOCK)
            near = pl.ds(pl.multiple_of(block * BLOCK, BLOCK), SPAN)
            key, value = (k_ref[0, near, lanes], v_ref[0, near, lanes])
            mask = block_mask(first_ref[0], block, limit, 2 * BLOCK)
            probs = stacked_probs(stack_heads(q_ref[here, lanes]), key, table, mask)
            both = nn(probs.astype(jnp.bfloat16), value)
            both = jnp.where(head_lanes(0), both[:BLOCK], both[BLOCK:])
            mixed[here, lanes] = both.astype(jnp.bfloat16)
            return carry

        lax.fori_loop(0, rows // BLOCK, attend_block, 0)
        if pair_at % 2:
            ticker.advance()
    keeps = [
        fetch(source, target, local.at[1 + at])
        for at, (source, target) in enumerate(
            ((q_ref, q_out), (k_ref, k_out), (v_ref, v_out), (mixed, mixed_out))
        )
    ]
    ticker.until(4)
    ticker.advance()
    product_rows(mixed, stream(outs[4].at[0]).take(), total)
    stored.wait()
    join_rows(resid, total, 1.0, squares, 2)
    stored = fetch(resid, x2, local.at[0])
    norm_rows(resid, gains[pl.ds(2, 1), :], entry)
    ticker.until(5)
    weights = stream(*[outs[5].at[0, :, pl.ds(at * width, width)] for at in range(2)])
    value_part, gate_part = (weights.take(), weights.take())

    def open_columns(cols):
        value = nn(entry[...], value_part[:, cols])
        gate = nn(entry[...], gate_part[:, cols])
        held_a[:, cols] = value.astype(jnp.bfloat16)
        held_b[:, cols] = gate.astype(jnp.bfloat16)
        opened = (value * jax.nn.sigmoid(gate)).astype(jnp.bfloat16)
        glu[pl.ds(32, rows), cols] = opened.astype(jnp.float32)

    ticker.advance()
    row_blocks(width, 256, open_columns)
    halo = pltpu.make_async_remote_copy(
        src_ref=glu.at[pl.ds(rows, 32)],
        dst_ref=glu.at[pl.ds(0, 32)],
        send_sem=halo_sems.at[0, 4],
        recv_sem=halo_sems.at[1, 4],
        device_id={"seq": (seq + 1) % span},
        device_id_type=MESH,
    )
    halo.start()
    keeps += [
        fetch(held, joined.at[:, pl.ds(at * width, width)], local.at[5 + at])
        for at, held in enumerate(pair)
    ]
    ticker.advance()
    halo.wait()
    ahead = pl.ds(0, 32)
    glu[ahead, :] = jnp.where(seq > 0, glu[ahead, :], jnp.zeros((32, width), jnp.float32))
    depthwise_rows(glu, gains, norms, total, ticker)
    kept = fetch(total, summed, local.at[7])
    swish_rows(total, gains[pl.ds(3, 1), :], entry)
    ticker.until(6)
    ticker.advance()
    conv = glu.at[pl.ds(0, rows)]
    product_rows(entry, stream(outs[6].at[0]).take(), conv)
    stored.wait()
    join_rows(resid, conv, 1.0, squares, 3)
    stored = fetch(resid, x3, local.at[0])
    norm_rows(resid, gains[pl.ds(4, 1), :], entry)
    kept.wait()
    for keep in keeps:
        keep.wait()
    ticker.until(7)
    weights = module_streams(outs[7], outs[8])
    module_forward(ticker, weights, entry, hidden, total, pair, u1, saved_sems, 8)
    stored.wait()
    join_rows(resid, total, 0.5, squares, 4)
    stored = fetch(resid, x4, local.at[0])
    squares[pl.ds(0, 1), :] = jnp.zeros((1, width), jnp.float32)

    def tally(at):
        squares[pl.ds(0, 1), :] += jnp.sum(resid[at, :] * resid[at, :], 0, keepdims=True)

    row_blocks(rows, 128, tally)
    norm_rows(resid, gains[pl.ds(5, 1), :], entry)
    last = fetch(entry, out, local.at[1])
    ticker.finish()
    stored.wait()
    last.wait()


def gather_plan(shards, sources, halve):
    groups = lax.axis_size("group")
    width = shards[1].shape[1] * groups
    part = width // groups
    plan = [(0, 0, 0, 0, shards[0].shape[1:], 0)]
    for number, (source, first, layers) in enumerate(sources):
        for layer in range(layers if source else 0):
            for low in range(0, shards[source].shape[1], part):
                for left in range(0, shards[source].shape[2], width):
                    cut = 2 if halve and len(plan) % 3 else 1
                    plan.append((number, layer, low, left, (part, width), cut))
    return plan


def gather_outputs(shards, sources):
    groups = lax.axis_size("group")
    return [
        jax.ShapeDtypeStruct(
            (layers, groups * shards[source].shape[1], shards[source].shape[2]), jnp.bfloat16
        )
        for source, _, layers in sources
    ]


def gather_scratch(plan, sources):
    total = sum((2, 6, 8)[member[-1]] * depth_of() for member in plan)
    return [
        pltpu.SemaphoreType.DMA((total,)),
        pltpu.SemaphoreType.DMA((total,)),
        pltpu.SemaphoreType.DMA((2, len(sources))),
    ]


def gather_weights(shards, sources, halve):
    plan = gather_plan(shards, sources, halve)
    return pl.pallas_call(
        functools.partial(
            gather_kernel, plan, [(source, first) for source, first, _ in sources], len(shards)
        ),
        in_specs=[pl.BlockSpec(memory_space=pl.ANY)] * len(shards),
        out_specs=[pl.BlockSpec(memory_space=pl.ANY)] * len(sources),
        out_shape=gather_outputs(shards, sources),
        scratch_shapes=[pltpu.VMEM(shard.shape, jnp.bfloat16) for shard in shards]
        + gather_scratch(plan, sources),
        compiler_params=pltpu.CompilerParams(
            collective_id=1, has_side_effects=True, vmem_limit_bytes=24 << 20
        ),
        name="gather_weights",
    )(*shards)


def forward(tokens, shards, sources, norms, table, halve):
    rows, width = tokens.shape
    plan = gather_plan(shards, sources, halve)
    groups = lax.axis_size("group")
    first = lax.axis_index("seq").astype(jnp.int32)[None] * rows
    limit = rows * lax.axis_size("seq")
    ext = rows + LEFT + BACK_PAD
    inner = shards[1].shape[2]
    lines = shards[0].shape[1]
    hbm = pl.BlockSpec(memory_space=pl.ANY)
    vmem = pl.BlockSpec(memory_space=pltpu.VMEM)
    low = lambda *shape: jax.ShapeDtypeStruct(shape, jnp.bfloat16)
    wide = lambda *shape: jax.ShapeDtypeStruct(shape, jnp.float32)
    settings = (plan, [member[:2] for member in sources], len(shards), norms, rows, limit)
    results = pl.pallas_call(
        functools.partial(forward_kernel, settings),
        in_specs=[pl.BlockSpec(memory_space=pltpu.SMEM), vmem] + [hbm] * (1 + len(shards)),
        out_specs=[hbm] * len(sources) + [hbm, vmem] + [hbm] * 12,
        out_shape=gather_outputs(shards, sources)
        + [low(rows, width), wide(8, width)]
        + [wide(rows, width)] * 4
        + [low(rows, inner)] * 2
        + [low(rows, width), low(1, ext, width), low(1, ext, width), low(rows, width)]
        + [low(rows, 2 * width), wide(rows, width)],
        scratch_shapes=[pltpu.VMEM(shard.shape, jnp.bfloat16) for shard in shards]
        + [
            pltpu.VMEM((rows, width), jnp.float32),
            pltpu.VMEM((rows, width), jnp.float32),
            pltpu.VMEM((rows + 32, width), jnp.float32),
            pltpu.VMEM((lines, width), jnp.bfloat16),
            pltpu.VMEM((lines, width), jnp.float32),
        ]
        + [
            pltpu.VMEM((rows, width), jnp.bfloat16),
            pltpu.VMEM((inner // width, rows, width), jnp.bfloat16),
        ]
        + [pltpu.VMEM((rows, width), jnp.bfloat16)] * 3
        + [
            pltpu.VMEM((1, ext, width), jnp.bfloat16),
            pltpu.VMEM((1, ext, width), jnp.bfloat16),
            pltpu.VMEM((rows, width), jnp.bfloat16),
            pltpu.VMEM((3, width, width), jnp.bfloat16),
            pltpu.SemaphoreType.DMA((8,)),
            pltpu.SemaphoreType.DMA((3, groups)),
            pltpu.SemaphoreType.DMA((inner // width,)),
            pltpu.SemaphoreType.DMA((2, 5)),
        ]
        + gather_scratch(plan, sources),
        compiler_params=pltpu.CompilerParams(
            collective_id=5, has_side_effects=True, vmem_limit_bytes=56 << 20
        ),
        name="forward",
    )(first, wide_table(table), tokens, *shards)
    return results[: len(sources)], results[len(sources) :]


def swap(value, axis, bit=1):
    return lax.ppermute(value, axis, [(i, i ^ bit) for i in range(lax.axis_size(axis))])


def butterfly(value):
    for axis in ("replica", "seq", "group"):
        bit = 1
        while bit < lax.axis_size(axis):
            value = value + swap(value, axis, bit)
            bit *= 2
    return value


def add_slabs(count, target, *sources):
    def body(at, carry):
        total = sources[0](at)[...].astype(jnp.float32)
        for source in sources[1:]:
            total = total + source(at)[...].astype(jnp.float32)
        target(at)[...] = total.astype(jnp.bfloat16)
        return carry

    lax.fori_loop(0, count, body, 0)


class Reduce:
    def __init__(self, pool, number, target, low, left):
        self.pool, self.number = (pool, number)
        self.target, self.low, self.left = (target, low, left)
        self.source = pool.kept.at[number]
        self.stage = pool.stage.at[number % 2]
        self.kept = False
        self.depth, self.width = (depth_of(), pool.width)
        self.half, self.unit = (pool.rows // 2, pool.rows // 8)
        self.started = []
        self.stages = [
            self.exchange_twin,
            self.exchange_seq,
            self.exchange_across,
            self.exchange_deep,
            self.settle,
            self.hand_over,
            self.close,
        ]
        self.done_stages = 0
        slot = number % pool.ring
        self.own, self.came = (pool.own.at[slot], pool.came.at[slot])
        self.from_x, self.from_seq = (pool.from_x.at[slot], pool.from_seq.at[slot])
        self.from_z, self.shared = (pool.from_z.at[number], pool.shared.at[number])
        self.alone = pool.finished.at[slot, pl.ds(0, self.unit)]
        self.joint = pool.finished.at[slot, pl.ds(self.unit, 2 * self.unit)]

    def locate(self):
        self.z, self.x, self.seq, self.replica = place()
        self.deep, self.across, self.beside, self.twin = neighbours()

    def rows(self, first, count):
        return pl.ds(pl.multiple_of(first, self.unit), count * self.unit)

    def near(self):
        return self.rows(self.seq * self.unit, 3)

    def lone(self):
        return self.rows(3 * self.unit * self.seq, 1)

    def far(self):
        return self.rows(3 * self.unit * (1 - self.seq), 1)

    def both(self):
        return pl.ds(self.unit, 2 * self.unit)

    def side(self, replica):
        return pl.ds(pl.multiple_of(replica * self.half, self.half), self.half)

    def remote(self, source, target, slot, peer):
        return pltpu.make_async_remote_copy(
            src_ref=source,
            dst_ref=target,
            send_sem=self.pool.sends.at[self.number, slot],
            recv_sem=self.pool.recvs.at[self.number, slot],
            device_id=peer,
            device_id_type=MESH,
        )

    def send(self, ends, slot, peer):
        make = lambda peer: self.remote(*ends(), slot, peer)
        make(peer).start()
        self.started.append(make)

    def wait(self, target, slot):
        self.remote(target, target, slot, self.twin).wait_recv()

    def keep(self):
        return pltpu.make_async_copy(self.stage, self.source, self.pool.local.at[self.number, 0])

    def await_kept(self):
        if not self.kept:
            self.keep().wait()
            self.kept = True

    def load(self):
        source = self.source.at[:, :, self.side(self.replica)]
        return pltpu.make_async_copy(source, self.own, self.pool.local.at[self.number, 1])

    def credit(self, kind):
        if self.number >= self.pool.ring:
            pl.semaphore_wait(self.pool.credits.at[kind], 1)

    def release(self, kind, peer):
        if self.number + self.pool.ring < self.pool.total:
            pl.semaphore_signal(
                self.pool.credits.at[kind], inc=1, device_id=peer, device_id_type=MESH
            )

    def exchange_twin(self):
        self.await_kept()
        self.credit(0)
        self.load().start()
        ends = lambda: (self.source.at[:, :, self.side(1 - self.replica)], self.came)
        self.send(ends, 0, self.twin)

    def exchange_seq(self):
        self.load().wait()
        self.wait(self.came, 0)
        far = self.far()
        own = lambda at: self.own.at[at // 2, at % 2, far]
        add_slabs(2 * self.depth, own, own, lambda at: self.came.at[at // 2, at % 2, far])
        self.credit(1)
        self.send(lambda: (self.own.at[:, :, self.far()], self.from_seq), 1, self.beside)

    def gather(self, x, arrived):
        both, lone = (self.both(), self.lone())
        refs = [self.own.at[:, x], self.came.at[:, x]]
        pick = lambda rows: [lambda at, ref=ref: ref.at[at, rows] for ref in refs]
        shared, alone = (pick(both), pick(lone))
        alone.append(lambda at: self.from_seq.at[at, x])
        if arrived:
            both_here = self.rows(self.unit * (1 - self.seq), 2)
            lone_here = self.rows(2 * self.unit * self.seq, 1)
            shared.append(lambda at: self.from_x.at[at, both_here])
            alone.append(lambda at: self.from_x.at[at, lone_here])
        add_slabs(self.depth, shared[0], *shared)
        add_slabs(self.depth, alone[0], *alone)

    def exchange_across(self):
        self.wait(self.from_seq, 1)
        self.gather(1 - self.x, False)
        self.credit(2)
        self.send(lambda: (self.own.at[:, 1 - self.x, self.near()], self.from_x), 2, self.across)

    def exchange_deep(self):
        self.wait(self.from_x, 2)
        self.gather(self.x, True)
        for steps, peer in enumerate(self.deep, 1):
            ends = lambda steps=steps: (
                self.own.at[(self.z + steps) % self.depth, self.x, self.near()],
                self.from_z.at[steps - 1],
            )
            self.send(ends, 2 + steps, peer)
        self.release(0, self.twin)
        self.release(1, self.beside)
        self.release(2, self.across)

    def settle(self):
        for steps in range(1, self.depth):
            self.wait(self.from_z.at[steps - 1], 2 + steps)
        self.flush()
        both_here = self.rows(self.unit * (1 - self.seq), 2)
        lone_here = self.rows(2 * self.unit * self.seq, 1)
        for target, own, here in (
            (self.shared.at[self.seq], self.both(), both_here),
            (self.alone, self.lone(), lone_here),
        ):
            sources = [lambda at, own=own: self.own.at[self.z, self.x, own]]
            sources += [
                lambda at, steps=steps, here=here: self.from_z.at[steps, here]
                for steps in range(self.depth - 1)
            ]
            add_slabs(1, lambda at, target=target: target, *sources)
        self.last = 2 + self.depth
        ends = lambda: (self.shared.at[self.seq], self.shared.at[self.seq])
        self.send(ends, self.last, self.beside)
        self.store(0).start()
        self.send(lambda: (self.alone, self.spot(self.lone_out())), self.last + 1, self.beside)
        self.send(lambda: (self.alone, self.spot(self.lone_out())), self.last + 2, self.twin)

    def spot(self, first, count=1):
        return self.target.at[self.rows(first, count), pl.ds(self.left, self.width)]

    def lone_out(self, dy=0, dc=0):
        seq = self.seq if dy == 0 else 1 - self.seq
        replica = self.replica if dc == 0 else 1 - self.replica
        return self.low + replica * self.half + 3 * self.unit * seq

    def both_out(self, dc=0):
        replica = self.replica if dc == 0 else 1 - self.replica
        return self.low + replica * self.half + self.unit

    def store(self, kind):
        source = self.joint if kind else self.alone
        target = self.spot(self.both_out(), 2) if kind else self.spot(self.lone_out())
        return pltpu.make_async_copy(source, target, self.pool.local.at[self.number, 2 + kind])

    def hand_over(self):
        self.wait(self.spot(self.lone_out(1)), self.last + 1)
        spot = lambda: self.spot(self.lone_out(1))
        self.send(lambda: (spot(), spot()), self.last + 3, self.twin)
        self.wait(self.shared.at[1 - self.seq], self.last)
        sources = [lambda at, turn=turn: self.shared.at[turn] for turn in range(2)]
        add_slabs(1, lambda at: self.joint, *sources)
        self.store(1).start()
        self.send(lambda: (self.joint, self.spot(self.both_out(), 2)), self.last + 4, self.twin)

    def close(self):
        self.wait(self.spot(self.lone_out(0, 1)), self.last + 2)
        self.wait(self.spot(self.lone_out(1, 1)), self.last + 3)
        self.wait(self.spot(self.both_out(1), 2), self.last + 4)
        self.store(0).wait()
        self.store(1).wait()
        self.flush()

    def flush(self):
        for make in self.started:
            make(self.twin).wait_send()
        self.started = []

    def step(self):
        self.locate()
        self.stages[self.done_stages]()
        self.done_stages += 1


class Pool:
    ring = 7

    def __init__(self, rows, width, total, kept, refs):
        self.rows, self.width, self.total, self.kept = (rows, width, total, kept)
        names = list(Pool.shapes(rows, width, total))
        for name, ref in zip(names, refs):
            setattr(self, name, ref)
        self.sends, self.recvs, self.local, self.credits = refs[len(names) :]
        self.jobs = []

    @staticmethod
    def shapes(rows, width, total):
        depth, ring = (depth_of(), Pool.ring)
        unit = rows // 8
        return {
            "own": (ring, depth, 2, rows // 2, width),
            "came": (ring, depth, 2, rows // 2, width),
            "from_x": (ring, depth, 3 * unit, width),
            "from_seq": (ring, depth, 2, unit, width),
            "from_z": (total, depth - 1, 3 * unit, width),
            "shared": (total, 2, 2 * unit, width),
            "finished": (ring, 3 * unit, width),
            "stage": (2, depth, 2, rows, width),
        }

    @staticmethod
    def scratch(rows, width, total):
        slots = 7 + depth_of()
        return [pltpu.VMEM(shape, jnp.bfloat16) for shape in Pool.shapes(rows, width, total).values()] + [
            pltpu.SemaphoreType.DMA((total, slots)),
            pltpu.SemaphoreType.DMA((total, slots)),
            pltpu.SemaphoreType.DMA((total, 4)),
            pltpu.SemaphoreType.REGULAR((3,)),
        ]

    def add(self, target, low, left):
        number = len(self.jobs)
        if number >= 2:
            self.jobs[number - 2].await_kept()
        job = Reduce(self, number, target, low, left)
        self.jobs.append(job)
        return job

    def free(self, number):
        return number < self.ring or self.jobs[number - self.ring].done_stages >= 5

    def pump(self):
        active = [job for job in self.jobs if 0 < job.done_stages < 7]
        fresh = [job for job in self.jobs if job.done_stages == 0][:1]
        for job in fresh:
            if self.free(job.number):
                job.step()
        for job in reversed(active):
            job.step()

    def drain(self):
        while any(job.done_stages < 7 for job in self.jobs):
            self.pump()


def row_blocks(total, size, body):
    def step(at, carry):
        body(pl.ds(pl.multiple_of(at * size, size), size))
        return carry

    lax.fori_loop(0, total // size, step, 0)


def norm_parts(values):
    centered = values - jnp.mean(values, -1, keepdims=True)
    inverse = lax.rsqrt(jnp.mean(centered * centered, -1, keepdims=True) + EPSILON)
    return (centered * inverse, inverse)


def norm_rows(source, gain, target):
    def body(rows):
        normal, _ = norm_parts(source[rows, :].astype(jnp.float32))
        target[rows, :] = (normal * gain).astype(target.dtype)

    row_blocks(source.shape[0], 128, body)


def norm_back_rows(source, gain, grads, resid, sums, line):
    sums[pl.ds(line, 1), :] = jnp.zeros_like(sums[pl.ds(line, 1), :])

    def body(rows):
        normal, inverse = norm_parts(source[rows, :].astype(jnp.float32))
        grad = grads[rows, :]
        grad_normal = grad * gain
        resid[rows, :] += inverse * (
            grad_normal
            - jnp.mean(grad_normal, -1, keepdims=True)
            - normal * jnp.mean(grad_normal * normal, -1, keepdims=True)
        )
        sums[pl.ds(line, 1), :] += jnp.sum(grad * normal, 0, keepdims=True)

    row_blocks(source.shape[0], 128, body)


def cast_rows(source, target, scale=1.0):
    def body(rows):
        target[rows, :] = (source[rows, :] * scale).astype(jnp.bfloat16)

    row_blocks(source.shape[0], 128, body)


def transposed_rows(left, right, target, size=256):
    def body(cols):
        target[:, cols] = nt(left[...], right[cols, :]).astype(target.dtype)

    row_blocks(right.shape[0], size, body)


def add_transposed(left, right, target, size=256):
    def body(cols):
        target[:, cols] += nt(left[...], right[cols, :])

    row_blocks(right.shape[0], size, body)


def gradient_into(job, left, right):
    depth, _, rows, width = job.stage.shape

    def step(z, carry):
        cols = pl.ds(pl.multiple_of(z * 2 * rows, 2 * rows), 2 * rows)
        value = tn(left[:, cols], right[...]).astype(jnp.bfloat16)
        job.stage[z, 0] = value[:rows]
        job.stage[z, 1] = value[rows:]
        return carry

    lax.fori_loop(0, depth, step, 0)
    job.keep().start()


class Stream:
    def __init__(self, buffers, sems, copies):
        self.buffers, self.sems, self.copies = (buffers, sems, copies)
        self.issued = self.taken = 0
        for _ in range(len(buffers) - 1):
            self.issue()

    def parts(self, number):
        slot = number % len(self.buffers)
        made = self.copies[number](self.buffers[slot])
        return [
            pltpu.make_async_copy(source, target, self.sems.at[slot, at])
            for at, (source, target) in enumerate(made)
        ]

    def issue(self):
        if self.issued < len(self.copies):
            for copy in self.parts(self.issued):
                copy.start()
            self.issued += 1

    def take(self):
        for copy in self.parts(self.taken):
            copy.wait()
        self.taken += 1
        self.issue()
        return self.buffers[(self.taken - 1) % len(self.buffers)]


def module_copies(w_in, w_out, groups):
    chunks = w_out.shape[1]
    rows = w_out.shape[2]
    copies = []
    for chunk in range(chunks):
        copies.append(
            lambda slot, chunk=chunk: [
                (w_out.at[group, chunk], slot.at[pl.ds(group * rows, rows)])
                for group in range(groups)
            ]
        )
        copies.append(
            lambda slot, chunk=chunk: [
                (
                    w_in.at[:, pl.ds((group * chunks + chunk) * rows, rows)],
                    slot.at[:, pl.ds(group * rows, rows)],
                )
                for group in range(groups)
            ]
        )
    return copies


def saved_copies(saved, groups, rows):
    chunks = saved.shape[1] // (groups * rows)
    return [
        lambda slot, chunk=chunk: [
            (
                saved.at[:, pl.ds((group * chunks + chunk) * rows, rows)],
                slot.at[:, pl.ds(group * rows, rows)],
            )
            for group in range(groups)
        ]
        for chunk in range(chunks)
    ]


def module_back(pool, weights, saved, buffers, chunks, outs, often):
    pump = pool.pump
    entry, low, hidden, grad_hidden, total = buffers
    grad_in, grad_out = outs
    width = total.shape[1]
    total[...] = jnp.zeros_like(total)
    for chunk in range(chunks):
        before = saved.take()
        w_out = weights.take()

        def body(cols):
            value = before[:, cols].astype(jnp.float32)
            logistic = jax.nn.sigmoid(value)
            hidden[:, cols] = (value * logistic).astype(jnp.bfloat16)
            slope = logistic * (1.0 + value * (1.0 - logistic))
            grad = nt(low[...], w_out[cols, :]) * slope
            grad_hidden[:, cols] = grad.astype(jnp.bfloat16)

        row_blocks(width, 256, body)
        job = pool.add(grad_out, chunk * pool.rows, 0)
        gradient_into(job, hidden, low)
        job = pool.add(grad_in, 0, chunk * width)
        gradient_into(job, entry, grad_hidden)
        if often:
            pump()
        add_transposed(grad_hidden, weights.take(), total)
        if often or chunk % 2:
            pump()
def middle_rows(source, gain, grads, entry, sums, line):
    sums[pl.ds(line, 1), :] = jnp.zeros_like(sums[pl.ds(line, 1), :])

    def body(rows):
        normal, inverse = norm_parts(source[rows, :])
        middle = normal * gain
        logistic = jax.nn.sigmoid(middle)
        entry[rows, :] = (middle * logistic).astype(jnp.bfloat16)
        grad = grads[rows, :] * (logistic + middle * logistic * (1.0 - logistic))
        grad_normal = grad * gain
        grads[rows, :] = inverse * (
            grad_normal
            - jnp.mean(grad_normal, -1, keepdims=True)
            - normal * jnp.mean(grad_normal * normal, -1, keepdims=True)
        )
        sums[pl.ds(line, 1), :] += jnp.sum(grad * normal, 0, keepdims=True)

    row_blocks(source.shape[0], 128, body)


def depthwise_back(grads, taps, value, gate, grad_value, grad_gate, tap_sums, pump):
    total, width = value.shape
    tap_sums[...] = jnp.zeros_like(tap_sums)
    for column in range(width // LANES):
        lanes = pl.ds(column * LANES, LANES)

        def body(at, carry):
            first = pl.multiple_of(at * LANES, LANES)
            rows = pl.ds(first, LANES)
            held = value[rows, lanes].astype(jnp.float32)
            opened = jax.nn.sigmoid(gate[rows, lanes].astype(jnp.float32))
            glu = (held * opened).astype(jnp.bfloat16).astype(jnp.float32)
            grad = jnp.zeros((LANES, LANES), jnp.float32)
            window = grads[pl.ds(first, LANES + 32), lanes]
            for tap in range(KERNEL):
                ahead = KERNEL - 1 - tap
                moved = window[ahead : ahead + LANES]
                grad = grad + moved * taps[pl.ds(tap, 1), lanes]
                tap_sums[pl.ds(tap, 1), lanes] += jnp.sum(glu * moved, 0, keepdims=True)
            grad_value[rows, lanes] = (grad * opened).astype(jnp.bfloat16)
            grad_gate[rows, lanes] = (grad * held * opened * (1.0 - opened)).astype(jnp.bfloat16)
            return carry

        lax.fori_loop(0, total // LANES, body, 0)
        if column % 4 == 3:
            pump()


def fetch(source, target, sem):
    copy = pltpu.make_async_copy(source, target, sem)
    copy.start()
    return copy


def back_kernel(settings, *refs):
    count, clips, rows, limit = settings
    first_ref, table_ref, gains, taps, squares = refs[:5]
    refs = refs[1:]
    cot, x4, x3, x2, x1, x0, u1, u0, joined, summed = refs[4:14]
    mixed, query, keys, values, c_in, c_out, a_out, qkv = refs[14:22]
    second_in, second_out, w_in, w_out = refs[22:26]
    grad_x, tally = refs[26:28]
    refs = refs[:26] + (None, None) + refs[26:]
    to_second_out, to_second_in, to_conv_out, to_conv_in = refs[30:34]
    to_attn, to_q, to_k, to_v, to_out, to_in, kept = refs[34:41]
    refs = refs[41:]
    resid, total_ext, resid_in, low, entry, mixed_grad, q_ref, dq_ref = refs[:8]
    k_ref, v_ref, dk_ref, dv_ref, later, earlier, dk_sum, dv_sum, slots = refs[8:17]
    local, slot_sems, saved_sems, halo_sems, arrivals, tally_sems, dt_ref = refs[17:24]
    gain_sums, tap_sums = (tally.at[pl.ds(0, 8)], tally.at[pl.ds(8, 32)])
    width = resid.shape[1]
    total = total_ext.at[pl.ds(0, rows)]
    groups = lax.axis_size("group")
    part = width // groups
    span = lax.axis_size("seq")
    chunks = w_out.shape[1]
    reduce_greet()
    pool = Pool(part, width, count, kept, refs[24:])
    pump = pool.pump
    copies = module_copies(second_in, second_out, groups)
    copies += [lambda slot: [(c_out, slot)]]
    copies += [
        lambda slot, at=at: [(c_in.at[:, pl.ds(at * width, width)], slot)] for at in range(2)
    ]
    copies += [lambda slot: [(a_out, slot)]]
    copies += [lambda slot, at=at: [(qkv.at[at], slot)] for at in range(3)]
    copies += module_copies(w_in, w_out, groups)
    load = fetch(x4, resid_in, local.at[0])
    arrival = fetch(cot, low, local.at[1])
    weights = Stream([slots.at[at] for at in range(3)], slot_sems, copies)
    free = [ref.at[0, pl.ds(0, rows)] for ref in (k_ref, v_ref)]
    saved = Stream(free, saved_sems, saved_copies(u1, groups, part))
    halves = [ref.at[0, pl.ds(0, rows)] for ref in (dk_ref, dv_ref)]
    opening = [
        fetch(joined.at[:, pl.ds(at * width, width)], half, local.at[2 + at])
        for at, half in enumerate(halves)
    ]
    resid[...] = jnp.zeros_like(resid)
    arrival.wait()
    load.wait()

    def widen(at):
        total[at, :] = low[at, :].astype(jnp.float32)

    row_blocks(rows, 128, widen)
    norm_back_rows(resid_in, gains[pl.ds(5, 1), :], total, resid, gain_sums, 5)
    load = fetch(x3, resid_in, local.at[0])
    cast_rows(resid, low, 0.5)
    load.wait()
    norm_rows(resid_in, gains[pl.ds(4, 1), :], entry)
    buffers = (entry, low, mixed_grad, q_ref, total)
    module_back(
        pool, weights, saved, buffers, chunks, (to_second_in, to_second_out), False
    )
    norm_back_rows(resid_in, gains[pl.ds(4, 1), :], total, resid, gain_sums, 4)
    load = fetch(summed, resid_in, local.at[0])
    cast_rows(resid, low)
    transposed_rows(low, weights.take(), total)
    load.wait()
    middle_rows(resid_in, gains[pl.ds(3, 1), :], total, entry, gain_sums, 3)
    _, _, seq, _ = place()
    halo = pltpu.make_async_remote_copy(
        src_ref=total_ext.at[pl.ds(0, 32)],
        dst_ref=total_ext.at[pl.ds(rows, 32)],
        send_sem=halo_sems.at[0, 4],
        recv_sem=halo_sems.at[1, 4],
        device_id={"seq": (seq + span - 1) % span},
        device_id_type=MESH,
    )
    halo.start()
    load = fetch(x2, resid_in, local.at[0])
    job = pool.add(to_conv_out, 0, 0)
    gradient_into(job, entry, low)
    pump()
    for copy in opening:
        copy.wait()
    load.wait()
    norm_rows(resid_in, gains[pl.ds(2, 1), :], entry)
    halo.wait()
    beyond = pl.ds(rows, 32)
    nothing = jnp.zeros((32, width), jnp.float32)
    total_ext[beyond, :] = jnp.where(seq < span - 1, total_ext[beyond, :], nothing)
    depthwise_back(total_ext, taps, *halves, mixed_grad, q_ref, tap_sums, pump)
    total[...] = jnp.zeros_like(total)
    for at, flat in enumerate((mixed_grad, q_ref)):
        job = pool.add(to_conv_in, 0, at * width)
        gradient_into(job, entry, flat)
        add_transposed(flat, weights.take(), total)
        pump()
    norm_back_rows(resid_in, gains[pl.ds(2, 1), :], total, resid, gain_sums, 2)
    loads = [
        fetch(source, target, local.at[at])
        for at, (source, target) in enumerate(
            ((mixed, entry), (query, q_ref), (keys, k_ref), (values, v_ref), (x1, resid_in))
        )
    ]
    cast_rows(resid, low)
    transposed_rows(low, weights.take(), mixed_grad)
    loads[0].wait()
    job = pool.add(to_attn, 0, 0)
    gradient_into(job, entry, low)
    pump()
    for load in loads[1:]:
        load.wait()
    table = table_ref[...]
    across = lax.broadcasted_iota(jnp.int32, (2 * BLOCK, 2 * BLOCK), 0)
    across = across + lax.broadcasted_iota(jnp.int32, (2 * BLOCK, 2 * BLOCK), 1)
    flip = (across == 2 * BLOCK - 1).astype(jnp.float32).astype(jnp.bfloat16)
    dt_ref[...] = jnp.zeros_like(dt_ref)
    blocks = rows // BLOCK
    for pair in range(width // LANES):
        lanes = pl.ds(pair * LANES, LANES)
        dk_sum[...] = jnp.zeros_like(dk_sum)
        dv_sum[...] = jnp.zeros_like(dv_sum)

        def attend_block(at, carry):
            clip, block = (at // blocks, at % blocks)
            here = pl.ds(pl.multiple_of(at * BLOCK, BLOCK), BLOCK)
            near = pl.ds(pl.multiple_of(block * BLOCK, BLOCK), SPAN)
            key = k_ref[clip, near, lanes]
            value = v_ref[clip, near, lanes]
            mask = block_mask(first_ref[0], block, limit, 2 * BLOCK)
            q = stack_heads(q_ref[here, lanes])
            g = stack_heads(mixed_grad[here, lanes])
            probs = stacked_probs(q, key, table, mask)
            grad_probs = nt(g, value)
            grad_raw = probs * (grad_probs - jnp.sum(probs * grad_probs, -1, keepdims=True))
            grad_raw = grad_raw.astype(jnp.bfloat16)
            dv_sum[clip, near, :] += tn(probs.astype(jnp.bfloat16), g)
            dk_sum[clip, near, :] += tn(grad_raw, q)
            turned = roll_halves(nn(flip, grad_raw), SPAN - BLOCK + 1).astype(jnp.bfloat16)
            dt_ref[...] += tn(turned, nn(flip, q).astype(jnp.bfloat16))
            relative = nn(turned, table)
            relative = jnp.where(head_lanes(0), relative[BLOCK:], relative[:BLOCK])
            relative = nn(flip[:BLOCK, BLOCK:], relative.astype(jnp.bfloat16))
            direct = nn(grad_raw, key)
            direct = jnp.where(head_lanes(0), direct[:BLOCK], direct[BLOCK:])
            dq_ref[here, lanes] = ((direct + relative) * HEAD_DIM**-0.5).astype(jnp.bfloat16)
            return carry

        lax.fori_loop(0, clips * blocks, attend_block, 0, unroll=2)
        dk_ref[:, :, lanes] = (dk_sum[...] * HEAD_DIM**-0.5).astype(jnp.bfloat16)
        dv_ref[:, :, lanes] = dv_sum[...].astype(jnp.bfloat16)
        pump()

    saved = Stream(free, saved_sems, saved_copies(u0, groups, part))
    edges = []
    for at, ref in enumerate((dk_ref, dv_ref)):
        for way, (target, low_row, size, step) in enumerate(
            ((later, 0, LEFT, span - 1), (earlier, LEFT + rows, 2 * RIGHT, 1))
        ):
            edges.append(
                pltpu.make_async_remote_copy(
                    src_ref=ref.at[:, pl.ds(low_row, size)],
                    dst_ref=target.at[at],
                    send_sem=halo_sems.at[0, 2 * at + way],
                    recv_sem=halo_sems.at[1, 2 * at + way],
                    device_id={"seq": (seq + step) % span},
                    device_id_type=MESH,
                )
            )
    for edge in edges:
        edge.start()
    gain = gains[pl.ds(1, 1), :]
    norm_rows(resid_in, gain, entry)
    job = pool.add(to_q, 0, 0)
    gradient_into(job, entry, dq_ref)
    total[...] = jnp.zeros_like(total)
    add_transposed(dq_ref, weights.take(), total)
    pump()
    for edge in edges:
        edge.wait()
    for at, (ref, flat) in enumerate(((dk_ref, mixed_grad), (dv_ref, q_ref))):
        for clip in range(clips):
            base = clip * rows
            flat[pl.ds(base, rows), :] = ref[clip, pl.ds(LEFT, rows), :]
            tail = pl.ds(base + rows - LEFT, LEFT)
            zero_tail = jnp.zeros((LEFT, width), jnp.float32)
            came = jnp.where(seq < span - 1, later[at, clip].astype(jnp.float32), zero_tail)
            flat[tail, :] = (flat[tail, :].astype(jnp.float32) + came).astype(jnp.bfloat16)
            head = pl.ds(base, 2 * RIGHT)
            zero_head = jnp.zeros((2 * RIGHT, width), jnp.float32)
            came = jnp.where(seq > 0, earlier[at, clip].astype(jnp.float32), zero_head)
            flat[head, :] = (flat[head, :].astype(jnp.float32) + came).astype(jnp.bfloat16)
    for target, flat in ((to_k, mixed_grad), (to_v, q_ref)):
        job = pool.add(target, 0, 0)
        gradient_into(job, entry, flat)
        pump()
        add_transposed(flat, weights.take(), total)
        pump()
    norm_back_rows(resid_in, gain, total, resid, gain_sums, 1)
    load = pltpu.make_async_copy(x0, dq_ref, local.at[0])
    load.start()
    cast_rows(resid, low, 0.5)
    load.wait()
    gain = gains[pl.ds(0, 1), :]
    norm_rows(dq_ref, gain, entry)
    buffers = (entry, low, mixed_grad, q_ref, total)
    module_back(pool, weights, saved, buffers, chunks, (to_in, to_out), True)
    norm_back_rows(dq_ref, gain, total, resid, gain_sums, 0)
    cast_rows(resid, low)
    store = pltpu.make_async_copy(low, grad_x, local.at[1])
    store.start()
    for block in range(10):
        spot = pl.ds(40 + block // 8 * 8, 8)
        tally[spot, pl.ds(block % 8 * LANES, LANES)] = dt_ref[pl.ds(block * 8, 8), :]
    tally[pl.ds(48, 8), pl.ds(2 * LANES, width - 2 * LANES)] = jnp.zeros(
        (8, width - 2 * LANES), jnp.float32
    )
    tally[pl.ds(56, 8), :] = squares[...]
    for turn, peer in enumerate(partners()):
        copy = pltpu.make_async_remote_copy(
            src_ref=tally,
            dst_ref=arrivals.at[turn],
            send_sem=tally_sems.at[0, turn],
            recv_sem=tally_sems.at[1, turn],
            device_id=peer,
            device_id_type=MESH,
        )
        copy.start()
        pool.pump()
        copy.wait()
        tally[...] += arrivals[turn]
    pool.drain()
    store.wait()


def partners():
    group = lax.axis_index("group")
    peers = [{"replica": 1 - lax.axis_index("replica")}, {"seq": 1 - lax.axis_index("seq")}]
    bit = 1
    while bit < lax.axis_size("group"):
        peers.append({"group": group + bit * (1 - 2 * (group // bit % 2))})
        bit *= 2
    return peers


def reduce_greet():
    deep, across, _, twin = neighbours()
    span = lax.axis_size("seq")
    seq = lax.axis_index("seq")
    greet(deep + [across, twin] + [{"seq": (seq + steps) % span} for steps in range(1, span)])


def back(cot, resids, saved, kept, table, gains, taps, squares, weights, rows):
    joined, summed, u1, u0 = saved
    query, keys, values, mixed = kept
    c_in, c_out, a_out, qkv, second_in, second_out, w_in, w_out = weights
    clips, ext, width = keys.shape
    groups = lax.axis_size("group")
    part = width // groups
    chunks = w_out.shape[0] // width
    count = 7 + 4 * chunks
    first = lax.axis_index("seq").astype(jnp.int32)[None] * rows
    limit = rows * lax.axis_size("seq")
    hbm = pl.BlockSpec(memory_space=pl.ANY)
    vmem = pl.BlockSpec(memory_space=pltpu.VMEM)
    low = lambda *shape: jax.ShapeDtypeStruct(shape, jnp.bfloat16)
    wide = lambda *shape: jax.ShapeDtypeStruct(shape, jnp.float32)
    turns = 2 + (groups - 1).bit_length()
    holds = [pltpu.VMEM((rows + more, width), jnp.float32) for more in (0, 32, 0)]
    holds += [pltpu.VMEM((rows, width), jnp.bfloat16)] * 5
    holds += [pltpu.VMEM((clips, ext, width), jnp.bfloat16)] * 4
    holds += [
        pltpu.VMEM((2, clips, LEFT, width), jnp.bfloat16),
        pltpu.VMEM((2, clips, 2 * RIGHT, width), jnp.bfloat16),
        pltpu.VMEM((clips, ext, LANES), jnp.float32),
        pltpu.VMEM((clips, ext, LANES), jnp.float32),
        pltpu.VMEM((3, width, width), jnp.bfloat16),
        pltpu.SemaphoreType.DMA((6,)),
        pltpu.SemaphoreType.DMA((3, groups)),
        pltpu.SemaphoreType.DMA((2, groups)),
        pltpu.SemaphoreType.DMA((2, 5)),
        pltpu.VMEM((turns, 64, width), jnp.float32),
        pltpu.SemaphoreType.DMA((2, turns)),
        pltpu.VMEM((SPAN, LANES), jnp.float32),
    ]
    grad_out = low(chunks * part, width)
    grad_in = low(part, chunks * width)
    by_chunk = lambda weight: weight.reshape(groups, chunks, part, width)
    results = pl.pallas_call(
        functools.partial(back_kernel, (count, clips, rows, limit)),
        in_specs=[pl.BlockSpec(memory_space=pltpu.SMEM)] + [vmem] * 4 + [hbm] * 22,
        out_specs=[hbm, vmem] + [hbm] * 11,
        out_shape=[low(rows, width), wide(64, width)]
        + [grad_out, grad_in, low(part, width), low(part, 2 * width)]
        + [low(part, width)] * 4
        + [grad_out, grad_in, low(count, groups // 2, 2, part, width)],
        scratch_shapes=holds + Pool.scratch(part, width, count),
        compiler_params=pltpu.CompilerParams(
            collective_id=3, has_side_effects=True, vmem_limit_bytes=63 << 20
        ),
        name="back",
    )(
        first,
        wide_table(table),
        gains,
        taps,
        squares,
        cot,
        *resids,
        u1,
        u0,
        joined,
        summed,
        mixed,
        query.reshape(rows, width),
        keys,
        values,
        c_in,
        c_out,
        a_out,
        qkv,
        second_in,
        by_chunk(second_out),
        w_in,
        by_chunk(w_out),
    )
    grad_x, tally = results[:2]
    tables = tally[40:56].reshape(2, 8, width // LANES, LANES).transpose(0, 2, 1, 3)
    dt = tables.reshape(-1, LANES)
    dt = (dt[:WIN, :HEAD_DIM] + dt[:WIN, HEAD_DIM:]) * HEAD_DIM**-0.5
    return grad_x, tally, dt, results[2:]


def unmix(grad, groups):
    rows, width = grad.shape
    chunks = width // (rows * groups)
    return grad.reshape(rows, chunks, groups, rows).transpose(0, 2, 1, 3).reshape(rows, width)


def feed_forward(resid, gain, w_in, w_out):
    normed, normal, inverse = norm_forward(resid, gain)
    entry = normed.astype(jnp.bfloat16)
    hidden_pre = matmul(entry, w_in)
    hidden = (hidden_pre * jax.nn.sigmoid(hidden_pre)).astype(jnp.bfloat16)
    return (matmul(hidden, w_out), (normal, inverse, entry, hidden_pre, hidden))


def feed_back(grad_branch, kept, gain, w_in, w_out):
    normal, inverse, entry, hidden_pre, hidden = kept
    grad_low = grad_branch.astype(jnp.bfloat16)
    grad_w_out = matmul_left_t(hidden, grad_low).astype(jnp.bfloat16)
    grad_hidden = (matmul_right_t(grad_low, w_out) * swish_grad(hidden_pre)).astype(jnp.bfloat16)
    grad_w_in = matmul_left_t(entry, grad_hidden).astype(jnp.bfloat16)
    grad_in, grad_gain = norm_backward(matmul_right_t(grad_hidden, w_in), normal, inverse, gain)
    return (grad_in, grad_gain, grad_w_in, grad_w_out)


def attention_forward(resid, gain, qkv, attn_out, table, shape):
    clips, rows, width = shape
    normed, normal, inverse = norm_forward(resid, gain)
    entry = normed.astype(jnp.bfloat16)
    query, keys, values = [
        matmul(entry, qkv[part]).astype(jnp.bfloat16).reshape(shape) for part in range(3)
    ]
    tail = jnp.zeros((clips, BACK_PAD - RIGHT, width), jnp.bfloat16)

    def extend(value):
        before = from_behind(value[:, rows - LEFT :], "seq", 1)
        after = from_behind(value[:, :RIGHT], "seq", -1)
        return jnp.concatenate([before, value, after, tail], 1)

    keys, values = (extend(keys), extend(values))
    mixed = attend(query, keys, values, table, rows).reshape(clips * rows, width)
    return (matmul(mixed, attn_out), (normal, inverse, entry, query, keys, values, mixed))


def attention_back(grad_branch, kept, gain, qkv, attn_out, table, shape):
    clips, rows, width = shape
    normal, inverse, entry, query, keys, values, mixed = kept
    grad_low = grad_branch.astype(jnp.bfloat16)
    grad_attn_out = matmul_left_t(mixed, grad_low).astype(jnp.bfloat16)
    grad_mixed = matmul_right_t(grad_low, attn_out).astype(jnp.bfloat16).reshape(shape)
    grad_query, grad_keys, grad_values, grad_table = attend_back(
        query, keys, values, table, grad_mixed, rows
    )

    def fold(grad):
        from_later = from_behind(grad[:, :LEFT], "seq", -1).astype(jnp.float32)
        from_earlier = from_behind(grad[:, LEFT + rows : LEFT + rows + RIGHT], "seq", 1)
        own = grad[:, LEFT : LEFT + rows].astype(jnp.float32)
        own = own + jnp.pad(from_later, ((0, 0), (rows - LEFT, 0), (0, 0)))
        own = own + jnp.pad(from_earlier.astype(jnp.float32), ((0, 0), (0, rows - RIGHT), (0, 0)))
        return own.astype(jnp.bfloat16).reshape(clips * rows, width)

    parts = [grad_query.reshape(clips * rows, width), fold(grad_keys), fold(grad_values)]
    grad_qkv = [matmul_left_t(entry, part).astype(jnp.bfloat16) for part in parts]
    grad_entry = sum(matmul_right_t(part, qkv[at]) for at, part in enumerate(parts))
    grad_in, grad_gain = norm_backward(grad_entry, normal, inverse, gain)
    return (grad_in, grad_gain, grad_qkv, grad_attn_out, grad_table)


def conv_forward(resid, gain_in, gain_mid, conv_in, depthwise, conv_out, shape):
    clips, rows, width = shape
    normed, normal, inverse = norm_forward(resid, gain_in)
    entry = normed.astype(jnp.bfloat16)
    joined = matmul(entry, conv_in)
    opened = jax.nn.sigmoid(joined[:, width:])
    glu = (joined[:, :width] * opened).astype(jnp.bfloat16).reshape(clips, rows, width)
    before = from_behind(glu[:, rows - (KERNEL - 1) :], "seq", 1)
    padded = jnp.concatenate([before, glu], 1).astype(jnp.float32)
    taps = depthwise.astype(jnp.float32)
    summed = jnp.zeros((clips, rows, width), jnp.float32)
    for tap in range(KERNEL):
        summed = summed + taps[tap] * padded[:, tap : tap + rows]
    middle, mid_normal, mid_inverse = norm_forward(summed.reshape(clips * rows, width), gain_mid)
    swished = (middle * jax.nn.sigmoid(middle)).astype(jnp.bfloat16)
    kept = (
        normal,
        inverse,
        entry,
        joined,
        opened,
        padded,
        middle,
        mid_normal,
        mid_inverse,
        swished,
    )
    return (matmul(swished, conv_out), summed.reshape(clips * rows, width), kept)


def conv_back(grad_branch, kept, gain_in, gain_mid, conv_in, depthwise, conv_out, shape):
    clips, rows, width = shape
    normal, inverse, entry, joined, opened, padded, middle, mid_normal, mid_inverse, swished = kept
    taps = depthwise.astype(jnp.float32)
    grad_low = grad_branch.astype(jnp.bfloat16)
    grad_conv_out = matmul_left_t(swished, grad_low).astype(jnp.bfloat16)
    grad_middle = matmul_right_t(grad_low, conv_out) * swish_grad(middle)
    grad_summed, grad_gain_mid = norm_backward(grad_middle, mid_normal, mid_inverse, gain_mid)
    grad_summed = grad_summed.reshape(clips, rows, width)
    grad_taps = jnp.stack(
        [jnp.sum(grad_summed * padded[:, tap : tap + rows], (0, 1)) for tap in range(KERNEL)]
    )
    grad_padded = jnp.zeros((clips, rows + KERNEL - 1, width), jnp.float32)
    for tap in range(KERNEL):
        grad_padded = grad_padded + jnp.pad(
            grad_summed * taps[tap], ((0, 0), (tap, KERNEL - 1 - tap), (0, 0))
        )
    from_later = from_behind(grad_padded[:, : KERNEL - 1].astype(jnp.bfloat16), "seq", -1).astype(
        jnp.float32
    )
    grad_glu = (
        grad_padded[:, KERNEL - 1 :]
        .at[:, rows - (KERNEL - 1) :]
        .add(from_later)
        .reshape(clips * rows, width)
    )
    value_part = joined[:, :width]
    grad_joined = jnp.concatenate(
        [grad_glu * opened, grad_glu * value_part * opened * (1.0 - opened)], 1
    )
    grad_joined = grad_joined.astype(jnp.bfloat16)
    grad_conv_in = matmul_left_t(entry, grad_joined).astype(jnp.bfloat16)
    grad_in, grad_gain_in = norm_backward(
        matmul_right_t(grad_joined, conv_in), normal, inverse, gain_in
    )
    return (grad_in, grad_gain_in, grad_gain_mid, grad_conv_in, grad_taps, grad_conv_out)


def on_device(
    tokens,
    ffn_in,
    ffn_out,
    qkv,
    attn_out,
    conv_in,
    conv_out,
    depthwise,
    gains,
    rel_table,
    cotangent,
):
    clips, rows, width = tokens.shape
    shape = (clips, rows, width)
    flat_rows = clips * rows
    halve = lax.axis_size("seq") == 2
    norms, taps = (gains.shape[0], depthwise.shape[0])
    lines = -(-(norms + taps) // 16) * 16
    small = jnp.concatenate([gains, depthwise], 0)
    small = jnp.pad(small, ((0, lines - norms - taps), (0, 0)))[None]
    shards = (small, ffn_in, ffn_out, qkv, attn_out[None], conv_in[None], conv_out[None])
    sources = (
        (0, 0, 1),
        (1, 0, 1),
        (2, 0, 1),
        (3, 0, 3),
        (4, 0, 1),
        (5, 0, 1),
        (6, 0, 1),
        (1, 1, 1),
        (2, 1, 1),
    )
    quick = halve and clips == 1 and gains.shape[1] % LANES == 0
    if quick:
        flat = tokens.reshape(flat_rows, width)
        gathered, saved = forward(flat, shards, sources, norms, rel_table, halve)
    else:
        gathered = gather_weights(shards, sources, halve)
    small = gathered[0].reshape(-1, lines, gains.shape[1]).transpose(1, 0, 2).reshape(lines, width)
    gain_f = small[:norms].astype(jnp.float32)
    depth = small[norms : norms + taps]
    f_in = (gathered[1][0], gathered[7][0])
    f_out = (gathered[2][0], gathered[8][0])
    proj, a_out, c_in, c_out = (gathered[3], gathered[4][0], gathered[5][0], gathered[6][0])
    if quick:
        result, squares, x1, x2, x3, x4, u0, u1, query, keys, values, mixed, joined, summed = saved
        grad, totals, total_table, shares = back(
            cotangent.reshape(flat_rows, width),
            (x4, x3, x2, x1, flat),
            (joined, summed, u1, u0),
            (query, keys, values, mixed),
            rel_table,
            small[:8].astype(jnp.float32),
            jnp.pad(depth.astype(jnp.float32), ((0, 32 - taps), (0, 0))),
            squares,
            (c_in, c_out, a_out, proj, f_in[1], f_out[1], f_in[0], f_out[0]),
            rows,
        )
        sums = jnp.sum(totals[56:61], 1)
        totals = jnp.concatenate([totals[:norms], totals[8 : 8 + taps]], 0)
        groups = lax.axis_size("group")
        grad_in_first, grad_in_second = (unmix(shares[9], groups), unmix(shares[1], groups))
        grad_out_first, grad_out_second = (shares[8], shares[0])
        grad_conv_out, grad_conv_in, grad_attn_out = shares[2:5]
        grad_qkv = shares[5:8]
    else:
        start = tokens.reshape(flat_rows, width).astype(jnp.float32)
        first_branch, first_kept = feed_forward(start, gain_f[0], f_in[0], f_out[0])
        after_first = start + 0.5 * first_branch
        attn_branch, attn_kept = attention_forward(
            after_first, gain_f[1], proj, a_out, rel_table, shape
        )
        after_attn = after_first + attn_branch
        conv_branch, summed, conv_kept = conv_forward(
            after_attn, gain_f[2], gain_f[3], c_in, depth, c_out, shape
        )
        after_conv = after_attn + conv_branch
        second_branch, second_kept = feed_forward(after_conv, gain_f[4], f_in[1], f_out[1])
        final = after_conv + 0.5 * second_branch
        result, final_normal, final_inverse = norm_forward(final, gain_f[5])
        squares = jnp.stack(
            [
                jnp.sum(member * member)
                for member in (final, first_branch, attn_branch, conv_branch, second_branch)
            ]
        )
        grad = cotangent.reshape(flat_rows, width).astype(jnp.float32)
        grad, grad_gain_final = norm_backward(grad, final_normal, final_inverse, gain_f[5])
        back_in, grad_gain_second, grad_in_second, grad_out_second = feed_back(
            0.5 * grad, second_kept, gain_f[4], f_in[1], f_out[1]
        )
        grad = grad + back_in
        back_in, grad_gain_conv, grad_gain_mid, grad_conv_in, grad_taps, grad_conv_out = conv_back(
            grad, conv_kept, gain_f[2], gain_f[3], c_in, depth, c_out, shape
        )
        grad = grad + back_in
        back_in, grad_gain_attn, grad_qkv, grad_attn_out, grad_table = attention_back(
            grad, attn_kept, gain_f[1], proj, a_out, rel_table, shape
        )
        grad = grad + back_in
        back_in, grad_gain_first, grad_in_first, grad_out_first = feed_back(
            0.5 * grad, first_kept, gain_f[0], f_in[0], f_out[0]
        )
        grad = grad + back_in
        matrices = [grad_in_first, grad_in_second, grad_out_first, grad_out_second]
        matrices += [grad_attn_out, grad_conv_in, grad_conv_out] + grad_qkv
        matrices = [
            lax.psum(lax.psum_scatter(member, "group", tiled=True), ("seq", "replica"))
            for member in matrices
        ]
        grad_in_first, grad_in_second, grad_out_first, grad_out_second = matrices[:4]
        grad_attn_out, grad_conv_in, grad_conv_out = matrices[4:7]
        grad_qkv = matrices[7:]
        gain_grads = jnp.stack(
            [
                grad_gain_first,
                grad_gain_attn,
                grad_gain_conv,
                grad_gain_mid,
                grad_gain_second,
                grad_gain_final,
            ]
        )
        loose = jnp.concatenate([grad_table.reshape(-1), squares])
        lines = -(-loose.shape[0] // width)
        loose = jnp.pad(loose, (0, lines * width - loose.shape[0])).reshape(lines, width)
        totals = butterfly(jnp.concatenate([gain_grads, grad_taps, loose], 0))
        loose = totals[norms + taps :].reshape(-1)
        totals = totals[: norms + taps]
        table_size = rel_table.shape[0] * rel_table.shape[1]
        total_table = loose[:table_size].reshape(rel_table.shape)
        sums = loose[table_size : table_size + 5]
    owned = lax.dynamic_slice_in_dim(
        totals, lax.axis_index("group") * gains.shape[1], gains.shape[1], 1
    )
    count = (
        flat_rows * width * lax.axis_size("seq") * lax.axis_size("group") * lax.axis_size("replica")
    )
    stats = jnp.sqrt(sums / count)
    return (
        result.astype(jnp.bfloat16).reshape(shape),
        grad.astype(jnp.bfloat16).reshape(shape),
        jnp.stack([grad_in_first, grad_in_second]).astype(jnp.float32),
        jnp.stack([grad_out_first, grad_out_second]).astype(jnp.float32),
        jnp.stack(grad_qkv).astype(jnp.float32),
        grad_attn_out.astype(jnp.float32),
        grad_conv_in.astype(jnp.float32),
        grad_conv_out.astype(jnp.float32),
        owned[norms:],
        owned[:norms],
        total_table,
        stats,
    )


def solution(mesh):
    in_specs = (
        P(("group", "replica"), "seq", None),
        P(None, "group", None),
        P(None, "group", None),
        P(None, "group", None),
        P("group", None),
        P("group", None),
        P("group", None),
        P(None, "group"),
        P(None, "group"),
        P(),
        P(("group", "replica"), "seq", None),
    )
    out_specs = (
        P(("group", "replica"), "seq", None),
        P(("group", "replica"), "seq", None),
        P(None, "group", None),
        P(None, "group", None),
        P(None, "group", None),
        P("group", None),
        P("group", None),
        P("group", None),
        P(None, "group"),
        P(None, "group"),
        P(),
        P(),
    )
    return jax.shard_map(
        on_device, mesh=mesh, in_specs=in_specs, out_specs=out_specs, check_vma=False
    )
```
